32 devices in a mesh: grp: 8 (over y, x, core), cli: 4 (over z).
Axes of the slice: x: 2, y: 2, z: 4, core: 2. Of those that a mesh axis runs over, the one named last changes fastest.
Arguments:
- token_ids: int32 [32, 128], P(('grp', 'cli')), may hold values from 0 to 51199
- target_ids: int32 [32, 128], P(('grp', 'cli')), may hold values from 0 to 51199
- segment_ids: int32 [32, 128], P(('grp', 'cli')), may hold values from 0 to 3, never falling along the last dimension, each value on 1 to 64 neighbouring positions
- chosen: int32 [32], P(('grp', 'cli')), may hold values from 0 to 3, as said below
- table: float32 [4, 51200, 768], P(None, ('grp', 'cli')), may hold values from -0.4375 to 0.4375
- table_momentum: float32 [4, 51200, 768], P(None, ('grp', 'cli')), may hold values from -0.00390625 to 0.00390625
- stack: float32 [4, 9344, 768], P(None, ('grp', 'cli')), may hold values from -0.21875 to 0.21875
- stack_momentum: float32 [4, 9344, 768], P(None, ('grp', 'cli')), may hold values from -0.009765625 to 0.009765625
- vectors: float32 [4, 14, 768], replicated, may hold values from -1 to 1.4
- vector_momentum: float32 [4, 14, 768], replicated, may hold values from -0.0546875 to 0.0546875
Outputs:
- loss: float32 [], replicated
- client_losses: float32 [32, 4], P(('grp', 'cli'))
- table_grad: float32 [4, 51200, 768], P(None, ('grp', 'cli'))
- table_momentum_new: float32 [4, 51200, 768], P(None, ('grp', 'cli'))
- table_new: float32 [4, 51200, 768], P(None, ('grp', 'cli'))
- stack_grad: float32 [4, 9344, 768], P(None, ('grp', 'cli'))
- stack_momentum_new: float32 [4, 9344, 768], P(None, ('grp', 'cli'))
- stack_new: float32 [4, 9344, 768], P(None, ('grp', 'cli'))
- vector_grad: float32 [4, 14, 768], replicated
- vector_momentum_new: float32 [4, 14, 768], replicated
- vector_new: float32 [4, 14, 768], replicated
The draws below stay inside these ranges and needn't reach their ends.
Inputs may be any that keep to these rules, and one draw needn't show every extreme that they name: Every one of the 4 models is chosen by at least one client.
All inputs are finite; a program needn't handle non-finite values.
Results may differ from the reference program's by a relative error of at most 0.0095.
Values may be sent and summed in bfloat16 or wider, within the bound.
A program may use at most 1 GiB of HBM per device.

```python
import math
import jax
import jax.numpy as jnp
import numpy as np
from jax import lax

D = 768
HEADS = 12
HEAD_DIM = 64
FF = 3072
V = 51200
K = 4
NVEC = 14
SEQ = 128
CLIENTS = 32
MC = 9344
N_GRP = 8
N_CLI = 4


def draw_chosen(key, part):
    first, second = jax.random.split(key)
    base = jax.random.randint(first, (N_GRP * N_CLI,), 0, K, dtype=jnp.int32)
    order = jax.random.permutation(second, N_GRP * N_CLI)
    return base.at[order[:K]].set(jnp.arange(K, dtype=jnp.int32))


def draw_vectors(key, part):
    first, second = jax.random.split(key)
    gains = jnp.clip(1.0 + 0.12 * jax.random.normal(first, (K, NVEC, D), jnp.float32), 0.6, 1.4)
    shifts = jnp.clip(0.2 * jax.random.normal(second, (K, NVEC, D), jnp.float32), -1.0, 1.0)
    row_index = jnp.arange(NVEC)[None, :, None]
    is_gain = (row_index == 0) | (row_index == 2) | (row_index == 4)
    return jnp.where(is_gain, gains, shifts)


def set_ends(array, own_key, low, high):
    spot = [jax.random.randint(jax.random.fold_in(own_key, axis), (), 0, length) for axis, length in enumerate(array.shape)]
    main_axis = array.shape.index(max(array.shape))
    beside = spot[:main_axis] + [(spot[main_axis] + 1) % array.shape[main_axis]] + spot[main_axis + 1:]
    return array.at[tuple(spot)].set(low).at[tuple(beside)].set(high)


def block_levels(stream_key, shape, shards, low, top_value):
    def one(position, shards_of):
        steps = jax.random.uniform(jax.random.fold_in(jax.random.fold_in(stream_key, 6), position), (shards_of,), jnp.float32, low / len(shards), top_value / len(shards))
        return jnp.repeat(jnp.exp(steps), shape[position] // shards_of).reshape((-1,) + (1,) * (len(shape) - position - 1))

    loudness = one(*shards[0])
    for cut in shards[1:]:
        loudness = loudness * one(*cut)
    return loudness


def rank_table(amount, slope):
    weights = [(1 << 20) // math.isqrt(standing ** slope) + 1 for standing in range(1, amount + 1)]
    width = 1 + sum(weights) // (1 << 30)
    return np.cumsum(np.array([max(1, weight // width) for weight in weights]))


def ranked(own_key, extent, number_of, skew):
    listing = rank_table(number_of, skew)
    lot = jax.random.randint(jax.random.fold_in(own_key, 1), extent, 0, int(listing[number_of - 1]))
    standing = jnp.searchsorted(jnp.asarray(listing, jnp.int32), lot, side="right")
    return jax.random.permutation(jax.random.fold_in(own_key, 2), number_of)[standing].astype(jnp.int32)


def profile(amount, total, most, skew):
    loads = [(1 << 20) // math.isqrt(grade ** skew) + 1 for grade in range(2, amount + 1)]
    spare, given = total - most - (amount - 1), [1] * (amount - 1)
    while spare > 0:
        candidates = [i for i in range(amount - 1) if given[i] < most]
        mass, budget = sum([loads[i] for i in candidates]), spare
        for i in candidates:
            extra = min(most - given[i], max(1, budget * loads[i] // mass), spare)
            given[i] = given[i] + extra
            spare = spare - extra
    return np.array([most] + given)


def uneven_parts(own_key, amount, total, most, slope):
    if amount == 2:
        one = jax.random.randint(own_key, (), max(1, total - most), min(most, total - 1) + 1)
        return jnp.stack([one, total - one])
    lengths = jnp.asarray(profile(amount, total, most, slope), jnp.int32)
    pairs = (amount - 1) // 2
    donor, taker = lengths[1:1 + 2 * pairs:2], lengths[2:2 + 2 * pairs:2]
    slack = jnp.minimum(donor - 1, most - taker)
    moved = jax.random.randint(jax.random.fold_in(own_key, 1), (pairs,), 0, 1 << 20) % (slack + 1)
    lengths = lengths.at[1:1 + 2 * pairs:2].set(donor - moved).at[2:2 + 2 * pairs:2].set(taker + moved)
    return lengths[jax.random.permutation(jax.random.fold_in(own_key, 2), amount)]


def bell_draw(rng, dims, scale, bound, shards=(), held_as=jnp.bfloat16):
    values = jax.random.normal(rng, dims, jnp.float32) * scale
    if len(shards) > 0:
        values = block_levels(rng, dims, shards, -0.22, 0.18) * values
    return jnp.clip(values, min=-bound, max=bound).astype(held_as)


def setup_inputs(seed: int = 0) -> dict:
    keys = jax.random.split(jax.random.key(seed), 11)
    token_ids = set_ends(ranked(keys[0], (CLIENTS, SEQ), V, 2), jax.random.fold_in(keys[0], 3), 0, V - 1).astype(jnp.int32)
    target_ids = set_ends(ranked(keys[1], (CLIENTS, SEQ), V, 2), jax.random.fold_in(keys[1], 3), 0, V - 1).astype(jnp.int32)
    segment_ids = jax.vmap(lambda own: jnp.searchsorted(jnp.cumsum(uneven_parts(own, SEQ // 32, SEQ, SEQ // 2, 1)), jnp.arange(SEQ), side="right"))(jax.random.split(keys[2], CLIENTS)).reshape((CLIENTS, SEQ)).astype(jnp.int32)
    chosen = draw_chosen(jax.random.fold_in(keys[10], 71), 0)
    table = bell_draw(keys[4], (K, V, D), (D // 4) ** -0.5, 0.4375, ((1, 32),), jnp.float32)
    table_momentum = bell_draw(keys[5], (K, V, D), (0.02 * (K / (SEQ * N_GRP * N_CLI)) ** 0.5), 0.00390625, ((1, 32),), jnp.float32)
    stack = bell_draw(keys[6], (K, MC, D), D ** -0.5, 0.21875, ((1, 32),), jnp.float32)
    stack_momentum = bell_draw(keys[7], (K, MC, D), (0.05 * (K / (SEQ * N_GRP * N_CLI)) ** 0.5), 0.009765625, ((1, 32),), jnp.float32)
    vectors = draw_vectors(jax.random.fold_in(keys[10], 71), 0)
    vector_momentum = bell_draw(keys[9], (K, NVEC, D), (0.3 * (K / (SEQ * N_GRP * N_CLI)) ** 0.5), 0.0546875, (), jnp.float32)
    return {"token_ids": token_ids, "target_ids": target_ids, "segment_ids": segment_ids, "chosen": chosen, "table": table, "table_momentum": table_momentum, "stack": stack, "stack_momentum": stack_momentum, "vectors": vectors, "vector_momentum": vector_momentum}


exact_mode = lax.Precision.HIGHEST
epsilon = 1e-05
momentum_decay = 0.9
table_rate = 4.0
stack_rate = 4.0
vector_rate = 50.0

@jax.custom_vjp
def low(v):
    return lax.optimization_barrier(v.astype(jnp.bfloat16)).astype(jnp.float32)

@jax.custom_vjp
def low_back(v):
    return v

def low_keep(v):
    return (low(v), None)

def low_pass(kept, grad):
    return (grad,)

def back_keep(v):
    return (v, None)

def back_low(kept, grad):
    return (low(grad),)
low.defvjp(low_keep, low_pass)
low_back.defvjp(back_keep, back_low)

def layer_norm(inputs, gain_row, shift_row):
    centred = inputs - lax.optimization_barrier(jnp.mean(inputs, -1, keepdims=True))
    spread = lax.optimization_barrier(jnp.mean(centred * centred, -1, keepdims=True))
    return centred * lax.rsqrt(spread + epsilon) * gain_row + shift_row

def rounded(inputs):
    return low_back(low(inputs))

def project(inputs, matrix):
    return jnp.dot(inputs, matrix.T, precision=exact_mode)

def token_losses(table_one, stack_one, vector_one, token_row, target_row, segment_row):
    table_low = low(table_one)
    stack_low = low(stack_one)
    embedded = low_back(table_low[token_row])
    inputs = embedded + stack_low[12 * D:]
    normed = low(layer_norm(inputs, vector_one[0], vector_one[1]))
    queries = rounded(project(normed, stack_low[0:D]) + vector_one[6])
    key_rows = rounded(project(normed, stack_low[D:2 * D]))
    values = rounded(project(normed, stack_low[2 * D:3 * D]) + vector_one[7])
    head_shape = (SEQ, HEADS, HEAD_DIM)
    scores = jnp.einsum('qhd,khd->hqk', queries.reshape(head_shape), key_rows.reshape(head_shape), precision=exact_mode) * HEAD_DIM ** (-0.5)
    scores = low_back(scores)
    positions = jnp.arange(SEQ)
    allowed = (positions[None, :] <= positions[:, None]) & (segment_row[None, :] == segment_row[:, None])
    attention = jax.nn.softmax(jnp.where(allowed[None], scores, -1e+30), axis=-1)
    mixture = jnp.einsum('hqk,khd->qhd', low(attention), values.reshape(head_shape), precision=exact_mode).reshape(SEQ, D)
    mixture = rounded(mixture)
    middle = inputs + low_back(project(mixture, stack_low[3 * D:4 * D]) + vector_one[8])
    normed_two = low(layer_norm(middle, vector_one[2], vector_one[3]))
    hidden = low_back(project(normed_two, stack_low[4 * D:8 * D]) + vector_one[10:14].reshape(FF))
    active = low(jax.nn.gelu(hidden, approximate=True))
    residual = middle + low_back(jnp.dot(active, stack_low[8 * D:12 * D], precision=exact_mode) + vector_one[9])
    normed_out = low(layer_norm(residual, vector_one[4], vector_one[5]))
    logits = low_back(project(normed_out, table_low))
    return jax.nn.logsumexp(logits, axis=-1) - jnp.take_along_axis(logits, target_row[:, None], axis=-1)[:, 0]

def update(weight, momentum, gradient, step_rate):
    renewed = momentum_decay * momentum + gradient
    return (renewed, weight - step_rate * (gradient + momentum_decay * renewed))

def reference(token_ids, target_ids, segment_ids, chosen, table, table_momentum, stack, stack_momentum, vectors, vector_momentum):
    valid_mask = jnp.concatenate([(segment_ids[:, :-1] == segment_ids[:, 1:]).astype(jnp.float32), jnp.zeros((CLIENTS, 1), jnp.float32)], axis=1)
    counts = lax.optimization_barrier(jnp.sum(valid_mask, axis=1))
    choice_table = (chosen[:, None] == jnp.arange(K, dtype=jnp.int32)[None, :]).astype(jnp.float32)
    totals = lax.optimization_barrier(jnp.sum(choice_table * counts[:, None], axis=0))

    def evaluate(element):
        token_row, target_row, segment_row, valid_row, count_row = element

        def one_model(params):
            losses = token_losses(params[0], params[1], params[2], token_row, target_row, segment_row)
            return jnp.sum(losses * valid_row) / count_row
        return lax.map(one_model, (table, stack, vectors))
    client_losses = lax.map(evaluate, (token_ids, target_ids, segment_ids, valid_mask, counts))

    def objective(table_all, stack_all, vector_all):

        def per_client(running, element):
            token_row, target_row, segment_row, valid_row, model_index = element
            losses = token_losses(table_all[model_index], stack_all[model_index], vector_all[model_index], token_row, target_row, segment_row)
            return (running + jnp.sum(losses * valid_row) / totals[model_index], None)
        running, _ = lax.scan(jax.checkpoint(per_client), jnp.zeros((), jnp.float32), (token_ids, target_ids, segment_ids, valid_mask, chosen))
        return running
    loss, pullback = jax.vjp(objective, table, stack, vectors)
    table_grad, stack_grad, vector_grad = pullback(jnp.ones((), jnp.float32))
    table_momentum_new, table_new = update(table, table_momentum, table_grad, table_rate)
    stack_momentum_new, stack_new = update(stack, stack_momentum, stack_grad, stack_rate)
    vector_momentum_new, vector_new = update(vectors, vector_momentum, vector_grad, vector_rate)
    return (loss, client_losses, table_grad, table_momentum_new, table_new, stack_grad, stack_momentum_new, stack_new, vector_grad, vector_momentum_new, vector_new)
```

```python
import functools

import jax
import jax.numpy as jnp
from jax import lax
from jax.experimental import pallas as pl
from jax.experimental.pallas import tpu as pltpu
from jax.sharding import PartitionSpec as P

HEADS = 12
HEAD_DIM = 64


epsilon = 1e-05
momentum_decay = 0.9
table_rate = 4.0
stack_rate = 4.0
vector_rate = 50.0

ROUND_ROWS = 128
MIB = 1 << 20


def layer_norm(inputs, gain_row, shift_row):
    centred = inputs - jnp.mean(inputs, -1, keepdims=True)
    spread = jnp.mean(centred * centred, -1, keepdims=True)
    return centred * lax.rsqrt(spread + epsilon) * gain_row + shift_row


def project(inputs, matrix):
    return lax.dot_general(
        inputs, matrix, (((1,), (1,)), ((), ())), preferred_element_type=jnp.float32
    )


def product(inputs, matrix):
    return jnp.dot(inputs, matrix, preferred_element_type=jnp.float32)


def outer_rows(left, right):
    return lax.dot_general(
        left, right, (((0,), (0,)), ((), ())), preferred_element_type=jnp.float32
    )


def split_heads(rows, seq_len):
    return rows.reshape(-1, seq_len, HEADS, HEAD_DIM)


def attend(queries, key_rows, segment_rows):
    seq_len = segment_rows.shape[1]
    scores = jnp.einsum(
        "nqhd,nkhd->nhqk",
        split_heads(queries, seq_len),
        split_heads(key_rows, seq_len),
        preferred_element_type=jnp.float32,
    ) * HEAD_DIM ** (-0.5)
    positions = jnp.arange(seq_len)
    allowed = (positions[None, None, :] <= positions[None, :, None]) & (
        segment_rows[:, None, :] == segment_rows[:, :, None]
    )
    return jax.nn.softmax(jnp.where(allowed[:, None], scores, -1e30), axis=-1)


def layer_forward(weights, vector_one, inputs, segment_rows):
    row_count, model_width = inputs.shape
    seq_len = segment_rows.shape[1]
    normed = layer_norm(inputs, vector_one[0], vector_one[1]).astype(jnp.bfloat16)
    queries = (project(normed, weights[0:model_width]) + vector_one[6]).astype(jnp.bfloat16)
    key_rows = project(normed, weights[model_width : 2 * model_width]).astype(jnp.bfloat16)
    values = (project(normed, weights[2 * model_width : 3 * model_width]) + vector_one[7]).astype(
        jnp.bfloat16
    )
    attention = attend(queries, key_rows, segment_rows)
    mixture = jnp.einsum(
        "nhqk,nkhd->nqhd",
        attention.astype(jnp.bfloat16),
        split_heads(values, seq_len),
        preferred_element_type=jnp.float32,
    )
    mixture = mixture.reshape(row_count, model_width).astype(jnp.bfloat16)
    middle = inputs + (project(mixture, weights[3 * model_width : 4 * model_width]) + vector_one[8])
    normed_two = layer_norm(middle, vector_one[2], vector_one[3]).astype(jnp.bfloat16)
    hidden = project(normed_two, weights[4 * model_width : 8 * model_width]) + vector_one[
        10:14
    ].reshape(-1)
    active = jax.nn.gelu(hidden, approximate=True).astype(jnp.bfloat16)
    residual = middle + (
        product(active, weights[8 * model_width : 12 * model_width]) + vector_one[9]
    )
    normed_out = layer_norm(residual, vector_one[4], vector_one[5]).astype(jnp.bfloat16)
    return (
        normed,
        queries,
        key_rows,
        values,
        attention,
        mixture,
        middle,
        normed_two,
        hidden,
        active,
        residual,
        normed_out,
    )


def norm_grad(operand, gain_row, shift_row, cotangent):
    outcome, pullback = jax.vjp(layer_norm, operand, gain_row, shift_row)
    return pullback(cotangent)


def gelu_tanh(hidden):
    return jax.nn.gelu(hidden, approximate=True)


def layer_backward(weights, vector_one, inputs, segment_rows, saved, grad_out):
    row_count, model_width = inputs.shape
    seq_len = segment_rows.shape[1]
    scaling = HEAD_DIM ** (-0.5)
    (
        normed,
        queries,
        key_rows,
        values,
        attention,
        mixture,
        middle,
        normed_two,
        hidden,
        active,
        residual,
        normed_out,
    ) = saved
    d_residual, d_gain_out, d_shift_out = norm_grad(
        residual, vector_one[4], vector_one[5], grad_out
    )
    d_outer = d_residual.astype(jnp.bfloat16)
    d_bias_out = jnp.sum(d_outer.astype(jnp.float32), 0)
    grad_down = outer_rows(active, d_outer)
    d_active = project(d_outer, weights[8 * model_width : 12 * model_width])
    gelu_value, gelu_pull = jax.vjp(gelu_tanh, hidden)
    d_hidden = gelu_pull(d_active)[0].astype(jnp.bfloat16)
    d_bias_hidden = jnp.sum(d_hidden.astype(jnp.float32), 0)
    grad_up = outer_rows(d_hidden, normed_two)
    d_normed_two = product(d_hidden, weights[4 * model_width : 8 * model_width])
    d_middle_norm, d_gain_two, d_shift_two = norm_grad(
        middle, vector_one[2], vector_one[3], d_normed_two
    )
    d_middle = d_residual + d_middle_norm
    d_branch = d_middle.astype(jnp.bfloat16)
    d_bias_branch = jnp.sum(d_branch.astype(jnp.float32), 0)
    grad_mix = outer_rows(d_branch, mixture)
    d_mixture = split_heads(
        product(d_branch, weights[3 * model_width : 4 * model_width]).astype(jnp.bfloat16), seq_len
    )
    d_attention = jnp.einsum(
        "nqhd,nkhd->nhqk", d_mixture, split_heads(values, seq_len), preferred_element_type=jnp.float32
    )
    d_values = jnp.einsum(
        "nhqk,nqhd->nkhd",
        attention.astype(jnp.bfloat16),
        d_mixture,
        preferred_element_type=jnp.float32,
    )
    d_values = d_values.reshape(row_count, model_width).astype(jnp.bfloat16)
    d_scores = (
        attention * (d_attention - jnp.sum(attention * d_attention, -1, keepdims=True))
    ).astype(jnp.bfloat16)
    d_queries = (
        jnp.einsum(
            "nhqk,nkhd->nqhd",
            d_scores,
            split_heads(key_rows, seq_len),
            preferred_element_type=jnp.float32,
        )
        * scaling
    )
    d_queries = d_queries.reshape(row_count, model_width).astype(jnp.bfloat16)
    d_keys = (
        jnp.einsum(
            "nhqk,nqhd->nkhd",
            d_scores,
            split_heads(queries, seq_len),
            preferred_element_type=jnp.float32,
        )
        * scaling
    )
    d_keys = d_keys.reshape(row_count, model_width).astype(jnp.bfloat16)
    d_joined = jnp.concatenate([d_queries, d_keys, d_values], axis=1)
    grad_joined = outer_rows(d_joined, normed)
    d_normed = product(d_joined, weights[0 : 3 * model_width])
    d_inputs_norm, d_gain_one, d_shift_one = norm_grad(
        inputs, vector_one[0], vector_one[1], d_normed
    )
    d_inputs = d_middle + d_inputs_norm
    grad_places = jnp.sum(d_inputs.reshape(-1, seq_len, model_width), axis=0)
    stack_rows = jnp.concatenate(
        [
            piece.astype(jnp.bfloat16)
            for piece in (grad_joined, grad_mix, grad_up, grad_down, grad_places)
        ],
        axis=0,
    )
    bias_query = jnp.sum(d_queries.astype(jnp.float32), 0)
    bias_value = jnp.sum(d_values.astype(jnp.float32), 0)
    vector_rows = jnp.concatenate(
        [
            jnp.stack(
                [
                    d_gain_one,
                    d_shift_one,
                    d_gain_two,
                    d_shift_two,
                    d_gain_out,
                    d_shift_out,
                    bias_query,
                    bias_value,
                    d_bias_branch,
                    d_bias_out,
                ]
            ),
            d_bias_hidden.reshape(4, model_width),
        ],
        axis=0,
    )
    return (stack_rows, vector_rows, d_inputs)


def update(weight, momentum, gradient, step_rate):
    renewed = momentum_decay * momentum + gradient
    return (renewed, weight - step_rate * (gradient + momentum_decay * renewed))


def stats_kernel(outs_ref, table_ref, target_ref, stat_ref):
    logits = project(table_ref[0], outs_ref[0])
    highest = jnp.max(logits, axis=0, keepdims=True)
    total = jnp.sum(jnp.exp(logits - highest), axis=0, keepdims=True)
    rows = lax.broadcasted_iota(jnp.int32, logits.shape, 0)
    hit = jnp.sum(jnp.where(rows == target_ref[0], logits, 0.0), axis=0, keepdims=True)
    stat_ref[0, 0:1, :] = highest + jnp.log(total)
    stat_ref[0, 1:2, :] = hit


def head_stats(outs_all, table_low, target_blocks, groups, members, share):
    blocks, rows, width = outs_all.shape
    part_rows = table_low.shape[1]
    return pl.pallas_call(
        stats_kernel,
        out_shape=jax.ShapeDtypeStruct((blocks, 2, rows), jnp.float32),
        grid=(members, groups),
        in_specs=[
            pl.BlockSpec((1, rows, width), lambda z, g: (g * members + z, 0, 0)),
            pl.BlockSpec((1, part_rows, width), lambda z, g: (z // share, 0, 0)),
            pl.BlockSpec((1, 1, rows), lambda z, g: (g * share + z % share, 0, 0)),
        ],
        out_specs=pl.BlockSpec((1, 2, rows), lambda z, g: (g * members + z, 0, 0)),
        compiler_params=pltpu.CompilerParams(vmem_limit_bytes=56 * MIB),
        cost_estimate=pl.CostEstimate(
            flops=2 * blocks * rows * part_rows * width,
            bytes_accessed=2 * outs_all.size + 2 * table_low.size,
            transcendentals=blocks * rows * part_rows,
        ),
    )(outs_all, table_low, target_blocks)


def back_kernel(
    model_ref, fresh_ref, first_ref, second_ref, a_ref, b_ref, table_ref, info_ref, target_ref, d_outs_ref, grad_ref
):
    step = pl.program_id(0)
    seq_len = a_ref.shape[1]
    outs = jnp.concatenate([a_ref[0], b_ref[0]], axis=0)
    logits = project(table_ref[0], outs)
    rows = lax.broadcasted_iota(jnp.int32, logits.shape, 0)
    soft = jnp.exp(logits - info_ref[0, 0:1, :])
    hit = (rows == target_ref[0]).astype(jnp.float32)
    d_logits = (info_ref[0, 1:2, :] * (soft - hit)).astype(jnp.bfloat16)
    d_outs = outer_rows(d_logits, table_ref[0])
    d_outs_ref[0] = d_outs[:seq_len].astype(d_outs_ref.dtype)
    d_outs_ref[1] = d_outs[seq_len:].astype(d_outs_ref.dtype)
    gain = product(d_logits, outs)

    @pl.when(fresh_ref[step] == 1)
    def start():
        grad_ref[0] = gain

    @pl.when(fresh_ref[step] == 0)
    def more():
        grad_ref[0] += gain


def head_back(outs_pieces, table_low, model_of, fresh, first, second, info, target):
    steps = model_of.shape[0]
    models, part_rows, width = table_low.shape
    seq_len = outs_pieces.shape[1]
    return pl.pallas_call(
        back_kernel,
        out_shape=(
            jax.ShapeDtypeStruct((2 * steps, seq_len, width), jnp.bfloat16),
            jax.ShapeDtypeStruct((models, part_rows, width), jnp.float32),
        ),
        grid_spec=pltpu.PrefetchScalarGridSpec(
            num_scalar_prefetch=4,
            grid=(steps,),
            in_specs=[
                pl.BlockSpec((1, seq_len, width), lambda s, m, f, a, b: (a[s], 0, 0)),
                pl.BlockSpec((1, seq_len, width), lambda s, m, f, a, b: (b[s], 0, 0)),
                pl.BlockSpec((1, part_rows, width), lambda s, m, f, a, b: (m[s], 0, 0)),
                pl.BlockSpec((1, 2, 2 * seq_len), lambda s, m, f, a, b: (s, 0, 0)),
                pl.BlockSpec((1, 1, 2 * seq_len), lambda s, m, f, a, b: (s, 0, 0)),
            ],
            out_specs=(
                pl.BlockSpec((2, seq_len, width), lambda s, m, f, a, b: (s, 0, 0)),
                pl.BlockSpec((1, part_rows, width), lambda s, m, f, a, b: (m[s], 0, 0)),
            ),
        ),
        compiler_params=pltpu.CompilerParams(vmem_limit_bytes=56 * MIB),
        cost_estimate=pl.CostEstimate(
            flops=12 * steps * seq_len * part_rows * width,
            bytes_accessed=4 * steps * seq_len * width * 2 + 6 * table_low.size,
            transcendentals=2 * steps * seq_len * part_rows,
        ),
    )(model_of, fresh, first, second, outs_pieces, outs_pieces, table_low, info, target)


def finish_kernel(
    model_ref, fresh_ref, final_ref, first_ref, second_ref, a_ref, b_ref, ids_ref, head_ref, table_ref, momentum_ref,
    grad_ref, momentum_new_ref, table_new_ref,
):
    tile = pl.program_id(0)
    step = pl.program_id(1)
    tile_rows = grad_ref.shape[1]
    rows = lax.broadcasted_iota(jnp.int32, (tile_rows, ids_ref.shape[2]), 0) + tile * tile_rows
    hits = (rows == ids_ref[0]).astype(jnp.float32).astype(jnp.bfloat16)
    outs = jnp.concatenate([a_ref[0], b_ref[0]], axis=0)
    gain = product(hits, outs)

    @pl.when(fresh_ref[step] == 1)
    def start():
        grad_ref[0] = head_ref[0] + gain

    @pl.when(fresh_ref[step] == 0)
    def more():
        grad_ref[0] += gain

    @pl.when(final_ref[step] == 1)
    def close():
        renewed, fresh_table = update(table_ref[0], momentum_ref[0], grad_ref[0], table_rate)
        momentum_new_ref[0] = renewed
        table_new_ref[0] = fresh_table


def finish_table(d_inputs, head_grad, table, momentum, model_of, fresh, final, first, second, ids):
    steps = model_of.shape[0]
    models, part_rows, width = table.shape
    seq_len = d_inputs.shape[1]
    tile_rows = part_rows // 2
    state = jax.ShapeDtypeStruct(table.shape, jnp.float32)
    piece = pl.BlockSpec((1, tile_rows, width), lambda t, s, m, f, l, a, b: (m[s], t, 0))
    return pl.pallas_call(
        finish_kernel,
        out_shape=(state, state, state),
        grid_spec=pltpu.PrefetchScalarGridSpec(
            num_scalar_prefetch=5,
            grid=(part_rows // tile_rows, steps),
            in_specs=[
                pl.BlockSpec((1, seq_len, width), lambda t, s, m, f, l, a, b: (a[s], 0, 0)),
                pl.BlockSpec((1, seq_len, width), lambda t, s, m, f, l, a, b: (b[s], 0, 0)),
                pl.BlockSpec((1, 1, 2 * seq_len), lambda t, s, m, f, l, a, b: (s, 0, 0)),
                piece,
                piece,
                piece,
            ],
            out_specs=(piece, piece, piece),
        ),
        compiler_params=pltpu.CompilerParams(vmem_limit_bytes=56 * MIB),
        cost_estimate=pl.CostEstimate(
            flops=4 * steps * seq_len * part_rows * width,
            bytes_accessed=24 * table.size,
            transcendentals=0,
        ),
    )(model_of, fresh, final, first, second, d_inputs, d_inputs, ids, head_grad, table, momentum)


def body(
    token_ids,
    target_ids,
    segment_ids,
    chosen,
    table,
    table_momentum,
    stack,
    stack_momentum,
    vectors,
    vector_momentum,
):
    both = ("grp", "cli")
    models, block_rows, model_width = table.shape
    stack_part = stack.shape[1]
    seq_len = token_ids.shape[1]
    groups = lax.axis_size("grp")
    members = lax.axis_size("cli")
    devices = groups * members
    share = members // models
    local = members // share
    device_index = lax.axis_index(both)
    group_index = lax.axis_index("grp")
    member_index = lax.axis_index("cli")
    model_own = member_index // share
    part_own = member_index % share
    model_range = jnp.arange(models, dtype=jnp.int32)

    def per_member(rows):
        return jnp.repeat(rows, share, axis=0) if share > 1 else rows

    stack_low = per_member(stack.astype(jnp.bfloat16))
    stack_turned = lax.all_to_all(stack_low, "cli", 0, 0, tiled=True)
    weights = lax.all_gather(stack_turned, "grp", axis=0, tiled=True).reshape(
        devices * stack_part, model_width
    )

    facts = lax.all_gather(
        jnp.concatenate([token_ids, target_ids, segment_ids, chosen[:, None]], axis=1),
        both,
        axis=0,
        tiled=True,
    )
    tokens = facts[:, :seq_len]
    targets = facts[:, seq_len : 2 * seq_len]
    segments = facts[:, 2 * seq_len : 3 * seq_len]
    choices = facts[:, 3 * seq_len]
    valid = jnp.concatenate(
        [
            (segments[:, :-1] == segments[:, 1:]).astype(jnp.float32),
            jnp.zeros((devices, 1), jnp.float32),
        ],
        axis=1,
    )
    counts = jnp.sum(valid, axis=1)
    choice_table = (choices[:, None] == model_range[None, :]).astype(jnp.float32)
    totals = jnp.sum(choice_table * counts[:, None], axis=0)
    total_of = jnp.sum(choice_table * totals[None, :], axis=1)

    table_low = table.astype(jnp.bfloat16)
    fine = 16 if block_rows % 64 else 64
    coarse = block_rows // fine
    flat_tokens = tokens.reshape(-1)
    high_hot = (
        (flat_tokens // fine)[:, None] == jnp.arange(devices * coarse, dtype=jnp.int32)[None, :]
    ).astype(jnp.bfloat16)
    low_hot = ((flat_tokens % fine)[:, None] == jnp.arange(fine, dtype=jnp.int32)[None, :]).astype(
        jnp.bfloat16
    )
    seen = (outer_rows(high_hot, low_hot) > 0).astype(jnp.float32)
    before = product(
        seen.astype(jnp.bfloat16),
        jnp.triu(jnp.ones((fine, fine), jnp.bfloat16), 1),
    )
    sums = jnp.sum(seen, axis=1).reshape(devices, coarse)
    uniques = jnp.sum(sums, axis=1)
    ahead = jnp.sum(
        jnp.where(
            jnp.arange(coarse)[None, None, :] < jnp.arange(coarse)[None, :, None],
            sums[:, None, :],
            0.0,
        ),
        axis=2,
    )
    places = before + ahead.reshape(-1, 1)
    rounds = jnp.max(jnp.ceil(uniques / ROUND_ROWS)).astype(jnp.int32)
    own_places = lax.dynamic_slice(places, (device_index * coarse, 0), (coarse, fine)).reshape(-1)
    own_seen = lax.dynamic_slice(seen, (device_index * coarse, 0), (coarse, fine)).reshape(-1)
    own_places = jnp.where(own_seen > 0, own_places, -1.0).astype(jnp.int32)
    first_client = group_index * members + part_own * local
    my_tokens = lax.dynamic_slice(tokens, (first_client, 0), (local, seq_len)).reshape(-1)
    my_segments = lax.dynamic_slice(segments, (first_client, 0), (local, seq_len))
    my_choices = lax.dynamic_slice(choices, (first_client,), (local,))
    my_high = (
        (my_tokens // fine)[:, None] == jnp.arange(devices * coarse, dtype=jnp.int32)[None, :]
    ).astype(jnp.bfloat16)
    my_low = (my_tokens % fine)[:, None] == jnp.arange(fine, dtype=jnp.int32)[None, :]
    split_places = jnp.concatenate(
        [jnp.floor(places / 64.0), places - 64.0 * jnp.floor(places / 64.0)], axis=1
    ).astype(jnp.bfloat16)
    picked_places = product(my_high, split_places)
    picked_places = 64.0 * picked_places[:, :fine] + picked_places[:, fine:]
    my_places = jnp.sum(jnp.where(my_low, picked_places, 0.0), axis=1).astype(jnp.int32)
    my_owner = my_tokens // block_rows

    def fetch(round_index, embedded):
        start = round_index * ROUND_ROWS
        wanted = jnp.arange(ROUND_ROWS, dtype=jnp.int32) + start
        pick = (own_places[None, :] == wanted[:, None]).astype(jnp.bfloat16)
        rows = jnp.einsum("ur,krd->kud", pick, table_low, preferred_element_type=jnp.float32)
        rows = per_member(rows.astype(jnp.bfloat16))
        turned = lax.all_to_all(rows, "cli", 0, 0, tiled=True)
        pool = lax.all_gather(turned, "grp", axis=0, tiled=True).reshape(-1, model_width)
        offset = my_places - start
        inside = (offset >= 0) & (offset < ROUND_ROWS)
        found = jnp.take(pool, jnp.where(inside, my_owner * ROUND_ROWS + offset, 0), axis=0)
        return jnp.where(inside[:, None], found.astype(jnp.float32), embedded)

    embedded = fetch(jnp.int32(0), jnp.zeros((local * seq_len, model_width), jnp.float32))
    _, embedded = lax.while_loop(
        lambda carry: carry[0] < rounds,
        lambda carry: (carry[0] + 1, fetch(carry[0], carry[1])),
        (jnp.int32(1), embedded),
    )
    vector_one = lax.dynamic_index_in_dim(vectors, model_own, 0, keepdims=False)
    inputs = embedded + jnp.tile(weights[12 * model_width :].astype(jnp.float32), (local, 1))
    saved = layer_forward(weights, vector_one, inputs, my_segments)
    normed_out = saved[11]

    outs_all = lax.all_gather(normed_out[None], both, axis=0, tiled=True)
    target_local = targets - device_index * block_rows
    target_local = jnp.where((target_local >= 0) & (target_local < block_rows), target_local, -1)
    stats = head_stats(
        outs_all,
        table_low,
        target_local.reshape(groups * share, 1, local * seq_len),
        groups,
        members,
        share,
    )
    shares = lax.all_to_all(stats, both, 0, 0, tiled=True)
    log_total = jax.nn.logsumexp(shares[:, 0], axis=0)
    token_loss = log_total - jnp.sum(shares[:, 1], axis=0)
    everything = lax.all_gather(
        jnp.stack([log_total, token_loss])[None], both, axis=0, tiled=True
    )
    everything = (
        everything.reshape(groups, models, share, 2, local, seq_len)
        .transpose(3, 1, 0, 2, 4, 5)
        .reshape(2, models, devices, seq_len)
    )
    all_losses = jnp.sum(everything[1] * valid[None], axis=2)
    loss = jnp.sum(choice_table.T * all_losses / total_of[None, :])
    client_losses = lax.dynamic_slice(
        (all_losses / counts[None, :]).T, (device_index, 0), (1, models)
    )
    chosen_total = jnp.sum(choice_table.T[:, :, None] * everything[0], axis=0)

    numbers = jnp.sum(choice_table, axis=0)
    padded = 2.0 * jnp.ceil(numbers / 2.0)
    offsets = jnp.cumsum(padded) - padded
    earlier = (
        jnp.arange(devices)[None, :] < jnp.arange(devices)[:, None]
    ) & (choices[None, :] == choices[:, None])
    slot_of = jnp.sum(choice_table * offsets[None, :], axis=1) + jnp.sum(
        earlier.astype(jnp.float32), axis=1
    )
    slots = devices + models
    steps = slots // 2
    at_slot = jnp.arange(slots)[:, None] == slot_of.astype(jnp.int32)[None, :]
    filled = jnp.any(at_slot, axis=1)
    client_at = jnp.sum(jnp.where(at_slot, jnp.arange(devices)[None, :], 0), axis=1).astype(
        jnp.int32
    )
    step_start = 2.0 * jnp.arange(steps)
    model_of = (
        jnp.sum((step_start[:, None] >= offsets[None, :]).astype(jnp.int32), axis=1) - 1
    ).astype(jnp.int32)
    fresh = jnp.concatenate(
        [jnp.ones((1,), jnp.int32), (model_of[1:] != model_of[:-1]).astype(jnp.int32)]
    )
    final = jnp.concatenate(
        [(model_of[1:] != model_of[:-1]).astype(jnp.int32), jnp.ones((1,), jnp.int32)]
    )
    within = client_at % members
    piece_at = (
        (client_at // members * members + jnp.repeat(model_of, 2) * share + within // local) * local
        + within % local
    ).astype(jnp.int32)
    weight_rows = valid / total_of[:, None]
    slot_log = jnp.where(filled[:, None], jnp.take(chosen_total, client_at, axis=0), 1e30)
    slot_weight = jnp.where(filled[:, None], jnp.take(weight_rows, client_at, axis=0), 0.0)
    slot_info = jnp.stack(
        [slot_log.reshape(steps, 2 * seq_len), slot_weight.reshape(steps, 2 * seq_len)], axis=1
    )
    slot_target = jnp.where(filled[:, None], jnp.take(target_local, client_at, axis=0), -1)
    d_slots, head_grad = head_back(
        outs_all.reshape(-1, seq_len, model_width),
        table_low,
        model_of,
        fresh,
        piece_at[0::2],
        piece_at[1::2],
        slot_info,
        slot_target.reshape(steps, 1, 2 * seq_len),
    )
    d_outs = jnp.take(d_slots, slot_of.astype(jnp.int32), axis=0)
    d_group = lax.psum_scatter(
        d_outs.reshape(devices * seq_len, model_width), "grp", scatter_dimension=0, tiled=True
    )
    d_group = lax.psum(d_group, "cli").reshape(members, seq_len, model_width)
    d_mine = lax.dynamic_slice(
        d_group, (part_own * local, 0, 0), (local, seq_len, model_width)
    ).astype(jnp.float32)
    d_final = jnp.where((my_choices == model_own)[:, None, None], d_mine, 0.0).reshape(
        local * seq_len, model_width
    )
    stack_rows, vector_rows, d_inputs = layer_backward(
        weights, vector_one, inputs, my_segments, saved, d_final
    )
    d_wide = d_inputs.astype(jnp.bfloat16)
    if share > 1:
        d_wide = lax.dynamic_update_slice(
            jnp.zeros((members * seq_len, model_width), jnp.bfloat16),
            d_wide,
            (part_own * local * seq_len, 0),
        )
    d_client = lax.psum_scatter(d_wide, "cli", scatter_dimension=0, tiled=True)
    d_all = lax.all_gather(d_client[None], both, axis=0, tiled=True)

    stack_sum = lax.psum_scatter(stack_rows, "grp", scatter_dimension=0, tiled=True)
    stack_back = lax.all_to_all(
        stack_sum.reshape(members, stack_part, model_width), "cli", 0, 0, tiled=True
    ).astype(jnp.float32)
    stack_grad = jnp.sum(
        stack_back.reshape(models, share, stack_part, model_width), axis=1
    )
    vector_masked = jnp.where((model_range == model_own)[:, None, None], vector_rows[None], 0.0)
    vector_grad = lax.psum(vector_masked, both)

    token_local = tokens - device_index * block_rows
    token_local = jnp.where((token_local >= 0) & (token_local < block_rows), token_local, -1)
    slot_token = jnp.where(filled[:, None], jnp.take(token_local, client_at, axis=0), -1)
    table_grad, table_momentum_new, table_new = finish_table(
        d_all,
        head_grad,
        table,
        table_momentum,
        model_of,
        fresh,
        final,
        client_at[0::2],
        client_at[1::2],
        slot_token.reshape(steps, 1, 2 * seq_len),
    )
    stack_momentum_new, stack_new = update(stack, stack_momentum, stack_grad, stack_rate)
    vector_momentum_new, vector_new = update(vectors, vector_momentum, vector_grad, vector_rate)
    return (
        loss,
        client_losses,
        table_grad,
        table_momentum_new,
        table_new,
        stack_grad,
        stack_momentum_new,
        stack_new,
        vector_grad,
        vector_momentum_new,
        vector_new,
    )


def solution(mesh):
    rows = P(("grp", "cli"), None)
    parts = P(None, ("grp", "cli"), None)
    return jax.shard_map(
        body,
        mesh=mesh,
        in_specs=(rows, rows, rows, P(("grp", "cli")), parts, parts, parts, parts, P(), P()),
        out_specs=(P(), rows, parts, parts, parts, parts, parts, parts, P(), P(), P()),
        check_vma=False,
    )
```

```python
import functools

import jax
import jax.numpy as jnp
from jax import lax
from jax.experimental import pallas as pl
from jax.experimental.pallas import tpu as pltpu
from jax.sharding import PartitionSpec as P

HEADS = 12
HEAD_DIM = 64


epsilon = 1e-05
momentum_decay = 0.9
table_rate = 4.0
stack_rate = 4.0
vector_rate = 50.0

ROUND_ROWS = 128
MIB = 1 << 20


def layer_norm(inputs, gain_row, shift_row):
    centred = inputs - jnp.mean(inputs, -1, keepdims=True)
    spread = jnp.mean(centred * centred, -1, keepdims=True)
    return centred * lax.rsqrt(spread + epsilon) * gain_row + shift_row


def project(inputs, matrix):
    return lax.dot_general(
        inputs, matrix, (((1,), (1,)), ((), ())), preferred_element_type=jnp.float32
    )


def product(inputs, matrix):
    return jnp.dot(inputs, matrix, preferred_element_type=jnp.float32)


def outer_rows(left, right):
    return lax.dot_general(
        left, right, (((0,), (0,)), ((), ())), preferred_element_type=jnp.float32
    )


def split_heads(rows, seq_len):
    return rows.reshape(-1, seq_len, HEADS, HEAD_DIM)


def attend(queries, key_rows, segment_rows):
    seq_len = segment_rows.shape[1]
    scores = jnp.einsum(
        "nqhd,nkhd->nhqk",
        split_heads(queries, seq_len),
        split_heads(key_rows, seq_len),
        preferred_element_type=jnp.float32,
    ) * HEAD_DIM ** (-0.5)
    positions = jnp.arange(seq_len)
    allowed = (positions[None, None, :] <= positions[None, :, None]) & (
        segment_rows[:, None, :] == segment_rows[:, :, None]
    )
    return jax.nn.softmax(jnp.where(allowed[:, None], scores, -1e30), axis=-1)


def layer_forward(weights, vector_one, inputs, segment_rows):
    row_count, model_width = inputs.shape
    seq_len = segment_rows.shape[1]
    normed = layer_norm(inputs, vector_one[0], vector_one[1]).astype(jnp.bfloat16)
    queries = (project(normed, weights[0:model_width]) + vector_one[6]).astype(jnp.bfloat16)
    key_rows = project(normed, weights[model_width : 2 * model_width]).astype(jnp.bfloat16)
    values = (project(normed, weights[2 * model_width : 3 * model_width]) + vector_one[7]).astype(
        jnp.bfloat16
    )
    attention = attend(queries, key_rows, segment_rows)
    mixture = jnp.einsum(
        "nhqk,nkhd->nqhd",
        attention.astype(jnp.bfloat16),
        split_heads(values, seq_len),
        preferred_element_type=jnp.float32,
    )
    mixture = mixture.reshape(row_count, model_width).astype(jnp.bfloat16)
    middle = inputs + (project(mixture, weights[3 * model_width : 4 * model_width]) + vector_one[8])
    normed_two = layer_norm(middle, vector_one[2], vector_one[3]).astype(jnp.bfloat16)
    hidden = project(normed_two, weights[4 * model_width : 8 * model_width]) + vector_one[
        10:14
    ].reshape(-1)
    active = jax.nn.gelu(hidden, approximate=True).astype(jnp.bfloat16)
    residual = middle + (
        product(active, weights[8 * model_width : 12 * model_width]) + vector_one[9]
    )
    normed_out = layer_norm(residual, vector_one[4], vector_one[5]).astype(jnp.bfloat16)
    return (
        normed,
        queries,
        key_rows,
        values,
        attention,
        mixture,
        middle,
        normed_two,
        hidden,
        active,
        residual,
        normed_out,
    )


def norm_grad(operand, gain_row, shift_row, cotangent):
    outcome, pullback = jax.vjp(layer_norm, operand, gain_row, shift_row)
    return pullback(cotangent)


def gelu_tanh(hidden):
    return jax.nn.gelu(hidden, approximate=True)


def layer_backward(weights, vector_one, inputs, segment_rows, saved, grad_out):
    row_count, model_width = inputs.shape
    seq_len = segment_rows.shape[1]
    scaling = HEAD_DIM ** (-0.5)
    (
        normed,
        queries,
        key_rows,
        values,
        attention,
        mixture,
        middle,
        normed_two,
        hidden,
        active,
        residual,
        normed_out,
    ) = saved
    d_residual, d_gain_out, d_shift_out = norm_grad(
        residual, vector_one[4], vector_one[5], grad_out
    )
    d_outer = d_residual.astype(jnp.bfloat16)
    d_bias_out = jnp.sum(d_outer.astype(jnp.float32), 0)
    grad_down = outer_rows(active, d_outer)
    d_active = project(d_outer, weights[8 * model_width : 12 * model_width])
    gelu_value, gelu_pull = jax.vjp(gelu_tanh, hidden)
    d_hidden = gelu_pull(d_active)[0].astype(jnp.bfloat16)
    d_bias_hidden = jnp.sum(d_hidden.astype(jnp.float32), 0)
    grad_up = outer_rows(d_hidden, normed_two)
    d_normed_two = product(d_hidden, weights[4 * model_width : 8 * model_width])
    d_middle_norm, d_gain_two, d_shift_two = norm_grad(
        middle, vector_one[2], vector_one[3], d_normed_two
    )
    d_middle = d_residual + d_middle_norm
    d_branch = d_middle.astype(jnp.bfloat16)
    d_bias_branch = jnp.sum(d_branch.astype(jnp.float32), 0)
    grad_mix = outer_rows(d_branch, mixture)
    d_mixture = split_heads(
        product(d_branch, weights[3 * model_width : 4 * model_width]).astype(jnp.bfloat16), seq_len
    )
    d_attention = jnp.einsum(
        "nqhd,nkhd->nhqk", d_mixture, split_heads(values, seq_len), preferred_element_type=jnp.float32
    )
    d_values = jnp.einsum(
        "nhqk,nqhd->nkhd",
        attention.astype(jnp.bfloat16),
        d_mixture,
        preferred_element_type=jnp.float32,
    )
    d_values = d_values.reshape(row_count, model_width).astype(jnp.bfloat16)
    d_scores = (
        attention * (d_attention - jnp.sum(attention * d_attention, -1, keepdims=True))
    ).astype(jnp.bfloat16)
    d_queries = (
        jnp.einsum(
            "nhqk,nkhd->nqhd",
            d_scores,
            split_heads(key_rows, seq_len),
            preferred_element_type=jnp.float32,
        )
        * scaling
    )
    d_queries = d_queries.reshape(row_count, model_width).astype(jnp.bfloat16)
    d_keys = (
        jnp.einsum(
            "nhqk,nqhd->nkhd",
            d_scores,
            split_heads(queries, seq_len),
            preferred_element_type=jnp.float32,
        )
        * scaling
    )
    d_keys = d_keys.reshape(row_count, model_width).astype(jnp.bfloat16)
    d_joined = jnp.concatenate([d_queries, d_keys, d_values], axis=1)
    grad_joined = outer_rows(d_joined, normed)
    d_normed = product(d_joined, weights[0 : 3 * model_width])
    d_inputs_norm, d_gain_one, d_shift_one = norm_grad(
        inputs, vector_one[0], vector_one[1], d_normed
    )
    d_inputs = d_middle + d_inputs_norm
    grad_places = jnp.sum(d_inputs.reshape(-1, seq_len, model_width), axis=0)
    stack_rows = jnp.concatenate(
        [
            piece.astype(jnp.bfloat16)
            for piece in (grad_joined, grad_mix, grad_up, grad_down, grad_places)
        ],
        axis=0,
    )
    bias_query = jnp.sum(d_queries.astype(jnp.float32), 0)
    bias_value = jnp.sum(d_values.astype(jnp.float32), 0)
    vector_rows = jnp.concatenate(
        [
            jnp.stack(
                [
                    d_gain_one,
                    d_shift_one,
                    d_gain_two,
                    d_shift_two,
                    d_gain_out,
                    d_shift_out,
                    bias_query,
                    bias_value,
                    d_bias_branch,
                    d_bias_out,
                ]
            ),
            d_bias_hidden.reshape(4, model_width),
        ],
        axis=0,
    )
    return (stack_rows, vector_rows, d_inputs)


def share_all(rows, axes, size):
    return lax.all_to_all(
        jnp.broadcast_to(rows[None], (size,) + rows.shape), axes, 0, 0, tiled=True
    )


def update(weight, momentum, gradient, step_rate):
    renewed = momentum_decay * momentum + gradient
    return (renewed, weight - step_rate * (gradient + momentum_decay * renewed))


def stats_kernel(outs_ref, table_ref, target_ref, stat_ref):
    logits = project(table_ref[0], outs_ref[0])
    highest = jnp.max(logits, axis=0, keepdims=True)
    total = jnp.sum(jnp.exp(logits - highest), axis=0, keepdims=True)
    rows = lax.broadcasted_iota(jnp.int32, logits.shape, 0)
    hit = jnp.sum(jnp.where(rows == target_ref[0], logits, 0.0), axis=0, keepdims=True)
    stat_ref[0, 0:1, :] = highest + jnp.log(total)
    stat_ref[0, 1:2, :] = hit


def head_stats(outs_all, table_low, target_blocks, groups, members, share):
    blocks, rows, width = outs_all.shape
    part_rows = table_low.shape[1]
    return pl.pallas_call(
        stats_kernel,
        out_shape=jax.ShapeDtypeStruct((blocks, 2, rows), jnp.float32),
        grid=(members, groups),
        in_specs=[
            pl.BlockSpec((1, rows, width), lambda z, g: (g * members + z, 0, 0)),
            pl.BlockSpec((1, part_rows, width), lambda z, g: (z // share, 0, 0)),
            pl.BlockSpec((1, 1, rows), lambda z, g: (g * share + z % share, 0, 0)),
        ],
        out_specs=pl.BlockSpec((1, 2, rows), lambda z, g: (g * members + z, 0, 0)),
        compiler_params=pltpu.CompilerParams(vmem_limit_bytes=56 * MIB),
        cost_estimate=pl.CostEstimate(
            flops=2 * blocks * rows * part_rows * width,
            bytes_accessed=2 * outs_all.size + 2 * table_low.size,
            transcendentals=blocks * rows * part_rows,
        ),
    )(outs_all, table_low, target_blocks)


def back_kernel(
    model_ref, fresh_ref, first_ref, second_ref, place_ref, a_ref, b_ref, table_ref, info_ref, target_ref, d_outs_ref,
    grad_ref, held, sems,
):
    step = pl.program_id(0)
    steps = pl.num_programs(0)
    seq_len = a_ref.shape[1]
    slot = lax.rem(step, 2)

    def leave(which, where, half):
        return pltpu.make_async_copy(
            held.at[which, half], d_outs_ref.at[where], sems.at[which, half]
        )

    @pl.when(step >= 2)
    def reuse():
        leave(slot, 0, 0).wait()
        leave(slot, 0, 1).wait()
    outs = jnp.concatenate([a_ref[0], b_ref[0]], axis=0)
    logits = project(table_ref[0], outs)
    rows = lax.broadcasted_iota(jnp.int32, logits.shape, 0)
    soft = jnp.exp(logits - info_ref[0, 0:1, :])
    hit = (rows == target_ref[0]).astype(jnp.float32)
    d_logits = (info_ref[0, 1:2, :] * (soft - hit)).astype(jnp.bfloat16)
    d_outs = outer_rows(d_logits, table_ref[0])
    held[slot, 0] = d_outs[:seq_len].astype(held.dtype)
    held[slot, 1] = d_outs[seq_len:].astype(held.dtype)
    leave(slot, place_ref[2 * step], 0).start()
    leave(slot, place_ref[2 * step + 1], 1).start()
    gain = product(d_logits, outs)

    @pl.when(fresh_ref[step] == 1)
    def start():
        grad_ref[0] = gain

    @pl.when(fresh_ref[step] == 0)
    def more():
        grad_ref[0] += gain

    @pl.when(step == steps - 1)
    def drain():
        for which in range(2):
            leave(which, 0, 0).wait()
            leave(which, 0, 1).wait()


def head_back(outs_pieces, table_low, model_of, fresh, first, second, place, info, target):
    steps = model_of.shape[0]
    models, part_rows, width = table_low.shape
    seq_len = outs_pieces.shape[1]
    return pl.pallas_call(
        back_kernel,
        out_shape=(
            jax.ShapeDtypeStruct((2 * steps, seq_len, width), jnp.bfloat16),
            jax.ShapeDtypeStruct((models, part_rows, width), jnp.float32),
        ),
        grid_spec=pltpu.PrefetchScalarGridSpec(
            num_scalar_prefetch=5,
            grid=(steps,),
            in_specs=[
                pl.BlockSpec((1, seq_len, width), lambda s, m, f, a, b, p: (a[s], 0, 0)),
                pl.BlockSpec((1, seq_len, width), lambda s, m, f, a, b, p: (b[s], 0, 0)),
                pl.BlockSpec((1, part_rows, width), lambda s, m, f, a, b, p: (m[s], 0, 0)),
                pl.BlockSpec((1, 2, 2 * seq_len), lambda s, m, f, a, b, p: (s, 0, 0)),
                pl.BlockSpec((1, 1, 2 * seq_len), lambda s, m, f, a, b, p: (s, 0, 0)),
            ],
            out_specs=(
                pl.BlockSpec(memory_space=pl.ANY),
                pl.BlockSpec((1, part_rows, width), lambda s, m, f, a, b, p: (m[s], 0, 0)),
            ),
            scratch_shapes=[
                pltpu.VMEM((2, 2, seq_len, width), jnp.bfloat16),
                pltpu.SemaphoreType.DMA((2, 2)),
            ],
        ),
        compiler_params=pltpu.CompilerParams(vmem_limit_bytes=56 * MIB),
        cost_estimate=pl.CostEstimate(
            flops=12 * steps * seq_len * part_rows * width,
            bytes_accessed=4 * steps * seq_len * width * 2 + 6 * table_low.size,
            transcendentals=2 * steps * seq_len * part_rows,
        ),
    )(model_of, fresh, first, second, place, outs_pieces, outs_pieces, table_low, info, target)


def finish_kernel(
    model_ref, fresh_ref, final_ref, first_ref, second_ref, a_ref, b_ref, ids_ref, head_ref, table_ref, momentum_ref,
    grad_ref, momentum_new_ref, table_new_ref,
):
    tile = pl.program_id(0)
    step = pl.program_id(1)
    tile_rows = grad_ref.shape[1]
    rows = lax.broadcasted_iota(jnp.int32, (tile_rows, ids_ref.shape[2]), 0) + tile * tile_rows
    hits = (rows == ids_ref[0]).astype(jnp.float32).astype(jnp.bfloat16)
    outs = jnp.concatenate([a_ref[0], b_ref[0]], axis=0)
    gain = product(hits, outs)

    @pl.when(fresh_ref[step] == 1)
    def start():
        grad_ref[0] = head_ref[0] + gain

    @pl.when(fresh_ref[step] == 0)
    def more():
        grad_ref[0] += gain

    @pl.when(final_ref[step] == 1)
    def close():
        renewed, fresh_table = update(table_ref[0], momentum_ref[0], grad_ref[0], table_rate)
        momentum_new_ref[0] = renewed
        table_new_ref[0] = fresh_table


def finish_table(d_inputs, head_grad, table, momentum, model_of, fresh, final, first, second, ids):
    steps = model_of.shape[0]
    models, part_rows, width = table.shape
    seq_len = d_inputs.shape[1]
    tile_rows = part_rows // 2
    state = jax.ShapeDtypeStruct(table.shape, jnp.float32)
    piece = pl.BlockSpec((1, tile_rows, width), lambda t, s, m, f, l, a, b: (m[s], t, 0))
    return pl.pallas_call(
        finish_kernel,
        out_shape=(state, state, state),
        grid_spec=pltpu.PrefetchScalarGridSpec(
            num_scalar_prefetch=5,
            grid=(part_rows // tile_rows, steps),
            in_specs=[
                pl.BlockSpec((1, seq_len, width), lambda t, s, m, f, l, a, b: (a[s], 0, 0)),
                pl.BlockSpec((1, seq_len, width), lambda t, s, m, f, l, a, b: (b[s], 0, 0)),
                pl.BlockSpec((1, 1, 2 * seq_len), lambda t, s, m, f, l, a, b: (s, 0, 0)),
                piece,
                piece,
                piece,
            ],
            out_specs=(piece, piece, piece),
        ),
        compiler_params=pltpu.CompilerParams(vmem_limit_bytes=56 * MIB),
        cost_estimate=pl.CostEstimate(
            flops=4 * steps * seq_len * part_rows * width,
            bytes_accessed=24 * table.size,
            transcendentals=0,
        ),
    )(model_of, fresh, final, first, second, d_inputs, d_inputs, ids, head_grad, table, momentum)


def body(
    token_ids,
    target_ids,
    segment_ids,
    chosen,
    table,
    table_momentum,
    stack,
    stack_momentum,
    vectors,
    vector_momentum,
):
    both = ("grp", "cli")
    models, block_rows, model_width = table.shape
    stack_part = stack.shape[1]
    seq_len = token_ids.shape[1]
    groups = lax.axis_size("grp")
    members = lax.axis_size("cli")
    devices = groups * members
    share = members // models
    local = members // share
    device_index = lax.axis_index(both)
    group_index = lax.axis_index("grp")
    member_index = lax.axis_index("cli")
    model_own = member_index // share
    part_own = member_index % share
    model_range = jnp.arange(models, dtype=jnp.int32)

    def per_member(rows):
        return jnp.repeat(rows, share, axis=0) if share > 1 else rows

    stack_low = per_member(stack.astype(jnp.bfloat16))
    stack_turned = lax.all_to_all(stack_low, "cli", 0, 0, tiled=True)
    weights = lax.all_gather(stack_turned, "grp", axis=0, tiled=True).reshape(
        devices * stack_part, model_width
    )

    facts = share_all(
        jnp.concatenate([token_ids[0], target_ids[0], segment_ids[0], chosen]), both, devices
    )
    tokens = facts[:, :seq_len]
    targets = facts[:, seq_len : 2 * seq_len]
    segments = facts[:, 2 * seq_len : 3 * seq_len]
    choices = facts[:, 3 * seq_len]
    valid = jnp.concatenate(
        [
            (segments[:, :-1] == segments[:, 1:]).astype(jnp.float32),
            jnp.zeros((devices, 1), jnp.float32),
        ],
        axis=1,
    )
    counts = jnp.sum(valid, axis=1)
    choice_table = (choices[:, None] == model_range[None, :]).astype(jnp.float32)
    totals = jnp.sum(choice_table * counts[:, None], axis=0)
    total_of = jnp.sum(choice_table * totals[None, :], axis=1)

    table_low = table.astype(jnp.bfloat16)
    fine = 16 if block_rows % 64 else 64
    coarse = block_rows // fine
    flat_tokens = tokens.reshape(-1)
    high_hot = (
        (flat_tokens // fine)[:, None] == jnp.arange(devices * coarse, dtype=jnp.int32)[None, :]
    ).astype(jnp.bfloat16)
    low_hot = ((flat_tokens % fine)[:, None] == jnp.arange(fine, dtype=jnp.int32)[None, :]).astype(
        jnp.bfloat16
    )
    seen = (outer_rows(high_hot, low_hot) > 0).astype(jnp.float32)
    before = product(
        seen.astype(jnp.bfloat16),
        jnp.triu(jnp.ones((fine, fine), jnp.bfloat16), 1),
    )
    sums = jnp.sum(seen, axis=1).reshape(devices, coarse)
    uniques = jnp.sum(sums, axis=1)
    ahead = jnp.sum(
        jnp.where(
            jnp.arange(coarse)[None, None, :] < jnp.arange(coarse)[None, :, None],
            sums[:, None, :],
            0.0,
        ),
        axis=2,
    )
    places = before + ahead.reshape(-1, 1)
    rounds = jnp.max(jnp.ceil(uniques / ROUND_ROWS)).astype(jnp.int32)
    own_places = lax.dynamic_slice(places, (device_index * coarse, 0), (coarse, fine)).reshape(-1)
    own_seen = lax.dynamic_slice(seen, (device_index * coarse, 0), (coarse, fine)).reshape(-1)
    own_places = jnp.where(own_seen > 0, own_places, -1.0).astype(jnp.int32)
    first_client = group_index * members + part_own * local
    my_tokens = lax.dynamic_slice(tokens, (first_client, 0), (local, seq_len)).reshape(-1)
    my_segments = lax.dynamic_slice(segments, (first_client, 0), (local, seq_len))
    my_choices = lax.dynamic_slice(choices, (first_client,), (local,))
    my_high = (
        (my_tokens // fine)[:, None] == jnp.arange(devices * coarse, dtype=jnp.int32)[None, :]
    ).astype(jnp.bfloat16)
    my_low = (my_tokens % fine)[:, None] == jnp.arange(fine, dtype=jnp.int32)[None, :]
    split_places = jnp.concatenate(
        [jnp.floor(places / 64.0), places - 64.0 * jnp.floor(places / 64.0)], axis=1
    ).astype(jnp.bfloat16)
    picked_places = product(my_high, split_places)
    picked_places = 64.0 * picked_places[:, :fine] + picked_places[:, fine:]
    my_places = jnp.sum(jnp.where(my_low, picked_places, 0.0), axis=1).astype(jnp.int32)
    my_owner = my_tokens // block_rows

    def fetch(round_index, embedded):
        start = round_index * ROUND_ROWS
        wanted = jnp.arange(ROUND_ROWS, dtype=jnp.int32) + start
        pick = (own_places[None, :] == wanted[:, None]).astype(jnp.bfloat16)
        rows = jnp.einsum("ur,krd->kud", pick, table_low, preferred_element_type=jnp.float32)
        rows = per_member(rows.astype(jnp.bfloat16))
        turned = lax.all_to_all(rows, "cli", 0, 0, tiled=True)
        pool = lax.all_gather(turned, "grp", axis=0, tiled=True).reshape(-1, model_width)
        offset = my_places - start
        inside = (offset >= 0) & (offset < ROUND_ROWS)
        found = jnp.take(pool, jnp.where(inside, my_owner * ROUND_ROWS + offset, 0), axis=0)
        return jnp.where(inside[:, None], found.astype(jnp.float32), embedded)

    embedded = fetch(jnp.int32(0), jnp.zeros((local * seq_len, model_width), jnp.float32))
    _, embedded = lax.while_loop(
        lambda carry: carry[0] < rounds,
        lambda carry: (carry[0] + 1, fetch(carry[0], carry[1])),
        (jnp.int32(1), embedded),
    )
    vector_one = lax.dynamic_index_in_dim(vectors, model_own, 0, keepdims=False)
    inputs = embedded + jnp.tile(weights[12 * model_width :].astype(jnp.float32), (local, 1))
    saved = layer_forward(weights, vector_one, inputs, my_segments)
    normed_out = saved[11]

    outs_all = lax.all_gather(normed_out[None], both, axis=0, tiled=True)
    target_local = targets - device_index * block_rows
    target_local = jnp.where((target_local >= 0) & (target_local < block_rows), target_local, -1)
    stats = head_stats(
        outs_all,
        table_low,
        target_local.reshape(groups * share, 1, local * seq_len),
        groups,
        members,
        share,
    )
    shares = lax.all_to_all(stats, both, 0, 0, tiled=True)
    log_total = jax.nn.logsumexp(shares[:, 0], axis=0)
    token_loss = log_total - jnp.sum(shares[:, 1], axis=0)
    everything = share_all(jnp.stack([log_total, token_loss]), both, devices)
    everything = (
        everything.reshape(groups, models, share, 2, local, seq_len)
        .transpose(3, 1, 0, 2, 4, 5)
        .reshape(2, models, devices, seq_len)
    )
    all_losses = jnp.sum(everything[1] * valid[None], axis=2)
    loss = jnp.sum(choice_table.T * all_losses / total_of[None, :])
    client_losses = lax.dynamic_slice(
        (all_losses / counts[None, :]).T, (device_index, 0), (1, models)
    )
    chosen_total = jnp.sum(choice_table.T[:, :, None] * everything[0], axis=0)

    numbers = jnp.sum(choice_table, axis=0)
    padded = 2.0 * jnp.ceil(numbers / 2.0)
    offsets = jnp.cumsum(padded) - padded
    earlier = (
        jnp.arange(devices)[None, :] < jnp.arange(devices)[:, None]
    ) & (choices[None, :] == choices[:, None])
    slot_of = jnp.sum(choice_table * offsets[None, :], axis=1) + jnp.sum(
        earlier.astype(jnp.float32), axis=1
    )
    slots = devices + models
    steps = slots // 2
    at_slot = jnp.arange(slots)[:, None] == slot_of.astype(jnp.int32)[None, :]
    filled = jnp.any(at_slot, axis=1)
    client_at = jnp.sum(jnp.where(at_slot, jnp.arange(devices)[None, :], 0), axis=1).astype(
        jnp.int32
    )
    step_start = 2.0 * jnp.arange(steps)
    model_of = (
        jnp.sum((step_start[:, None] >= offsets[None, :]).astype(jnp.int32), axis=1) - 1
    ).astype(jnp.int32)
    fresh = jnp.concatenate(
        [jnp.ones((1,), jnp.int32), (model_of[1:] != model_of[:-1]).astype(jnp.int32)]
    )
    final = jnp.concatenate(
        [(model_of[1:] != model_of[:-1]).astype(jnp.int32), jnp.ones((1,), jnp.int32)]
    )
    within = client_at % members
    piece_at = (
        (client_at // members * members + jnp.repeat(model_of, 2) * share + within // local) * local
        + within % local
    ).astype(jnp.int32)
    weight_rows = valid / total_of[:, None]
    slot_log = jnp.where(filled[:, None], jnp.take(chosen_total, client_at, axis=0), 1e30)
    slot_weight = jnp.where(filled[:, None], jnp.take(weight_rows, client_at, axis=0), 0.0)
    slot_info = jnp.stack(
        [slot_log.reshape(steps, 2 * seq_len), slot_weight.reshape(steps, 2 * seq_len)], axis=1
    )
    slot_target = jnp.where(filled[:, None], jnp.take(target_local, client_at, axis=0), -1)
    spare = devices + jnp.cumsum(1 - filled.astype(jnp.int32)) - 1
    d_outs, head_grad = head_back(
        outs_all.reshape(-1, seq_len, model_width),
        table_low,
        model_of,
        fresh,
        piece_at[0::2],
        piece_at[1::2],
        jnp.where(filled, client_at, spare).astype(jnp.int32),
        slot_info,
        slot_target.reshape(steps, 1, 2 * seq_len),
    )
    d_group = lax.psum_scatter(
        d_outs[:devices].reshape(devices * seq_len, model_width),
        "grp",
        scatter_dimension=0,
        tiled=True,
    )
    d_group = lax.psum(d_group, "cli").reshape(members, seq_len, model_width)
    d_mine = lax.dynamic_slice(
        d_group, (part_own * local, 0, 0), (local, seq_len, model_width)
    ).astype(jnp.float32)
    d_final = jnp.where((my_choices == model_own)[:, None, None], d_mine, 0.0).reshape(
        local * seq_len, model_width
    )
    stack_rows, vector_rows, d_inputs = layer_backward(
        weights, vector_one, inputs, my_segments, saved, d_final
    )
    d_wide = d_inputs.astype(jnp.bfloat16)
    if share > 1:
        d_wide = lax.dynamic_update_slice(
            jnp.zeros((members * seq_len, model_width), jnp.bfloat16),
            d_wide,
            (part_own * local * seq_len, 0),
        )
    d_client = lax.psum_scatter(d_wide, "cli", scatter_dimension=0, tiled=True)
    d_all = lax.all_gather(d_client[None], both, axis=0, tiled=True)

    stack_sum = lax.psum_scatter(stack_rows, "grp", scatter_dimension=0, tiled=True)
    stack_back = lax.all_to_all(
        stack_sum.reshape(members, stack_part, model_width), "cli", 0, 0, tiled=True
    ).astype(jnp.float32)
    stack_grad = jnp.sum(
        stack_back.reshape(models, share, stack_part, model_width), axis=1
    )
    vector_piece = vector_rows.size // groups
    vector_part = jnp.sum(
        lax.all_to_all(vector_rows.reshape(groups, vector_piece), "grp", 0, 0, tiled=True), axis=0
    )
    vector_grad = jnp.sum(
        share_all(vector_part, both, devices).reshape(groups, models, share, vector_piece), axis=2
    )
    vector_grad = vector_grad.transpose(1, 0, 2).reshape(vectors.shape)

    token_local = tokens - device_index * block_rows
    token_local = jnp.where((token_local >= 0) & (token_local < block_rows), token_local, -1)
    slot_token = jnp.where(filled[:, None], jnp.take(token_local, client_at, axis=0), -1)
    table_grad, table_momentum_new, table_new = finish_table(
        d_all,
        head_grad,
        table,
        table_momentum,
        model_of,
        fresh,
        final,
        client_at[0::2],
        client_at[1::2],
        slot_token.reshape(steps, 1, 2 * seq_len),
    )
    stack_momentum_new, stack_new = update(stack, stack_momentum, stack_grad, stack_rate)
    vector_momentum_new, vector_new = update(vectors, vector_momentum, vector_grad, vector_rate)
    return (
        loss,
        client_losses,
        table_grad,
        table_momentum_new,
        table_new,
        stack_grad,
        stack_momentum_new,
        stack_new,
        vector_grad,
        vector_momentum_new,
        vector_new,
    )


def solution(mesh):
    rows = P(("grp", "cli"), None)
    parts = P(None, ("grp", "cli"), None)
    return jax.shard_map(
        body,
        mesh=mesh,
        in_specs=(rows, rows, rows, P(("grp", "cli")), parts, parts, parts, parts, P(), P()),
        out_specs=(P(), rows, parts, parts, parts, parts, parts, parts, P(), P(), P()),
        check_vma=False,
    )
```

```python
import functools

import jax
import jax.numpy as jnp
from jax import lax
from jax.experimental import pallas as pl
from jax.experimental.pallas import tpu as pltpu
from jax.sharding import PartitionSpec as P

HEADS = 12
HEAD_DIM = 64


epsilon = 1e-05
momentum_decay = 0.9
table_rate = 4.0
stack_rate = 4.0
vector_rate = 50.0

ROUND_ROWS = 128
SLAB_STEP = 32
MIB = 1 << 20
POOL_BYTES = 32 * MIB
MESH = pl.DeviceIdType.MESH


def layer_norm(inputs, gain_row, shift_row):
    centred = inputs - jnp.mean(inputs, -1, keepdims=True)
    spread = jnp.mean(centred * centred, -1, keepdims=True)
    return centred * lax.rsqrt(spread + epsilon) * gain_row + shift_row


def project(inputs, matrix):
    return lax.dot_general(
        inputs, matrix, (((1,), (1,)), ((), ())), preferred_element_type=jnp.float32
    )


def product(inputs, matrix):
    return jnp.dot(inputs, matrix, preferred_element_type=jnp.float32)


def outer_rows(left, right):
    return lax.dot_general(
        left, right, (((0,), (0,)), ((), ())), preferred_element_type=jnp.float32
    )


def split_heads(rows, seq_len):
    return rows.reshape(-1, seq_len, HEADS, HEAD_DIM)


def attend(queries, key_rows, segment_rows):
    seq_len = segment_rows.shape[1]
    scores = jnp.einsum(
        "nqhd,nkhd->nhqk",
        split_heads(queries, seq_len),
        split_heads(key_rows, seq_len),
        preferred_element_type=jnp.float32,
    ) * HEAD_DIM ** (-0.5)
    positions = jnp.arange(seq_len)
    allowed = (positions[None, None, :] <= positions[None, :, None]) & (
        segment_rows[:, None, :] == segment_rows[:, :, None]
    )
    return jax.nn.softmax(jnp.where(allowed[:, None], scores, -1e30), axis=-1)


def layer_forward(weights, vector_one, inputs, segment_rows):
    row_count, model_width = inputs.shape
    seq_len = segment_rows.shape[1]
    normed = layer_norm(inputs, vector_one[0], vector_one[1]).astype(jnp.bfloat16)
    queries = (project(normed, weights[0:model_width]) + vector_one[6]).astype(jnp.bfloat16)
    key_rows = project(normed, weights[model_width : 2 * model_width]).astype(jnp.bfloat16)
    values = (project(normed, weights[2 * model_width : 3 * model_width]) + vector_one[7]).astype(
        jnp.bfloat16
    )
    attention = attend(queries, key_rows, segment_rows)
    mixture = jnp.einsum(
        "nhqk,nkhd->nqhd",
        attention.astype(jnp.bfloat16),
        split_heads(values, seq_len),
        preferred_element_type=jnp.float32,
    )
    mixture = mixture.reshape(row_count, model_width).astype(jnp.bfloat16)
    middle = inputs + (project(mixture, weights[3 * model_width : 4 * model_width]) + vector_one[8])
    normed_two = layer_norm(middle, vector_one[2], vector_one[3]).astype(jnp.bfloat16)
    hidden = project(normed_two, weights[4 * model_width : 8 * model_width]) + vector_one[
        10:14
    ].reshape(-1)
    active = jax.nn.gelu(hidden, approximate=True).astype(jnp.bfloat16)
    residual = middle + (
        product(active, weights[8 * model_width : 12 * model_width]) + vector_one[9]
    )
    normed_out = layer_norm(residual, vector_one[4], vector_one[5]).astype(jnp.bfloat16)
    return (
        normed,
        queries,
        key_rows,
        values,
        attention,
        mixture,
        middle,
        normed_two,
        hidden,
        active,
        residual,
        normed_out,
    )


def norm_grad(operand, gain_row, shift_row, cotangent):
    outcome, pullback = jax.vjp(layer_norm, operand, gain_row, shift_row)
    return pullback(cotangent)


def gelu_tanh(hidden):
    return jax.nn.gelu(hidden, approximate=True)


def layer_backward(weights, vector_one, inputs, segment_rows, saved, grad_out):
    row_count, model_width = inputs.shape
    seq_len = segment_rows.shape[1]
    scaling = HEAD_DIM ** (-0.5)
    (
        normed,
        queries,
        key_rows,
        values,
        attention,
        mixture,
        middle,
        normed_two,
        hidden,
        active,
        residual,
        normed_out,
    ) = saved
    d_residual, d_gain_out, d_shift_out = norm_grad(
        residual, vector_one[4], vector_one[5], grad_out
    )
    d_outer = d_residual.astype(jnp.bfloat16)
    d_bias_out = jnp.sum(d_outer.astype(jnp.float32), 0)
    grad_down = outer_rows(active, d_outer)
    d_active = project(d_outer, weights[8 * model_width : 12 * model_width])
    gelu_value, gelu_pull = jax.vjp(gelu_tanh, hidden)
    d_hidden = gelu_pull(d_active)[0].astype(jnp.bfloat16)
    d_bias_hidden = jnp.sum(d_hidden.astype(jnp.float32), 0)
    grad_up = outer_rows(d_hidden, normed_two)
    d_normed_two = product(d_hidden, weights[4 * model_width : 8 * model_width])
    d_middle_norm, d_gain_two, d_shift_two = norm_grad(
        middle, vector_one[2], vector_one[3], d_normed_two
    )
    d_middle = d_residual + d_middle_norm
    d_branch = d_middle.astype(jnp.bfloat16)
    d_bias_branch = jnp.sum(d_branch.astype(jnp.float32), 0)
    grad_mix = outer_rows(d_branch, mixture)
    d_mixture = split_heads(
        product(d_branch, weights[3 * model_width : 4 * model_width]).astype(jnp.bfloat16), seq_len
    )
    d_attention = jnp.einsum(
        "nqhd,nkhd->nhqk", d_mixture, split_heads(values, seq_len), preferred_element_type=jnp.float32
    )
    d_values = jnp.einsum(
        "nhqk,nqhd->nkhd",
        attention.astype(jnp.bfloat16),
        d_mixture,
        preferred_element_type=jnp.float32,
    )
    d_values = d_values.reshape(row_count, model_width).astype(jnp.bfloat16)
    d_scores = (
        attention * (d_attention - jnp.sum(attention * d_attention, -1, keepdims=True))
    ).astype(jnp.bfloat16)
    d_queries = (
        jnp.einsum(
            "nhqk,nkhd->nqhd",
            d_scores,
            split_heads(key_rows, seq_len),
            preferred_element_type=jnp.float32,
        )
        * scaling
    )
    d_queries = d_queries.reshape(row_count, model_width).astype(jnp.bfloat16)
    d_keys = (
        jnp.einsum(
            "nhqk,nqhd->nkhd",
            d_scores,
            split_heads(queries, seq_len),
            preferred_element_type=jnp.float32,
        )
        * scaling
    )
    d_keys = d_keys.reshape(row_count, model_width).astype(jnp.bfloat16)
    d_joined = jnp.concatenate([d_queries, d_keys, d_values], axis=1)
    grad_joined = outer_rows(d_joined, normed)
    d_normed = product(d_joined, weights[0 : 3 * model_width])
    d_inputs_norm, d_gain_one, d_shift_one = norm_grad(
        inputs, vector_one[0], vector_one[1], d_normed
    )
    d_inputs = d_middle + d_inputs_norm
    grad_places = jnp.sum(d_inputs.reshape(-1, seq_len, model_width), axis=0)
    stack_rows = jnp.concatenate(
        [
            piece.astype(jnp.bfloat16)
            for piece in (grad_joined, grad_mix, grad_up, grad_down, grad_places)
        ],
        axis=0,
    )
    bias_query = jnp.sum(d_queries.astype(jnp.float32), 0)
    bias_value = jnp.sum(d_values.astype(jnp.float32), 0)
    vector_rows = jnp.concatenate(
        [
            jnp.stack(
                [
                    d_gain_one,
                    d_shift_one,
                    d_gain_two,
                    d_shift_two,
                    d_gain_out,
                    d_shift_out,
                    bias_query,
                    bias_value,
                    d_bias_branch,
                    d_bias_out,
                ]
            ),
            d_bias_hidden.reshape(4, model_width),
        ],
        axis=0,
    )
    return (stack_rows, vector_rows, d_inputs)


def share_all(rows, axes, size):
    return lax.all_to_all(
        jnp.broadcast_to(rows[None], (size,) + rows.shape), axes, 0, 0, tiled=True
    )


def update(weight, momentum, gradient, step_rate):
    renewed = momentum_decay * momentum + gradient
    return (renewed, weight - step_rate * (gradient + momentum_decay * renewed))


def flipped(value, offset, size):
    bit = 1
    while bit < size:
        digit = lax.rem(lax.div(offset, bit), 2)
        value = value + digit * bit * (1 - 2 * lax.rem(lax.div(value, bit), 2))
        bit *= 2
    return value


class Place:
    def __init__(self, groups, members):
        self.groups, self.members = groups, members
        self.ys = 2
        self.xs = groups // 4
        self.grp = lax.axis_index("grp")
        self.cli = lax.axis_index("cli")
        self.core = lax.rem(self.grp, 2)
        self.x = lax.rem(lax.div(self.grp, 2), self.xs)
        self.y = lax.div(self.grp, 2 * self.xs)

    def group(self, jx=0, jy=0, jc=0):
        x = flipped(self.x, jx, self.xs)
        y = flipped(self.y, jy, self.ys)
        core = self.core + jc * (1 - 2 * self.core)
        return (y * self.xs + x) * 2 + core

    def block(self, jx, jy, level, jc=0):
        return self.group(jx, jy, jc) * self.members + level

    def peer(self, jx=0, jy=0, jc=0):
        return (self.group(jx, jy, jc), self.cli)

    def level(self, level):
        return (self.grp, level)

    def nearest(self, i):
        z, last = self.cli, self.members - 1
        low = jnp.where(2 * z < last, 1, 0)
        sign = 2 * low - 1
        margin = low * z + (1 - low) * (last - z)
        step = lax.div(i + 1, 2)
        odd = lax.rem(i, 2)
        near = z + sign * step * (2 * odd - 1)
        far = z + sign * (i - margin)
        return jnp.where(i <= 2 * margin, near, far)


def greet(place):
    barrier = pltpu.get_barrier_semaphore()
    peers = [place.peer(jx=j) for j in range(1, place.xs)] + [place.peer(jy=j) for j in range(1, place.ys)]
    peers.append(place.peer(jc=1))
    peers += [place.level(lax.rem(place.cli + j, place.members)) for j in range(1, place.members)]
    for peer in peers:
        pl.semaphore_signal(barrier, inc=1, device_id=peer, device_id_type=MESH)
    pl.semaphore_wait(barrier, len(peers))


def spread_sems(groups, members, pieces):
    xs, ys, items = groups // 4, 2, members * pieces
    dma = pltpu.SemaphoreType.DMA
    shapes = [(items,)] * 3 + [(items, xs)] * 2 + [(items, ys)] * 2 + [(items, xs, ys)] * 6
    return [dma] + [dma(shape) for shape in shapes]


def spread_body(place, chain, pieces, src, out, sems, consume, ready=None):
    (own_sem, z_up, z_down, z_recv, x_send, x_recv, y_send, y_recv, k_send, k_recv, p_send, p_recv,
     c_send, c_recv) = sems
    xs, ys, members = place.xs, place.ys, place.members
    items = members * pieces
    size = out.shape[1] // pieces
    z = place.cli
    partner = z + 1 - 2 * lax.rem(z, 2)
    inner_x, inner_y = range(1, xs), range(1, ys)

    def move(source, target, send, recv, device):
        return pltpu.make_async_remote_copy(
            src_ref=source, dst_ref=target, send_sem=send, recv_sem=recv, device_id=device, device_id_type=MESH
        )

    class Item:
        def __init__(self, k):
            self.level = place.nearest(lax.div(k, pieces))
            self.piece = lax.rem(k, pieces)
            self.slot = self.level * pieces + self.piece
            self.even = lax.rem(self.piece, 2) == 0
            self.mine = lax.rem(self.level + z, 2) == 0 if chain else self.level >= 0
            self.rows = pl.ds(self.piece * size, size)

        def part(self, jx, jy, level=None):
            return out.at[place.block(jx, jy, self.level if level is None else level), self.rows]

        def here(self, own):
            return src.at[z if not chain else 0, self.rows] if own else self.part(0, 0)

        def up(self, own=False):
            return move(self.here(own), self.part(0, 0), z_up.at[self.slot], z_recv.at[self.slot], place.level(z + 1))

        def down(self, own=False):
            return move(self.here(own), self.part(0, 0), z_down.at[self.slot], z_recv.at[self.slot], place.level(z - 1))

        def straight(self):
            return move(
                src.at[self.level, self.rows], self.part(0, 0, z), z_up.at[self.slot],
                z_recv.at[z * pieces + self.piece], place.level(self.level),
            )

        def landed(self):
            part = self.part(0, 0)
            return move(part, part, z_up.at[self.slot], z_recv.at[self.slot], place.level(partner))

        def to_x(self, jx, own=False):
            return move(self.here(own), self.part(0, 0), x_send.at[self.slot, jx], x_recv.at[self.slot, jx], place.peer(jx=jx))

        def to_y(self, jy, own=False):
            return move(self.here(own), self.part(0, 0), y_send.at[self.slot, jy], y_recv.at[self.slot, jy], place.peer(jy=jy))

        def corner_a(self, jx, jy):
            part = self.part(jx, 0)
            return move(part, part, k_send.at[self.slot, jx, jy], k_recv.at[self.slot, jx, jy], place.peer(jy=jy))

        def corner_b(self, jx, jy):
            part = self.part(0, jy)
            return move(part, part, k_send.at[self.slot, jx, jy], k_recv.at[self.slot, jx, jy], place.peer(jx=jx))

        def corner_z(self, jx, jy):
            part = self.part(jx, jy)
            return move(part, part, p_send.at[self.slot, jx, jy], p_recv.at[self.slot, jx, jy], place.level(partner))

        def to_core(self, jx, jy, own=False):
            part = self.part(jx, jy)
            return move(self.here(True) if own else part, part, c_send.at[self.slot, jx, jy], c_recv.at[self.slot, jx, jy], place.peer(jc=1))

    own = pltpu.make_async_copy(src.at[z if not chain else 0], out.at[place.block(0, 0, z)], own_sem)
    own.start()
    if not chain:
        for piece in range(pieces):
            Item(pieces + piece).straight().start()

    def columns(k):
        item = Item(k)
        level = item.level

        @pl.when(k < pieces)
        def mine_first():
            if chain:
                @pl.when(z + 1 < members)
                def onward():
                    item.up(True).start()

                @pl.when(z > 0)
                def back():
                    item.down(True).start()

            for jx in inner_x:
                item.to_x(jx, True).start()
            for jy in inner_y:
                item.to_y(jy, True).start()
            item.to_core(0, 0, True).start()

        @pl.when(k >= pieces)
        def arrive():
            item.landed().wait_recv()
            if chain:
                @pl.when((level < z) & (z + 1 < members))
                def onward():
                    item.up().start()

                @pl.when((level > z) & (z > 0))
                def back():
                    item.down().start()
            else:
                @pl.when(k + pieces < items)
                def following():
                    Item(k + pieces).straight().start()

            for jx in inner_x:
                item.to_x(jx).start()
            for jy in inner_y:
                item.to_y(jy).start()
            item.to_core(0, 0).start()

    def edges(k):
        item = Item(k)
        for jx in inner_x:
            item.to_x(jx).wait_recv()

            @pl.when(item.mine & item.even)
            def pass_a():
                for jy in inner_y:
                    item.corner_a(jx, jy).start()

            item.to_core(jx, 0).start()
        for jy in inner_y:
            item.to_y(jy).wait_recv()

            @pl.when(item.mine & jnp.logical_not(item.even))
            def pass_b():
                for jx in inner_x:
                    item.corner_b(jx, jy).start()

            item.to_core(0, jy).start()

    def corners(k):
        item = Item(k)

        @pl.when(item.mine)
        def mine_now():
            for jx in inner_x:
                for jy in inner_y:
                    item.corner_a(jx, jy).wait_recv()
                    if chain:
                        item.corner_z(jx, jy).start()
                    item.to_core(jx, jy).start()

    def handed(k):
        item = Item(k)

        @pl.when(jnp.logical_not(item.mine))
        def from_partner():
            for jx in inner_x:
                for jy in inner_y:
                    item.corner_z(jx, jy).wait_recv()
                    item.to_core(jx, jy).start()

    spots = xs * ys
    lag_edge, lag_corner = (2, 4) if chain else (1, 3)
    lag_handed = pieces + 6 if chain else lag_corner
    lag_end = lag_handed + 1

    def tick(t, carry):
        @pl.when(t < items)
        def arrivals():
            columns(t)

        @pl.when((t >= lag_edge) & (t < items + lag_edge))
        def sides():
            edges(t - lag_edge)

        @pl.when((t >= lag_corner) & (t < items + lag_corner))
        def far():
            corners(t - lag_corner)

        if chain:
            @pl.when((t >= lag_handed) & (t < items + lag_handed))
            def others():
                handed(t - lag_handed)

        def visit(e, carry):
            jc = lax.div(e, spots)
            spot = lax.rem(e, spots)
            jx, jy = lax.rem(spot, xs), lax.div(spot, xs)
            far = jnp.minimum(jx, 1) + jnp.minimum(jy, 1)
            lag = jnp.where(far == 0, 1, jnp.where(far == 1, lag_edge + 1, lag_end))
            k = t - lag

            @pl.when((k >= 0) & (k < items))
            def valid():
                item = Item(k)

                @pl.when(jc == 1)
                def shared():
                    item.to_core(jx, jy).wait_recv()

                if consume is not None:
                    consume(place.block(jx, jy, item.level, jc), item.level, item.piece)

            return carry

        return lax.fori_loop(0, 2 * spots, visit, carry)

    if ready is not None:
        own.wait()
        ready()
    lax.fori_loop(0, items + lag_end, tick, 0)

    def close(k, carry):
        item = Item(k)
        level = item.level
        if chain:
            @pl.when((level <= z) & (z + 1 < members))
            def onward():
                item.up().wait_send()

            @pl.when((level >= z) & (z > 0))
            def back():
                item.down().wait_send()
        else:
            @pl.when(k >= pieces)
            def sent():
                item.straight().wait_send()

        for jx in inner_x:
            item.to_x(jx).wait_send()
        for jy in inner_y:
            item.to_y(jy).wait_send()
        for jx in range(xs):
            for jy in range(ys):
                item.to_core(jx, jy).wait_send()

        @pl.when(item.mine)
        def mine_done():
            for jx in inner_x:
                for jy in inner_y:
                    item.corner_a(jx, jy).wait_send()
                    if chain:
                        item.corner_z(jx, jy).wait_send()

        return carry

    lax.fori_loop(0, items, close, 0)
    if ready is None:
        own.wait()


def spread_kernel(groups, members, chain, pieces, src, out, *sems):
    place = Place(groups, members)
    greet(place)
    spread_body(place, chain, pieces, src, out, sems, None)


def spread(src, groups, members, collective_id, chain, pieces):
    count, rows, width = src.shape
    return pl.pallas_call(
        functools.partial(spread_kernel, groups, members, chain, pieces),
        out_shape=jax.ShapeDtypeStruct((groups * members, rows, width), src.dtype),
        in_specs=[pl.BlockSpec(memory_space=pl.ANY)],
        out_specs=pl.BlockSpec(memory_space=pl.ANY),
        scratch_shapes=spread_sems(groups, members, pieces),
        compiler_params=pltpu.CompilerParams(collective_id=collective_id, has_side_effects=True),
        cost_estimate=pl.CostEstimate(
            flops=0, bytes_accessed=4 * groups * members * rows * width, transcendentals=0
        ),
    )(src)


def score_kernel(groups, members, share, pieces, src, table, target, out, stat, *rest):
    part, pool, part_sem, out_sems = rest[:4]
    sems = rest[4:]
    place = Place(groups, members)
    load_table = pltpu.make_async_copy(table, part, part_sem)
    load_table.start()
    greet(place)
    rows = pool.shape[1]
    size = rows // pieces

    def keep(block, piece):
        here = pl.ds(pl.multiple_of(piece * size, size), size)
        return pltpu.make_async_copy(pool.at[block, here], out.at[block, here], out_sems.at[block, piece])

    def consume(block, level, piece):
        keep(block, piece).start()
        here = pl.ds(pl.multiple_of(piece * size, size), size)
        model = lax.div(level, share)
        logits = project(part[model], pool[block, here])
        highest = jnp.max(logits, axis=0, keepdims=True)
        total = jnp.sum(jnp.exp(logits - highest), axis=0, keepdims=True)
        tokens = lax.broadcasted_iota(jnp.int32, logits.shape, 0)
        wanted = target[lax.div(block, members) * share + lax.rem(level, share), :, here]
        hit = jnp.sum(jnp.where(tokens == wanted, logits, 0.0), axis=0, keepdims=True)
        stat[block, 0:1, here] = highest + jnp.log(total)
        stat[block, 1:2, here] = hit

    spread_body(place, True, pieces, src, pool, sems, consume, load_table.wait)

    def close(block, carry):
        for piece in range(pieces):
            keep(block, piece).wait()
        return carry

    lax.fori_loop(0, groups * members, close, 0)


def spread_score(src, table_low, target_blocks, groups, members, share, collective_id, pieces=2):
    _, rows, width = src.shape
    blocks = groups * members
    return pl.pallas_call(
        functools.partial(score_kernel, groups, members, share, pieces),
        out_shape=(
            jax.ShapeDtypeStruct((blocks, rows, width), src.dtype),
            jax.ShapeDtypeStruct((blocks, 2, rows), jnp.float32),
        ),
        in_specs=[
            pl.BlockSpec(memory_space=pl.ANY),
            pl.BlockSpec(memory_space=pl.ANY),
            pl.BlockSpec(memory_space=pltpu.VMEM),
        ],
        out_specs=(pl.BlockSpec(memory_space=pl.ANY), pl.BlockSpec(memory_space=pltpu.VMEM)),
        scratch_shapes=[
            pltpu.VMEM(table_low.shape, table_low.dtype),
            pltpu.VMEM((blocks, rows, width), src.dtype),
            pltpu.SemaphoreType.DMA,
            pltpu.SemaphoreType.DMA((blocks, pieces)),
        ]
        + spread_sems(groups, members, pieces),
        compiler_params=pltpu.CompilerParams(
            collective_id=collective_id, has_side_effects=True, vmem_limit_bytes=60 * MIB
        ),
        cost_estimate=pl.CostEstimate(
            flops=2 * blocks * rows * table_low.shape[1] * width,
            bytes_accessed=2 * blocks * rows * width * 2,
            transcendentals=blocks * rows * table_low.shape[1],
        ),
    )(src, table_low, target_blocks)


def stats_kernel(outs_ref, table_ref, target_ref, stat_ref):
    logits = project(table_ref[0], outs_ref[0])
    highest = jnp.max(logits, axis=0, keepdims=True)
    total = jnp.sum(jnp.exp(logits - highest), axis=0, keepdims=True)
    rows = lax.broadcasted_iota(jnp.int32, logits.shape, 0)
    hit = jnp.sum(jnp.where(rows == target_ref[0], logits, 0.0), axis=0, keepdims=True)
    stat_ref[0, 0:1, :] = highest + jnp.log(total)
    stat_ref[0, 1:2, :] = hit


def head_stats(outs_all, table_low, target_blocks, groups, members, share):
    blocks, rows, width = outs_all.shape
    part_rows = table_low.shape[1]
    return pl.pallas_call(
        stats_kernel,
        out_shape=jax.ShapeDtypeStruct((blocks, 2, rows), jnp.float32),
        grid=(members, groups),
        in_specs=[
            pl.BlockSpec((1, rows, width), lambda z, g: (g * members + z, 0, 0)),
            pl.BlockSpec((1, part_rows, width), lambda z, g: (z // share, 0, 0)),
            pl.BlockSpec((1, 1, rows), lambda z, g: (g * share + z % share, 0, 0)),
        ],
        out_specs=pl.BlockSpec((1, 2, rows), lambda z, g: (g * members + z, 0, 0)),
        compiler_params=pltpu.CompilerParams(vmem_limit_bytes=56 * MIB),
        cost_estimate=pl.CostEstimate(
            flops=2 * blocks * rows * part_rows * width,
            bytes_accessed=2 * outs_all.size + 2 * table_low.size,
            transcendentals=blocks * rows * part_rows,
        ),
    )(outs_all, table_low, target_blocks)


def back_kernel(
    model_ref, fresh_ref, first_ref, second_ref, place_ref, a_ref, b_ref, table_ref, info_ref, target_ref, d_outs_ref,
    grad_ref, held, sems,
):
    step = pl.program_id(0)
    steps = pl.num_programs(0)
    seq_len = a_ref.shape[1]
    slot = lax.rem(step, 2)

    def leave(which, where, half):
        return pltpu.make_async_copy(
            held.at[which, half], d_outs_ref.at[where], sems.at[which, half]
        )

    @pl.when(step >= 2)
    def reuse():
        leave(slot, 0, 0).wait()
        leave(slot, 0, 1).wait()
    outs = jnp.concatenate([a_ref[0], b_ref[0]], axis=0)
    logits = project(table_ref[0], outs)
    rows = lax.broadcasted_iota(jnp.int32, logits.shape, 0)
    soft = jnp.exp(logits - info_ref[0, 0:1, :])
    hit = (rows == target_ref[0]).astype(jnp.float32)
    d_logits = (info_ref[0, 1:2, :] * (soft - hit)).astype(jnp.bfloat16)
    d_outs = outer_rows(d_logits, table_ref[0])
    held[slot, 0] = d_outs[:seq_len].astype(held.dtype)
    held[slot, 1] = d_outs[seq_len:].astype(held.dtype)
    leave(slot, place_ref[2 * step], 0).start()
    leave(slot, place_ref[2 * step + 1], 1).start()
    gain = product(d_logits, outs)

    @pl.when(fresh_ref[step] == 1)
    def start():
        grad_ref[0] = gain

    @pl.when(fresh_ref[step] == 0)
    def more():
        grad_ref[0] += gain

    @pl.when(step == steps - 1)
    def drain():
        for which in range(2):
            leave(which, 0, 0).wait()
            leave(which, 0, 1).wait()


def head_back(outs_pieces, table_low, model_of, fresh, first, second, place, info, target):
    steps = model_of.shape[0]
    models, part_rows, width = table_low.shape
    seq_len = outs_pieces.shape[1]
    return pl.pallas_call(
        back_kernel,
        out_shape=(
            jax.ShapeDtypeStruct((2 * steps, seq_len, width), jnp.bfloat16),
            jax.ShapeDtypeStruct((models, part_rows, width), jnp.float32),
        ),
        grid_spec=pltpu.PrefetchScalarGridSpec(
            num_scalar_prefetch=5,
            grid=(steps,),
            in_specs=[
                pl.BlockSpec((1, seq_len, width), lambda s, m, f, a, b, p: (a[s], 0, 0)),
                pl.BlockSpec((1, seq_len, width), lambda s, m, f, a, b, p: (b[s], 0, 0)),
                pl.BlockSpec((1, part_rows, width), lambda s, m, f, a, b, p: (m[s], 0, 0)),
                pl.BlockSpec((1, 2, 2 * seq_len), lambda s, m, f, a, b, p: (s, 0, 0)),
                pl.BlockSpec((1, 1, 2 * seq_len), lambda s, m, f, a, b, p: (s, 0, 0)),
            ],
            out_specs=(
                pl.BlockSpec(memory_space=pl.ANY),
                pl.BlockSpec((1, part_rows, width), lambda s, m, f, a, b, p: (m[s], 0, 0)),
            ),
            scratch_shapes=[
                pltpu.VMEM((2, 2, seq_len, width), jnp.bfloat16),
                pltpu.SemaphoreType.DMA((2, 2)),
            ],
        ),
        compiler_params=pltpu.CompilerParams(vmem_limit_bytes=56 * MIB),
        cost_estimate=pl.CostEstimate(
            flops=12 * steps * seq_len * part_rows * width,
            bytes_accessed=4 * steps * seq_len * width * 2 + 6 * table_low.size,
            transcendentals=2 * steps * seq_len * part_rows,
        ),
    )(model_of, fresh, first, second, place, outs_pieces, outs_pieces, table_low, info, target)


def finish_kernel(
    model_ref, fresh_ref, final_ref, first_ref, second_ref, a_ref, b_ref, ids_ref, head_ref, table_ref, momentum_ref,
    grad_ref, momentum_new_ref, table_new_ref,
):
    tile = pl.program_id(0)
    step = pl.program_id(1)
    tile_rows = grad_ref.shape[1]
    rows = lax.broadcasted_iota(jnp.int32, (tile_rows, ids_ref.shape[2]), 0) + tile * tile_rows
    hits = (rows == ids_ref[0]).astype(jnp.float32).astype(jnp.bfloat16)
    outs = jnp.concatenate([a_ref[0], b_ref[0]], axis=0)
    gain = product(hits, outs)

    @pl.when(fresh_ref[step] == 1)
    def start():
        grad_ref[0] = head_ref[0] + gain

    @pl.when(fresh_ref[step] == 0)
    def more():
        grad_ref[0] += gain

    @pl.when(final_ref[step] == 1)
    def close():
        renewed, fresh_table = update(table_ref[0], momentum_ref[0], grad_ref[0], table_rate)
        momentum_new_ref[0] = renewed
        table_new_ref[0] = fresh_table


def finish_table(d_inputs, head_grad, table, momentum, model_of, fresh, final, first, second, ids):
    steps = model_of.shape[0]
    models, part_rows, width = table.shape
    seq_len = d_inputs.shape[1]
    tile_rows = part_rows // 2
    state = jax.ShapeDtypeStruct(table.shape, jnp.float32)
    piece = pl.BlockSpec((1, tile_rows, width), lambda t, s, m, f, l, a, b: (m[s], t, 0))
    return pl.pallas_call(
        finish_kernel,
        out_shape=(state, state, state),
        grid_spec=pltpu.PrefetchScalarGridSpec(
            num_scalar_prefetch=5,
            grid=(part_rows // tile_rows, steps),
            in_specs=[
                pl.BlockSpec((1, seq_len, width), lambda t, s, m, f, l, a, b: (a[s], 0, 0)),
                pl.BlockSpec((1, seq_len, width), lambda t, s, m, f, l, a, b: (b[s], 0, 0)),
                pl.BlockSpec((1, 1, 2 * seq_len), lambda t, s, m, f, l, a, b: (s, 0, 0)),
                piece,
                piece,
                piece,
            ],
            out_specs=(piece, piece, piece),
        ),
        compiler_params=pltpu.CompilerParams(vmem_limit_bytes=56 * MIB),
        cost_estimate=pl.CostEstimate(
            flops=4 * steps * seq_len * part_rows * width,
            bytes_accessed=24 * table.size,
            transcendentals=0,
        ),
    )(model_of, fresh, final, first, second, d_inputs, d_inputs, ids, head_grad, table, momentum)


def body(
    token_ids,
    target_ids,
    segment_ids,
    chosen,
    table,
    table_momentum,
    stack,
    stack_momentum,
    vectors,
    vector_momentum,
):
    both = ("grp", "cli")
    models, block_rows, model_width = table.shape
    stack_part = stack.shape[1]
    seq_len = token_ids.shape[1]
    groups = lax.axis_size("grp")
    members = lax.axis_size("cli")
    devices = groups * members
    share = members // models
    local = members // share
    device_index = lax.axis_index(both)
    group_index = lax.axis_index("grp")
    member_index = lax.axis_index("cli")
    model_own = member_index // share
    part_own = member_index % share
    model_range = jnp.arange(models, dtype=jnp.int32)

    def per_member(rows):
        return jnp.repeat(rows, share, axis=0) if share > 1 else rows

    slab = -(-(stack_part + ROUND_ROWS) // SLAB_STEP) * SLAB_STEP
    round_rows = slab - stack_part

    facts = share_all(
        jnp.concatenate([token_ids[0], target_ids[0], segment_ids[0], chosen]), both, devices
    )
    tokens = facts[:, :seq_len]
    targets = facts[:, seq_len : 2 * seq_len]
    segments = facts[:, 2 * seq_len : 3 * seq_len]
    choices = facts[:, 3 * seq_len]
    valid = jnp.concatenate(
        [
            (segments[:, :-1] == segments[:, 1:]).astype(jnp.float32),
            jnp.zeros((devices, 1), jnp.float32),
        ],
        axis=1,
    )
    counts = jnp.sum(valid, axis=1)
    choice_table = (choices[:, None] == model_range[None, :]).astype(jnp.float32)
    totals = jnp.sum(choice_table * counts[:, None], axis=0)
    total_of = jnp.sum(choice_table * totals[None, :], axis=1)

    table_low = table.astype(jnp.bfloat16)
    fine = 16 if block_rows % 64 else 64
    coarse = block_rows // fine
    flat_tokens = tokens.reshape(-1)
    high_hot = (
        (flat_tokens // fine)[:, None] == jnp.arange(devices * coarse, dtype=jnp.int32)[None, :]
    ).astype(jnp.bfloat16)
    low_hot = ((flat_tokens % fine)[:, None] == jnp.arange(fine, dtype=jnp.int32)[None, :]).astype(
        jnp.bfloat16
    )
    seen = (outer_rows(high_hot, low_hot) > 0).astype(jnp.float32)
    before = product(
        seen.astype(jnp.bfloat16),
        jnp.triu(jnp.ones((fine, fine), jnp.bfloat16), 1),
    )
    sums = jnp.sum(seen, axis=1).reshape(devices, coarse)
    uniques = jnp.sum(sums, axis=1)
    ahead = jnp.sum(
        jnp.where(
            jnp.arange(coarse)[None, None, :] < jnp.arange(coarse)[None, :, None],
            sums[:, None, :],
            0.0,
        ),
        axis=2,
    )
    places = before + ahead.reshape(-1, 1)
    rounds = jnp.max(jnp.ceil(uniques / round_rows)).astype(jnp.int32)
    own_places = lax.dynamic_slice(places, (device_index * coarse, 0), (coarse, fine)).reshape(-1)
    own_seen = lax.dynamic_slice(seen, (device_index * coarse, 0), (coarse, fine)).reshape(-1)
    own_places = jnp.where(own_seen > 0, own_places, -1.0).astype(jnp.int32)
    first_client = group_index * members + part_own * local
    my_tokens = lax.dynamic_slice(tokens, (first_client, 0), (local, seq_len)).reshape(-1)
    my_segments = lax.dynamic_slice(segments, (first_client, 0), (local, seq_len))
    my_choices = lax.dynamic_slice(choices, (first_client,), (local,))
    my_high = (
        (my_tokens // fine)[:, None] == jnp.arange(devices * coarse, dtype=jnp.int32)[None, :]
    ).astype(jnp.bfloat16)
    my_low = (my_tokens % fine)[:, None] == jnp.arange(fine, dtype=jnp.int32)[None, :]
    split_places = jnp.concatenate(
        [jnp.floor(places / 64.0), places - 64.0 * jnp.floor(places / 64.0)], axis=1
    ).astype(jnp.bfloat16)
    picked_places = product(my_high, split_places)
    picked_places = 64.0 * picked_places[:, :fine] + picked_places[:, fine:]
    my_places = jnp.sum(jnp.where(my_low, picked_places, 0.0), axis=1).astype(jnp.int32)
    my_owner = my_tokens // block_rows

    def offered(start):
        wanted = jnp.arange(round_rows, dtype=jnp.int32) + start
        pick = (own_places[None, :] == wanted[:, None]).astype(jnp.bfloat16)
        rows = jnp.einsum("ur,krd->kud", pick, table_low, preferred_element_type=jnp.float32)
        return rows.astype(jnp.bfloat16)

    def taken(pool, lead, start, embedded):
        offset = my_places - start
        inside = (offset >= 0) & (offset < round_rows)
        at = my_owner * (lead + round_rows) + lead + offset
        found = jnp.take(pool.reshape(-1, model_width), jnp.where(inside, at, 0), axis=0)
        return jnp.where(inside[:, None], found.astype(jnp.float32), embedded)

    def another(carry):
        index, embedded = carry
        start = index * round_rows
        turned = lax.all_to_all(per_member(offered(start)), "cli", 0, 0, tiled=True)
        pool = lax.all_gather(turned, "grp", axis=0, tiled=True)
        return (index + 1, taken(pool, 0, start, embedded))

    slabs = jnp.concatenate([stack.astype(jnp.bfloat16), offered(0)], axis=1)
    pool = spread(per_member(slabs), groups, members, 1, False, 2)
    weights = pool[:, :stack_part].reshape(devices * stack_part, model_width)
    embedded = taken(
        pool, stack_part, 0, jnp.zeros((local * seq_len, model_width), jnp.float32)
    )
    _, embedded = lax.while_loop(
        lambda carry: carry[0] < rounds, another, (jnp.int32(1), embedded)
    )
    vector_one = lax.dynamic_index_in_dim(vectors, model_own, 0, keepdims=False)
    inputs = embedded + jnp.tile(weights[12 * model_width :].astype(jnp.float32), (local, 1))
    saved = layer_forward(weights, vector_one, inputs, my_segments)
    normed_out = saved[11]

    target_local = targets - device_index * block_rows
    target_local = jnp.where((target_local >= 0) & (target_local < block_rows), target_local, -1)
    target_blocks = target_local.reshape(groups * share, 1, local * seq_len)
    if devices * normed_out.size * 2 <= POOL_BYTES:
        outs_all, stats = spread_score(
            normed_out[None], table_low, target_blocks, groups, members, share, 2
        )
    else:
        outs_all = spread(normed_out[None], groups, members, 2, True, 2)
        stats = head_stats(outs_all, table_low, target_blocks, groups, members, share)
    shares = lax.all_to_all(stats, both, 0, 0, tiled=True)
    log_total = jax.nn.logsumexp(shares[:, 0], axis=0)
    token_loss = log_total - jnp.sum(shares[:, 1], axis=0)
    everything = share_all(jnp.stack([log_total, token_loss]), both, devices)
    everything = (
        everything.reshape(groups, models, share, 2, local, seq_len)
        .transpose(3, 1, 0, 2, 4, 5)
        .reshape(2, models, devices, seq_len)
    )
    all_losses = jnp.sum(everything[1] * valid[None], axis=2)
    loss = jnp.sum(choice_table.T * all_losses / total_of[None, :])
    client_losses = lax.dynamic_slice(
        (all_losses / counts[None, :]).T, (device_index, 0), (1, models)
    )
    chosen_total = jnp.sum(choice_table.T[:, :, None] * everything[0], axis=0)

    numbers = jnp.sum(choice_table, axis=0)
    padded = 2.0 * jnp.ceil(numbers / 2.0)
    offsets = jnp.cumsum(padded) - padded
    earlier = (
        jnp.arange(devices)[None, :] < jnp.arange(devices)[:, None]
    ) & (choices[None, :] == choices[:, None])
    slot_of = jnp.sum(choice_table * offsets[None, :], axis=1) + jnp.sum(
        earlier.astype(jnp.float32), axis=1
    )
    slots = devices + models
    steps = slots // 2
    at_slot = jnp.arange(slots)[:, None] == slot_of.astype(jnp.int32)[None, :]
    filled = jnp.any(at_slot, axis=1)
    client_at = jnp.sum(jnp.where(at_slot, jnp.arange(devices)[None, :], 0), axis=1).astype(
        jnp.int32
    )
    step_start = 2.0 * jnp.arange(steps)
    model_of = (
        jnp.sum((step_start[:, None] >= offsets[None, :]).astype(jnp.int32), axis=1) - 1
    ).astype(jnp.int32)
    fresh = jnp.concatenate(
        [jnp.ones((1,), jnp.int32), (model_of[1:] != model_of[:-1]).astype(jnp.int32)]
    )
    final = jnp.concatenate(
        [(model_of[1:] != model_of[:-1]).astype(jnp.int32), jnp.ones((1,), jnp.int32)]
    )
    within = client_at % members
    piece_at = (
        (client_at // members * members + jnp.repeat(model_of, 2) * share + within // local) * local
        + within % local
    ).astype(jnp.int32)
    weight_rows = valid / total_of[:, None]
    slot_log = jnp.where(filled[:, None], jnp.take(chosen_total, client_at, axis=0), 1e30)
    slot_weight = jnp.where(filled[:, None], jnp.take(weight_rows, client_at, axis=0), 0.0)
    slot_info = jnp.stack(
        [slot_log.reshape(steps, 2 * seq_len), slot_weight.reshape(steps, 2 * seq_len)], axis=1
    )
    slot_target = jnp.where(filled[:, None], jnp.take(target_local, client_at, axis=0), -1)
    spare = devices + jnp.cumsum(1 - filled.astype(jnp.int32)) - 1
    d_outs, head_grad = head_back(
        outs_all.reshape(-1, seq_len, model_width),
        table_low,
        model_of,
        fresh,
        piece_at[0::2],
        piece_at[1::2],
        jnp.where(filled, client_at, spare).astype(jnp.int32),
        slot_info,
        slot_target.reshape(steps, 1, 2 * seq_len),
    )
    d_group = lax.psum_scatter(
        d_outs[:devices].reshape(devices * seq_len, model_width),
        "grp",
        scatter_dimension=0,
        tiled=True,
    )
    d_group = lax.psum(d_group, "cli").reshape(members, seq_len, model_width)
    d_mine = lax.dynamic_slice(
        d_group, (part_own * local, 0, 0), (local, seq_len, model_width)
    ).astype(jnp.float32)
    d_final = jnp.where((my_choices == model_own)[:, None, None], d_mine, 0.0).reshape(
        local * seq_len, model_width
    )
    stack_rows, vector_rows, d_inputs = layer_backward(
        weights, vector_one, inputs, my_segments, saved, d_final
    )
    d_wide = d_inputs.astype(jnp.bfloat16)
    if share > 1:
        d_wide = lax.dynamic_update_slice(
            jnp.zeros((members * seq_len, model_width), jnp.bfloat16),
            d_wide,
            (part_own * local * seq_len, 0),
        )
    d_turned = lax.all_to_all(
        d_wide.reshape(members, seq_len, model_width), "cli", 0, 0, tiled=True
    )
    d_client = jnp.sum(d_turned.astype(jnp.float32), axis=0, keepdims=True).astype(jnp.bfloat16)
    d_all = spread(d_client, groups, members, 3, True, 2)

    stack_sum = lax.psum_scatter(stack_rows, "grp", scatter_dimension=0, tiled=True)
    stack_back = lax.all_to_all(
        stack_sum.reshape(members, stack_part, model_width), "cli", 0, 0, tiled=True
    ).astype(jnp.float32)
    stack_grad = jnp.sum(
        stack_back.reshape(models, share, stack_part, model_width), axis=1
    )
    vector_piece = vector_rows.size // groups
    vector_part = jnp.sum(
        lax.all_to_all(vector_rows.reshape(groups, vector_piece), "grp", 0, 0, tiled=True), axis=0
    )
    vector_grad = jnp.sum(
        share_all(vector_part, both, devices).reshape(groups, models, share, vector_piece), axis=2
    )
    vector_grad = vector_grad.transpose(1, 0, 2).reshape(vectors.shape)

    token_local = tokens - device_index * block_rows
    token_local = jnp.where((token_local >= 0) & (token_local < block_rows), token_local, -1)
    slot_token = jnp.where(filled[:, None], jnp.take(token_local, client_at, axis=0), -1)
    table_grad, table_momentum_new, table_new = finish_table(
        d_all,
        head_grad,
        table,
        table_momentum,
        model_of,
        fresh,
        final,
        client_at[0::2],
        client_at[1::2],
        slot_token.reshape(steps, 1, 2 * seq_len),
    )
    stack_momentum_new, stack_new = update(stack, stack_momentum, stack_grad, stack_rate)
    vector_momentum_new, vector_new = update(vectors, vector_momentum, vector_grad, vector_rate)
    return (
        loss,
        client_losses,
        table_grad,
        table_momentum_new,
        table_new,
        stack_grad,
        stack_momentum_new,
        stack_new,
        vector_grad,
        vector_momentum_new,
        vector_new,
    )


def solution(mesh):
    rows = P(("grp", "cli"), None)
    parts = P(None, ("grp", "cli"), None)
    return jax.shard_map(
        body,
        mesh=mesh,
        in_specs=(rows, rows, rows, P(("grp", "cli")), parts, parts, parts, parts, P(), P()),
        out_specs=(P(), rows, parts, parts, parts, parts, parts, parts, P(), P(), P()),
        check_vma=False,
    )
```

```python
import functools
import math

import jax
import jax.numpy as jnp
from jax import lax
from jax.experimental import pallas as pl
from jax.experimental.pallas import tpu as pltpu
from jax.sharding import PartitionSpec as P

HEADS = 12
HEAD_DIM = 64


epsilon = 1e-05
momentum_decay = 0.9
table_rate = 4.0
stack_rate = 4.0
vector_rate = 50.0

ROUND_ROWS = 128
SLAB_STEP = 32
MIB = 1 << 20
POOL_BYTES = 32 * MIB
MESH = pl.DeviceIdType.MESH


def layer_norm(inputs, gain_row, shift_row):
    centred = inputs - jnp.mean(inputs, -1, keepdims=True)
    spread = jnp.mean(centred * centred, -1, keepdims=True)
    return centred * lax.rsqrt(spread + epsilon) * gain_row + shift_row


def project(inputs, matrix):
    return lax.dot_general(
        inputs, matrix, (((1,), (1,)), ((), ())), preferred_element_type=jnp.float32
    )


def product(inputs, matrix):
    return jnp.dot(inputs, matrix, preferred_element_type=jnp.float32)


def outer_rows(left, right):
    return lax.dot_general(
        left, right, (((0,), (0,)), ((), ())), preferred_element_type=jnp.float32
    )


def split_heads(rows, seq_len):
    return rows.reshape(-1, seq_len, HEADS, HEAD_DIM)


def attend(queries, key_rows, segment_rows):
    seq_len = segment_rows.shape[1]
    scores = jnp.einsum(
        "nqhd,nkhd->nhqk",
        split_heads(queries, seq_len),
        split_heads(key_rows, seq_len),
        preferred_element_type=jnp.float32,
    ) * HEAD_DIM ** (-0.5)
    positions = jnp.arange(seq_len)
    allowed = (positions[None, None, :] <= positions[None, :, None]) & (
        segment_rows[:, None, :] == segment_rows[:, :, None]
    )
    return jax.nn.softmax(jnp.where(allowed[:, None], scores, -1e30), axis=-1)


def layer_forward(weights, vector_one, inputs, segment_rows):
    row_count, model_width = inputs.shape
    seq_len = segment_rows.shape[1]
    normed = layer_norm(inputs, vector_one[0], vector_one[1]).astype(jnp.bfloat16)
    queries = (project(normed, weights[0:model_width]) + vector_one[6]).astype(jnp.bfloat16)
    key_rows = project(normed, weights[model_width : 2 * model_width]).astype(jnp.bfloat16)
    values = (project(normed, weights[2 * model_width : 3 * model_width]) + vector_one[7]).astype(
        jnp.bfloat16
    )
    attention = attend(queries, key_rows, segment_rows)
    mixture = jnp.einsum(
        "nhqk,nkhd->nqhd",
        attention.astype(jnp.bfloat16),
        split_heads(values, seq_len),
        preferred_element_type=jnp.float32,
    )
    mixture = mixture.reshape(row_count, model_width).astype(jnp.bfloat16)
    middle = inputs + (project(mixture, weights[3 * model_width : 4 * model_width]) + vector_one[8])
    normed_two = layer_norm(middle, vector_one[2], vector_one[3]).astype(jnp.bfloat16)
    hidden = project(normed_two, weights[4 * model_width : 8 * model_width]) + vector_one[
        10:14
    ].reshape(-1)
    active = jax.nn.gelu(hidden, approximate=True).astype(jnp.bfloat16)
    residual = middle + (
        product(active, weights[8 * model_width : 12 * model_width]) + vector_one[9]
    )
    normed_out = layer_norm(residual, vector_one[4], vector_one[5]).astype(jnp.bfloat16)
    return (
        normed,
        queries,
        key_rows,
        values,
        attention,
        mixture,
        middle,
        normed_two,
        hidden,
        active,
        residual,
        normed_out,
    )


def norm_grad(operand, gain_row, shift_row, cotangent):
    outcome, pullback = jax.vjp(layer_norm, operand, gain_row, shift_row)
    return pullback(cotangent)


def gelu_tanh(hidden):
    return jax.nn.gelu(hidden, approximate=True)


def layer_backward(weights, vector_one, inputs, segment_rows, saved, grad_out):
    row_count, model_width = inputs.shape
    seq_len = segment_rows.shape[1]
    scaling = HEAD_DIM ** (-0.5)
    (
        normed,
        queries,
        key_rows,
        values,
        attention,
        mixture,
        middle,
        normed_two,
        hidden,
        active,
        residual,
        normed_out,
    ) = saved
    d_residual, d_gain_out, d_shift_out = norm_grad(
        residual, vector_one[4], vector_one[5], grad_out
    )
    d_outer = d_residual.astype(jnp.bfloat16)
    d_bias_out = jnp.sum(d_outer.astype(jnp.float32), 0)
    grad_down = outer_rows(active, d_outer)
    d_active = project(d_outer, weights[8 * model_width : 12 * model_width])
    gelu_value, gelu_pull = jax.vjp(gelu_tanh, hidden)
    d_hidden = gelu_pull(d_active)[0].astype(jnp.bfloat16)
    d_bias_hidden = jnp.sum(d_hidden.astype(jnp.float32), 0)
    grad_up = outer_rows(d_hidden, normed_two)
    d_normed_two = product(d_hidden, weights[4 * model_width : 8 * model_width])
    d_middle_norm, d_gain_two, d_shift_two = norm_grad(
        middle, vector_one[2], vector_one[3], d_normed_two
    )
    d_middle = d_residual + d_middle_norm
    d_branch = d_middle.astype(jnp.bfloat16)
    d_bias_branch = jnp.sum(d_branch.astype(jnp.float32), 0)
    grad_mix = outer_rows(d_branch, mixture)
    d_mixture = split_heads(
        product(d_branch, weights[3 * model_width : 4 * model_width]).astype(jnp.bfloat16), seq_len
    )
    d_attention = jnp.einsum(
        "nqhd,nkhd->nhqk", d_mixture, split_heads(values, seq_len), preferred_element_type=jnp.float32
    )
    d_values = jnp.einsum(
        "nhqk,nqhd->nkhd",
        attention.astype(jnp.bfloat16),
        d_mixture,
        preferred_element_type=jnp.float32,
    )
    d_values = d_values.reshape(row_count, model_width).astype(jnp.bfloat16)
    d_scores = (
        attention * (d_attention - jnp.sum(attention * d_attention, -1, keepdims=True))
    ).astype(jnp.bfloat16)
    d_queries = (
        jnp.einsum(
            "nhqk,nkhd->nqhd",
            d_scores,
            split_heads(key_rows, seq_len),
            preferred_element_type=jnp.float32,
        )
        * scaling
    )
    d_queries = d_queries.reshape(row_count, model_width).astype(jnp.bfloat16)
    d_keys = (
        jnp.einsum(
            "nhqk,nqhd->nkhd",
            d_scores,
            split_heads(queries, seq_len),
            preferred_element_type=jnp.float32,
        )
        * scaling
    )
    d_keys = d_keys.reshape(row_count, model_width).astype(jnp.bfloat16)
    d_joined = jnp.concatenate([d_queries, d_keys, d_values], axis=1)
    grad_joined = outer_rows(d_joined, normed)
    d_normed = product(d_joined, weights[0 : 3 * model_width])
    d_inputs_norm, d_gain_one, d_shift_one = norm_grad(
        inputs, vector_one[0], vector_one[1], d_normed
    )
    d_inputs = d_middle + d_inputs_norm
    grad_places = jnp.sum(d_inputs.reshape(-1, seq_len, model_width), axis=0)
    stack_rows = jnp.concatenate(
        [
            piece.astype(jnp.bfloat16)
            for piece in (grad_joined, grad_mix, grad_up, grad_down, grad_places)
        ],
        axis=0,
    )
    bias_query = jnp.sum(d_queries.astype(jnp.float32), 0)
    bias_value = jnp.sum(d_values.astype(jnp.float32), 0)
    vector_rows = jnp.concatenate(
        [
            jnp.stack(
                [
                    d_gain_one,
                    d_shift_one,
                    d_gain_two,
                    d_shift_two,
                    d_gain_out,
                    d_shift_out,
                    bias_query,
                    bias_value,
                    d_bias_branch,
                    d_bias_out,
                ]
            ),
            d_bias_hidden.reshape(4, model_width),
        ],
        axis=0,
    )
    return (stack_rows, vector_rows, d_inputs)


def share_all(rows, axes, size):
    return lax.all_to_all(
        jnp.broadcast_to(rows[None], (size,) + rows.shape), axes, 0, 0, tiled=True
    )


def update(weight, momentum, gradient, step_rate):
    renewed = momentum_decay * momentum + gradient
    return (renewed, weight - step_rate * (gradient + momentum_decay * renewed))


def flipped(value, offset, size):
    bit = 1
    while bit < size:
        digit = lax.rem(lax.div(offset, bit), 2)
        value = value + digit * bit * (1 - 2 * lax.rem(lax.div(value, bit), 2))
        bit *= 2
    return value


class Place:
    def __init__(self, groups, members):
        self.groups, self.members = groups, members
        self.ys = 2
        self.xs = groups // 4
        self.grp = lax.axis_index("grp")
        self.cli = lax.axis_index("cli")
        self.core = lax.rem(self.grp, 2)
        self.x = lax.rem(lax.div(self.grp, 2), self.xs)
        self.y = lax.div(self.grp, 2 * self.xs)

    def group(self, jx=0, jy=0, jc=0):
        x = flipped(self.x, jx, self.xs)
        y = flipped(self.y, jy, self.ys)
        core = self.core + jc * (1 - 2 * self.core)
        return (y * self.xs + x) * 2 + core

    def block(self, jx, jy, level, jc=0):
        return self.group(jx, jy, jc) * self.members + level

    def peer(self, jx=0, jy=0, jc=0):
        return (self.group(jx, jy, jc), self.cli)

    def level(self, level):
        return (self.grp, level)

    def nearest(self, i):
        z, last = self.cli, self.members - 1
        low = jnp.where(2 * z < last, 1, 0)
        sign = 2 * low - 1
        margin = low * z + (1 - low) * (last - z)
        step = lax.div(i + 1, 2)
        odd = lax.rem(i, 2)
        near = z + sign * step * (2 * odd - 1)
        far = z + sign * (i - margin)
        return jnp.where(i <= 2 * margin, near, far)


def greet(place):
    barrier = pltpu.get_barrier_semaphore()
    peers = [place.peer(jx=j) for j in range(1, place.xs)] + [place.peer(jy=j) for j in range(1, place.ys)]
    peers.append(place.peer(jc=1))
    peers += [place.level(lax.rem(place.cli + j, place.members)) for j in range(1, place.members)]
    for peer in peers:
        pl.semaphore_signal(barrier, inc=1, device_id=peer, device_id_type=MESH)
    pl.semaphore_wait(barrier, len(peers))


def spread_sems(groups, members, pieces):
    xs, ys, items = groups // 4, 2, members * pieces
    dma = pltpu.SemaphoreType.DMA
    shapes = [(items,)] * 3 + [(items, xs)] * 2 + [(items, ys)] * 2 + [(items, xs, ys)] * 6
    return [dma] + [dma(shape) for shape in shapes]


def spread_body(place, chain, pieces, src, out, sems, consume, ready=None):
    (own_sem, z_up, z_down, z_recv, x_send, x_recv, y_send, y_recv, k_send, k_recv, p_send, p_recv,
     c_send, c_recv) = sems
    xs, ys, members = place.xs, place.ys, place.members
    items = members * pieces
    size = out.shape[1] // pieces
    z = place.cli
    partner = z + 1 - 2 * lax.rem(z, 2)
    inner_x, inner_y = range(1, xs), range(1, ys)

    def move(source, target, send, recv, device):
        return pltpu.make_async_remote_copy(
            src_ref=source, dst_ref=target, send_sem=send, recv_sem=recv, device_id=device, device_id_type=MESH
        )

    class Item:
        def __init__(self, k):
            self.level = place.nearest(lax.div(k, pieces))
            self.piece = lax.rem(k, pieces)
            self.slot = self.level * pieces + self.piece
            self.even = lax.rem(self.piece, 2) == 0
            self.mine = lax.rem(self.level + z, 2) == 0 if chain else self.level >= 0
            self.rows = pl.ds(self.piece * size, size)

        def part(self, jx, jy, level=None):
            return out.at[place.block(jx, jy, self.level if level is None else level), self.rows]

        def here(self, own):
            return src.at[z if not chain else 0, self.rows] if own else self.part(0, 0)

        def up(self, own=False):
            return move(self.here(own), self.part(0, 0), z_up.at[self.slot], z_recv.at[self.slot], place.level(z + 1))

        def down(self, own=False):
            return move(self.here(own), self.part(0, 0), z_down.at[self.slot], z_recv.at[self.slot], place.level(z - 1))

        def straight(self):
            return move(
                src.at[self.level, self.rows], self.part(0, 0, z), z_up.at[self.slot],
                z_recv.at[z * pieces + self.piece], place.level(self.level),
            )

        def landed(self):
            part = self.part(0, 0)
            return move(part, part, z_up.at[self.slot], z_recv.at[self.slot], place.level(partner))

        def to_x(self, jx, own=False):
            return move(self.here(own), self.part(0, 0), x_send.at[self.slot, jx], x_recv.at[self.slot, jx], place.peer(jx=jx))

        def to_y(self, jy, own=False):
            return move(self.here(own), self.part(0, 0), y_send.at[self.slot, jy], y_recv.at[self.slot, jy], place.peer(jy=jy))

        def corner_a(self, jx, jy):
            part = self.part(jx, 0)
            return move(part, part, k_send.at[self.slot, jx, jy], k_recv.at[self.slot, jx, jy], place.peer(jy=jy))

        def corner_b(self, jx, jy):
            part = self.part(0, jy)
            return move(part, part, k_send.at[self.slot, jx, jy], k_recv.at[self.slot, jx, jy], place.peer(jx=jx))

        def corner_z(self, jx, jy):
            part = self.part(jx, jy)
            return move(part, part, p_send.at[self.slot, jx, jy], p_recv.at[self.slot, jx, jy], place.level(partner))

        def to_core(self, jx, jy, own=False):
            part = self.part(jx, jy)
            return move(self.here(True) if own else part, part, c_send.at[self.slot, jx, jy], c_recv.at[self.slot, jx, jy], place.peer(jc=1))

    own = pltpu.make_async_copy(src.at[z if not chain else 0], out.at[place.block(0, 0, z)], own_sem)
    own.start()
    if not chain:
        for piece in range(pieces):
            Item(pieces + piece).straight().start()

    def columns(k):
        item = Item(k)
        level = item.level

        @pl.when(k < pieces)
        def mine_first():
            if chain:
                @pl.when(z + 1 < members)
                def onward():
                    item.up(True).start()

                @pl.when(z > 0)
                def back():
                    item.down(True).start()

            for jx in inner_x:
                item.to_x(jx, True).start()
            for jy in inner_y:
                item.to_y(jy, True).start()
            item.to_core(0, 0, True).start()

        @pl.when(k >= pieces)
        def arrive():
            item.landed().wait_recv()
            if chain:
                @pl.when((level < z) & (z + 1 < members))
                def onward():
                    item.up().start()

                @pl.when((level > z) & (z > 0))
                def back():
                    item.down().start()
            else:
                @pl.when(k + pieces < items)
                def following():
                    Item(k + pieces).straight().start()

            for jx in inner_x:
                item.to_x(jx).start()
            for jy in inner_y:
                item.to_y(jy).start()
            item.to_core(0, 0).start()

    def edges(k):
        item = Item(k)
        for jx in inner_x:
            item.to_x(jx).wait_recv()

            @pl.when(item.mine & item.even)
            def pass_a():
                for jy in inner_y:
                    item.corner_a(jx, jy).start()

            item.to_core(jx, 0).start()
        for jy in inner_y:
            item.to_y(jy).wait_recv()

            @pl.when(item.mine & jnp.logical_not(item.even))
            def pass_b():
                for jx in inner_x:
                    item.corner_b(jx, jy).start()

            item.to_core(0, jy).start()

    def corners(k):
        item = Item(k)

        @pl.when(item.mine)
        def mine_now():
            for jx in inner_x:
                for jy in inner_y:
                    item.corner_a(jx, jy).wait_recv()
                    if chain:
                        item.corner_z(jx, jy).start()
                    item.to_core(jx, jy).start()

    def handed(k):
        item = Item(k)

        @pl.when(jnp.logical_not(item.mine))
        def from_partner():
            for jx in inner_x:
                for jy in inner_y:
                    item.corner_z(jx, jy).wait_recv()
                    item.to_core(jx, jy).start()

    spots = xs * ys
    lag_edge, lag_corner = (2, 4) if chain else (1, 3)
    lag_handed = pieces + 6 if chain else lag_corner
    lag_end = lag_handed + 1

    def tick(t, carry):
        @pl.when(t < items)
        def arrivals():
            columns(t)

        @pl.when((t >= lag_edge) & (t < items + lag_edge))
        def sides():
            edges(t - lag_edge)

        @pl.when((t >= lag_corner) & (t < items + lag_corner))
        def far():
            corners(t - lag_corner)

        if chain:
            @pl.when((t >= lag_handed) & (t < items + lag_handed))
            def others():
                handed(t - lag_handed)

        def visit(e, carry):
            jc = lax.div(e, spots)
            spot = lax.rem(e, spots)
            jx, jy = lax.rem(spot, xs), lax.div(spot, xs)
            far = jnp.minimum(jx, 1) + jnp.minimum(jy, 1)
            lag = jnp.where(far == 0, 1, jnp.where(far == 1, lag_edge + 1, lag_end))
            k = t - lag

            @pl.when((k >= 0) & (k < items))
            def valid():
                item = Item(k)

                @pl.when(jc == 1)
                def shared():
                    item.to_core(jx, jy).wait_recv()

                if consume is not None:
                    consume(place.block(jx, jy, item.level, jc), item.level, item.piece)

            return carry

        return lax.fori_loop(0, 2 * spots, visit, carry)

    if ready is not None:
        own.wait()
        ready()
    lax.fori_loop(0, items + lag_end, tick, 0)

    def close(k, carry):
        item = Item(k)
        level = item.level
        if chain:
            @pl.when((level <= z) & (z + 1 < members))
            def onward():
                item.up().wait_send()

            @pl.when((level >= z) & (z > 0))
            def back():
                item.down().wait_send()
        else:
            @pl.when(k >= pieces)
            def sent():
                item.straight().wait_send()

        for jx in inner_x:
            item.to_x(jx).wait_send()
        for jy in inner_y:
            item.to_y(jy).wait_send()
        for jx in range(xs):
            for jy in range(ys):
                item.to_core(jx, jy).wait_send()

        @pl.when(item.mine)
        def mine_done():
            for jx in inner_x:
                for jy in inner_y:
                    item.corner_a(jx, jy).wait_send()
                    if chain:
                        item.corner_z(jx, jy).wait_send()

        return carry

    lax.fori_loop(0, items, close, 0)
    if ready is None:
        own.wait()


def spread_kernel(groups, members, chain, pieces, src, out, *sems):
    place = Place(groups, members)
    greet(place)
    spread_body(place, chain, pieces, src, out, sems, None)


def spread(src, groups, members, collective_id, chain, pieces):
    count, rows, width = src.shape
    return pl.pallas_call(
        functools.partial(spread_kernel, groups, members, chain, pieces),
        out_shape=jax.ShapeDtypeStruct((groups * members, rows, width), src.dtype),
        in_specs=[pl.BlockSpec(memory_space=pl.ANY)],
        out_specs=pl.BlockSpec(memory_space=pl.ANY),
        scratch_shapes=spread_sems(groups, members, pieces),
        compiler_params=pltpu.CompilerParams(collective_id=collective_id, has_side_effects=True),
        cost_estimate=pl.CostEstimate(
            flops=0, bytes_accessed=4 * groups * members * rows * width, transcendentals=0
        ),
    )(src)


def score_kernel(groups, members, share, pieces, src, table, target, out, stat, *rest):
    part, pool, part_sem, out_sems = rest[:4]
    sems = rest[4:]
    place = Place(groups, members)
    load_table = pltpu.make_async_copy(table, part, part_sem)
    load_table.start()
    greet(place)
    rows = pool.shape[1]
    size = rows // pieces

    def keep(block, piece):
        here = pl.ds(pl.multiple_of(piece * size, size), size)
        return pltpu.make_async_copy(pool.at[block, here], out.at[block, here], out_sems.at[block, piece])

    def consume(block, level, piece):
        keep(block, piece).start()
        here = pl.ds(pl.multiple_of(piece * size, size), size)
        model = lax.div(level, share)
        logits = project(part[model], pool[block, here])
        highest = jnp.max(logits, axis=0, keepdims=True)
        total = jnp.sum(jnp.exp(logits - highest), axis=0, keepdims=True)
        tokens = lax.broadcasted_iota(jnp.int32, logits.shape, 0)
        wanted = target[lax.div(block, members) * share + lax.rem(level, share), :, here]
        hit = jnp.sum(jnp.where(tokens == wanted, logits, 0.0), axis=0, keepdims=True)
        stat[block, 0:1, here] = highest + jnp.log(total)
        stat[block, 1:2, here] = hit

    spread_body(place, True, pieces, src, pool, sems, consume, load_table.wait)

    def close(block, carry):
        for piece in range(pieces):
            keep(block, piece).wait()
        return carry

    lax.fori_loop(0, groups * members, close, 0)


def spread_score(src, table_low, target_blocks, groups, members, share, collective_id, pieces=2):
    _, rows, width = src.shape
    blocks = groups * members
    return pl.pallas_call(
        functools.partial(score_kernel, groups, members, share, pieces),
        out_shape=(
            jax.ShapeDtypeStruct((blocks, rows, width), src.dtype),
            jax.ShapeDtypeStruct((blocks, 2, rows), jnp.float32),
        ),
        in_specs=[
            pl.BlockSpec(memory_space=pl.ANY),
            pl.BlockSpec(memory_space=pl.ANY),
            pl.BlockSpec(memory_space=pltpu.VMEM),
        ],
        out_specs=(pl.BlockSpec(memory_space=pl.ANY), pl.BlockSpec(memory_space=pltpu.VMEM)),
        scratch_shapes=[
            pltpu.VMEM(table_low.shape, table_low.dtype),
            pltpu.VMEM((blocks, rows, width), src.dtype),
            pltpu.SemaphoreType.DMA,
            pltpu.SemaphoreType.DMA((blocks, pieces)),
        ]
        + spread_sems(groups, members, pieces),
        compiler_params=pltpu.CompilerParams(
            collective_id=collective_id, has_side_effects=True, vmem_limit_bytes=60 * MIB
        ),
        cost_estimate=pl.CostEstimate(
            flops=2 * blocks * rows * table_low.shape[1] * width,
            bytes_accessed=2 * blocks * rows * width * 2,
            transcendentals=blocks * rows * table_low.shape[1],
        ),
    )(src, table_low, target_blocks)


def stats_kernel(outs_ref, table_ref, target_ref, stat_ref):
    logits = project(table_ref[0], outs_ref[0])
    highest = jnp.max(logits, axis=0, keepdims=True)
    total = jnp.sum(jnp.exp(logits - highest), axis=0, keepdims=True)
    rows = lax.broadcasted_iota(jnp.int32, logits.shape, 0)
    hit = jnp.sum(jnp.where(rows == target_ref[0], logits, 0.0), axis=0, keepdims=True)
    stat_ref[0, 0:1, :] = highest + jnp.log(total)
    stat_ref[0, 1:2, :] = hit


def head_stats(outs_all, table_low, target_blocks, groups, members, share):
    blocks, rows, width = outs_all.shape
    part_rows = table_low.shape[1]
    return pl.pallas_call(
        stats_kernel,
        out_shape=jax.ShapeDtypeStruct((blocks, 2, rows), jnp.float32),
        grid=(members, groups),
        in_specs=[
            pl.BlockSpec((1, rows, width), lambda z, g: (g * members + z, 0, 0)),
            pl.BlockSpec((1, part_rows, width), lambda z, g: (z // share, 0, 0)),
            pl.BlockSpec((1, 1, rows), lambda z, g: (g * share + z % share, 0, 0)),
        ],
        out_specs=pl.BlockSpec((1, 2, rows), lambda z, g: (g * members + z, 0, 0)),
        compiler_params=pltpu.CompilerParams(vmem_limit_bytes=56 * MIB),
        cost_estimate=pl.CostEstimate(
            flops=2 * blocks * rows * part_rows * width,
            bytes_accessed=2 * outs_all.size + 2 * table_low.size,
            transcendentals=blocks * rows * part_rows,
        ),
    )(outs_all, table_low, target_blocks)


def unpack_kernel(start, part, at_ref, pool_ref, weights_ref, rows_ref):
    step = pl.program_id(0)
    owners, slab, width = pool_ref.shape
    weights_ref[...] = jnp.concatenate([pool_ref[j, :part] for j in range(owners)], axis=0)
    columns = lax.broadcasted_iota(jnp.int32, (at_ref.shape[0], slab - start), 1) + start
    found = jnp.zeros(rows_ref.shape, jnp.float32)
    for j in range(owners):
        at = at_ref[...] - (step * owners + j) * slab
        hits = (columns == at).astype(jnp.float32).astype(jnp.bfloat16)
        found = found + product(hits, pool_ref[j, start:])

    @pl.when(step == 0)
    def begin():
        rows_ref[...] = found

    @pl.when(step > 0)
    def more():
        rows_ref[...] += found


def unpack(pool, part, at):
    devices, slab, width = pool.shape
    owners = 8 // math.gcd(part, 8)
    start = part // 16 * 16
    tokens = at.shape[0]
    return pl.pallas_call(
        functools.partial(unpack_kernel, start, part),
        out_shape=(
            jax.ShapeDtypeStruct((devices * part, width), pool.dtype),
            jax.ShapeDtypeStruct((tokens, width), jnp.float32),
        ),
        grid=(devices // owners,),
        in_specs=[
            pl.BlockSpec((tokens, 1), lambda i: (0, 0)),
            pl.BlockSpec((owners, slab, width), lambda i: (i, 0, 0)),
        ],
        out_specs=(
            pl.BlockSpec((owners * part, width), lambda i: (i, 0)),
            pl.BlockSpec((tokens, width), lambda i: (0, 0)),
        ),
        compiler_params=pltpu.CompilerParams(vmem_limit_bytes=40 * MIB),
        cost_estimate=pl.CostEstimate(
            flops=2 * devices * tokens * (slab - start) * width,
            bytes_accessed=4 * pool.size,
            transcendentals=0,
        ),
    )(at, pool)


def back_kernel(
    model_ref, fresh_ref, first_ref, second_ref, place_ref, a_ref, b_ref, table_ref, info_ref, target_ref, d_outs_ref,
    grad_ref, held, sems,
):
    step = pl.program_id(0)
    steps = pl.num_programs(0)
    seq_len = a_ref.shape[1]
    slot = lax.rem(step, 2)

    def leave(which, where, half):
        return pltpu.make_async_copy(
            held.at[which, half], d_outs_ref.at[where], sems.at[which, half]
        )

    @pl.when(step >= 2)
    def reuse():
        leave(slot, 0, 0).wait()
        leave(slot, 0, 1).wait()
    outs = jnp.concatenate([a_ref[0], b_ref[0]], axis=0)
    logits = project(table_ref[0], outs)
    rows = lax.broadcasted_iota(jnp.int32, logits.shape, 0)
    soft = jnp.exp(logits - info_ref[0, 0:1, :])
    hit = (rows == target_ref[0]).astype(jnp.float32)
    d_logits = (info_ref[0, 1:2, :] * (soft - hit)).astype(jnp.bfloat16)
    d_outs = outer_rows(d_logits, table_ref[0])
    held[slot, 0] = d_outs[:seq_len].astype(held.dtype)
    held[slot, 1] = d_outs[seq_len:].astype(held.dtype)
    leave(slot, place_ref[2 * step], 0).start()
    leave(slot, place_ref[2 * step + 1], 1).start()
    gain = product(d_logits, outs)

    @pl.when(fresh_ref[step] == 1)
    def start():
        grad_ref[0] = gain

    @pl.when(fresh_ref[step] == 0)
    def more():
        grad_ref[0] += gain

    @pl.when(step == steps - 1)
    def drain():
        for which in range(2):
            leave(which, 0, 0).wait()
            leave(which, 0, 1).wait()


def head_back(outs_pieces, table_low, model_of, fresh, first, second, place, info, target):
    steps = model_of.shape[0]
    models, part_rows, width = table_low.shape
    seq_len = outs_pieces.shape[1]
    return pl.pallas_call(
        back_kernel,
        out_shape=(
            jax.ShapeDtypeStruct((2 * steps, seq_len, width), jnp.bfloat16),
            jax.ShapeDtypeStruct((models, part_rows, width), jnp.float32),
        ),
        grid_spec=pltpu.PrefetchScalarGridSpec(
            num_scalar_prefetch=5,
            grid=(steps,),
            in_specs=[
                pl.BlockSpec((1, seq_len, width), lambda s, m, f, a, b, p: (a[s], 0, 0)),
                pl.BlockSpec((1, seq_len, width), lambda s, m, f, a, b, p: (b[s], 0, 0)),
                pl.BlockSpec((1, part_rows, width), lambda s, m, f, a, b, p: (m[s], 0, 0)),
                pl.BlockSpec((1, 2, 2 * seq_len), lambda s, m, f, a, b, p: (s, 0, 0)),
                pl.BlockSpec((1, 1, 2 * seq_len), lambda s, m, f, a, b, p: (s, 0, 0)),
            ],
            out_specs=(
                pl.BlockSpec(memory_space=pl.ANY),
                pl.BlockSpec((1, part_rows, width), lambda s, m, f, a, b, p: (m[s], 0, 0)),
            ),
            scratch_shapes=[
                pltpu.VMEM((2, 2, seq_len, width), jnp.bfloat16),
                pltpu.SemaphoreType.DMA((2, 2)),
            ],
        ),
        compiler_params=pltpu.CompilerParams(vmem_limit_bytes=56 * MIB),
        cost_estimate=pl.CostEstimate(
            flops=12 * steps * seq_len * part_rows * width,
            bytes_accessed=4 * steps * seq_len * width * 2 + 6 * table_low.size,
            transcendentals=2 * steps * seq_len * part_rows,
        ),
    )(model_of, fresh, first, second, place, outs_pieces, outs_pieces, table_low, info, target)


def finish_kernel(
    model_ref, fresh_ref, final_ref, first_ref, second_ref, a_ref, b_ref, ids_ref, head_ref, table_ref, momentum_ref,
    grad_ref, momentum_new_ref, table_new_ref,
):
    tile = pl.program_id(0)
    step = pl.program_id(1)
    tile_rows = grad_ref.shape[1]
    rows = lax.broadcasted_iota(jnp.int32, (tile_rows, ids_ref.shape[2]), 0) + tile * tile_rows
    hits = (rows == ids_ref[0]).astype(jnp.float32).astype(jnp.bfloat16)
    outs = jnp.concatenate([a_ref[0], b_ref[0]], axis=0)
    gain = product(hits, outs)

    @pl.when(fresh_ref[step] == 1)
    def start():
        grad_ref[0] = head_ref[0] + gain

    @pl.when(fresh_ref[step] == 0)
    def more():
        grad_ref[0] += gain

    @pl.when(final_ref[step] == 1)
    def close():
        renewed, fresh_table = update(table_ref[0], momentum_ref[0], grad_ref[0], table_rate)
        momentum_new_ref[0] = renewed
        table_new_ref[0] = fresh_table


def finish_table(d_inputs, head_grad, table, momentum, model_of, fresh, final, first, second, ids):
    steps = model_of.shape[0]
    models, part_rows, width = table.shape
    seq_len = d_inputs.shape[1]
    tile_rows = part_rows // 2
    state = jax.ShapeDtypeStruct(table.shape, jnp.float32)
    piece = pl.BlockSpec((1, tile_rows, width), lambda t, s, m, f, l, a, b: (m[s], t, 0))
    return pl.pallas_call(
        finish_kernel,
        out_shape=(state, state, state),
        grid_spec=pltpu.PrefetchScalarGridSpec(
            num_scalar_prefetch=5,
            grid=(part_rows // tile_rows, steps),
            in_specs=[
                pl.BlockSpec((1, seq_len, width), lambda t, s, m, f, l, a, b: (a[s], 0, 0)),
                pl.BlockSpec((1, seq_len, width), lambda t, s, m, f, l, a, b: (b[s], 0, 0)),
                pl.BlockSpec((1, 1, 2 * seq_len), lambda t, s, m, f, l, a, b: (s, 0, 0)),
                piece,
                piece,
                piece,
            ],
            out_specs=(piece, piece, piece),
        ),
        compiler_params=pltpu.CompilerParams(vmem_limit_bytes=56 * MIB),
        cost_estimate=pl.CostEstimate(
            flops=4 * steps * seq_len * part_rows * width,
            bytes_accessed=24 * table.size,
            transcendentals=0,
        ),
    )(model_of, fresh, final, first, second, d_inputs, d_inputs, ids, head_grad, table, momentum)


def body(
    token_ids,
    target_ids,
    segment_ids,
    chosen,
    table,
    table_momentum,
    stack,
    stack_momentum,
    vectors,
    vector_momentum,
):
    both = ("grp", "cli")
    models, block_rows, model_width = table.shape
    stack_part = stack.shape[1]
    seq_len = token_ids.shape[1]
    groups = lax.axis_size("grp")
    members = lax.axis_size("cli")
    devices = groups * members
    share = members // models
    local = members // share
    device_index = lax.axis_index(both)
    group_index = lax.axis_index("grp")
    member_index = lax.axis_index("cli")
    model_own = member_index // share
    part_own = member_index % share
    model_range = jnp.arange(models, dtype=jnp.int32)

    def per_member(rows):
        return jnp.repeat(rows, share, axis=0) if share > 1 else rows

    slab = -(-(stack_part + ROUND_ROWS) // SLAB_STEP) * SLAB_STEP
    round_rows = slab - stack_part

    facts = share_all(
        jnp.concatenate([token_ids[0], target_ids[0], segment_ids[0], chosen]), both, devices
    )
    tokens = facts[:, :seq_len]
    targets = facts[:, seq_len : 2 * seq_len]
    segments = facts[:, 2 * seq_len : 3 * seq_len]
    choices = facts[:, 3 * seq_len]
    valid = jnp.concatenate(
        [
            (segments[:, :-1] == segments[:, 1:]).astype(jnp.float32),
            jnp.zeros((devices, 1), jnp.float32),
        ],
        axis=1,
    )
    counts = jnp.sum(valid, axis=1)
    choice_table = (choices[:, None] == model_range[None, :]).astype(jnp.float32)
    totals = jnp.sum(choice_table * counts[:, None], axis=0)
    total_of = jnp.sum(choice_table * totals[None, :], axis=1)

    table_low = table.astype(jnp.bfloat16)
    fine = 16 if block_rows % 64 else 64
    coarse = block_rows // fine
    flat_tokens = tokens.reshape(-1)
    high_hot = (
        (flat_tokens // fine)[:, None] == jnp.arange(devices * coarse, dtype=jnp.int32)[None, :]
    ).astype(jnp.bfloat16)
    low_hot = ((flat_tokens % fine)[:, None] == jnp.arange(fine, dtype=jnp.int32)[None, :]).astype(
        jnp.bfloat16
    )
    seen = (outer_rows(high_hot, low_hot) > 0).astype(jnp.float32)
    before = product(
        seen.astype(jnp.bfloat16),
        jnp.triu(jnp.ones((fine, fine), jnp.bfloat16), 1),
    )
    sums = jnp.sum(seen, axis=1).reshape(devices, coarse)
    uniques = jnp.sum(sums, axis=1)
    ahead = jnp.sum(
        jnp.where(
            jnp.arange(coarse)[None, None, :] < jnp.arange(coarse)[None, :, None],
            sums[:, None, :],
            0.0,
        ),
        axis=2,
    )
    places = before + ahead.reshape(-1, 1)
    rounds = jnp.max(jnp.ceil(uniques / round_rows)).astype(jnp.int32)
    own_places = lax.dynamic_slice(places, (device_index * coarse, 0), (coarse, fine)).reshape(-1)
    own_seen = lax.dynamic_slice(seen, (device_index * coarse, 0), (coarse, fine)).reshape(-1)
    own_places = jnp.where(own_seen > 0, own_places, -1.0).astype(jnp.int32)
    first_client = group_index * members + part_own * local
    my_tokens = lax.dynamic_slice(tokens, (first_client, 0), (local, seq_len)).reshape(-1)
    my_segments = lax.dynamic_slice(segments, (first_client, 0), (local, seq_len))
    my_choices = lax.dynamic_slice(choices, (first_client,), (local,))
    my_high = (
        (my_tokens // fine)[:, None] == jnp.arange(devices * coarse, dtype=jnp.int32)[None, :]
    ).astype(jnp.bfloat16)
    my_low = (my_tokens % fine)[:, None] == jnp.arange(fine, dtype=jnp.int32)[None, :]
    split_places = jnp.concatenate(
        [jnp.floor(places / 64.0), places - 64.0 * jnp.floor(places / 64.0)], axis=1
    ).astype(jnp.bfloat16)
    picked_places = product(my_high, split_places)
    picked_places = 64.0 * picked_places[:, :fine] + picked_places[:, fine:]
    my_places = jnp.sum(jnp.where(my_low, picked_places, 0.0), axis=1).astype(jnp.int32)
    my_owner = my_tokens // block_rows

    def offered(start):
        wanted = jnp.arange(round_rows, dtype=jnp.int32) + start
        pick = (own_places[None, :] == wanted[:, None]).astype(jnp.bfloat16)
        rows = jnp.einsum("ur,krd->kud", pick, table_low, preferred_element_type=jnp.float32)
        return rows.astype(jnp.bfloat16)

    def inside(start):
        offset = my_places - start
        return ((offset >= 0) & (offset < round_rows), offset)

    def another(carry):
        index, embedded = carry
        start = index * round_rows
        turned = lax.all_to_all(per_member(offered(start)), "cli", 0, 0, tiled=True)
        pool = lax.all_gather(turned, "grp", axis=0, tiled=True).reshape(-1, model_width)
        here, offset = inside(start)
        found = jnp.take(pool, jnp.where(here, my_owner * round_rows + offset, 0), axis=0)
        return (index + 1, jnp.where(here[:, None], found.astype(jnp.float32), embedded))

    slabs = jnp.concatenate([stack.astype(jnp.bfloat16), offered(0)], axis=1)
    pool = spread(per_member(slabs), groups, members, 1, False, 2)
    here, offset = inside(0)
    at = jnp.where(here, my_owner * slab + stack_part + offset, -1)
    weights, embedded = unpack(pool, stack_part, at[:, None])
    _, embedded = lax.while_loop(
        lambda carry: carry[0] < rounds, another, (jnp.int32(1), embedded)
    )
    vector_one = lax.dynamic_index_in_dim(vectors, model_own, 0, keepdims=False)
    inputs = embedded + jnp.tile(weights[12 * model_width :].astype(jnp.float32), (local, 1))
    saved = layer_forward(weights, vector_one, inputs, my_segments)
    normed_out = saved[11]

    target_local = targets - device_index * block_rows
    target_local = jnp.where((target_local >= 0) & (target_local < block_rows), target_local, -1)
    target_blocks = target_local.reshape(groups * share, 1, local * seq_len)
    if devices * normed_out.size * 2 <= POOL_BYTES:
        outs_all, stats = spread_score(
            normed_out[None], table_low, target_blocks, groups, members, share, 2
        )
    else:
        outs_all = spread(normed_out[None], groups, members, 2, True, 2)
        stats = head_stats(outs_all, table_low, target_blocks, groups, members, share)
    shares = lax.all_to_all(stats, both, 0, 0, tiled=True)
    log_total = jax.nn.logsumexp(shares[:, 0], axis=0)
    token_loss = log_total - jnp.sum(shares[:, 1], axis=0)
    everything = share_all(jnp.stack([log_total, token_loss]), both, devices)
    everything = (
        everything.reshape(groups, models, share, 2, local, seq_len)
        .transpose(3, 1, 0, 2, 4, 5)
        .reshape(2, models, devices, seq_len)
    )
    all_losses = jnp.sum(everything[1] * valid[None], axis=2)
    loss = jnp.sum(choice_table.T * all_losses / total_of[None, :])
    client_losses = lax.dynamic_slice(
        (all_losses / counts[None, :]).T, (device_index, 0), (1, models)
    )
    chosen_total = jnp.sum(choice_table.T[:, :, None] * everything[0], axis=0)

    numbers = jnp.sum(choice_table, axis=0)
    padded = 2.0 * jnp.ceil(numbers / 2.0)
    offsets = jnp.cumsum(padded) - padded
    earlier = (
        jnp.arange(devices)[None, :] < jnp.arange(devices)[:, None]
    ) & (choices[None, :] == choices[:, None])
    slot_of = jnp.sum(choice_table * offsets[None, :], axis=1) + jnp.sum(
        earlier.astype(jnp.float32), axis=1
    )
    slots = devices + models
    steps = slots // 2
    at_slot = jnp.arange(slots)[:, None] == slot_of.astype(jnp.int32)[None, :]
    filled = jnp.any(at_slot, axis=1)
    client_at = jnp.sum(jnp.where(at_slot, jnp.arange(devices)[None, :], 0), axis=1).astype(
        jnp.int32
    )
    step_start = 2.0 * jnp.arange(steps)
    model_of = (
        jnp.sum((step_start[:, None] >= offsets[None, :]).astype(jnp.int32), axis=1) - 1
    ).astype(jnp.int32)
    fresh = jnp.concatenate(
        [jnp.ones((1,), jnp.int32), (model_of[1:] != model_of[:-1]).astype(jnp.int32)]
    )
    final = jnp.concatenate(
        [(model_of[1:] != model_of[:-1]).astype(jnp.int32), jnp.ones((1,), jnp.int32)]
    )
    within = client_at % members
    piece_at = (
        (client_at // members * members + jnp.repeat(model_of, 2) * share + within // local) * local
        + within % local
    ).astype(jnp.int32)
    weight_rows = valid / total_of[:, None]
    slot_log = jnp.where(filled[:, None], jnp.take(chosen_total, client_at, axis=0), 1e30)
    slot_weight = jnp.where(filled[:, None], jnp.take(weight_rows, client_at, axis=0), 0.0)
    slot_info = jnp.stack(
        [slot_log.reshape(steps, 2 * seq_len), slot_weight.reshape(steps, 2 * seq_len)], axis=1
    )
    slot_target = jnp.where(filled[:, None], jnp.take(target_local, client_at, axis=0), -1)
    spare = devices + jnp.cumsum(1 - filled.astype(jnp.int32)) - 1
    d_outs, head_grad = head_back(
        outs_all.reshape(-1, seq_len, model_width),
        table_low,
        model_of,
        fresh,
        piece_at[0::2],
        piece_at[1::2],
        jnp.where(filled, client_at, spare).astype(jnp.int32),
        slot_info,
        slot_target.reshape(steps, 1, 2 * seq_len),
    )
    d_group = lax.psum_scatter(
        d_outs[:devices].reshape(devices * seq_len, model_width),
        "grp",
        scatter_dimension=0,
        tiled=True,
    )
    d_level = lax.all_to_all(
        d_group.reshape(members, seq_len, model_width), "cli", 0, 0, tiled=True
    )
    d_level = jnp.sum(d_level.astype(jnp.float32), axis=0).astype(jnp.bfloat16)
    d_group = share_all(d_level, "cli", members)
    d_mine = lax.dynamic_slice(
        d_group, (part_own * local, 0, 0), (local, seq_len, model_width)
    ).astype(jnp.float32)
    d_final = jnp.where((my_choices == model_own)[:, None, None], d_mine, 0.0).reshape(
        local * seq_len, model_width
    )
    stack_rows, vector_rows, d_inputs = layer_backward(
        weights, vector_one, inputs, my_segments, saved, d_final
    )
    d_wide = d_inputs.astype(jnp.bfloat16)
    if share > 1:
        d_wide = lax.dynamic_update_slice(
            jnp.zeros((members * seq_len, model_width), jnp.bfloat16),
            d_wide,
            (part_own * local * seq_len, 0),
        )
    d_turned = lax.all_to_all(
        d_wide.reshape(members, seq_len, model_width), "cli", 0, 0, tiled=True
    )
    d_client = jnp.sum(d_turned.astype(jnp.float32), axis=0, keepdims=True).astype(jnp.bfloat16)
    d_all = spread(d_client, groups, members, 3, True, 2)

    stack_sum = lax.psum_scatter(stack_rows, "grp", scatter_dimension=0, tiled=True)
    vector_piece = vector_rows.size // groups
    vector_part = jnp.sum(
        lax.all_to_all(vector_rows.reshape(groups, vector_piece), "grp", 0, 0, tiled=True), axis=0
    )
    vector_grad = jnp.sum(
        share_all(vector_part, both, devices).reshape(groups, models, share, vector_piece), axis=2
    )
    vector_grad = vector_grad.transpose(1, 0, 2).reshape(vectors.shape)

    token_local = tokens - device_index * block_rows
    token_local = jnp.where((token_local >= 0) & (token_local < block_rows), token_local, -1)
    slot_token = jnp.where(filled[:, None], jnp.take(token_local, client_at, axis=0), -1)
    table_grad, table_momentum_new, table_new = finish_table(
        d_all,
        head_grad,
        table,
        table_momentum,
        model_of,
        fresh,
        final,
        client_at[0::2],
        client_at[1::2],
        slot_token.reshape(steps, 1, 2 * seq_len),
    )
    stack_sum, table_grad = lax.optimization_barrier((stack_sum, table_grad))
    stack_back = lax.all_to_all(
        stack_sum.reshape(members, stack_part, model_width), "cli", 0, 0, tiled=True
    ).astype(jnp.float32)
    stack_grad = jnp.sum(stack_back.reshape(models, share, stack_part, model_width), axis=1)
    stack_momentum_new, stack_new = update(stack, stack_momentum, stack_grad, stack_rate)
    vector_momentum_new, vector_new = update(vectors, vector_momentum, vector_grad, vector_rate)
    return (
        loss,
        client_losses,
        table_grad,
        table_momentum_new,
        table_new,
        stack_grad,
        stack_momentum_new,
        stack_new,
        vector_grad,
        vector_momentum_new,
        vector_new,
    )


def solution(mesh):
    rows = P(("grp", "cli"), None)
    parts = P(None, ("grp", "cli"), None)
    return jax.shard_map(
        body,
        mesh=mesh,
        in_specs=(rows, rows, rows, P(("grp", "cli")), parts, parts, parts, parts, P(), P()),
        out_specs=(P(), rows, parts, parts, parts, parts, parts, parts, P(), P(), P()),
        check_vma=False,
    )
```

```python
import functools
import math

import jax
import jax.numpy as jnp
from jax import lax
from jax.experimental import pallas as pl
from jax.experimental.pallas import tpu as pltpu
from jax.sharding import PartitionSpec as P

HEADS = 12
HEAD_DIM = 64


epsilon = 1e-05
momentum_decay = 0.9
table_rate = 4.0
stack_rate = 4.0
vector_rate = 50.0

ROUND_ROWS = 104
SLAB_STEP = 16
TILE = 400
MIB = 1 << 20
POOL_BYTES = 32 * MIB
MESH = pl.DeviceIdType.MESH


def layer_norm(inputs, gain_row, shift_row):
    centred = inputs - jnp.mean(inputs, -1, keepdims=True)
    spread = jnp.mean(centred * centred, -1, keepdims=True)
    return centred * lax.rsqrt(spread + epsilon) * gain_row + shift_row


def project(inputs, matrix):
    return lax.dot_general(
        inputs, matrix, (((1,), (1,)), ((), ())), preferred_element_type=jnp.float32
    )


def product(inputs, matrix):
    return jnp.dot(inputs, matrix, preferred_element_type=jnp.float32)


def outer_rows(left, right):
    return lax.dot_general(
        left, right, (((0,), (0,)), ((), ())), preferred_element_type=jnp.float32
    )


def split_heads(rows, seq_len):
    return rows.reshape(-1, seq_len, HEADS, HEAD_DIM)


def attend(queries, key_rows, segment_rows):
    seq_len = segment_rows.shape[1]
    scores = jnp.einsum(
        "nqhd,nkhd->nhqk",
        split_heads(queries, seq_len),
        split_heads(key_rows, seq_len),
        preferred_element_type=jnp.float32,
    ) * HEAD_DIM ** (-0.5)
    positions = jnp.arange(seq_len)
    allowed = (positions[None, None, :] <= positions[None, :, None]) & (
        segment_rows[:, None, :] == segment_rows[:, :, None]
    )
    return jax.nn.softmax(jnp.where(allowed[:, None], scores, -1e30), axis=-1)


def layer_forward(weights, vector_one, inputs, segment_rows):
    row_count, model_width = inputs.shape
    seq_len = segment_rows.shape[1]
    normed = layer_norm(inputs, vector_one[0], vector_one[1]).astype(jnp.bfloat16)
    queries = (project(normed, weights[0:model_width]) + vector_one[6]).astype(jnp.bfloat16)
    key_rows = project(normed, weights[model_width : 2 * model_width]).astype(jnp.bfloat16)
    values = (project(normed, weights[2 * model_width : 3 * model_width]) + vector_one[7]).astype(
        jnp.bfloat16
    )
    attention = attend(queries, key_rows, segment_rows)
    mixture = jnp.einsum(
        "nhqk,nkhd->nqhd",
        attention.astype(jnp.bfloat16),
        split_heads(values, seq_len),
        preferred_element_type=jnp.float32,
    )
    mixture = mixture.reshape(row_count, model_width).astype(jnp.bfloat16)
    middle = inputs + (project(mixture, weights[3 * model_width : 4 * model_width]) + vector_one[8])
    normed_two = layer_norm(middle, vector_one[2], vector_one[3]).astype(jnp.bfloat16)
    hidden = project(normed_two, weights[4 * model_width : 8 * model_width]) + vector_one[
        10:14
    ].reshape(-1)
    active = jax.nn.gelu(hidden, approximate=True).astype(jnp.bfloat16)
    residual = middle + (
        product(active, weights[8 * model_width : 12 * model_width]) + vector_one[9]
    )
    normed_out = layer_norm(residual, vector_one[4], vector_one[5]).astype(jnp.bfloat16)
    return (
        normed,
        queries,
        key_rows,
        values,
        attention,
        mixture,
        middle,
        normed_two,
        hidden,
        active,
        residual,
        normed_out,
    )


def norm_grad(operand, gain_row, shift_row, cotangent):
    outcome, pullback = jax.vjp(layer_norm, operand, gain_row, shift_row)
    return pullback(cotangent)


def gelu_tanh(hidden):
    return jax.nn.gelu(hidden, approximate=True)


def layer_backward(weights, vector_one, inputs, segment_rows, saved, grad_out):
    row_count, model_width = inputs.shape
    seq_len = segment_rows.shape[1]
    scaling = HEAD_DIM ** (-0.5)
    (
        normed,
        queries,
        key_rows,
        values,
        attention,
        mixture,
        middle,
        normed_two,
        hidden,
        active,
        residual,
        normed_out,
    ) = saved
    d_residual, d_gain_out, d_shift_out = norm_grad(
        residual, vector_one[4], vector_one[5], grad_out
    )
    d_outer = d_residual.astype(jnp.bfloat16)
    d_bias_out = jnp.sum(d_outer.astype(jnp.float32), 0)
    grad_down = outer_rows(active, d_outer)
    d_active = project(d_outer, weights[8 * model_width : 12 * model_width])
    gelu_value, gelu_pull = jax.vjp(gelu_tanh, hidden)
    d_hidden = gelu_pull(d_active)[0].astype(jnp.bfloat16)
    d_bias_hidden = jnp.sum(d_hidden.astype(jnp.float32), 0)
    grad_up = outer_rows(d_hidden, normed_two)
    d_normed_two = product(d_hidden, weights[4 * model_width : 8 * model_width])
    d_middle_norm, d_gain_two, d_shift_two = norm_grad(
        middle, vector_one[2], vector_one[3], d_normed_two
    )
    d_middle = d_residual + d_middle_norm
    d_branch = d_middle.astype(jnp.bfloat16)
    d_bias_branch = jnp.sum(d_branch.astype(jnp.float32), 0)
    grad_mix = outer_rows(d_branch, mixture)
    d_mixture = split_heads(
        product(d_branch, weights[3 * model_width : 4 * model_width]).astype(jnp.bfloat16), seq_len
    )
    d_attention = jnp.einsum(
        "nqhd,nkhd->nhqk", d_mixture, split_heads(values, seq_len), preferred_element_type=jnp.float32
    )
    d_values = jnp.einsum(
        "nhqk,nqhd->nkhd",
        attention.astype(jnp.bfloat16),
        d_mixture,
        preferred_element_type=jnp.float32,
    )
    d_values = d_values.reshape(row_count, model_width).astype(jnp.bfloat16)
    d_scores = (
        attention * (d_attention - jnp.sum(attention * d_attention, -1, keepdims=True))
    ).astype(jnp.bfloat16)
    d_queries = (
        jnp.einsum(
            "nhqk,nkhd->nqhd",
            d_scores,
            split_heads(key_rows, seq_len),
            preferred_element_type=jnp.float32,
        )
        * scaling
    )
    d_queries = d_queries.reshape(row_count, model_width).astype(jnp.bfloat16)
    d_keys = (
        jnp.einsum(
            "nhqk,nqhd->nkhd",
            d_scores,
            split_heads(queries, seq_len),
            preferred_element_type=jnp.float32,
        )
        * scaling
    )
    d_keys = d_keys.reshape(row_count, model_width).astype(jnp.bfloat16)
    d_joined = jnp.concatenate([d_queries, d_keys, d_values], axis=1)
    grad_joined = outer_rows(d_joined, normed)
    d_normed = product(d_joined, weights[0 : 3 * model_width])
    d_inputs_norm, d_gain_one, d_shift_one = norm_grad(
        inputs, vector_one[0], vector_one[1], d_normed
    )
    d_inputs = d_middle + d_inputs_norm
    grad_places = jnp.sum(d_inputs.reshape(-1, seq_len, model_width), axis=0)
    stack_rows = jnp.concatenate(
        [
            piece.astype(jnp.bfloat16)
            for piece in (grad_joined, grad_mix, grad_up, grad_down, grad_places)
        ],
        axis=0,
    )
    bias_query = jnp.sum(d_queries.astype(jnp.float32), 0)
    bias_value = jnp.sum(d_values.astype(jnp.float32), 0)
    vector_rows = jnp.concatenate(
        [
            jnp.stack(
                [
                    d_gain_one,
                    d_shift_one,
                    d_gain_two,
                    d_shift_two,
                    d_gain_out,
                    d_shift_out,
                    bias_query,
                    bias_value,
                    d_bias_branch,
                    d_bias_out,
                ]
            ),
            d_bias_hidden.reshape(4, model_width),
        ],
        axis=0,
    )
    return (stack_rows, vector_rows, d_inputs)


def share_all(rows, axes, size):
    return lax.all_to_all(
        jnp.broadcast_to(rows[None], (size,) + rows.shape), axes, 0, 0, tiled=True
    )


def update(weight, momentum, gradient, step_rate):
    renewed = momentum_decay * momentum + gradient
    return (renewed, weight - step_rate * (gradient + momentum_decay * renewed))


def flipped(value, offset, size):
    bit = 1
    while bit < size:
        digit = lax.rem(lax.div(offset, bit), 2)
        value = value + digit * bit * (1 - 2 * lax.rem(lax.div(value, bit), 2))
        bit *= 2
    return value


class Place:
    def __init__(self, groups, members):
        self.groups, self.members = groups, members
        self.ys = 2
        self.xs = groups // 4
        self.grp = lax.axis_index("grp")
        self.cli = lax.axis_index("cli")
        self.core = lax.rem(self.grp, 2)
        self.x = lax.rem(lax.div(self.grp, 2), self.xs)
        self.y = lax.div(self.grp, 2 * self.xs)

    def group(self, jx=0, jy=0, jc=0):
        x = flipped(self.x, jx, self.xs)
        y = flipped(self.y, jy, self.ys)
        core = self.core + jc * (1 - 2 * self.core)
        return (y * self.xs + x) * 2 + core

    def block(self, jx, jy, level, jc=0):
        return self.group(jx, jy, jc) * self.members + level

    def peer(self, jx=0, jy=0, jc=0):
        return (self.group(jx, jy, jc), self.cli)

    def level(self, level):
        return (self.grp, level)

    def nearest(self, i):
        z, last = self.cli, self.members - 1
        low = jnp.where(2 * z < last, 1, 0)
        sign = 2 * low - 1
        margin = low * z + (1 - low) * (last - z)
        step = lax.div(i + 1, 2)
        odd = lax.rem(i, 2)
        near = z + sign * step * (2 * odd - 1)
        far = z + sign * (i - margin)
        return jnp.where(i <= 2 * margin, near, far)


def greet(place):
    barrier = pltpu.get_barrier_semaphore()
    peers = [place.peer(jx=j) for j in range(1, place.xs)] + [place.peer(jy=j) for j in range(1, place.ys)]
    peers.append(place.peer(jc=1))
    peers += [place.level(lax.rem(place.cli + j, place.members)) for j in range(1, place.members)]
    for peer in peers:
        pl.semaphore_signal(barrier, inc=1, device_id=peer, device_id_type=MESH)
    pl.semaphore_wait(barrier, len(peers))


def spread_sems(groups, members, pieces):
    xs, ys, items = groups // 4, 2, members * pieces
    dma = pltpu.SemaphoreType.DMA
    shapes = [(items,)] * 3 + [(items, xs)] * 2 + [(items, ys)] * 2 + [(items, xs, ys)] * 6
    return [dma] + [dma(shape) for shape in shapes]


def spread_body(place, chain, pieces, src, out, sems, consume, ready=None):
    (own_sem, z_up, z_down, z_recv, x_send, x_recv, y_send, y_recv, k_send, k_recv, p_send, p_recv,
     c_send, c_recv) = sems
    xs, ys, members = place.xs, place.ys, place.members
    items = members * pieces
    size = out.shape[1] // pieces
    z = place.cli
    partner = z + 1 - 2 * lax.rem(z, 2)
    inner_x, inner_y = range(1, xs), range(1, ys)

    def move(source, target, send, recv, device):
        return pltpu.make_async_remote_copy(
            src_ref=source, dst_ref=target, send_sem=send, recv_sem=recv, device_id=device, device_id_type=MESH
        )

    class Item:
        def __init__(self, k):
            self.level = place.nearest(lax.div(k, pieces))
            self.piece = lax.rem(k, pieces)
            self.slot = self.level * pieces + self.piece
            self.even = lax.rem(self.piece, 2) == 0
            self.mine = lax.rem(self.level + z, 2) == 0 if chain else self.level >= 0
            self.rows = pl.ds(self.piece * size, size)

        def part(self, jx, jy, level=None):
            return out.at[place.block(jx, jy, self.level if level is None else level), self.rows]

        def here(self, own):
            return src.at[z if not chain else 0, self.rows] if own else self.part(0, 0)

        def up(self, own=False):
            return move(self.here(own), self.part(0, 0), z_up.at[self.slot], z_recv.at[self.slot], place.level(z + 1))

        def down(self, own=False):
            return move(self.here(own), self.part(0, 0), z_down.at[self.slot], z_recv.at[self.slot], place.level(z - 1))

        def straight(self):
            return move(
                src.at[self.level, self.rows], self.part(0, 0, z), z_up.at[self.slot],
                z_recv.at[z * pieces + self.piece], place.level(self.level),
            )

        def landed(self):
            part = self.part(0, 0)
            return move(part, part, z_up.at[self.slot], z_recv.at[self.slot], place.level(partner))

        def to_x(self, jx, own=False):
            return move(self.here(own), self.part(0, 0), x_send.at[self.slot, jx], x_recv.at[self.slot, jx], place.peer(jx=jx))

        def to_y(self, jy, own=False):
            return move(self.here(own), self.part(0, 0), y_send.at[self.slot, jy], y_recv.at[self.slot, jy], place.peer(jy=jy))

        def corner_a(self, jx, jy):
            part = self.part(jx, 0)
            return move(part, part, k_send.at[self.slot, jx, jy], k_recv.at[self.slot, jx, jy], place.peer(jy=jy))

        def corner_b(self, jx, jy):
            part = self.part(0, jy)
            return move(part, part, k_send.at[self.slot, jx, jy], k_recv.at[self.slot, jx, jy], place.peer(jx=jx))

        def corner_z(self, jx, jy):
            part = self.part(jx, jy)
            return move(part, part, p_send.at[self.slot, jx, jy], p_recv.at[self.slot, jx, jy], place.level(partner))

        def to_core(self, jx, jy, own=False):
            part = self.part(jx, jy)
            return move(self.here(True) if own else part, part, c_send.at[self.slot, jx, jy], c_recv.at[self.slot, jx, jy], place.peer(jc=1))

    own = pltpu.make_async_copy(src.at[z if not chain else 0], out.at[place.block(0, 0, z)], own_sem)
    own.start()
    if not chain:
        for piece in range(pieces):
            Item(pieces + piece).straight().start()

    def columns(k):
        item = Item(k)
        level = item.level

        @pl.when(k < pieces)
        def mine_first():
            if chain:
                @pl.when(z + 1 < members)
                def onward():
                    item.up(True).start()

                @pl.when(z > 0)
                def back():
                    item.down(True).start()

            for jx in inner_x:
                item.to_x(jx, True).start()
            for jy in inner_y:
                item.to_y(jy, True).start()
            item.to_core(0, 0, True).start()

        @pl.when(k >= pieces)
        def arrive():
            item.landed().wait_recv()
            if chain:
                @pl.when((level < z) & (z + 1 < members))
                def onward():
                    item.up().start()

                @pl.when((level > z) & (z > 0))
                def back():
                    item.down().start()
            else:
                @pl.when(k + pieces < items)
                def following():
                    Item(k + pieces).straight().start()

            for jx in inner_x:
                item.to_x(jx).start()
            for jy in inner_y:
                item.to_y(jy).start()
            item.to_core(0, 0).start()

    def edges(k):
        item = Item(k)
        for jx in inner_x:
            item.to_x(jx).wait_recv()

            @pl.when(item.mine & item.even)
            def pass_a():
                for jy in inner_y:
                    item.corner_a(jx, jy).start()

            item.to_core(jx, 0).start()
        for jy in inner_y:
            item.to_y(jy).wait_recv()

            @pl.when(item.mine & jnp.logical_not(item.even))
            def pass_b():
                for jx in inner_x:
                    item.corner_b(jx, jy).start()

            item.to_core(0, jy).start()

    def corners(k):
        item = Item(k)

        @pl.when(item.mine)
        def mine_now():
            for jx in inner_x:
                for jy in inner_y:
                    item.corner_a(jx, jy).wait_recv()
                    if chain:
                        item.corner_z(jx, jy).start()
                    item.to_core(jx, jy).start()

    def handed(k):
        item = Item(k)

        @pl.when(jnp.logical_not(item.mine))
        def from_partner():
            for jx in inner_x:
                for jy in inner_y:
                    item.corner_z(jx, jy).wait_recv()
                    item.to_core(jx, jy).start()

    spots = xs * ys
    lag_edge, lag_corner = (2, 4) if chain else (1, 3)
    lag_handed = pieces + 6 if chain else lag_corner
    lag_end = lag_handed + 1

    def tick(t, carry):
        @pl.when(t < items)
        def arrivals():
            columns(t)

        @pl.when((t >= lag_edge) & (t < items + lag_edge))
        def sides():
            edges(t - lag_edge)

        @pl.when((t >= lag_corner) & (t < items + lag_corner))
        def far():
            corners(t - lag_corner)

        if chain:
            @pl.when((t >= lag_handed) & (t < items + lag_handed))
            def others():
                handed(t - lag_handed)

        def visit(e, carry):
            jc = lax.div(e, spots)
            spot = lax.rem(e, spots)
            jx, jy = lax.rem(spot, xs), lax.div(spot, xs)
            far = jnp.minimum(jx, 1) + jnp.minimum(jy, 1)
            lag = jnp.where(far == 0, 1, jnp.where(far == 1, lag_edge + 1, lag_end))
            k = t - lag

            @pl.when((k >= 0) & (k < items))
            def valid():
                item = Item(k)

                @pl.when(jc == 1)
                def shared():
                    item.to_core(jx, jy).wait_recv()

                if consume is not None:
                    consume(place.block(jx, jy, item.level, jc), item.level, item.piece)

            return carry

        return lax.fori_loop(0, 2 * spots, visit, carry)

    if ready is not None:
        own.wait()
        ready()
    lax.fori_loop(0, items + lag_end, tick, 0)

    def close(k, carry):
        item = Item(k)
        level = item.level
        if chain:
            @pl.when((level <= z) & (z + 1 < members))
            def onward():
                item.up().wait_send()

            @pl.when((level >= z) & (z > 0))
            def back():
                item.down().wait_send()
        else:
            @pl.when(k >= pieces)
            def sent():
                item.straight().wait_send()

        for jx in inner_x:
            item.to_x(jx).wait_send()
        for jy in inner_y:
            item.to_y(jy).wait_send()
        for jx in range(xs):
            for jy in range(ys):
                item.to_core(jx, jy).wait_send()

        @pl.when(item.mine)
        def mine_done():
            for jx in inner_x:
                for jy in inner_y:
                    item.corner_a(jx, jy).wait_send()
                    if chain:
                        item.corner_z(jx, jy).wait_send()

        return carry

    lax.fori_loop(0, items, close, 0)
    if ready is None:
        own.wait()


def spread_kernel(groups, members, chain, pieces, src, out, *sems):
    place = Place(groups, members)
    greet(place)
    spread_body(place, chain, pieces, src, out, sems, None)


def spread(src, groups, members, collective_id, chain, pieces):
    count, rows, width = src.shape
    return pl.pallas_call(
        functools.partial(spread_kernel, groups, members, chain, pieces),
        out_shape=jax.ShapeDtypeStruct((groups * members, rows, width), src.dtype),
        in_specs=[pl.BlockSpec(memory_space=pl.ANY)],
        out_specs=pl.BlockSpec(memory_space=pl.ANY),
        scratch_shapes=spread_sems(groups, members, pieces),
        compiler_params=pltpu.CompilerParams(collective_id=collective_id, has_side_effects=True),
        cost_estimate=pl.CostEstimate(
            flops=0, bytes_accessed=4 * groups * members * rows * width, transcendentals=0
        ),
    )(src)


def tile_of(part_rows):
    return TILE if part_rows % TILE == 0 else part_rows


def score_kernel(groups, members, share, pieces, src, table, target, out, stat, *rest):
    part, pool, part_sem, out_sems = rest[:4]
    sems = rest[4:]
    place = Place(groups, members)
    load_table = pltpu.make_async_copy(table, part, part_sem)
    load_table.start()
    greet(place)
    rows = pool.shape[1]
    size = rows // pieces

    def keep(block, piece):
        here = pl.ds(pl.multiple_of(piece * size, size), size)
        return pltpu.make_async_copy(pool.at[block, here], out.at[block, here], out_sems.at[block, piece])

    def consume(block, level, piece):
        keep(block, piece).start()
        here = pl.ds(pl.multiple_of(piece * size, size), size)
        model = lax.div(level, share)
        wanted = target[lax.div(block, members) * share + lax.rem(level, share), :, here]
        outs = pool[block, here]
        part_rows = part.shape[1]
        tile = tile_of(part_rows)
        marks = lax.broadcasted_iota(jnp.int32, (tile, size), 0)
        tops, totals, hits = [], [], []
        for first in range(0, part_rows, tile):
            logits = project(part[model, pl.ds(first, tile)], outs)
            hit = jnp.where(marks == wanted - first, logits, 0.0).reshape(-1, 8, size)
            hits.append(jnp.sum(hit, axis=0))
            logits = logits.reshape(-1, 8, size)
            top = jnp.max(logits, axis=0)
            tops.append(top)
            totals.append(jnp.sum(jnp.exp(logits - top[None]), axis=0))
        highest = jnp.max(functools.reduce(jnp.maximum, tops), axis=0, keepdims=True)
        total = sum(t * jnp.exp(m - highest) for t, m in zip(totals, tops))
        stat[block, 0:1, here] = highest + jnp.log(jnp.sum(total, axis=0, keepdims=True))
        stat[block, 1:2, here] = jnp.sum(sum(hits), axis=0, keepdims=True)

    spread_body(place, True, pieces, src, pool, sems, consume, load_table.wait)

    def close(block, carry):
        for piece in range(pieces):
            keep(block, piece).wait()
        return carry

    lax.fori_loop(0, groups * members, close, 0)


def spread_score(src, table_low, target_blocks, groups, members, share, collective_id, pieces=2):
    _, rows, width = src.shape
    blocks = groups * members
    return pl.pallas_call(
        functools.partial(score_kernel, groups, members, share, pieces),
        out_shape=(
            jax.ShapeDtypeStruct((blocks, rows, width), src.dtype),
            jax.ShapeDtypeStruct((blocks, 2, rows), jnp.float32),
        ),
        in_specs=[
            pl.BlockSpec(memory_space=pl.ANY),
            pl.BlockSpec(memory_space=pl.ANY),
            pl.BlockSpec(memory_space=pltpu.VMEM),
        ],
        out_specs=(pl.BlockSpec(memory_space=pl.ANY), pl.BlockSpec(memory_space=pltpu.VMEM)),
        scratch_shapes=[
            pltpu.VMEM(table_low.shape, table_low.dtype),
            pltpu.VMEM((blocks, rows, width), src.dtype),
            pltpu.SemaphoreType.DMA,
            pltpu.SemaphoreType.DMA((blocks, pieces)),
        ]
        + spread_sems(groups, members, pieces),
        compiler_params=pltpu.CompilerParams(
            collective_id=collective_id, has_side_effects=True, vmem_limit_bytes=60 * MIB
        ),
        cost_estimate=pl.CostEstimate(
            flops=2 * blocks * rows * table_low.shape[1] * width,
            bytes_accessed=2 * blocks * rows * width * 2,
            transcendentals=blocks * rows * table_low.shape[1],
        ),
    )(src, table_low, target_blocks)


def stats_kernel(outs_ref, table_ref, target_ref, stat_ref):
    logits = project(table_ref[0], outs_ref[0])
    highest = jnp.max(logits, axis=0, keepdims=True)
    total = jnp.sum(jnp.exp(logits - highest), axis=0, keepdims=True)
    rows = lax.broadcasted_iota(jnp.int32, logits.shape, 0)
    hit = jnp.sum(jnp.where(rows == target_ref[0], logits, 0.0), axis=0, keepdims=True)
    stat_ref[0, 0:1, :] = highest + jnp.log(total)
    stat_ref[0, 1:2, :] = hit


def head_stats(outs_all, table_low, target_blocks, groups, members, share):
    blocks, rows, width = outs_all.shape
    part_rows = table_low.shape[1]
    return pl.pallas_call(
        stats_kernel,
        out_shape=jax.ShapeDtypeStruct((blocks, 2, rows), jnp.float32),
        grid=(members, groups),
        in_specs=[
            pl.BlockSpec((1, rows, width), lambda z, g: (g * members + z, 0, 0)),
            pl.BlockSpec((1, part_rows, width), lambda z, g: (z // share, 0, 0)),
            pl.BlockSpec((1, 1, rows), lambda z, g: (g * share + z % share, 0, 0)),
        ],
        out_specs=pl.BlockSpec((1, 2, rows), lambda z, g: (g * members + z, 0, 0)),
        compiler_params=pltpu.CompilerParams(vmem_limit_bytes=56 * MIB),
        cost_estimate=pl.CostEstimate(
            flops=2 * blocks * rows * part_rows * width,
            bytes_accessed=2 * outs_all.size + 2 * table_low.size,
            transcendentals=blocks * rows * part_rows,
        ),
    )(outs_all, table_low, target_blocks)


def unpack_kernel(start, part, at_ref, pool_ref, weights_ref, rows_ref):
    step = pl.program_id(0)
    owners, slab, width = pool_ref.shape
    weights_ref[...] = jnp.concatenate([pool_ref[j, :part] for j in range(owners)], axis=0)
    columns = lax.broadcasted_iota(jnp.int32, (at_ref.shape[0], slab - start), 1) + start
    found = jnp.zeros(rows_ref.shape, jnp.float32)
    for j in range(owners):
        at = at_ref[...] - (step * owners + j) * slab
        hits = (columns == at).astype(jnp.float32).astype(jnp.bfloat16)
        found = found + product(hits, pool_ref[j, start:])

    @pl.when(step == 0)
    def begin():
        rows_ref[...] = found

    @pl.when(step > 0)
    def more():
        rows_ref[...] += found


def unpack(pool, part, at):
    devices, slab, width = pool.shape
    owners = 8 // math.gcd(part, 8)
    start = part // 16 * 16
    tokens = at.shape[0]
    return pl.pallas_call(
        functools.partial(unpack_kernel, start, part),
        out_shape=(
            jax.ShapeDtypeStruct((devices * part, width), pool.dtype),
            jax.ShapeDtypeStruct((tokens, width), jnp.float32),
        ),
        grid=(devices // owners,),
        in_specs=[
            pl.BlockSpec((tokens, 1), lambda i: (0, 0)),
            pl.BlockSpec((owners, slab, width), lambda i: (i, 0, 0)),
        ],
        out_specs=(
            pl.BlockSpec((owners * part, width), lambda i: (i, 0)),
            pl.BlockSpec((tokens, width), lambda i: (0, 0)),
        ),
        compiler_params=pltpu.CompilerParams(vmem_limit_bytes=40 * MIB),
        cost_estimate=pl.CostEstimate(
            flops=2 * devices * tokens * (slab - start) * width,
            bytes_accessed=4 * pool.size,
            transcendentals=0,
        ),
    )(at, pool)


def back_kernel(
    model_ref, fresh_ref, first_ref, second_ref, place_ref, a_ref, b_ref, table_ref, info_ref, target_ref, d_outs_ref,
    grad_ref, held, sems,
):
    step = pl.program_id(0)
    steps = pl.num_programs(0)
    seq_len = a_ref.shape[1]
    slot = lax.rem(step, 2)

    def leave(which, where, half):
        return pltpu.make_async_copy(
            held.at[which, half], d_outs_ref.at[where], sems.at[which, half]
        )

    @pl.when(step >= 2)
    def reuse():
        leave(slot, 0, 0).wait()
        leave(slot, 0, 1).wait()
    outs = jnp.concatenate([a_ref[0], b_ref[0]], axis=0)
    @pl.when(fresh_ref[step] == 1)
    def start():
        grad_ref[...] = jnp.zeros_like(grad_ref)

    part_rows = table_ref.shape[1]
    size = tile_of(part_rows)
    d_outs = jnp.zeros((2 * seq_len, outs.shape[1]), jnp.float32)
    for first_row in range(0, part_rows, size):
        here = pl.ds(first_row, size)
        table_rows = table_ref[0, here]
        logits = project(table_rows, outs)
        rows = lax.broadcasted_iota(jnp.int32, logits.shape, 0) + first_row
        soft = jnp.exp(logits - info_ref[0, 0:1, :])
        soft = jnp.where(rows == target_ref[0], soft - 1.0, soft)
        d_logits = (info_ref[0, 1:2, :] * soft).astype(jnp.bfloat16)
        d_outs = d_outs + outer_rows(d_logits, table_rows)
        grad_ref[0, here] += product(d_logits, outs)
    held[slot, 0] = d_outs[:seq_len].astype(held.dtype)
    held[slot, 1] = d_outs[seq_len:].astype(held.dtype)
    leave(slot, place_ref[2 * step], 0).start()
    leave(slot, place_ref[2 * step + 1], 1).start()

    @pl.when(step == steps - 1)
    def drain():
        for which in range(2):
            leave(which, 0, 0).wait()
            leave(which, 0, 1).wait()


def head_back(outs_pieces, table_low, model_of, fresh, first, second, place, info, target):
    steps = model_of.shape[0]
    models, part_rows, width = table_low.shape
    seq_len = outs_pieces.shape[1]
    return pl.pallas_call(
        back_kernel,
        out_shape=(
            jax.ShapeDtypeStruct((2 * steps, seq_len, width), jnp.bfloat16),
            jax.ShapeDtypeStruct((models, part_rows, width), jnp.float32),
        ),
        grid_spec=pltpu.PrefetchScalarGridSpec(
            num_scalar_prefetch=5,
            grid=(steps,),
            in_specs=[
                pl.BlockSpec((1, seq_len, width), lambda s, m, f, a, b, p: (a[s], 0, 0)),
                pl.BlockSpec((1, seq_len, width), lambda s, m, f, a, b, p: (b[s], 0, 0)),
                pl.BlockSpec((1, part_rows, width), lambda s, m, f, a, b, p: (m[s], 0, 0)),
                pl.BlockSpec((1, 2, 2 * seq_len), lambda s, m, f, a, b, p: (s, 0, 0)),
                pl.BlockSpec((1, 1, 2 * seq_len), lambda s, m, f, a, b, p: (s, 0, 0)),
            ],
            out_specs=(
                pl.BlockSpec(memory_space=pl.ANY),
                pl.BlockSpec((1, part_rows, width), lambda s, m, f, a, b, p: (m[s], 0, 0)),
            ),
            scratch_shapes=[
                pltpu.VMEM((2, 2, seq_len, width), jnp.bfloat16),
                pltpu.SemaphoreType.DMA((2, 2)),
            ],
        ),
        compiler_params=pltpu.CompilerParams(vmem_limit_bytes=56 * MIB),
        cost_estimate=pl.CostEstimate(
            flops=12 * steps * seq_len * part_rows * width,
            bytes_accessed=4 * steps * seq_len * width * 2 + 6 * table_low.size,
            transcendentals=2 * steps * seq_len * part_rows,
        ),
    )(model_of, fresh, first, second, place, outs_pieces, outs_pieces, table_low, info, target)


def finish_kernel(
    first_tile, model_ref, fresh_ref, final_ref, first_ref, second_ref, a_ref, b_ref, ids_ref, head_ref, table_ref,
    momentum_ref, *rest,
):
    grad_ref, momentum_new_ref, table_new_ref = rest[-3:]
    tile = pl.program_id(0) + first_tile
    step = pl.program_id(1)
    tile_rows = grad_ref.shape[1]
    rows = lax.broadcasted_iota(jnp.int32, (tile_rows, ids_ref.shape[2]), 0) + tile * tile_rows
    hits = (rows == ids_ref[0]).astype(jnp.float32).astype(jnp.bfloat16)
    outs = jnp.concatenate([a_ref[0], b_ref[0]], axis=0)
    gain = product(hits, outs)

    @pl.when(fresh_ref[step] == 1)
    def start():
        grad_ref[0] = head_ref[0] + gain

    @pl.when(fresh_ref[step] == 0)
    def more():
        grad_ref[0] += gain

    @pl.when(final_ref[step] == 1)
    def close():
        renewed, fresh_table = update(table_ref[0], momentum_ref[0], grad_ref[0], table_rate)
        momentum_new_ref[0] = renewed
        table_new_ref[0] = fresh_table


def finish_table(d_inputs, head_grad, table, momentum, schedule, ids, first_tile, tiles, earlier):
    model_of, fresh, final, first, second = schedule
    steps = model_of.shape[0]
    models, part_rows, width = table.shape
    seq_len = d_inputs.shape[1]
    tile_rows = part_rows // 2
    state = jax.ShapeDtypeStruct(table.shape, jnp.float32)
    piece = pl.BlockSpec((1, tile_rows, width), lambda t, s, m, f, l, a, b: (m[s], t + first_tile, 0))
    return pl.pallas_call(
        functools.partial(finish_kernel, first_tile),
        out_shape=(state, state, state),
        grid_spec=pltpu.PrefetchScalarGridSpec(
            num_scalar_prefetch=5,
            grid=(tiles, steps),
            in_specs=[
                pl.BlockSpec((1, seq_len, width), lambda t, s, m, f, l, a, b: (a[s], 0, 0)),
                pl.BlockSpec((1, seq_len, width), lambda t, s, m, f, l, a, b: (b[s], 0, 0)),
                pl.BlockSpec((1, 1, 2 * seq_len), lambda t, s, m, f, l, a, b: (s, 0, 0)),
                piece,
                piece,
                piece,
            ]
            + [pl.BlockSpec(memory_space=pl.ANY)] * len(earlier),
            out_specs=(piece, piece, piece),
        ),
        input_output_aliases={11 + i: i for i in range(len(earlier))},
        compiler_params=pltpu.CompilerParams(vmem_limit_bytes=56 * MIB),
        cost_estimate=pl.CostEstimate(
            flops=4 * steps * seq_len * tiles * tile_rows * width,
            bytes_accessed=24 * models * tiles * tile_rows * width,
            transcendentals=0,
        ),
    )(*schedule, d_inputs, d_inputs, ids, head_grad, table, momentum, *earlier)


def body(
    token_ids,
    target_ids,
    segment_ids,
    chosen,
    table,
    table_momentum,
    stack,
    stack_momentum,
    vectors,
    vector_momentum,
):
    both = ("grp", "cli")
    models, block_rows, model_width = table.shape
    stack_part = stack.shape[1]
    seq_len = token_ids.shape[1]
    groups = lax.axis_size("grp")
    members = lax.axis_size("cli")
    devices = groups * members
    share = members // models
    local = members // share
    device_index = lax.axis_index(both)
    group_index = lax.axis_index("grp")
    member_index = lax.axis_index("cli")
    model_own = member_index // share
    part_own = member_index % share
    model_range = jnp.arange(models, dtype=jnp.int32)

    def per_member(rows):
        return jnp.repeat(rows, share, axis=0) if share > 1 else rows

    slab = -(-(stack_part + ROUND_ROWS) // SLAB_STEP) * SLAB_STEP
    round_rows = slab - stack_part

    facts = share_all(
        jnp.concatenate([token_ids[0], target_ids[0], segment_ids[0], chosen]), both, devices
    )
    tokens = facts[:, :seq_len]
    targets = facts[:, seq_len : 2 * seq_len]
    segments = facts[:, 2 * seq_len : 3 * seq_len]
    choices = facts[:, 3 * seq_len]
    valid = jnp.concatenate(
        [
            (segments[:, :-1] == segments[:, 1:]).astype(jnp.float32),
            jnp.zeros((devices, 1), jnp.float32),
        ],
        axis=1,
    )
    counts = jnp.sum(valid, axis=1)
    choice_table = (choices[:, None] == model_range[None, :]).astype(jnp.float32)
    totals = jnp.sum(choice_table * counts[:, None], axis=0)
    total_of = jnp.sum(choice_table * totals[None, :], axis=1)

    table_low = table.astype(jnp.bfloat16)
    fine = 16 if block_rows % 64 else 64
    coarse = block_rows // fine
    flat_tokens = tokens.reshape(-1)
    high_hot = (
        (flat_tokens // fine)[:, None] == jnp.arange(devices * coarse, dtype=jnp.int32)[None, :]
    ).astype(jnp.bfloat16)
    low_hot = ((flat_tokens % fine)[:, None] == jnp.arange(fine, dtype=jnp.int32)[None, :]).astype(
        jnp.bfloat16
    )
    seen = (outer_rows(high_hot, low_hot) > 0).astype(jnp.float32)
    before = product(
        seen.astype(jnp.bfloat16),
        jnp.triu(jnp.ones((fine, fine), jnp.bfloat16), 1),
    )
    sums = jnp.sum(seen, axis=1).reshape(devices, coarse)
    uniques = jnp.sum(sums, axis=1)
    ahead = jnp.sum(
        jnp.where(
            jnp.arange(coarse)[None, None, :] < jnp.arange(coarse)[None, :, None],
            sums[:, None, :],
            0.0,
        ),
        axis=2,
    )
    places = before + ahead.reshape(-1, 1)
    rounds = jnp.max(jnp.ceil(uniques / round_rows)).astype(jnp.int32)
    own_places = lax.dynamic_slice(places, (device_index * coarse, 0), (coarse, fine)).reshape(-1)
    own_seen = lax.dynamic_slice(seen, (device_index * coarse, 0), (coarse, fine)).reshape(-1)
    own_places = jnp.where(own_seen > 0, own_places, -1.0).astype(jnp.int32)
    first_client = group_index * members + part_own * local
    my_tokens = lax.dynamic_slice(tokens, (first_client, 0), (local, seq_len)).reshape(-1)
    my_segments = lax.dynamic_slice(segments, (first_client, 0), (local, seq_len))
    my_choices = lax.dynamic_slice(choices, (first_client,), (local,))
    my_high = (
        (my_tokens // fine)[:, None] == jnp.arange(devices * coarse, dtype=jnp.int32)[None, :]
    ).astype(jnp.bfloat16)
    my_low = (my_tokens % fine)[:, None] == jnp.arange(fine, dtype=jnp.int32)[None, :]
    split_places = jnp.concatenate(
        [jnp.floor(places / 64.0), places - 64.0 * jnp.floor(places / 64.0)], axis=1
    ).astype(jnp.bfloat16)
    picked_places = product(my_high, split_places)
    picked_places = 64.0 * picked_places[:, :fine] + picked_places[:, fine:]
    my_places = jnp.sum(jnp.where(my_low, picked_places, 0.0), axis=1).astype(jnp.int32)
    my_owner = my_tokens // block_rows

    def offered(start):
        wanted = jnp.arange(round_rows, dtype=jnp.int32) + start
        pick = (own_places[None, :] == wanted[:, None]).astype(jnp.bfloat16)
        rows = jnp.einsum("ur,krd->kud", pick, table_low, preferred_element_type=jnp.float32)
        return rows.astype(jnp.bfloat16)

    def inside(start):
        offset = my_places - start
        return ((offset >= 0) & (offset < round_rows), offset)

    def another(carry):
        index, embedded = carry
        start = index * round_rows
        turned = lax.all_to_all(per_member(offered(start)), "cli", 0, 0, tiled=True)
        pool = lax.all_gather(turned, "grp", axis=0, tiled=True).reshape(-1, model_width)
        here, offset = inside(start)
        found = jnp.take(pool, jnp.where(here, my_owner * round_rows + offset, 0), axis=0)
        return (index + 1, jnp.where(here[:, None], found.astype(jnp.float32), embedded))

    slabs = jnp.concatenate([stack.astype(jnp.bfloat16), offered(0)], axis=1)
    pool = spread(per_member(slabs), groups, members, 1, False, 2)
    here, offset = inside(0)
    at = jnp.where(here, my_owner * slab + stack_part + offset, -1)
    weights, embedded = unpack(pool, stack_part, at[:, None])
    _, embedded = lax.while_loop(
        lambda carry: carry[0] < rounds, another, (jnp.int32(1), embedded)
    )
    vector_one = lax.dynamic_index_in_dim(vectors, model_own, 0, keepdims=False)
    inputs = embedded + jnp.tile(weights[12 * model_width :].astype(jnp.float32), (local, 1))
    saved = layer_forward(weights, vector_one, inputs, my_segments)
    normed_out = saved[11]

    target_local = targets - device_index * block_rows
    target_local = jnp.where((target_local >= 0) & (target_local < block_rows), target_local, -1)
    target_blocks = target_local.reshape(groups * share, 1, local * seq_len)
    if devices * normed_out.size * 2 <= POOL_BYTES:
        outs_all, stats = spread_score(
            normed_out[None], table_low, target_blocks, groups, members, share, 2
        )
    else:
        outs_all = spread(normed_out[None], groups, members, 2, True, 2)
        stats = head_stats(outs_all, table_low, target_blocks, groups, members, share)
    shares = lax.all_to_all(stats, both, 0, 0, tiled=True)
    log_total = jax.nn.logsumexp(shares[:, 0], axis=0)
    token_loss = log_total - jnp.sum(shares[:, 1], axis=0)
    everything = share_all(jnp.stack([log_total, token_loss]), both, devices)
    everything = (
        everything.reshape(groups, models, share, 2, local, seq_len)
        .transpose(3, 1, 0, 2, 4, 5)
        .reshape(2, models, devices, seq_len)
    )
    all_losses = jnp.sum(everything[1] * valid[None], axis=2)
    loss = jnp.sum(choice_table.T * all_losses / total_of[None, :])
    client_losses = lax.dynamic_slice(
        (all_losses / counts[None, :]).T, (device_index, 0), (1, models)
    )
    chosen_total = jnp.sum(choice_table.T[:, :, None] * everything[0], axis=0)

    numbers = jnp.sum(choice_table, axis=0)
    padded = 2.0 * jnp.ceil(numbers / 2.0)
    offsets = jnp.cumsum(padded) - padded
    earlier = (
        jnp.arange(devices)[None, :] < jnp.arange(devices)[:, None]
    ) & (choices[None, :] == choices[:, None])
    slot_of = jnp.sum(choice_table * offsets[None, :], axis=1) + jnp.sum(
        earlier.astype(jnp.float32), axis=1
    )
    slots = devices + models
    steps = slots // 2
    at_slot = jnp.arange(slots)[:, None] == slot_of.astype(jnp.int32)[None, :]
    filled = jnp.any(at_slot, axis=1)
    client_at = jnp.sum(jnp.where(at_slot, jnp.arange(devices)[None, :], 0), axis=1).astype(
        jnp.int32
    )
    step_start = 2.0 * jnp.arange(steps)
    model_of = (
        jnp.sum((step_start[:, None] >= offsets[None, :]).astype(jnp.int32), axis=1) - 1
    ).astype(jnp.int32)
    fresh = jnp.concatenate(
        [jnp.ones((1,), jnp.int32), (model_of[1:] != model_of[:-1]).astype(jnp.int32)]
    )
    final = jnp.concatenate(
        [(model_of[1:] != model_of[:-1]).astype(jnp.int32), jnp.ones((1,), jnp.int32)]
    )
    within = client_at % members
    piece_at = (
        (client_at // members * members + jnp.repeat(model_of, 2) * share + within // local) * local
        + within % local
    ).astype(jnp.int32)
    weight_rows = valid / total_of[:, None]
    slot_log = jnp.where(filled[:, None], jnp.take(chosen_total, client_at, axis=0), 1e30)
    slot_weight = jnp.where(filled[:, None], jnp.take(weight_rows, client_at, axis=0), 0.0)
    slot_info = jnp.stack(
        [slot_log.reshape(steps, 2 * seq_len), slot_weight.reshape(steps, 2 * seq_len)], axis=1
    )
    slot_target = jnp.where(filled[:, None], jnp.take(target_local, client_at, axis=0), -1)
    spare = devices + jnp.cumsum(1 - filled.astype(jnp.int32)) - 1
    d_outs, head_grad = head_back(
        outs_all.reshape(-1, seq_len, model_width),
        table_low,
        model_of,
        fresh,
        piece_at[0::2],
        piece_at[1::2],
        jnp.where(filled, client_at, spare).astype(jnp.int32),
        slot_info,
        slot_target.reshape(steps, 1, 2 * seq_len),
    )
    d_group = lax.psum_scatter(
        d_outs[:devices].reshape(devices * seq_len, model_width),
        "grp",
        scatter_dimension=0,
        tiled=True,
    )
    d_level = lax.all_to_all(
        d_group.reshape(members, seq_len, model_width), "cli", 0, 0, tiled=True
    )
    d_level = jnp.sum(d_level.astype(jnp.float32), axis=0).astype(jnp.bfloat16)
    d_group = share_all(d_level, "cli", members)
    d_mine = lax.dynamic_slice(
        d_group, (part_own * local, 0, 0), (local, seq_len, model_width)
    ).astype(jnp.float32)
    d_final = jnp.where((my_choices == model_own)[:, None, None], d_mine, 0.0).reshape(
        local * seq_len, model_width
    )
    stack_rows, vector_rows, d_inputs = layer_backward(
        weights, vector_one, inputs, my_segments, saved, d_final
    )
    d_wide = d_inputs.astype(jnp.bfloat16)
    if share > 1:
        d_wide = lax.dynamic_update_slice(
            jnp.zeros((members * seq_len, model_width), jnp.bfloat16),
            d_wide,
            (part_own * local * seq_len, 0),
        )
    d_turned = lax.all_to_all(
        d_wide.reshape(members, seq_len, model_width), "cli", 0, 0, tiled=True
    )
    d_client = jnp.sum(d_turned.astype(jnp.float32), axis=0, keepdims=True).astype(jnp.bfloat16)
    d_all = spread(d_client, groups, members, 3, True, 2)

    stack_sum = lax.psum_scatter(stack_rows, "grp", scatter_dimension=0, tiled=True)
    vector_piece = vector_rows.size // groups
    vector_part = jnp.sum(
        lax.all_to_all(vector_rows.reshape(groups, vector_piece), "grp", 0, 0, tiled=True), axis=0
    )
    vector_grad = jnp.sum(
        share_all(vector_part, both, devices).reshape(groups, models, share, vector_piece), axis=2
    )
    vector_grad = vector_grad.transpose(1, 0, 2).reshape(vectors.shape)

    token_local = tokens - device_index * block_rows
    token_local = jnp.where((token_local >= 0) & (token_local < block_rows), token_local, -1)
    slot_token = jnp.where(filled[:, None], jnp.take(token_local, client_at, axis=0), -1)
    schedule = (model_of, fresh, final, client_at[0::2], client_at[1::2])
    slot_token = slot_token.reshape(steps, 1, 2 * seq_len)
    upper = finish_table(d_all, head_grad, table, table_momentum, schedule, slot_token, 0, 1, ())
    stack_sum, upper = lax.optimization_barrier((stack_sum, upper))
    stack_back = lax.all_to_all(
        stack_sum.reshape(members, stack_part, model_width), "cli", 0, 0, tiled=True
    ).astype(jnp.float32)
    table_grad, table_momentum_new, table_new = finish_table(
        d_all, head_grad, table, table_momentum, schedule, slot_token, 1, 1, upper
    )
    stack_grad = jnp.sum(stack_back.reshape(models, share, stack_part, model_width), axis=1)
    stack_momentum_new, stack_new = update(stack, stack_momentum, stack_grad, stack_rate)
    vector_momentum_new, vector_new = update(vectors, vector_momentum, vector_grad, vector_rate)
    return (
        loss,
        client_losses,
        table_grad,
        table_momentum_new,
        table_new,
        stack_grad,
        stack_momentum_new,
        stack_new,
        vector_grad,
        vector_momentum_new,
        vector_new,
    )


def solution(mesh):
    rows = P(("grp", "cli"), None)
    parts = P(None, ("grp", "cli"), None)
    return jax.shard_map(
        body,
        mesh=mesh,
        in_specs=(rows, rows, rows, P(("grp", "cli")), parts, parts, parts, parts, P(), P()),
        out_specs=(P(), rows, parts, parts, parts, parts, parts, parts, P(), P(), P()),
        check_vma=False,
    )
```

```python
import functools
import math

import jax
import jax.numpy as jnp
from jax import lax
from jax.experimental import pallas as pl
from jax.experimental.pallas import tpu as pltpu
from jax.sharding import PartitionSpec as P

HEADS = 12
HEAD_DIM = 64


epsilon = 1e-05
momentum_decay = 0.9
table_rate = 4.0
stack_rate = 4.0
vector_rate = 50.0

ROUND_ROWS = 104
SLAB_STEP = 16
TILE = 400
MIB = 1 << 20
POOL_BYTES = 32 * MIB
MESH = pl.DeviceIdType.MESH


def layer_norm(inputs, gain_row, shift_row):
    centred = inputs - jnp.mean(inputs, -1, keepdims=True)
    spread = jnp.mean(centred * centred, -1, keepdims=True)
    return centred * lax.rsqrt(spread + epsilon) * gain_row + shift_row


def project(inputs, matrix):
    return lax.dot_general(
        inputs, matrix, (((1,), (1,)), ((), ())), preferred_element_type=jnp.float32
    )


def product(inputs, matrix):
    return jnp.dot(inputs, matrix, preferred_element_type=jnp.float32)


def outer_rows(left, right):
    return lax.dot_general(
        left, right, (((0,), (0,)), ((), ())), preferred_element_type=jnp.float32
    )


def split_heads(rows, seq_len):
    return rows.reshape(-1, seq_len, HEADS, HEAD_DIM)


def attend(queries, key_rows, segment_rows):
    seq_len = segment_rows.shape[1]
    scores = jnp.einsum(
        "nqhd,nkhd->nhqk",
        split_heads(queries, seq_len),
        split_heads(key_rows, seq_len),
        preferred_element_type=jnp.float32,
    ) * HEAD_DIM ** (-0.5)
    positions = jnp.arange(seq_len)
    allowed = (positions[None, None, :] <= positions[None, :, None]) & (
        segment_rows[:, None, :] == segment_rows[:, :, None]
    )
    return jax.nn.softmax(jnp.where(allowed[:, None], scores, -1e30), axis=-1)


def layer_forward(weights, vector_one, inputs, segment_rows):
    row_count, model_width = inputs.shape
    seq_len = segment_rows.shape[1]
    normed = layer_norm(inputs, vector_one[0], vector_one[1]).astype(jnp.bfloat16)
    queries = (project(normed, weights[0:model_width]) + vector_one[6]).astype(jnp.bfloat16)
    key_rows = project(normed, weights[model_width : 2 * model_width]).astype(jnp.bfloat16)
    values = (project(normed, weights[2 * model_width : 3 * model_width]) + vector_one[7]).astype(
        jnp.bfloat16
    )
    attention = attend(queries, key_rows, segment_rows)
    mixture = jnp.einsum(
        "nhqk,nkhd->nqhd",
        attention.astype(jnp.bfloat16),
        split_heads(values, seq_len),
        preferred_element_type=jnp.float32,
    )
    mixture = mixture.reshape(row_count, model_width).astype(jnp.bfloat16)
    middle = inputs + (project(mixture, weights[3 * model_width : 4 * model_width]) + vector_one[8])
    normed_two = layer_norm(middle, vector_one[2], vector_one[3]).astype(jnp.bfloat16)
    hidden = project(normed_two, weights[4 * model_width : 8 * model_width]) + vector_one[
        10:14
    ].reshape(-1)
    active = jax.nn.gelu(hidden, approximate=True).astype(jnp.bfloat16)
    residual = middle + (
        product(active, weights[8 * model_width : 12 * model_width]) + vector_one[9]
    )
    normed_out = layer_norm(residual, vector_one[4], vector_one[5]).astype(jnp.bfloat16)
    return (
        normed,
        queries,
        key_rows,
        values,
        attention,
        mixture,
        middle,
        normed_two,
        hidden,
        active,
        residual,
        normed_out,
    )


def norm_grad(operand, gain_row, shift_row, cotangent):
    outcome, pullback = jax.vjp(layer_norm, operand, gain_row, shift_row)
    return pullback(cotangent)


def gelu_tanh(hidden):
    return jax.nn.gelu(hidden, approximate=True)


def layer_backward(weights, vector_one, inputs, segment_rows, saved, grad_out):
    row_count, model_width = inputs.shape
    seq_len = segment_rows.shape[1]
    scaling = HEAD_DIM ** (-0.5)
    (
        normed,
        queries,
        key_rows,
        values,
        attention,
        mixture,
        middle,
        normed_two,
        hidden,
        active,
        residual,
        normed_out,
    ) = saved
    d_residual, d_gain_out, d_shift_out = norm_grad(
        residual, vector_one[4], vector_one[5], grad_out
    )
    d_outer = d_residual.astype(jnp.bfloat16)
    d_bias_out = jnp.sum(d_outer.astype(jnp.float32), 0)
    grad_down = outer_rows(active, d_outer)
    d_active = project(d_outer, weights[8 * model_width : 12 * model_width])
    gelu_value, gelu_pull = jax.vjp(gelu_tanh, hidden)
    d_hidden = gelu_pull(d_active)[0].astype(jnp.bfloat16)
    d_bias_hidden = jnp.sum(d_hidden.astype(jnp.float32), 0)
    grad_up = outer_rows(d_hidden, normed_two)
    d_normed_two = product(d_hidden, weights[4 * model_width : 8 * model_width])
    d_middle_norm, d_gain_two, d_shift_two = norm_grad(
        middle, vector_one[2], vector_one[3], d_normed_two
    )
    d_middle = d_residual + d_middle_norm
    d_branch = d_middle.astype(jnp.bfloat16)
    d_bias_branch = jnp.sum(d_branch.astype(jnp.float32), 0)
    grad_mix = outer_rows(d_branch, mixture)
    d_mixture = split_heads(
        product(d_branch, weights[3 * model_width : 4 * model_width]).astype(jnp.bfloat16), seq_len
    )
    d_attention = jnp.einsum(
        "nqhd,nkhd->nhqk", d_mixture, split_heads(values, seq_len), preferred_element_type=jnp.float32
    )
    d_values = jnp.einsum(
        "nhqk,nqhd->nkhd",
        attention.astype(jnp.bfloat16),
        d_mixture,
        preferred_element_type=jnp.float32,
    )
    d_values = d_values.reshape(row_count, model_width).astype(jnp.bfloat16)
    d_scores = (
        attention * (d_attention - jnp.sum(attention * d_attention, -1, keepdims=True))
    ).astype(jnp.bfloat16)
    d_queries = (
        jnp.einsum(
            "nhqk,nkhd->nqhd",
            d_scores,
            split_heads(key_rows, seq_len),
            preferred_element_type=jnp.float32,
        )
        * scaling
    )
    d_queries = d_queries.reshape(row_count, model_width).astype(jnp.bfloat16)
    d_keys = (
        jnp.einsum(
            "nhqk,nqhd->nkhd",
            d_scores,
            split_heads(queries, seq_len),
            preferred_element_type=jnp.float32,
        )
        * scaling
    )
    d_keys = d_keys.reshape(row_count, model_width).astype(jnp.bfloat16)
    d_joined = jnp.concatenate([d_queries, d_keys, d_values], axis=1)
    grad_joined = outer_rows(d_joined, normed)
    d_normed = product(d_joined, weights[0 : 3 * model_width])
    d_inputs_norm, d_gain_one, d_shift_one = norm_grad(
        inputs, vector_one[0], vector_one[1], d_normed
    )
    d_inputs = d_middle + d_inputs_norm
    grad_places = jnp.sum(d_inputs.reshape(-1, seq_len, model_width), axis=0)
    stack_rows = jnp.concatenate(
        [
            piece.astype(jnp.bfloat16)
            for piece in (grad_joined, grad_mix, grad_up, grad_down, grad_places)
        ],
        axis=0,
    )
    bias_query = jnp.sum(d_queries.astype(jnp.float32), 0)
    bias_value = jnp.sum(d_values.astype(jnp.float32), 0)
    vector_rows = jnp.concatenate(
        [
            jnp.stack(
                [
                    d_gain_one,
                    d_shift_one,
                    d_gain_two,
                    d_shift_two,
                    d_gain_out,
                    d_shift_out,
                    bias_query,
                    bias_value,
                    d_bias_branch,
                    d_bias_out,
                ]
            ),
            d_bias_hidden.reshape(4, model_width),
        ],
        axis=0,
    )
    return (stack_rows, vector_rows, d_inputs)


def share_all(rows, axes, size):
    return lax.all_to_all(
        jnp.broadcast_to(rows[None], (size,) + rows.shape), axes, 0, 0, tiled=True
    )


def update(weight, momentum, gradient, step_rate):
    renewed = momentum_decay * momentum + gradient
    return (renewed, weight - step_rate * (gradient + momentum_decay * renewed))


def flipped(value, offset, size):
    bit = 1
    while bit < size:
        digit = lax.rem(lax.div(offset, bit), 2)
        value = value + digit * bit * (1 - 2 * lax.rem(lax.div(value, bit), 2))
        bit *= 2
    return value


class Place:
    def __init__(self, groups, members):
        self.groups, self.members = groups, members
        self.ys = 2
        self.xs = groups // 4
        self.grp = lax.axis_index("grp")
        self.cli = lax.axis_index("cli")
        self.core = lax.rem(self.grp, 2)
        self.x = lax.rem(lax.div(self.grp, 2), self.xs)
        self.y = lax.div(self.grp, 2 * self.xs)

    def group(self, jx=0, jy=0, jc=0):
        x = flipped(self.x, jx, self.xs)
        y = flipped(self.y, jy, self.ys)
        core = self.core + jc * (1 - 2 * self.core)
        return (y * self.xs + x) * 2 + core

    def block(self, jx, jy, level, jc=0):
        return self.group(jx, jy, jc) * self.members + level

    def peer(self, jx=0, jy=0, jc=0):
        return (self.group(jx, jy, jc), self.cli)

    def level(self, level):
        return (self.grp, level)

    def nearest(self, i):
        z, last = self.cli, self.members - 1
        low = jnp.where(2 * z < last, 1, 0)
        sign = 2 * low - 1
        margin = low * z + (1 - low) * (last - z)
        step = lax.div(i + 1, 2)
        odd = lax.rem(i, 2)
        near = z + sign * step * (2 * odd - 1)
        far = z + sign * (i - margin)
        return jnp.where(i <= 2 * margin, near, far)


def greet(place):
    barrier = pltpu.get_barrier_semaphore()
    peers = [place.peer(jx=j) for j in range(1, place.xs)] + [place.peer(jy=j) for j in range(1, place.ys)]
    peers.append(place.peer(jc=1))
    peers += [place.level(lax.rem(place.cli + j, place.members)) for j in range(1, place.members)]
    for peer in peers:
        pl.semaphore_signal(barrier, inc=1, device_id=peer, device_id_type=MESH)
    pl.semaphore_wait(barrier, len(peers))


def spread_sems(groups, members, pieces):
    xs, ys, items = groups // 4, 2, members * pieces
    dma = pltpu.SemaphoreType.DMA
    shapes = [(items,)] * 3 + [(items, xs)] * 2 + [(items, ys)] * 2 + [(items, xs, ys)] * 6
    return [dma] + [dma(shape) for shape in shapes]


def spread_body(place, chain, pieces, src, out, sems, consume, ready=None):
    (own_sem, z_up, z_down, z_recv, x_send, x_recv, y_send, y_recv, k_send, k_recv, p_send, p_recv,
     c_send, c_recv) = sems
    xs, ys, members = place.xs, place.ys, place.members
    items = members * pieces
    size = out.shape[1] // pieces
    z = place.cli
    partner = z + 1 - 2 * lax.rem(z, 2)
    inner_x, inner_y = range(1, xs), range(1, ys)

    def move(source, target, send, recv, device):
        return pltpu.make_async_remote_copy(
            src_ref=source, dst_ref=target, send_sem=send, recv_sem=recv, device_id=device, device_id_type=MESH
        )

    class Item:
        def __init__(self, k):
            self.level = place.nearest(lax.div(k, pieces))
            self.piece = lax.rem(k, pieces)
            self.slot = self.level * pieces + self.piece
            self.even = lax.rem(self.piece, 2) == 0
            self.mine = lax.rem(self.level + z, 2) == 0 if chain else self.level >= 0
            self.rows = pl.ds(self.piece * size, size)

        def part(self, jx, jy, level=None):
            return out.at[place.block(jx, jy, self.level if level is None else level), self.rows]

        def here(self, own):
            return src.at[z if not chain else 0, self.rows] if own else self.part(0, 0)

        def up(self, own=False):
            return move(self.here(own), self.part(0, 0), z_up.at[self.slot], z_recv.at[self.slot], place.level(z + 1))

        def down(self, own=False):
            return move(self.here(own), self.part(0, 0), z_down.at[self.slot], z_recv.at[self.slot], place.level(z - 1))

        def straight(self):
            return move(
                src.at[self.level, self.rows], self.part(0, 0, z), z_up.at[self.slot],
                z_recv.at[z * pieces + self.piece], place.level(self.level),
            )

        def landed(self):
            part = self.part(0, 0)
            return move(part, part, z_up.at[self.slot], z_recv.at[self.slot], place.level(partner))

        def to_x(self, jx, own=False):
            return move(self.here(own), self.part(0, 0), x_send.at[self.slot, jx], x_recv.at[self.slot, jx], place.peer(jx=jx))

        def to_y(self, jy, own=False):
            return move(self.here(own), self.part(0, 0), y_send.at[self.slot, jy], y_recv.at[self.slot, jy], place.peer(jy=jy))

        def corner_a(self, jx, jy):
            part = self.part(jx, 0)
            return move(part, part, k_send.at[self.slot, jx, jy], k_recv.at[self.slot, jx, jy], place.peer(jy=jy))

        def corner_b(self, jx, jy):
            part = self.part(0, jy)
            return move(part, part, k_send.at[self.slot, jx, jy], k_recv.at[self.slot, jx, jy], place.peer(jx=jx))

        def corner_z(self, jx, jy):
            part = self.part(jx, jy)
            return move(part, part, p_send.at[self.slot, jx, jy], p_recv.at[self.slot, jx, jy], place.level(partner))

        def to_core(self, jx, jy, own=False):
            part = self.part(jx, jy)
            return move(self.here(True) if own else part, part, c_send.at[self.slot, jx, jy], c_recv.at[self.slot, jx, jy], place.peer(jc=1))

    own = pltpu.make_async_copy(src.at[z if not chain else 0], out.at[place.block(0, 0, z)], own_sem)
    own.start()
    if not chain:
        for piece in range(pieces):
            Item(pieces + piece).straight().start()

    def columns(k):
        item = Item(k)
        level = item.level

        @pl.when(k < pieces)
        def mine_first():
            if chain:
                @pl.when(z + 1 < members)
                def onward():
                    item.up(True).start()

                @pl.when(z > 0)
                def back():
                    item.down(True).start()

            for jx in inner_x:
                item.to_x(jx, True).start()
            for jy in inner_y:
                item.to_y(jy, True).start()
            item.to_core(0, 0, True).start()

        @pl.when(k >= pieces)
        def arrive():
            item.landed().wait_recv()
            if chain:
                @pl.when((level < z) & (z + 1 < members))
                def onward():
                    item.up().start()

                @pl.when((level > z) & (z > 0))
                def back():
                    item.down().start()
            else:
                @pl.when(k + pieces < items)
                def following():
                    Item(k + pieces).straight().start()

            for jx in inner_x:
                item.to_x(jx).start()
            for jy in inner_y:
                item.to_y(jy).start()
            item.to_core(0, 0).start()

    def edges(k):
        item = Item(k)
        for jx in inner_x:
            item.to_x(jx).wait_recv()

            @pl.when(item.mine & item.even)
            def pass_a():
                for jy in inner_y:
                    item.corner_a(jx, jy).start()

            item.to_core(jx, 0).start()
        for jy in inner_y:
            item.to_y(jy).wait_recv()

            @pl.when(item.mine & jnp.logical_not(item.even))
            def pass_b():
                for jx in inner_x:
                    item.corner_b(jx, jy).start()

            item.to_core(0, jy).start()

    def corners(k):
        item = Item(k)

        @pl.when(item.mine)
        def mine_now():
            for jx in inner_x:
                for jy in inner_y:
                    item.corner_a(jx, jy).wait_recv()
                    if chain:
                        item.corner_z(jx, jy).start()
                    item.to_core(jx, jy).start()

    def handed(k):
        item = Item(k)

        @pl.when(jnp.logical_not(item.mine))
        def from_partner():
            for jx in inner_x:
                for jy in inner_y:
                    item.corner_z(jx, jy).wait_recv()
                    item.to_core(jx, jy).start()

    spots = xs * ys
    lag_edge, lag_corner = (2, 4) if chain else (1, 3)
    lag_handed = pieces + 6 if chain else lag_corner
    lag_end = lag_handed + 1

    def tick(t, carry):
        @pl.when(t < items)
        def arrivals():
            columns(t)

        @pl.when((t >= lag_edge) & (t < items + lag_edge))
        def sides():
            edges(t - lag_edge)

        @pl.when((t >= lag_corner) & (t < items + lag_corner))
        def far():
            corners(t - lag_corner)

        if chain:
            @pl.when((t >= lag_handed) & (t < items + lag_handed))
            def others():
                handed(t - lag_handed)

        def visit(e, carry):
            jc = lax.div(e, spots)
            spot = lax.rem(e, spots)
            jx, jy = lax.rem(spot, xs), lax.div(spot, xs)
            far = jnp.minimum(jx, 1) + jnp.minimum(jy, 1)
            lag = jnp.where(far == 0, 1, jnp.where(far == 1, lag_edge + 1, lag_end))
            k = t - lag

            @pl.when((k >= 0) & (k < items))
            def valid():
                item = Item(k)

                @pl.when(jc == 1)
                def shared():
                    item.to_core(jx, jy).wait_recv()

                if consume is not None:
                    consume(place.block(jx, jy, item.level, jc), item.level, item.piece)

            return carry

        return lax.fori_loop(0, 2 * spots, visit, carry)

    if ready is not None:
        own.wait()
        ready()
    lax.fori_loop(0, items + lag_end, tick, 0)

    def close(k, carry):
        item = Item(k)
        level = item.level
        if chain:
            @pl.when((level <= z) & (z + 1 < members))
            def onward():
                item.up().wait_send()

            @pl.when((level >= z) & (z > 0))
            def back():
                item.down().wait_send()
        else:
            @pl.when(k >= pieces)
            def sent():
                item.straight().wait_send()

        for jx in inner_x:
            item.to_x(jx).wait_send()
        for jy in inner_y:
            item.to_y(jy).wait_send()
        for jx in range(xs):
            for jy in range(ys):
                item.to_core(jx, jy).wait_send()

        @pl.when(item.mine)
        def mine_done():
            for jx in inner_x:
                for jy in inner_y:
                    item.corner_a(jx, jy).wait_send()
                    if chain:
                        item.corner_z(jx, jy).wait_send()

        return carry

    lax.fori_loop(0, items, close, 0)
    if ready is None:
        own.wait()


def spread_kernel(groups, members, chain, pieces, src, out, *sems):
    place = Place(groups, members)
    greet(place)
    spread_body(place, chain, pieces, src, out, sems, None)


def spread(src, groups, members, collective_id, chain, pieces):
    count, rows, width = src.shape
    return pl.pallas_call(
        functools.partial(spread_kernel, groups, members, chain, pieces),
        out_shape=jax.ShapeDtypeStruct((groups * members, rows, width), src.dtype),
        in_specs=[pl.BlockSpec(memory_space=pl.ANY)],
        out_specs=pl.BlockSpec(memory_space=pl.ANY),
        scratch_shapes=spread_sems(groups, members, pieces),
        compiler_params=pltpu.CompilerParams(collective_id=collective_id, has_side_effects=True),
        cost_estimate=pl.CostEstimate(
            flops=0, bytes_accessed=4 * groups * members * rows * width, transcendentals=0
        ),
    )(src)


def tile_of(part_rows):
    return TILE if part_rows % TILE == 0 else part_rows


def score_kernel(groups, members, share, pieces, src, table, target, out, stat, *rest):
    part, pool, part_sem, out_sems = rest[:4]
    sems = rest[4:]
    place = Place(groups, members)
    load_table = pltpu.make_async_copy(table, part, part_sem)
    load_table.start()
    greet(place)
    rows = pool.shape[1]
    size = rows // pieces

    def keep(block, piece):
        here = pl.ds(pl.multiple_of(piece * size, size), size)
        return pltpu.make_async_copy(pool.at[block, here], out.at[block, here], out_sems.at[block, piece])

    def consume(block, level, piece):
        keep(block, piece).start()
        here = pl.ds(pl.multiple_of(piece * size, size), size)
        model = lax.div(level, share)
        wanted = target[lax.div(block, members) * share + lax.rem(level, share), :, here]
        outs = pool[block, here]
        part_rows = part.shape[1]
        tile = tile_of(part_rows)
        marks = lax.broadcasted_iota(jnp.int32, (tile, size), 0)
        tops, totals, hits = [], [], []
        for first in range(0, part_rows, tile):
            logits = project(part[model, pl.ds(first, tile)], outs)
            hit = jnp.where(marks == wanted - first, logits, 0.0).reshape(-1, 8, size)
            hits.append(jnp.sum(hit, axis=0))
            logits = logits.reshape(-1, 8, size)
            top = jnp.max(logits, axis=0)
            tops.append(top)
            totals.append(jnp.sum(jnp.exp(logits - top[None]), axis=0))
        highest = jnp.max(functools.reduce(jnp.maximum, tops), axis=0, keepdims=True)
        total = sum(t * jnp.exp(m - highest) for t, m in zip(totals, tops))
        stat[block, 0:1, here] = highest + jnp.log(jnp.sum(total, axis=0, keepdims=True))
        stat[block, 1:2, here] = jnp.sum(sum(hits), axis=0, keepdims=True)

    spread_body(place, True, pieces, src, pool, sems, consume, load_table.wait)

    def close(block, carry):
        for piece in range(pieces):
            keep(block, piece).wait()
        return carry

    lax.fori_loop(0, groups * members, close, 0)


def spread_score(src, table_low, target_blocks, groups, members, share, collective_id, pieces=2):
    _, rows, width = src.shape
    blocks = groups * members
    return pl.pallas_call(
        functools.partial(score_kernel, groups, members, share, pieces),
        out_shape=(
            jax.ShapeDtypeStruct((blocks, rows, width), src.dtype),
            jax.ShapeDtypeStruct((blocks, 2, rows), jnp.float32),
        ),
        in_specs=[
            pl.BlockSpec(memory_space=pl.ANY),
            pl.BlockSpec(memory_space=pl.ANY),
            pl.BlockSpec(memory_space=pltpu.VMEM),
        ],
        out_specs=(pl.BlockSpec(memory_space=pl.ANY), pl.BlockSpec(memory_space=pltpu.VMEM)),
        scratch_shapes=[
            pltpu.VMEM(table_low.shape, table_low.dtype),
            pltpu.VMEM((blocks, rows, width), src.dtype),
            pltpu.SemaphoreType.DMA,
            pltpu.SemaphoreType.DMA((blocks, pieces)),
        ]
        + spread_sems(groups, members, pieces),
        compiler_params=pltpu.CompilerParams(
            collective_id=collective_id, has_side_effects=True, vmem_limit_bytes=60 * MIB
        ),
        cost_estimate=pl.CostEstimate(
            flops=2 * blocks * rows * table_low.shape[1] * width,
            bytes_accessed=2 * blocks * rows * width * 2,
            transcendentals=blocks * rows * table_low.shape[1],
        ),
    )(src, table_low, target_blocks)


def stats_kernel(outs_ref, table_ref, target_ref, stat_ref):
    logits = project(table_ref[0], outs_ref[0])
    highest = jnp.max(logits, axis=0, keepdims=True)
    total = jnp.sum(jnp.exp(logits - highest), axis=0, keepdims=True)
    rows = lax.broadcasted_iota(jnp.int32, logits.shape, 0)
    hit = jnp.sum(jnp.where(rows == target_ref[0], logits, 0.0), axis=0, keepdims=True)
    stat_ref[0, 0:1, :] = highest + jnp.log(total)
    stat_ref[0, 1:2, :] = hit


def head_stats(outs_all, table_low, target_blocks, groups, members, share):
    blocks, rows, width = outs_all.shape
    part_rows = table_low.shape[1]
    return pl.pallas_call(
        stats_kernel,
        out_shape=jax.ShapeDtypeStruct((blocks, 2, rows), jnp.float32),
        grid=(members, groups),
        in_specs=[
            pl.BlockSpec((1, rows, width), lambda z, g: (g * members + z, 0, 0)),
            pl.BlockSpec((1, part_rows, width), lambda z, g: (z // share, 0, 0)),
            pl.BlockSpec((1, 1, rows), lambda z, g: (g * share + z % share, 0, 0)),
        ],
        out_specs=pl.BlockSpec((1, 2, rows), lambda z, g: (g * members + z, 0, 0)),
        compiler_params=pltpu.CompilerParams(vmem_limit_bytes=56 * MIB),
        cost_estimate=pl.CostEstimate(
            flops=2 * blocks * rows * part_rows * width,
            bytes_accessed=2 * outs_all.size + 2 * table_low.size,
            transcendentals=blocks * rows * part_rows,
        ),
    )(outs_all, table_low, target_blocks)


def collect_kernel(groups, members, source, out, work, from_core, from_x, from_y, then_y, then_x, from_z, *sems):
    (load_sem, core_send, core_recv, x_send, x_recv, y_send, y_recv, yy_send, yy_recv, xx_send, xx_recv, z_send,
     z_recv, g_send, g_recv) = sems
    place = Place(groups, members)
    greet(place)
    xs, ys = place.xs, place.ys
    half = members // 2
    upper, lower = pl.ds(0, half), pl.ds(half, half)
    z = place.cli
    order = sorted(
        ((jx, jy) for jx in range(xs) for jy in range(ys)), key=lambda spot: -(spot[0] > 0) - (spot[1] > 0)
    )
    started = []

    def send(source_ref, target_ref, send_sem, recv_sem, device):
        copy = pltpu.make_async_remote_copy(
            src_ref=source_ref, dst_ref=target_ref, send_sem=send_sem, recv_sem=recv_sem, device_id=device,
            device_id_type=MESH,
        )
        copy.start()
        started.append(copy)

    def arrival(target_ref, send_sem, recv_sem, device):
        pltpu.make_async_remote_copy(
            src_ref=target_ref, dst_ref=target_ref, send_sem=send_sem, recv_sem=recv_sem, device_id=device,
            device_id_type=MESH,
        ).wait_recv()

    def spot_of(jx, jy):
        return jy * xs + jx

    def add(ref, others):
        total = ref[...].astype(jnp.float32)
        for other in others:
            total = total + other[...].astype(jnp.float32)
        ref[...] = total.astype(ref.dtype)

    for jx, jy in order:
        k = spot_of(jx, jy)
        send(
            source.at[pl.ds(place.group(jx, jy, 1) * members, members)], from_core.at[k], core_send.at[k],
            core_recv.at[k], place.peer(jc=1),
        )
    loads = {}
    for jx, jy in order:
        k = spot_of(jx, jy)
        loads[k] = pltpu.make_async_copy(
            source.at[pl.ds(place.group(jx, jy, 0) * members, members)], work.at[k], load_sem.at[k]
        )
        loads[k].start()
    for jx, jy in order:
        k = spot_of(jx, jy)
        loads[k].wait()
        arrival(from_core.at[k], core_send.at[k], core_recv.at[k], place.peer(jc=1))
        add(work.at[k], [from_core.at[k]])
        if jx:
            send(work.at[k, upper], from_x.at[jx, jy], x_send.at[jx, jy], x_recv.at[jx, jy], place.peer(jx=jx))
        if jy:
            send(work.at[k, lower], from_y.at[jx, jy], y_send.at[jx, jy], y_recv.at[jx, jy], place.peer(jy=jy))
    for jy in reversed(range(ys)):
        k = spot_of(0, jy)
        for jx in range(1, xs):
            arrival(from_x.at[jx, jy], x_send.at[jx, jy], x_recv.at[jx, jy], place.peer(jx=jx))
        add(work.at[k, upper], [from_x.at[jx, jy] for jx in range(1, xs)])
        if jy:
            send(work.at[k, upper], then_y.at[jy], yy_send.at[jy], yy_recv.at[jy], place.peer(jy=jy))
    for jx in reversed(range(xs)):
        k = spot_of(jx, 0)
        for jy in range(1, ys):
            arrival(from_y.at[jx, jy], y_send.at[jx, jy], y_recv.at[jx, jy], place.peer(jy=jy))
        add(work.at[k, lower], [from_y.at[jx, jy] for jy in range(1, ys)])
        if jx:
            send(work.at[k, lower], then_x.at[jx], xx_send.at[jx], xx_recv.at[jx], place.peer(jx=jx))
    own = work.at[0]
    for jy in range(1, ys):
        arrival(then_y.at[jy], yy_send.at[jy], yy_recv.at[jy], place.peer(jy=jy))
    add(own.at[upper], [then_y.at[jy] for jy in range(1, ys)])
    for jx in range(1, xs):
        arrival(then_x.at[jx], xx_send.at[jx], xx_recv.at[jx], place.peer(jx=jx))
    add(own.at[lower], [then_x.at[jx] for jx in range(1, xs)])

    for j in range(1, members):
        level = lax.rem(z + j, members)
        send(own.at[level], from_z.at[j], z_send.at[j], z_recv.at[j], place.level(level))
    total = work[0, z].astype(jnp.float32)
    for j in range(1, members):
        arrival(from_z.at[j], z_send.at[j], z_recv.at[j], place.level(lax.rem(z + members - j, members)))
        total = total + from_z[j].astype(jnp.float32)
    out[z] = total.astype(out.dtype)
    for j in range(1, members):
        send(out.at[z], out.at[z], g_send.at[j], g_recv.at[j], place.level(lax.rem(z + j, members)))
    for j in range(1, members):
        level = lax.rem(z + members - j, members)
        arrival(out.at[level], g_send.at[j], g_recv.at[j], place.level(level))
    for copy in started:
        copy.wait_send()


def collect(parts, groups, members, collective_id):
    _, seq_len, width = parts.shape
    xs, ys, half = groups // 4, 2, members // 2
    dma = pltpu.SemaphoreType.DMA

    def held(*shape):
        return pltpu.VMEM(shape + (seq_len, width), parts.dtype)

    return pl.pallas_call(
        functools.partial(collect_kernel, groups, members),
        out_shape=jax.ShapeDtypeStruct((members, seq_len, width), parts.dtype),
        in_specs=[pl.BlockSpec(memory_space=pl.ANY)],
        out_specs=pl.BlockSpec(memory_space=pltpu.VMEM),
        scratch_shapes=[
            held(xs * ys, members),
            held(xs * ys, members),
            held(xs, ys, half),
            held(xs, ys, half),
            held(ys, half),
            held(xs, half),
            held(members),
        ]
        + [dma((xs * ys,))] * 3
        + [dma((xs, ys))] * 4
        + [dma((ys,))] * 2
        + [dma((xs,))] * 2
        + [dma((members,))] * 4,
        compiler_params=pltpu.CompilerParams(
            collective_id=collective_id, has_side_effects=True, vmem_limit_bytes=56 * MIB
        ),
        cost_estimate=pl.CostEstimate(
            flops=0, bytes_accessed=4 * groups * members * seq_len * width, transcendentals=0
        ),
    )(parts)


def unpack_kernel(start, part, at_ref, pool_ref, weights_ref, rows_ref):
    step = pl.program_id(0)
    owners, slab, width = pool_ref.shape
    weights_ref[...] = jnp.concatenate([pool_ref[j, :part] for j in range(owners)], axis=0)
    columns = lax.broadcasted_iota(jnp.int32, (at_ref.shape[0], slab - start), 1) + start
    found = jnp.zeros(rows_ref.shape, jnp.float32)
    for j in range(owners):
        at = at_ref[...] - (step * owners + j) * slab
        hits = (columns == at).astype(jnp.float32).astype(jnp.bfloat16)
        found = found + product(hits, pool_ref[j, start:])

    @pl.when(step == 0)
    def begin():
        rows_ref[...] = found

    @pl.when(step > 0)
    def more():
        rows_ref[...] += found


def unpack(pool, part, at):
    devices, slab, width = pool.shape
    owners = 8 // math.gcd(part, 8)
    start = part // 16 * 16
    tokens = at.shape[0]
    return pl.pallas_call(
        functools.partial(unpack_kernel, start, part),
        out_shape=(
            jax.ShapeDtypeStruct((devices * part, width), pool.dtype),
            jax.ShapeDtypeStruct((tokens, width), jnp.float32),
        ),
        grid=(devices // owners,),
        in_specs=[
            pl.BlockSpec((tokens, 1), lambda i: (0, 0)),
            pl.BlockSpec((owners, slab, width), lambda i: (i, 0, 0)),
        ],
        out_specs=(
            pl.BlockSpec((owners * part, width), lambda i: (i, 0)),
            pl.BlockSpec((tokens, width), lambda i: (0, 0)),
        ),
        compiler_params=pltpu.CompilerParams(vmem_limit_bytes=40 * MIB),
        cost_estimate=pl.CostEstimate(
            flops=2 * devices * tokens * (slab - start) * width,
            bytes_accessed=4 * pool.size,
            transcendentals=0,
        ),
    )(at, pool)


def back_kernel(
    model_ref, fresh_ref, first_ref, second_ref, place_ref, a_ref, b_ref, table_ref, info_ref, target_ref, d_outs_ref,
    grad_ref, held, sems,
):
    step = pl.program_id(0)
    steps = pl.num_programs(0)
    seq_len = a_ref.shape[1]
    slot = lax.rem(step, 2)

    def leave(which, where, half):
        return pltpu.make_async_copy(
            held.at[which, half], d_outs_ref.at[where], sems.at[which, half]
        )

    @pl.when(step >= 2)
    def reuse():
        leave(slot, 0, 0).wait()
        leave(slot, 0, 1).wait()
    outs = jnp.concatenate([a_ref[0], b_ref[0]], axis=0)
    @pl.when(fresh_ref[step] == 1)
    def start():
        grad_ref[...] = jnp.zeros_like(grad_ref)

    part_rows = table_ref.shape[1]
    size = tile_of(part_rows)
    d_outs = jnp.zeros((2 * seq_len, outs.shape[1]), jnp.float32)
    for first_row in range(0, part_rows, size):
        here = pl.ds(first_row, size)
        table_rows = table_ref[0, here]
        logits = project(table_rows, outs)
        rows = lax.broadcasted_iota(jnp.int32, logits.shape, 0) + first_row
        soft = jnp.exp(logits - info_ref[0, 0:1, :])
        soft = jnp.where(rows == target_ref[0], soft - 1.0, soft)
        d_logits = (info_ref[0, 1:2, :] * soft).astype(jnp.bfloat16)
        d_outs = d_outs + outer_rows(d_logits, table_rows)
        grad_ref[0, here] += product(d_logits, outs)
    held[slot, 0] = d_outs[:seq_len].astype(held.dtype)
    held[slot, 1] = d_outs[seq_len:].astype(held.dtype)
    leave(slot, place_ref[2 * step], 0).start()
    leave(slot, place_ref[2 * step + 1], 1).start()

    @pl.when(step == steps - 1)
    def drain():
        for which in range(2):
            leave(which, 0, 0).wait()
            leave(which, 0, 1).wait()


def head_back(outs_pieces, table_low, model_of, fresh, first, second, place, info, target):
    steps = model_of.shape[0]
    models, part_rows, width = table_low.shape
    seq_len = outs_pieces.shape[1]
    return pl.pallas_call(
        back_kernel,
        out_shape=(
            jax.ShapeDtypeStruct((2 * steps, seq_len, width), jnp.bfloat16),
            jax.ShapeDtypeStruct((models, part_rows, width), jnp.float32),
        ),
        grid_spec=pltpu.PrefetchScalarGridSpec(
            num_scalar_prefetch=5,
            grid=(steps,),
            in_specs=[
                pl.BlockSpec((1, seq_len, width), lambda s, m, f, a, b, p: (a[s], 0, 0)),
                pl.BlockSpec((1, seq_len, width), lambda s, m, f, a, b, p: (b[s], 0, 0)),
                pl.BlockSpec((1, part_rows, width), lambda s, m, f, a, b, p: (m[s], 0, 0)),
                pl.BlockSpec((1, 2, 2 * seq_len), lambda s, m, f, a, b, p: (s, 0, 0)),
                pl.BlockSpec((1, 1, 2 * seq_len), lambda s, m, f, a, b, p: (s, 0, 0)),
            ],
            out_specs=(
                pl.BlockSpec(memory_space=pl.ANY),
                pl.BlockSpec((1, part_rows, width), lambda s, m, f, a, b, p: (m[s], 0, 0)),
            ),
            scratch_shapes=[
                pltpu.VMEM((2, 2, seq_len, width), jnp.bfloat16),
                pltpu.SemaphoreType.DMA((2, 2)),
            ],
        ),
        compiler_params=pltpu.CompilerParams(vmem_limit_bytes=56 * MIB),
        cost_estimate=pl.CostEstimate(
            flops=12 * steps * seq_len * part_rows * width,
            bytes_accessed=4 * steps * seq_len * width * 2 + 6 * table_low.size,
            transcendentals=2 * steps * seq_len * part_rows,
        ),
    )(model_of, fresh, first, second, place, outs_pieces, outs_pieces, table_low, info, target)


def finish_kernel(
    first_model, start_ref, first_ref, second_ref, d_ref, ids_ref, head_ref, table_ref, momentum_ref, *rest
):
    grad_ref, momentum_new_ref, table_new_ref = rest[-3:]
    model = pl.program_id(0) + first_model
    tile_rows = grad_ref.shape[1]
    tokens = ids_ref.shape[2]
    rows = lax.broadcasted_iota(jnp.int32, (tile_rows, tokens), 0) + pl.program_id(1) * tile_rows
    grad_ref[0] = head_ref[0]

    def pair(step, carry):
        hits = (rows == ids_ref[step]).astype(jnp.float32).astype(jnp.bfloat16)
        outs = jnp.concatenate([d_ref[first_ref[step]], d_ref[second_ref[step]]], axis=0)
        grad_ref[0] += product(hits, outs)
        return carry

    lax.fori_loop(start_ref[model], start_ref[model + 1], pair, 0)
    renewed, fresh_table = update(table_ref[0], momentum_ref[0], grad_ref[0], table_rate)
    momentum_new_ref[0] = renewed
    table_new_ref[0] = fresh_table


def finish_table(d_inputs, head_grad, table, momentum, schedule, ids, first_model, count, earlier):
    models, part_rows, width = table.shape
    tile_rows = tile_of(part_rows)
    state = jax.ShapeDtypeStruct(table.shape, jnp.float32)
    piece = pl.BlockSpec((1, tile_rows, width), lambda m, t, *_: (m + first_model, t, 0))
    whole = pl.BlockSpec(memory_space=pltpu.VMEM)
    return pl.pallas_call(
        functools.partial(finish_kernel, first_model),
        out_shape=(state, state, state),
        grid_spec=pltpu.PrefetchScalarGridSpec(
            num_scalar_prefetch=3,
            grid=(count, part_rows // tile_rows),
            in_specs=[whole, whole, piece, piece, piece]
            + [pl.BlockSpec(memory_space=pl.ANY)] * len(earlier),
            out_specs=(piece, piece, piece),
        ),
        input_output_aliases={8 + i: i for i in range(len(earlier))},
        compiler_params=pltpu.CompilerParams(vmem_limit_bytes=56 * MIB),
        cost_estimate=pl.CostEstimate(
            flops=2 * d_inputs.size * part_rows * count // models,
            bytes_accessed=24 * count * part_rows * width,
            transcendentals=0,
        ),
    )(*schedule, d_inputs, ids, head_grad, table, momentum, *earlier)


def body(
    token_ids,
    target_ids,
    segment_ids,
    chosen,
    table,
    table_momentum,
    stack,
    stack_momentum,
    vectors,
    vector_momentum,
):
    both = ("grp", "cli")
    models, block_rows, model_width = table.shape
    stack_part = stack.shape[1]
    seq_len = token_ids.shape[1]
    groups = lax.axis_size("grp")
    members = lax.axis_size("cli")
    devices = groups * members
    share = members // models
    local = members // share
    device_index = lax.axis_index(both)
    group_index = lax.axis_index("grp")
    member_index = lax.axis_index("cli")
    model_own = member_index // share
    part_own = member_index % share
    model_range = jnp.arange(models, dtype=jnp.int32)

    def per_member(rows):
        return jnp.repeat(rows, share, axis=0) if share > 1 else rows

    slab = -(-(stack_part + ROUND_ROWS) // SLAB_STEP) * SLAB_STEP
    round_rows = slab - stack_part

    facts = share_all(
        jnp.concatenate([token_ids[0], target_ids[0], segment_ids[0], chosen]), both, devices
    )
    tokens = facts[:, :seq_len]
    targets = facts[:, seq_len : 2 * seq_len]
    segments = facts[:, 2 * seq_len : 3 * seq_len]
    choices = facts[:, 3 * seq_len]
    valid = jnp.concatenate(
        [
            (segments[:, :-1] == segments[:, 1:]).astype(jnp.float32),
            jnp.zeros((devices, 1), jnp.float32),
        ],
        axis=1,
    )
    counts = jnp.sum(valid, axis=1)
    choice_table = (choices[:, None] == model_range[None, :]).astype(jnp.float32)
    totals = jnp.sum(choice_table * counts[:, None], axis=0)
    total_of = jnp.sum(choice_table * totals[None, :], axis=1)

    table_low = table.astype(jnp.bfloat16)
    fine = 16 if block_rows % 64 else 64
    coarse = block_rows // fine
    flat_tokens = tokens.reshape(-1)
    high_hot = (
        (flat_tokens // fine)[:, None] == jnp.arange(devices * coarse, dtype=jnp.int32)[None, :]
    ).astype(jnp.bfloat16)
    low_hot = ((flat_tokens % fine)[:, None] == jnp.arange(fine, dtype=jnp.int32)[None, :]).astype(
        jnp.bfloat16
    )
    seen = (outer_rows(high_hot, low_hot) > 0).astype(jnp.float32)
    before = product(
        seen.astype(jnp.bfloat16),
        jnp.triu(jnp.ones((fine, fine), jnp.bfloat16), 1),
    )
    sums = jnp.sum(seen, axis=1).reshape(devices, coarse)
    uniques = jnp.sum(sums, axis=1)
    ahead = jnp.sum(
        jnp.where(
            jnp.arange(coarse)[None, None, :] < jnp.arange(coarse)[None, :, None],
            sums[:, None, :],
            0.0,
        ),
        axis=2,
    )
    places = before + ahead.reshape(-1, 1)
    rounds = jnp.max(jnp.ceil(uniques / round_rows)).astype(jnp.int32)
    own_places = lax.dynamic_slice(places, (device_index * coarse, 0), (coarse, fine)).reshape(-1)
    own_seen = lax.dynamic_slice(seen, (device_index * coarse, 0), (coarse, fine)).reshape(-1)
    own_places = jnp.where(own_seen > 0, own_places, -1.0).astype(jnp.int32)
    first_client = group_index * members + part_own * local
    my_tokens = lax.dynamic_slice(tokens, (first_client, 0), (local, seq_len)).reshape(-1)
    my_segments = lax.dynamic_slice(segments, (first_client, 0), (local, seq_len))
    my_choices = lax.dynamic_slice(choices, (first_client,), (local,))
    my_high = (
        (my_tokens // fine)[:, None] == jnp.arange(devices * coarse, dtype=jnp.int32)[None, :]
    ).astype(jnp.bfloat16)
    my_low = (my_tokens % fine)[:, None] == jnp.arange(fine, dtype=jnp.int32)[None, :]
    split_places = jnp.concatenate(
        [jnp.floor(places / 64.0), places - 64.0 * jnp.floor(places / 64.0)], axis=1
    ).astype(jnp.bfloat16)
    picked_places = product(my_high, split_places)
    picked_places = 64.0 * picked_places[:, :fine] + picked_places[:, fine:]
    my_places = jnp.sum(jnp.where(my_low, picked_places, 0.0), axis=1).astype(jnp.int32)
    my_owner = my_tokens // block_rows

    def offered(start):
        wanted = jnp.arange(round_rows, dtype=jnp.int32) + start
        pick = (own_places[None, :] == wanted[:, None]).astype(jnp.bfloat16)
        rows = jnp.einsum("ur,krd->kud", pick, table_low, preferred_element_type=jnp.float32)
        return rows.astype(jnp.bfloat16)

    def inside(start):
        offset = my_places - start
        return ((offset >= 0) & (offset < round_rows), offset)

    def another(carry):
        index, embedded = carry
        start = index * round_rows
        turned = lax.all_to_all(per_member(offered(start)), "cli", 0, 0, tiled=True)
        pool = lax.all_gather(turned, "grp", axis=0, tiled=True).reshape(-1, model_width)
        here, offset = inside(start)
        found = jnp.take(pool, jnp.where(here, my_owner * round_rows + offset, 0), axis=0)
        return (index + 1, jnp.where(here[:, None], found.astype(jnp.float32), embedded))

    slabs = jnp.concatenate([stack.astype(jnp.bfloat16), offered(0)], axis=1)
    pool = spread(per_member(slabs), groups, members, 1, False, 2)
    here, offset = inside(0)
    at = jnp.where(here, my_owner * slab + stack_part + offset, -1)
    weights, embedded = unpack(pool, stack_part, at[:, None])
    _, embedded = lax.while_loop(
        lambda carry: carry[0] < rounds, another, (jnp.int32(1), embedded)
    )
    vector_one = lax.dynamic_index_in_dim(vectors, model_own, 0, keepdims=False)
    inputs = embedded + jnp.tile(weights[12 * model_width :].astype(jnp.float32), (local, 1))
    saved = layer_forward(weights, vector_one, inputs, my_segments)
    normed_out = saved[11]

    target_local = targets - device_index * block_rows
    target_local = jnp.where((target_local >= 0) & (target_local < block_rows), target_local, -1)
    target_blocks = target_local.reshape(groups * share, 1, local * seq_len)
    if devices * normed_out.size * 2 <= POOL_BYTES:
        outs_all, stats = spread_score(
            normed_out[None], table_low, target_blocks, groups, members, share, 2
        )
    else:
        outs_all = spread(normed_out[None], groups, members, 2, True, 2)
        stats = head_stats(outs_all, table_low, target_blocks, groups, members, share)
    shares = lax.all_to_all(stats, both, 0, 0, tiled=True)
    log_total = jax.nn.logsumexp(shares[:, 0], axis=0)
    token_loss = log_total - jnp.sum(shares[:, 1], axis=0)
    everything = share_all(jnp.stack([log_total, token_loss]), both, devices)
    everything = (
        everything.reshape(groups, models, share, 2, local, seq_len)
        .transpose(3, 1, 0, 2, 4, 5)
        .reshape(2, models, devices, seq_len)
    )
    all_losses = jnp.sum(everything[1] * valid[None], axis=2)
    loss = jnp.sum(choice_table.T * all_losses / total_of[None, :])
    client_losses = lax.dynamic_slice(
        (all_losses / counts[None, :]).T, (device_index, 0), (1, models)
    )
    chosen_total = jnp.sum(choice_table.T[:, :, None] * everything[0], axis=0)

    numbers = jnp.sum(choice_table, axis=0)
    padded = 2.0 * jnp.ceil(numbers / 2.0)
    offsets = jnp.cumsum(padded) - padded
    earlier = (
        jnp.arange(devices)[None, :] < jnp.arange(devices)[:, None]
    ) & (choices[None, :] == choices[:, None])
    slot_of = jnp.sum(choice_table * offsets[None, :], axis=1) + jnp.sum(
        earlier.astype(jnp.float32), axis=1
    )
    slots = devices + models
    steps = slots // 2
    at_slot = jnp.arange(slots)[:, None] == slot_of.astype(jnp.int32)[None, :]
    filled = jnp.any(at_slot, axis=1)
    client_at = jnp.sum(jnp.where(at_slot, jnp.arange(devices)[None, :], 0), axis=1).astype(
        jnp.int32
    )
    step_start = 2.0 * jnp.arange(steps)
    model_of = (
        jnp.sum((step_start[:, None] >= offsets[None, :]).astype(jnp.int32), axis=1) - 1
    ).astype(jnp.int32)
    fresh = jnp.concatenate(
        [jnp.ones((1,), jnp.int32), (model_of[1:] != model_of[:-1]).astype(jnp.int32)]
    )
    within = client_at % members
    piece_at = (
        (client_at // members * members + jnp.repeat(model_of, 2) * share + within // local) * local
        + within % local
    ).astype(jnp.int32)
    weight_rows = valid / total_of[:, None]
    slot_log = jnp.where(filled[:, None], jnp.take(chosen_total, client_at, axis=0), 1e30)
    slot_weight = jnp.where(filled[:, None], jnp.take(weight_rows, client_at, axis=0), 0.0)
    slot_info = jnp.stack(
        [slot_log.reshape(steps, 2 * seq_len), slot_weight.reshape(steps, 2 * seq_len)], axis=1
    )
    slot_target = jnp.where(filled[:, None], jnp.take(target_local, client_at, axis=0), -1)
    spare = devices + jnp.cumsum(1 - filled.astype(jnp.int32)) - 1
    d_outs, head_grad = head_back(
        outs_all.reshape(-1, seq_len, model_width),
        table_low,
        model_of,
        fresh,
        piece_at[0::2],
        piece_at[1::2],
        jnp.where(filled, client_at, spare).astype(jnp.int32),
        slot_info,
        slot_target.reshape(steps, 1, 2 * seq_len),
    )
    d_group = collect(d_outs, groups, members, 4)
    d_mine = lax.dynamic_slice(
        d_group, (part_own * local, 0, 0), (local, seq_len, model_width)
    ).astype(jnp.float32)
    d_final = jnp.where((my_choices == model_own)[:, None, None], d_mine, 0.0).reshape(
        local * seq_len, model_width
    )
    stack_rows, vector_rows, d_inputs = layer_backward(
        weights, vector_one, inputs, my_segments, saved, d_final
    )
    d_wide = d_inputs.astype(jnp.bfloat16)
    if share > 1:
        d_wide = lax.dynamic_update_slice(
            jnp.zeros((members * seq_len, model_width), jnp.bfloat16),
            d_wide,
            (part_own * local * seq_len, 0),
        )
    d_turned = lax.all_to_all(
        d_wide.reshape(members, seq_len, model_width), "cli", 0, 0, tiled=True
    )
    d_client = jnp.sum(d_turned.astype(jnp.float32), axis=0, keepdims=True).astype(jnp.bfloat16)
    vector_piece = vector_rows.size // groups
    vector_part = jnp.sum(
        lax.all_to_all(vector_rows.reshape(groups, vector_piece), "grp", 0, 0, tiled=True), axis=0
    )
    vector_parts = share_all(vector_part, both, devices)
    d_client, vector_parts = lax.optimization_barrier((d_client, vector_parts))
    d_all = spread(d_client, groups, members, 3, True, 2)

    middle = model_width // 2
    stack_left = lax.psum_scatter(stack_rows[:, :middle], "grp", scatter_dimension=0, tiled=True)
    stack_right = lax.psum_scatter(stack_rows[:, middle:], "grp", scatter_dimension=0, tiled=True)
    vector_grad = jnp.sum(vector_parts.reshape(groups, models, share, vector_piece), axis=2)
    vector_grad = vector_grad.transpose(1, 0, 2).reshape(vectors.shape)

    token_local = tokens - device_index * block_rows
    token_local = jnp.where((token_local >= 0) & (token_local < block_rows), token_local, -1)
    slot_token = jnp.where(filled[:, None], jnp.take(token_local, client_at, axis=0), -1)
    pair_start = jnp.concatenate([offsets, jnp.sum(padded)[None]]) / 2.0
    schedule = (pair_start.astype(jnp.int32), client_at[0::2], client_at[1::2])
    slot_token = slot_token.reshape(steps, 1, 2 * seq_len)
    lead = models // 2

    def to_owner(rows):
        back = lax.all_to_all(
            rows.reshape(members, stack_part, rows.shape[1]), "cli", 0, 0, tiled=True
        ).astype(jnp.float32)
        return jnp.sum(back.reshape(models, share, stack_part, rows.shape[1]), axis=1)

    states = finish_table(d_all, head_grad, table, table_momentum, schedule, slot_token, 0, lead, ())
    stack_left, states = lax.optimization_barrier((stack_left, states))
    grad_left = to_owner(stack_left)
    states = finish_table(
        d_all, head_grad, table, table_momentum, schedule, slot_token, lead, models - lead, states
    )
    stack_right, states, grad_left = lax.optimization_barrier((stack_right, states, grad_left))
    table_grad, table_momentum_new, table_new = states
    stack_grad = jnp.concatenate([grad_left, to_owner(stack_right)], axis=2)
    stack_momentum_new, stack_new = update(stack, stack_momentum, stack_grad, stack_rate)
    vector_momentum_new, vector_new = update(vectors, vector_momentum, vector_grad, vector_rate)
    return (
        loss,
        client_losses,
        table_grad,
        table_momentum_new,
        table_new,
        stack_grad,
        stack_momentum_new,
        stack_new,
        vector_grad,
        vector_momentum_new,
        vector_new,
    )


def solution(mesh):
    rows = P(("grp", "cli"), None)
    parts = P(None, ("grp", "cli"), None)
    return jax.shard_map(
        body,
        mesh=mesh,
        in_specs=(rows, rows, rows, P(("grp", "cli")), parts, parts, parts, parts, P(), P()),
        out_specs=(P(), rows, parts, parts, parts, parts, parts, parts, P(), P(), P()),
        check_vma=False,
    )
```

```python
import functools
import math

import jax
import jax.numpy as jnp
from jax import lax
from jax.experimental import pallas as pl
from jax.experimental.pallas import tpu as pltpu
from jax.sharding import PartitionSpec as P

HEADS = 12
HEAD_DIM = 64


epsilon = 1e-05
momentum_decay = 0.9
table_rate = 4.0
stack_rate = 4.0
vector_rate = 50.0

ROUND_ROWS = 104
SLAB_STEP = 16
TILE = 400
LANES = 128
MIB = 1 << 20
POOL_BYTES = 32 * MIB
MESH = pl.DeviceIdType.MESH


def layer_norm(inputs, gain_row, shift_row):
    centred = inputs - jnp.mean(inputs, -1, keepdims=True)
    spread = jnp.mean(centred * centred, -1, keepdims=True)
    return centred * lax.rsqrt(spread + epsilon) * gain_row + shift_row


def project(inputs, matrix):
    return lax.dot_general(
        inputs, matrix, (((1,), (1,)), ((), ())), preferred_element_type=jnp.float32
    )


def product(inputs, matrix):
    return jnp.dot(inputs, matrix, preferred_element_type=jnp.float32)


def outer_rows(left, right):
    return lax.dot_general(
        left, right, (((0,), (0,)), ((), ())), preferred_element_type=jnp.float32
    )


def split_heads(rows, seq_len):
    return rows.reshape(-1, seq_len, HEADS, HEAD_DIM)


def attend(queries, key_rows, segment_rows):
    seq_len = segment_rows.shape[1]
    scores = jnp.einsum(
        "nqhd,nkhd->nhqk",
        split_heads(queries, seq_len),
        split_heads(key_rows, seq_len),
        preferred_element_type=jnp.float32,
    ) * HEAD_DIM ** (-0.5)
    positions = jnp.arange(seq_len)
    allowed = (positions[None, None, :] <= positions[None, :, None]) & (
        segment_rows[:, None, :] == segment_rows[:, :, None]
    )
    return jax.nn.softmax(jnp.where(allowed[:, None], scores, -1e30), axis=-1)


def layer_forward(weights, vector_one, inputs, segment_rows):
    row_count, model_width = inputs.shape
    seq_len = segment_rows.shape[1]
    normed = layer_norm(inputs, vector_one[0], vector_one[1]).astype(jnp.bfloat16)
    queries = (project(normed, weights[0:model_width]) + vector_one[6]).astype(jnp.bfloat16)
    key_rows = project(normed, weights[model_width : 2 * model_width]).astype(jnp.bfloat16)
    values = (project(normed, weights[2 * model_width : 3 * model_width]) + vector_one[7]).astype(
        jnp.bfloat16
    )
    attention = attend(queries, key_rows, segment_rows)
    mixture = jnp.einsum(
        "nhqk,nkhd->nqhd",
        attention.astype(jnp.bfloat16),
        split_heads(values, seq_len),
        preferred_element_type=jnp.float32,
    )
    mixture = mixture.reshape(row_count, model_width).astype(jnp.bfloat16)
    middle = inputs + (project(mixture, weights[3 * model_width : 4 * model_width]) + vector_one[8])
    normed_two = layer_norm(middle, vector_one[2], vector_one[3]).astype(jnp.bfloat16)
    hidden = project(normed_two, weights[4 * model_width : 8 * model_width]) + vector_one[
        10:14
    ].reshape(-1)
    active = jax.nn.gelu(hidden, approximate=True).astype(jnp.bfloat16)
    residual = middle + (
        product(active, weights[8 * model_width : 12 * model_width]) + vector_one[9]
    )
    normed_out = layer_norm(residual, vector_one[4], vector_one[5]).astype(jnp.bfloat16)
    return (
        normed,
        queries,
        key_rows,
        values,
        attention,
        mixture,
        middle,
        normed_two,
        hidden,
        active,
        residual,
        normed_out,
    )


def norm_grad(operand, gain_row, shift_row, cotangent):
    outcome, pullback = jax.vjp(layer_norm, operand, gain_row, shift_row)
    return pullback(cotangent)


def gelu_tanh(hidden):
    return jax.nn.gelu(hidden, approximate=True)


def layer_backward(weights, vector_one, inputs, segment_rows, saved, grad_out):
    row_count, model_width = inputs.shape
    seq_len = segment_rows.shape[1]
    scaling = HEAD_DIM ** (-0.5)
    (
        normed,
        queries,
        key_rows,
        values,
        attention,
        mixture,
        middle,
        normed_two,
        hidden,
        active,
        residual,
        normed_out,
    ) = saved
    d_residual, d_gain_out, d_shift_out = norm_grad(
        residual, vector_one[4], vector_one[5], grad_out
    )
    d_outer = d_residual.astype(jnp.bfloat16)
    d_bias_out = jnp.sum(d_outer.astype(jnp.float32), 0)
    d_active = project(d_outer, weights[8 * model_width : 12 * model_width])
    gelu_value, gelu_pull = jax.vjp(gelu_tanh, hidden)
    d_hidden = gelu_pull(d_active)[0].astype(jnp.bfloat16)
    d_bias_hidden = jnp.sum(d_hidden.astype(jnp.float32), 0)
    d_normed_two = product(d_hidden, weights[4 * model_width : 8 * model_width])
    d_middle_norm, d_gain_two, d_shift_two = norm_grad(
        middle, vector_one[2], vector_one[3], d_normed_two
    )
    d_middle = d_residual + d_middle_norm
    d_branch = d_middle.astype(jnp.bfloat16)
    d_bias_branch = jnp.sum(d_branch.astype(jnp.float32), 0)
    d_mixture = split_heads(
        product(d_branch, weights[3 * model_width : 4 * model_width]).astype(jnp.bfloat16), seq_len
    )
    d_attention = jnp.einsum(
        "nqhd,nkhd->nhqk", d_mixture, split_heads(values, seq_len), preferred_element_type=jnp.float32
    )
    d_values = jnp.einsum(
        "nhqk,nqhd->nkhd",
        attention.astype(jnp.bfloat16),
        d_mixture,
        preferred_element_type=jnp.float32,
    )
    d_values = d_values.reshape(row_count, model_width).astype(jnp.bfloat16)
    d_scores = (
        attention * (d_attention - jnp.sum(attention * d_attention, -1, keepdims=True))
    ).astype(jnp.bfloat16)
    d_queries = (
        jnp.einsum(
            "nhqk,nkhd->nqhd",
            d_scores,
            split_heads(key_rows, seq_len),
            preferred_element_type=jnp.float32,
        )
        * scaling
    )
    d_queries = d_queries.reshape(row_count, model_width).astype(jnp.bfloat16)
    d_keys = (
        jnp.einsum(
            "nhqk,nqhd->nkhd",
            d_scores,
            split_heads(queries, seq_len),
            preferred_element_type=jnp.float32,
        )
        * scaling
    )
    d_keys = d_keys.reshape(row_count, model_width).astype(jnp.bfloat16)
    d_joined = jnp.concatenate([d_queries, d_keys, d_values], axis=1)
    d_normed = product(d_joined, weights[0 : 3 * model_width])
    d_inputs_norm, d_gain_one, d_shift_one = norm_grad(
        inputs, vector_one[0], vector_one[1], d_normed
    )
    d_inputs = d_middle + d_inputs_norm
    grad_places = jnp.sum(d_inputs.reshape(-1, seq_len, model_width), axis=0)
    pairs = (
        (d_joined, normed),
        (d_branch, mixture),
        (d_hidden, normed_two),
        (active, d_outer),
    )
    half = model_width // 2
    stack_halves = [
        jnp.concatenate(
            [outer_rows(left, right[:, cut]).astype(jnp.bfloat16) for left, right in pairs]
            + [grad_places[:, cut].astype(jnp.bfloat16)],
            axis=0,
        )
        for cut in (slice(0, half), slice(half, model_width))
    ]
    bias_query = jnp.sum(d_queries.astype(jnp.float32), 0)
    bias_value = jnp.sum(d_values.astype(jnp.float32), 0)
    vector_rows = jnp.concatenate(
        [
            jnp.stack(
                [
                    d_gain_one,
                    d_shift_one,
                    d_gain_two,
                    d_shift_two,
                    d_gain_out,
                    d_shift_out,
                    bias_query,
                    bias_value,
                    d_bias_branch,
                    d_bias_out,
                ]
            ),
            d_bias_hidden.reshape(4, model_width),
        ],
        axis=0,
    )
    return (stack_halves, vector_rows, d_inputs)


def share_all(rows, axes, size):
    return lax.all_to_all(
        jnp.broadcast_to(rows[None], (size,) + rows.shape), axes, 0, 0, tiled=True
    )


def update(weight, momentum, gradient, step_rate):
    renewed = momentum_decay * momentum + gradient
    return (renewed, weight - step_rate * (gradient + momentum_decay * renewed))


def flipped(value, offset, size):
    bit = 1
    while bit < size:
        digit = lax.rem(lax.div(offset, bit), 2)
        value = value + digit * bit * (1 - 2 * lax.rem(lax.div(value, bit), 2))
        bit *= 2
    return value


class Place:
    def __init__(self, groups, members):
        self.groups, self.members = groups, members
        self.ys = 2
        self.xs = groups // 4
        self.grp = lax.axis_index("grp")
        self.cli = lax.axis_index("cli")
        self.core = lax.rem(self.grp, 2)
        self.x = lax.rem(lax.div(self.grp, 2), self.xs)
        self.y = lax.div(self.grp, 2 * self.xs)

    def group(self, jx=0, jy=0, jc=0):
        x = flipped(self.x, jx, self.xs)
        y = flipped(self.y, jy, self.ys)
        core = self.core + jc * (1 - 2 * self.core)
        return (y * self.xs + x) * 2 + core

    def block(self, jx, jy, level, jc=0):
        return self.group(jx, jy, jc) * self.members + level

    def peer(self, jx=0, jy=0, jc=0):
        return (self.group(jx, jy, jc), self.cli)

    def level(self, level):
        return (self.grp, level)

    def nearest(self, i):
        z, last = self.cli, self.members - 1
        low = jnp.where(2 * z < last, 1, 0)
        sign = 2 * low - 1
        margin = low * z + (1 - low) * (last - z)
        step = lax.div(i + 1, 2)
        odd = lax.rem(i, 2)
        near = z + sign * step * (2 * odd - 1)
        far = z + sign * (i - margin)
        return jnp.where(i <= 2 * margin, near, far)


def greet(place):
    barrier = pltpu.get_barrier_semaphore()
    peers = [place.peer(jx=j) for j in range(1, place.xs)] + [place.peer(jy=j) for j in range(1, place.ys)]
    peers.append(place.peer(jc=1))
    peers += [place.level(lax.rem(place.cli + j, place.members)) for j in range(1, place.members)]
    for peer in peers:
        pl.semaphore_signal(barrier, inc=1, device_id=peer, device_id_type=MESH)
    pl.semaphore_wait(barrier, len(peers))


def spread_sems(groups, members, pieces):
    xs, ys, items = groups // 4, 2, members * pieces
    dma = pltpu.SemaphoreType.DMA
    shapes = [(items,)] * 3 + [(items, xs)] * 2 + [(items, ys)] * 2 + [(items, xs, ys)] * 6
    return [dma] + [dma(shape) for shape in shapes]


def spread_body(place, chain, pieces, src, out, sems, consume, ready=None):
    (own_sem, z_up, z_down, z_recv, x_send, x_recv, y_send, y_recv, k_send, k_recv, p_send, p_recv,
     c_send, c_recv) = sems
    xs, ys, members = place.xs, place.ys, place.members
    items = members * pieces
    size = out.shape[1] // pieces
    z = place.cli
    partner = z + 1 - 2 * lax.rem(z, 2)
    inner_x, inner_y = range(1, xs), range(1, ys)

    def move(source, target, send, recv, device):
        return pltpu.make_async_remote_copy(
            src_ref=source, dst_ref=target, send_sem=send, recv_sem=recv, device_id=device, device_id_type=MESH
        )

    class Item:
        def __init__(self, k):
            self.level = place.nearest(lax.div(k, pieces))
            self.piece = lax.rem(k, pieces)
            self.slot = self.level * pieces + self.piece
            self.even = lax.rem(self.piece, 2) == 0
            self.mine = lax.rem(self.level + z, 2) == 0 if chain else self.level >= 0
            self.rows = pl.ds(self.piece * size, size)

        def part(self, jx, jy, level=None):
            return out.at[place.block(jx, jy, self.level if level is None else level), self.rows]

        def here(self, own):
            return src.at[z if not chain else 0, self.rows] if own else self.part(0, 0)

        def up(self, own=False):
            return move(self.here(own), self.part(0, 0), z_up.at[self.slot], z_recv.at[self.slot], place.level(z + 1))

        def down(self, own=False):
            return move(self.here(own), self.part(0, 0), z_down.at[self.slot], z_recv.at[self.slot], place.level(z - 1))

        def straight(self):
            return move(
                src.at[self.level, self.rows], self.part(0, 0, z), z_up.at[self.slot],
                z_recv.at[z * pieces + self.piece], place.level(self.level),
            )

        def landed(self):
            part = self.part(0, 0)
            return move(part, part, z_up.at[self.slot], z_recv.at[self.slot], place.level(partner))

        def to_x(self, jx, own=False):
            return move(self.here(own), self.part(0, 0), x_send.at[self.slot, jx], x_recv.at[self.slot, jx], place.peer(jx=jx))

        def to_y(self, jy, own=False):
            return move(self.here(own), self.part(0, 0), y_send.at[self.slot, jy], y_recv.at[self.slot, jy], place.peer(jy=jy))

        def corner_a(self, jx, jy):
            part = self.part(jx, 0)
            return move(part, part, k_send.at[self.slot, jx, jy], k_recv.at[self.slot, jx, jy], place.peer(jy=jy))

        def corner_b(self, jx, jy):
            part = self.part(0, jy)
            return move(part, part, k_send.at[self.slot, jx, jy], k_recv.at[self.slot, jx, jy], place.peer(jx=jx))

        def corner_z(self, jx, jy):
            part = self.part(jx, jy)
            return move(part, part, p_send.at[self.slot, jx, jy], p_recv.at[self.slot, jx, jy], place.level(partner))

        def to_core(self, jx, jy, own=False):
            part = self.part(jx, jy)
            return move(self.here(True) if own else part, part, c_send.at[self.slot, jx, jy], c_recv.at[self.slot, jx, jy], place.peer(jc=1))

    own = pltpu.make_async_copy(src.at[z if not chain else 0], out.at[place.block(0, 0, z)], own_sem)
    own.start()
    if not chain:
        for piece in range(pieces):
            Item(pieces + piece).straight().start()

    def columns(k):
        item = Item(k)
        level = item.level

        @pl.when(k < pieces)
        def mine_first():
            if chain:
                @pl.when(z + 1 < members)
                def onward():
                    item.up(True).start()

                @pl.when(z > 0)
                def back():
                    item.down(True).start()

            for jx in inner_x:
                item.to_x(jx, True).start()
            for jy in inner_y:
                item.to_y(jy, True).start()
            item.to_core(0, 0, True).start()

        @pl.when(k >= pieces)
        def arrive():
            item.landed().wait_recv()
            if chain:
                @pl.when((level < z) & (z + 1 < members))
                def onward():
                    item.up().start()

                @pl.when((level > z) & (z > 0))
                def back():
                    item.down().start()
            else:
                @pl.when(k + pieces < items)
                def following():
                    Item(k + pieces).straight().start()

            for jx in inner_x:
                item.to_x(jx).start()
            for jy in inner_y:
                item.to_y(jy).start()
            item.to_core(0, 0).start()

    def edges(k):
        item = Item(k)
        for jx in inner_x:
            item.to_x(jx).wait_recv()

            @pl.when(item.mine & item.even)
            def pass_a():
                for jy in inner_y:
                    item.corner_a(jx, jy).start()

            item.to_core(jx, 0).start()
        for jy in inner_y:
            item.to_y(jy).wait_recv()

            @pl.when(item.mine & jnp.logical_not(item.even))
            def pass_b():
                for jx in inner_x:
                    item.corner_b(jx, jy).start()

            item.to_core(0, jy).start()

    def corners(k):
        item = Item(k)

        @pl.when(item.mine)
        def mine_now():
            for jx in inner_x:
                for jy in inner_y:
                    item.corner_a(jx, jy).wait_recv()
                    if chain:
                        item.corner_z(jx, jy).start()
                    item.to_core(jx, jy).start()

    def handed(k):
        item = Item(k)

        @pl.when(jnp.logical_not(item.mine))
        def from_partner():
            for jx in inner_x:
                for jy in inner_y:
                    item.corner_z(jx, jy).wait_recv()
                    item.to_core(jx, jy).start()

    spots = xs * ys
    lag_edge, lag_corner = (2, 4) if chain else (1, 3)
    lag_handed = pieces + 6 if chain else lag_corner
    lag_end = lag_handed + 1

    def tick(t, carry):
        @pl.when(t < items)
        def arrivals():
            columns(t)

        @pl.when((t >= lag_edge) & (t < items + lag_edge))
        def sides():
            edges(t - lag_edge)

        @pl.when((t >= lag_corner) & (t < items + lag_corner))
        def far():
            corners(t - lag_corner)

        if chain:
            @pl.when((t >= lag_handed) & (t < items + lag_handed))
            def others():
                handed(t - lag_handed)

        def visit(e, carry):
            jc = lax.div(e, spots)
            spot = lax.rem(e, spots)
            jx, jy = lax.rem(spot, xs), lax.div(spot, xs)
            far = jnp.minimum(jx, 1) + jnp.minimum(jy, 1)
            lag = jnp.where(far == 0, 1, jnp.where(far == 1, lag_edge + 1, lag_end))
            k = t - lag

            @pl.when((k >= 0) & (k < items))
            def valid():
                item = Item(k)

                @pl.when(jc == 1)
                def shared():
                    item.to_core(jx, jy).wait_recv()

                if consume is not None:
                    consume(place.block(jx, jy, item.level, jc), item.level, item.piece)

            return carry

        return lax.fori_loop(0, 2 * spots, visit, carry)

    if ready is not None:
        own.wait()
        ready()
    lax.fori_loop(0, items + lag_end, tick, 0)

    def close(k, carry):
        item = Item(k)
        level = item.level
        if chain:
            @pl.when((level <= z) & (z + 1 < members))
            def onward():
                item.up().wait_send()

            @pl.when((level >= z) & (z > 0))
            def back():
                item.down().wait_send()
        else:
            @pl.when(k >= pieces)
            def sent():
                item.straight().wait_send()

        for jx in inner_x:
            item.to_x(jx).wait_send()
        for jy in inner_y:
            item.to_y(jy).wait_send()
        for jx in range(xs):
            for jy in range(ys):
                item.to_core(jx, jy).wait_send()

        @pl.when(item.mine)
        def mine_done():
            for jx in inner_x:
                for jy in inner_y:
                    item.corner_a(jx, jy).wait_send()
                    if chain:
                        item.corner_z(jx, jy).wait_send()

        return carry

    lax.fori_loop(0, items, close, 0)
    if ready is None:
        own.wait()


def spread_kernel(groups, members, chain, pieces, src, out, *sems):
    place = Place(groups, members)
    greet(place)
    spread_body(place, chain, pieces, src, out, sems, None)


def spread(src, groups, members, collective_id, chain, pieces):
    count, rows, width = src.shape
    return pl.pallas_call(
        functools.partial(spread_kernel, groups, members, chain, pieces),
        out_shape=jax.ShapeDtypeStruct((groups * members, rows, width), src.dtype),
        in_specs=[pl.BlockSpec(memory_space=pl.ANY)],
        out_specs=pl.BlockSpec(memory_space=pl.ANY),
        scratch_shapes=spread_sems(groups, members, pieces),
        compiler_params=pltpu.CompilerParams(collective_id=collective_id, has_side_effects=True),
        cost_estimate=pl.CostEstimate(
            flops=0, bytes_accessed=4 * groups * members * rows * width, transcendentals=0
        ),
    )(src)


def tile_of(part_rows):
    return TILE if part_rows % TILE == 0 else part_rows


def opening_kernel(groups, members, facts_ref, table_ref, facts_out, low_ref, own_sem, send_sems, recv_sems):
    devices = groups * members
    tiles = pl.num_programs(1)
    step = pl.program_id(0) * tiles + pl.program_id(1)
    last = pl.num_programs(0) * tiles - 1
    me = lax.axis_index("grp") * members + lax.axis_index("cli")

    def other(j):
        return lax.rem(me + j, devices)

    def place(device):
        return (lax.div(device, members), lax.rem(device, members))

    def give(j):
        return pltpu.make_async_remote_copy(
            src_ref=facts_ref, dst_ref=facts_out.at[me], send_sem=send_sems.at[j], recv_sem=recv_sems.at[j],
            device_id=place(other(j)), device_id_type=MESH,
        )

    own = pltpu.make_async_copy(facts_ref, facts_out.at[me], own_sem)

    @pl.when(step == 0)
    def begin():
        barrier = pltpu.get_barrier_semaphore()

        def hello(j, carry):
            pl.semaphore_signal(barrier, inc=1, device_id=place(other(j)), device_id_type=MESH)
            return carry

        def start(j, carry):
            give(j).start()
            return carry

        own.start()
        lax.fori_loop(1, devices, hello, 0)
        pl.semaphore_wait(barrier, devices - 1)
        lax.fori_loop(1, devices, start, 0)

    low_ref[...] = table_ref[...].astype(low_ref.dtype)

    @pl.when(step == last)
    def end():
        def finish(j, carry):
            give(j).wait_send()
            pltpu.make_async_remote_copy(
                src_ref=facts_ref, dst_ref=facts_out.at[lax.rem(me + devices - j, devices)],
                send_sem=send_sems.at[j], recv_sem=recv_sems.at[j], device_id=place(other(j)), device_id_type=MESH,
            ).wait_recv()
            return carry

        lax.fori_loop(1, devices, finish, 0)
        own.wait()


def opening(facts, table, groups, members, collective_id):
    devices = groups * members
    models, part_rows, width = table.shape
    tile_rows = tile_of(part_rows)
    piece = pl.BlockSpec((1, tile_rows, width), lambda m, t: (m, t, 0))
    anywhere = pl.BlockSpec(memory_space=pl.ANY)
    dma = pltpu.SemaphoreType.DMA
    return pl.pallas_call(
        functools.partial(opening_kernel, groups, members),
        out_shape=(
            jax.ShapeDtypeStruct((devices,) + facts.shape, facts.dtype),
            jax.ShapeDtypeStruct(table.shape, jnp.bfloat16),
        ),
        grid=(models, part_rows // tile_rows),
        in_specs=[anywhere, piece],
        out_specs=(anywhere, piece),
        scratch_shapes=[dma, dma((devices,)), dma((devices,))],
        compiler_params=pltpu.CompilerParams(collective_id=collective_id, has_side_effects=True),
        cost_estimate=pl.CostEstimate(flops=0, bytes_accessed=6 * table.size, transcendentals=0),
    )(facts, table)


def score_kernel(groups, members, share, pieces, src, table, target, out, stat, *rest):
    part, pool, part_sem, out_sems = rest[:4]
    sems = rest[4:]
    place = Place(groups, members)
    load_table = pltpu.make_async_copy(table, part, part_sem)
    load_table.start()
    greet(place)
    rows = pool.shape[1]
    size = rows // pieces

    def keep(block, piece):
        here = pl.ds(pl.multiple_of(piece * size, size), size)
        return pltpu.make_async_copy(pool.at[block, here], out.at[block, here], out_sems.at[block, piece])

    def consume(block, level, piece):
        keep(block, piece).start()
        here = pl.ds(pl.multiple_of(piece * size, size), size)
        model = lax.div(level, share)
        wanted = target[lax.div(block, members) * share + lax.rem(level, share), :, here]
        outs = pool[block, here]
        part_rows = part.shape[1]
        tile = tile_of(part_rows)
        marks = lax.broadcasted_iota(jnp.int32, (tile, size), 0)
        tops, totals, hits = [], [], []
        for first in range(0, part_rows, tile):
            logits = project(part[model, pl.ds(first, tile)], outs)
            hit = jnp.where(marks == wanted - first, logits, 0.0).reshape(-1, 8, size)
            hits.append(jnp.sum(hit, axis=0))
            logits = logits.reshape(-1, 8, size)
            top = jnp.max(logits, axis=0)
            tops.append(top)
            totals.append(jnp.sum(jnp.exp(logits - top[None]), axis=0))
        highest = jnp.max(functools.reduce(jnp.maximum, tops), axis=0, keepdims=True)
        total = sum(t * jnp.exp(m - highest) for t, m in zip(totals, tops))
        stat[block, 0:1, here] = highest + jnp.log(jnp.sum(total, axis=0, keepdims=True))
        stat[block, 1:2, here] = jnp.sum(sum(hits), axis=0, keepdims=True)

    spread_body(place, True, pieces, src, pool, sems, consume, load_table.wait)

    def close(block, carry):
        for piece in range(pieces):
            keep(block, piece).wait()
        return carry

    lax.fori_loop(0, groups * members, close, 0)


def spread_score(src, table_low, target_blocks, groups, members, share, collective_id, pieces=2):
    _, rows, width = src.shape
    blocks = groups * members
    return pl.pallas_call(
        functools.partial(score_kernel, groups, members, share, pieces),
        out_shape=(
            jax.ShapeDtypeStruct((blocks, rows, width), src.dtype),
            jax.ShapeDtypeStruct((blocks, 2, rows), jnp.float32),
        ),
        in_specs=[
            pl.BlockSpec(memory_space=pl.ANY),
            pl.BlockSpec(memory_space=pl.ANY),
            pl.BlockSpec(memory_space=pltpu.VMEM),
        ],
        out_specs=(pl.BlockSpec(memory_space=pl.ANY), pl.BlockSpec(memory_space=pltpu.VMEM)),
        scratch_shapes=[
            pltpu.VMEM(table_low.shape, table_low.dtype),
            pltpu.VMEM((blocks, rows, width), src.dtype),
            pltpu.SemaphoreType.DMA,
            pltpu.SemaphoreType.DMA((blocks, pieces)),
        ]
        + spread_sems(groups, members, pieces),
        compiler_params=pltpu.CompilerParams(
            collective_id=collective_id, has_side_effects=True, vmem_limit_bytes=60 * MIB
        ),
        cost_estimate=pl.CostEstimate(
            flops=2 * blocks * rows * table_low.shape[1] * width,
            bytes_accessed=2 * blocks * rows * width * 2,
            transcendentals=blocks * rows * table_low.shape[1],
        ),
    )(src, table_low, target_blocks)


def stats_kernel(outs_ref, table_ref, target_ref, stat_ref):
    logits = project(table_ref[0], outs_ref[0])
    highest = jnp.max(logits, axis=0, keepdims=True)
    total = jnp.sum(jnp.exp(logits - highest), axis=0, keepdims=True)
    rows = lax.broadcasted_iota(jnp.int32, logits.shape, 0)
    hit = jnp.sum(jnp.where(rows == target_ref[0], logits, 0.0), axis=0, keepdims=True)
    stat_ref[0, 0:1, :] = highest + jnp.log(total)
    stat_ref[0, 1:2, :] = hit


def head_stats(outs_all, table_low, target_blocks, groups, members, share):
    blocks, rows, width = outs_all.shape
    part_rows = table_low.shape[1]
    return pl.pallas_call(
        stats_kernel,
        out_shape=jax.ShapeDtypeStruct((blocks, 2, rows), jnp.float32),
        grid=(members, groups),
        in_specs=[
            pl.BlockSpec((1, rows, width), lambda z, g: (g * members + z, 0, 0)),
            pl.BlockSpec((1, part_rows, width), lambda z, g: (z // share, 0, 0)),
            pl.BlockSpec((1, 1, rows), lambda z, g: (g * share + z % share, 0, 0)),
        ],
        out_specs=pl.BlockSpec((1, 2, rows), lambda z, g: (g * members + z, 0, 0)),
        compiler_params=pltpu.CompilerParams(vmem_limit_bytes=56 * MIB),
        cost_estimate=pl.CostEstimate(
            flops=2 * blocks * rows * part_rows * width,
            bytes_accessed=2 * outs_all.size + 2 * table_low.size,
            transcendentals=blocks * rows * part_rows,
        ),
    )(outs_all, table_low, target_blocks)


def collect_kernel(groups, members, source, out, work, from_core, from_x, from_y, then_y, then_x, from_z, *sems):
    (load_sem, core_send, core_recv, x_send, x_recv, y_send, y_recv, yy_send, yy_recv, xx_send, xx_recv, z_send,
     z_recv, g_send, g_recv) = sems
    place = Place(groups, members)
    greet(place)
    xs, ys = place.xs, place.ys
    half = members // 2
    z = place.cli
    order = sorted(
        ((jx, jy) for jx in range(xs) for jy in range(ys)), key=lambda spot: -(spot[0] > 0) - (spot[1] > 0)
    )
    started = []

    def send(source_ref, target_ref, send_sem, recv_sem, device):
        copy = pltpu.make_async_remote_copy(
            src_ref=source_ref, dst_ref=target_ref, send_sem=send_sem, recv_sem=recv_sem, device_id=device,
            device_id_type=MESH,
        )
        copy.start()
        started.append(copy)

    def arrival(target_ref, send_sem, recv_sem, device):
        pltpu.make_async_remote_copy(
            src_ref=target_ref, dst_ref=target_ref, send_sem=send_sem, recv_sem=recv_sem, device_id=device,
            device_id_type=MESH,
        ).wait_recv()

    def add(ref, others):
        total = ref[...].astype(jnp.float32)
        for other in others:
            total = total + other[...].astype(jnp.float32)
        ref[...] = total.astype(ref.dtype)

    def clients(p):
        return (p, p + half)

    spots = [(jy * xs + jx, jx, jy) for jx, jy in order]
    loads = {}
    for p in range(half):
        for k, jx, jy in spots:
            for c in clients(p):
                send(
                    source.at[place.group(jx, jy, 1) * members + c], from_core.at[k, c], core_send.at[k, c],
                    core_recv.at[k, c], place.peer(jc=1),
                )
                loads[k, c] = pltpu.make_async_copy(
                    source.at[place.group(jx, jy, 0) * members + c], work.at[k, c], load_sem.at[k, c]
                )
                loads[k, c].start()
    for p in range(half):
        a, b = clients(p)
        for k, jx, jy in spots:
            for c in (a, b):
                loads[k, c].wait()
                arrival(from_core.at[k, c], core_send.at[k, c], core_recv.at[k, c], place.peer(jc=1))
                add(work.at[k, c], [from_core.at[k, c]])
            if jx:
                send(work.at[k, a], from_x.at[p, jx, jy], x_send.at[p, jx, jy], x_recv.at[p, jx, jy], place.peer(jx=jx))
            if jy:
                send(work.at[k, b], from_y.at[p, jx, jy], y_send.at[p, jx, jy], y_recv.at[p, jx, jy], place.peer(jy=jy))

    def second(p):
        a, b = clients(p)
        for jy in reversed(range(ys)):
            k = jy * xs
            for jx in range(1, xs):
                arrival(from_x.at[p, jx, jy], x_send.at[p, jx, jy], x_recv.at[p, jx, jy], place.peer(jx=jx))
            add(work.at[k, a], [from_x.at[p, jx, jy] for jx in range(1, xs)])
            if jy:
                send(work.at[k, a], then_y.at[p, jy], yy_send.at[p, jy], yy_recv.at[p, jy], place.peer(jy=jy))
        for jx in reversed(range(xs)):
            for jy in range(1, ys):
                arrival(from_y.at[p, jx, jy], y_send.at[p, jx, jy], y_recv.at[p, jx, jy], place.peer(jy=jy))
            add(work.at[jx, b], [from_y.at[p, jx, jy] for jy in range(1, ys)])
            if jx:
                send(work.at[jx, b], then_x.at[p, jx], xx_send.at[p, jx], xx_recv.at[p, jx], place.peer(jx=jx))

    def third(p):
        a, b = clients(p)
        for jy in range(1, ys):
            arrival(then_y.at[p, jy], yy_send.at[p, jy], yy_recv.at[p, jy], place.peer(jy=jy))
        add(work.at[0, a], [then_y.at[p, jy] for jy in range(1, ys)])
        for jx in range(1, xs):
            arrival(then_x.at[p, jx], xx_send.at[p, jx], xx_recv.at[p, jx], place.peer(jx=jx))
        add(work.at[0, b], [then_x.at[p, jx] for jx in range(1, xs)])
        for c in (a, b):
            @pl.when(z != c)
            def give():
                pltpu.make_async_remote_copy(
                    src_ref=work.at[0, c], dst_ref=from_z.at[z], send_sem=z_send.at[c], recv_sem=z_recv.at[z],
                    device_id=place.level(c), device_id_type=MESH,
                ).start()

    for p in range(half + 1):
        if p < half:
            second(p)
        if p:
            third(p - 1)
    total = work[0, z].astype(jnp.float32)
    for j in range(1, members):
        level = lax.rem(z + members - j, members)
        arrival(from_z.at[level], z_send.at[level], z_recv.at[level], place.level(level))
        total = total + from_z[level].astype(jnp.float32)
    out[z] = total.astype(out.dtype)
    for j in range(1, members):
        send(out.at[z], out.at[z], g_send.at[j], g_recv.at[j], place.level(lax.rem(z + j, members)))
    for j in range(1, members):
        level = lax.rem(z + members - j, members)
        arrival(out.at[level], g_send.at[j], g_recv.at[j], place.level(level))
    for copy in started:
        copy.wait_send()
    for c in range(members):
        @pl.when(z != c)
        def given():
            pltpu.make_async_remote_copy(
                src_ref=work.at[0, c], dst_ref=from_z.at[z], send_sem=z_send.at[c], recv_sem=z_recv.at[z],
                device_id=place.level(c), device_id_type=MESH,
            ).wait_send()


def collect(parts, groups, members, collective_id):
    _, seq_len, width = parts.shape
    xs, ys, half = groups // 4, 2, members // 2
    dma = pltpu.SemaphoreType.DMA

    def held(*shape):
        return pltpu.VMEM(shape + (seq_len, width), parts.dtype)

    return pl.pallas_call(
        functools.partial(collect_kernel, groups, members),
        out_shape=jax.ShapeDtypeStruct((members, seq_len, width), parts.dtype),
        in_specs=[pl.BlockSpec(memory_space=pl.ANY)],
        out_specs=pl.BlockSpec(memory_space=pltpu.VMEM),
        scratch_shapes=[
            held(xs * ys, members),
            held(xs * ys, members),
            held(half, xs, ys),
            held(half, xs, ys),
            held(half, ys),
            held(half, xs),
            held(members),
        ]
        + [dma((xs * ys, members))] * 3
        + [dma((half, xs, ys))] * 4
        + [dma((half, ys))] * 2
        + [dma((half, xs))] * 2
        + [dma((members,))] * 4,
        compiler_params=pltpu.CompilerParams(
            collective_id=collective_id, has_side_effects=True, vmem_limit_bytes=56 * MIB
        ),
        cost_estimate=pl.CostEstimate(
            flops=0, bytes_accessed=4 * groups * members * seq_len * width, transcendentals=0
        ),
    )(parts)


def unpack_kernel(start, part, at_ref, pool_ref, weights_ref, rows_ref):
    step = pl.program_id(0)
    owners, slab, width = pool_ref.shape
    weights_ref[...] = jnp.concatenate([pool_ref[j, :part] for j in range(owners)], axis=0)
    columns = lax.broadcasted_iota(jnp.int32, (at_ref.shape[0], slab - start), 1) + start
    found = jnp.zeros(rows_ref.shape, jnp.float32)
    for j in range(owners):
        at = at_ref[...] - (step * owners + j) * slab
        hits = (columns == at).astype(jnp.float32).astype(jnp.bfloat16)
        found = found + product(hits, pool_ref[j, start:])

    @pl.when(step == 0)
    def begin():
        rows_ref[...] = found

    @pl.when(step > 0)
    def more():
        rows_ref[...] += found


def unpack(pool, part, at):
    devices, slab, width = pool.shape
    owners = 8 // math.gcd(part, 8)
    start = part // 16 * 16
    tokens = at.shape[0]
    return pl.pallas_call(
        functools.partial(unpack_kernel, start, part),
        out_shape=(
            jax.ShapeDtypeStruct((devices * part, width), pool.dtype),
            jax.ShapeDtypeStruct((tokens, width), jnp.float32),
        ),
        grid=(devices // owners,),
        in_specs=[
            pl.BlockSpec((tokens, 1), lambda i: (0, 0)),
            pl.BlockSpec((owners, slab, width), lambda i: (i, 0, 0)),
        ],
        out_specs=(
            pl.BlockSpec((owners * part, width), lambda i: (i, 0)),
            pl.BlockSpec((tokens, width), lambda i: (0, 0)),
        ),
        compiler_params=pltpu.CompilerParams(vmem_limit_bytes=40 * MIB),
        cost_estimate=pl.CostEstimate(
            flops=2 * devices * tokens * (slab - start) * width,
            bytes_accessed=4 * pool.size,
            transcendentals=0,
        ),
    )(at, pool)


def back_kernel(
    model_ref, fresh_ref, first_ref, second_ref, place_ref, a_ref, b_ref, table_ref, info_ref, target_ref, d_outs_ref,
    grad_ref, held, sems,
):
    step = pl.program_id(0)
    steps = pl.num_programs(0)
    seq_len = a_ref.shape[1]
    slot = lax.rem(step, 2)

    def leave(which, where, half):
        return pltpu.make_async_copy(
            held.at[which, half], d_outs_ref.at[where], sems.at[which, half]
        )

    @pl.when(step >= 2)
    def reuse():
        leave(slot, 0, 0).wait()
        leave(slot, 0, 1).wait()
    outs = jnp.concatenate([a_ref[0], b_ref[0]], axis=0)
    @pl.when(fresh_ref[step] == 1)
    def start():
        grad_ref[...] = jnp.zeros_like(grad_ref)

    part_rows = table_ref.shape[1]
    size = tile_of(part_rows)
    d_outs = jnp.zeros((2 * seq_len, outs.shape[1]), jnp.float32)
    for first_row in range(0, part_rows, size):
        here = pl.ds(first_row, size)
        table_rows = table_ref[0, here]
        logits = project(table_rows, outs)
        rows = lax.broadcasted_iota(jnp.int32, logits.shape, 0) + first_row
        soft = jnp.exp(logits - info_ref[0, 0:1, :])
        soft = jnp.where(rows == target_ref[0], soft - 1.0, soft)
        d_logits = (info_ref[0, 1:2, :] * soft).astype(jnp.bfloat16)
        d_outs = d_outs + outer_rows(d_logits, table_rows)
        grad_ref[0, here] += product(d_logits, outs)
    held[slot, 0] = d_outs[:seq_len].astype(held.dtype)
    held[slot, 1] = d_outs[seq_len:].astype(held.dtype)
    leave(slot, place_ref[2 * step], 0).start()
    leave(slot, place_ref[2 * step + 1], 1).start()

    @pl.when(step == steps - 1)
    def drain():
        for which in range(2):
            leave(which, 0, 0).wait()
            leave(which, 0, 1).wait()


def head_back(outs_pieces, table_low, model_of, fresh, first, second, place, info, target):
    steps = model_of.shape[0]
    models, part_rows, width = table_low.shape
    seq_len = outs_pieces.shape[1]
    return pl.pallas_call(
        back_kernel,
        out_shape=(
            jax.ShapeDtypeStruct((2 * steps, seq_len, width), jnp.bfloat16),
            jax.ShapeDtypeStruct((models, part_rows, width), jnp.float32),
        ),
        grid_spec=pltpu.PrefetchScalarGridSpec(
            num_scalar_prefetch=5,
            grid=(steps,),
            in_specs=[
                pl.BlockSpec((1, seq_len, width), lambda s, m, f, a, b, p: (a[s], 0, 0)),
                pl.BlockSpec((1, seq_len, width), lambda s, m, f, a, b, p: (b[s], 0, 0)),
                pl.BlockSpec((1, part_rows, width), lambda s, m, f, a, b, p: (m[s], 0, 0)),
                pl.BlockSpec((1, 2, 2 * seq_len), lambda s, m, f, a, b, p: (s, 0, 0)),
                pl.BlockSpec((1, 1, 2 * seq_len), lambda s, m, f, a, b, p: (s, 0, 0)),
            ],
            out_specs=(
                pl.BlockSpec(memory_space=pl.ANY),
                pl.BlockSpec((1, part_rows, width), lambda s, m, f, a, b, p: (m[s], 0, 0)),
            ),
            scratch_shapes=[
                pltpu.VMEM((2, 2, seq_len, width), jnp.bfloat16),
                pltpu.SemaphoreType.DMA((2, 2)),
            ],
        ),
        compiler_params=pltpu.CompilerParams(vmem_limit_bytes=56 * MIB),
        cost_estimate=pl.CostEstimate(
            flops=12 * steps * seq_len * part_rows * width,
            bytes_accessed=4 * steps * seq_len * width * 2 + 6 * table_low.size,
            transcendentals=2 * steps * seq_len * part_rows,
        ),
    )(model_of, fresh, first, second, place, outs_pieces, outs_pieces, table_low, info, target)


def finish_kernel(
    first_model, start_ref, first_ref, second_ref, d_ref, ids_ref, head_ref, table_ref, momentum_ref, *rest
):
    grad_ref, momentum_new_ref, table_new_ref = rest[-3:]
    model = pl.program_id(0) + first_model
    tile_rows = grad_ref.shape[1]
    tokens = ids_ref.shape[2]
    rows = lax.broadcasted_iota(jnp.int32, (tile_rows, tokens), 0) + pl.program_id(1) * tile_rows
    grad_ref[0] = head_ref[0]

    def pair(step, carry):
        hits = (rows == ids_ref[step]).astype(jnp.float32).astype(jnp.bfloat16)
        outs = jnp.concatenate([d_ref[first_ref[step]], d_ref[second_ref[step]]], axis=0)
        grad_ref[0] += product(hits, outs)
        return carry

    lax.fori_loop(start_ref[model], start_ref[model + 1], pair, 0)
    renewed, fresh_table = update(table_ref[0], momentum_ref[0], grad_ref[0], table_rate)
    momentum_new_ref[0] = renewed
    table_new_ref[0] = fresh_table


def finish_table(d_inputs, head_grad, table, momentum, schedule, ids, first_model, count, earlier):
    models, part_rows, width = table.shape
    tile_rows = tile_of(part_rows)
    state = jax.ShapeDtypeStruct(table.shape, jnp.float32)
    piece = pl.BlockSpec((1, tile_rows, width), lambda m, t, *_: (m + first_model, t, 0))
    whole = pl.BlockSpec(memory_space=pltpu.VMEM)
    return pl.pallas_call(
        functools.partial(finish_kernel, first_model),
        out_shape=(state, state, state),
        grid_spec=pltpu.PrefetchScalarGridSpec(
            num_scalar_prefetch=3,
            grid=(count, part_rows // tile_rows),
            in_specs=[whole, whole, piece, piece, piece]
            + [pl.BlockSpec(memory_space=pl.ANY)] * len(earlier),
            out_specs=(piece, piece, piece),
        ),
        input_output_aliases={8 + i: i for i in range(len(earlier))},
        compiler_params=pltpu.CompilerParams(vmem_limit_bytes=56 * MIB),
        cost_estimate=pl.CostEstimate(
            flops=2 * d_inputs.size * part_rows * count // models,
            bytes_accessed=24 * count * part_rows * width,
            transcendentals=0,
        ),
    )(*schedule, d_inputs, ids, head_grad, table, momentum, *earlier)


def body(
    token_ids,
    target_ids,
    segment_ids,
    chosen,
    table,
    table_momentum,
    stack,
    stack_momentum,
    vectors,
    vector_momentum,
):
    both = ("grp", "cli")
    models, block_rows, model_width = table.shape
    stack_part = stack.shape[1]
    seq_len = token_ids.shape[1]
    groups = lax.axis_size("grp")
    members = lax.axis_size("cli")
    devices = groups * members
    share = members // models
    local = members // share
    device_index = lax.axis_index(both)
    group_index = lax.axis_index("grp")
    member_index = lax.axis_index("cli")
    model_own = member_index // share
    part_own = member_index % share
    model_range = jnp.arange(models, dtype=jnp.int32)

    def per_member(rows):
        return jnp.repeat(rows, share, axis=0) if share > 1 else rows

    slab = -(-(stack_part + ROUND_ROWS) // SLAB_STEP) * SLAB_STEP
    round_rows = slab - stack_part

    facts = jnp.concatenate([token_ids[0], target_ids[0], segment_ids[0], chosen])
    facts = jnp.pad(facts, (0, -facts.size % LANES))[None]
    facts, table_low = opening(facts, table, groups, members, 5)
    facts = facts[:, 0]
    tokens = facts[:, :seq_len]
    targets = facts[:, seq_len : 2 * seq_len]
    segments = facts[:, 2 * seq_len : 3 * seq_len]
    choices = facts[:, 3 * seq_len]
    valid = jnp.concatenate(
        [
            (segments[:, :-1] == segments[:, 1:]).astype(jnp.float32),
            jnp.zeros((devices, 1), jnp.float32),
        ],
        axis=1,
    )
    counts = jnp.sum(valid, axis=1)
    choice_table = (choices[:, None] == model_range[None, :]).astype(jnp.float32)
    totals = jnp.sum(choice_table * counts[:, None], axis=0)
    total_of = jnp.sum(choice_table * totals[None, :], axis=1)

    fine = 16 if block_rows % 64 else 64
    coarse = block_rows // fine
    flat_tokens = tokens.reshape(-1)
    high_hot = (
        (flat_tokens // fine)[:, None] == jnp.arange(devices * coarse, dtype=jnp.int32)[None, :]
    ).astype(jnp.bfloat16)
    low_hot = ((flat_tokens % fine)[:, None] == jnp.arange(fine, dtype=jnp.int32)[None, :]).astype(
        jnp.bfloat16
    )
    seen = (outer_rows(high_hot, low_hot) > 0).astype(jnp.float32)
    before = product(
        seen.astype(jnp.bfloat16),
        jnp.triu(jnp.ones((fine, fine), jnp.bfloat16), 1),
    )
    sums = jnp.sum(seen, axis=1).reshape(devices, coarse)
    uniques = jnp.sum(sums, axis=1)
    ahead = jnp.sum(
        jnp.where(
            jnp.arange(coarse)[None, None, :] < jnp.arange(coarse)[None, :, None],
            sums[:, None, :],
            0.0,
        ),
        axis=2,
    )
    places = before + ahead.reshape(-1, 1)
    rounds = jnp.max(jnp.ceil(uniques / round_rows)).astype(jnp.int32)
    own_places = lax.dynamic_slice(places, (device_index * coarse, 0), (coarse, fine)).reshape(-1)
    own_seen = lax.dynamic_slice(seen, (device_index * coarse, 0), (coarse, fine)).reshape(-1)
    own_places = jnp.where(own_seen > 0, own_places, -1.0).astype(jnp.int32)
    first_client = group_index * members + part_own * local
    my_tokens = lax.dynamic_slice(tokens, (first_client, 0), (local, seq_len)).reshape(-1)
    my_segments = lax.dynamic_slice(segments, (first_client, 0), (local, seq_len))
    my_choices = lax.dynamic_slice(choices, (first_client,), (local,))
    my_high = (
        (my_tokens // fine)[:, None] == jnp.arange(devices * coarse, dtype=jnp.int32)[None, :]
    ).astype(jnp.bfloat16)
    my_low = (my_tokens % fine)[:, None] == jnp.arange(fine, dtype=jnp.int32)[None, :]
    split_places = jnp.concatenate(
        [jnp.floor(places / 64.0), places - 64.0 * jnp.floor(places / 64.0)], axis=1
    ).astype(jnp.bfloat16)
    picked_places = product(my_high, split_places)
    picked_places = 64.0 * picked_places[:, :fine] + picked_places[:, fine:]
    my_places = jnp.sum(jnp.where(my_low, picked_places, 0.0), axis=1).astype(jnp.int32)
    my_owner = my_tokens // block_rows

    def offered(start):
        wanted = jnp.arange(round_rows, dtype=jnp.int32) + start
        pick = (own_places[None, :] == wanted[:, None]).astype(jnp.bfloat16)
        rows = jnp.einsum("ur,krd->kud", pick, table_low, preferred_element_type=jnp.float32)
        return rows.astype(jnp.bfloat16)

    def inside(start):
        offset = my_places - start
        return ((offset >= 0) & (offset < round_rows), offset)

    def another(carry):
        index, embedded = carry
        start = index * round_rows
        turned = lax.all_to_all(per_member(offered(start)), "cli", 0, 0, tiled=True)
        pool = lax.all_gather(turned, "grp", axis=0, tiled=True).reshape(-1, model_width)
        here, offset = inside(start)
        found = jnp.take(pool, jnp.where(here, my_owner * round_rows + offset, 0), axis=0)
        return (index + 1, jnp.where(here[:, None], found.astype(jnp.float32), embedded))

    slabs = jnp.concatenate([stack.astype(jnp.bfloat16), offered(0)], axis=1)
    pool = spread(per_member(slabs), groups, members, 1, False, 2)
    here, offset = inside(0)
    at = jnp.where(here, my_owner * slab + stack_part + offset, -1)
    weights, embedded = unpack(pool, stack_part, at[:, None])
    _, embedded = lax.while_loop(
        lambda carry: carry[0] < rounds, another, (jnp.int32(1), embedded)
    )
    vector_one = lax.dynamic_index_in_dim(vectors, model_own, 0, keepdims=False)
    inputs = embedded + jnp.tile(weights[12 * model_width :].astype(jnp.float32), (local, 1))
    saved = layer_forward(weights, vector_one, inputs, my_segments)
    normed_out = saved[11]

    target_local = targets - device_index * block_rows
    target_local = jnp.where((target_local >= 0) & (target_local < block_rows), target_local, -1)
    target_blocks = target_local.reshape(groups * share, 1, local * seq_len)
    if devices * normed_out.size * 2 <= POOL_BYTES:
        outs_all, stats = spread_score(
            normed_out[None], table_low, target_blocks, groups, members, share, 2
        )
    else:
        outs_all = spread(normed_out[None], groups, members, 2, True, 2)
        stats = head_stats(outs_all, table_low, target_blocks, groups, members, share)
    shares = lax.all_to_all(stats, both, 0, 0, tiled=True)
    log_total = jax.nn.logsumexp(shares[:, 0], axis=0)
    token_loss = log_total - jnp.sum(shares[:, 1], axis=0)
    everything = share_all(jnp.stack([log_total, token_loss]), both, devices)
    everything = (
        everything.reshape(groups, models, share, 2, local, seq_len)
        .transpose(3, 1, 0, 2, 4, 5)
        .reshape(2, models, devices, seq_len)
    )
    all_losses = jnp.sum(everything[1] * valid[None], axis=2)
    loss = jnp.sum(choice_table.T * all_losses / total_of[None, :])
    client_losses = lax.dynamic_slice(
        (all_losses / counts[None, :]).T, (device_index, 0), (1, models)
    )
    chosen_total = jnp.sum(choice_table.T[:, :, None] * everything[0], axis=0)

    numbers = jnp.sum(choice_table, axis=0)
    padded = 2.0 * jnp.ceil(numbers / 2.0)
    offsets = jnp.cumsum(padded) - padded
    earlier = (
        jnp.arange(devices)[None, :] < jnp.arange(devices)[:, None]
    ) & (choices[None, :] == choices[:, None])
    slot_of = jnp.sum(choice_table * offsets[None, :], axis=1) + jnp.sum(
        earlier.astype(jnp.float32), axis=1
    )
    slots = devices + models
    steps = slots // 2
    at_slot = jnp.arange(slots)[:, None] == slot_of.astype(jnp.int32)[None, :]
    filled = jnp.any(at_slot, axis=1)
    client_at = jnp.sum(jnp.where(at_slot, jnp.arange(devices)[None, :], 0), axis=1).astype(
        jnp.int32
    )
    step_start = 2.0 * jnp.arange(steps)
    model_of = (
        jnp.sum((step_start[:, None] >= offsets[None, :]).astype(jnp.int32), axis=1) - 1
    ).astype(jnp.int32)
    fresh = jnp.concatenate(
        [jnp.ones((1,), jnp.int32), (model_of[1:] != model_of[:-1]).astype(jnp.int32)]
    )
    within = client_at % members
    piece_at = (
        (client_at // members * members + jnp.repeat(model_of, 2) * share + within // local) * local
        + within % local
    ).astype(jnp.int32)
    weight_rows = valid / total_of[:, None]
    slot_log = jnp.where(filled[:, None], jnp.take(chosen_total, client_at, axis=0), 1e30)
    slot_weight = jnp.where(filled[:, None], jnp.take(weight_rows, client_at, axis=0), 0.0)
    slot_info = jnp.stack(
        [slot_log.reshape(steps, 2 * seq_len), slot_weight.reshape(steps, 2 * seq_len)], axis=1
    )
    slot_target = jnp.where(filled[:, None], jnp.take(target_local, client_at, axis=0), -1)
    spare = devices + jnp.cumsum(1 - filled.astype(jnp.int32)) - 1
    d_outs, head_grad = head_back(
        outs_all.reshape(-1, seq_len, model_width),
        table_low,
        model_of,
        fresh,
        piece_at[0::2],
        piece_at[1::2],
        jnp.where(filled, client_at, spare).astype(jnp.int32),
        slot_info,
        slot_target.reshape(steps, 1, 2 * seq_len),
    )
    d_group = collect(d_outs, groups, members, 4)
    d_mine = lax.dynamic_slice(
        d_group, (part_own * local, 0, 0), (local, seq_len, model_width)
    ).astype(jnp.float32)
    d_final = jnp.where((my_choices == model_own)[:, None, None], d_mine, 0.0).reshape(
        local * seq_len, model_width
    )
    stack_halves, vector_rows, d_inputs = layer_backward(
        weights, vector_one, inputs, my_segments, saved, d_final
    )
    d_wide = d_inputs.astype(jnp.bfloat16)
    if share > 1:
        d_wide = lax.dynamic_update_slice(
            jnp.zeros((members * seq_len, model_width), jnp.bfloat16),
            d_wide,
            (part_own * local * seq_len, 0),
        )
    d_turned = lax.all_to_all(
        d_wide.reshape(members, seq_len, model_width), "cli", 0, 0, tiled=True
    )
    d_client = jnp.sum(d_turned.astype(jnp.float32), axis=0, keepdims=True).astype(jnp.bfloat16)
    vector_piece = vector_rows.size // groups
    vector_part = jnp.sum(
        lax.all_to_all(vector_rows.reshape(groups, vector_piece), "grp", 0, 0, tiled=True), axis=0
    )
    d_all = spread(d_client, groups, members, 3, True, 2)
    d_all, vector_part = lax.optimization_barrier((d_all, vector_part))
    vector_parts = share_all(vector_part, both, devices)

    stack_left, stack_right = (
        lax.psum_scatter(rows, "grp", scatter_dimension=0, tiled=True) for rows in stack_halves
    )

    token_local = tokens - device_index * block_rows
    token_local = jnp.where((token_local >= 0) & (token_local < block_rows), token_local, -1)
    slot_token = jnp.where(filled[:, None], jnp.take(token_local, client_at, axis=0), -1)
    pair_start = jnp.concatenate([offsets, jnp.sum(padded)[None]]) / 2.0
    schedule = (pair_start.astype(jnp.int32), client_at[0::2], client_at[1::2])
    slot_token = slot_token.reshape(steps, 1, 2 * seq_len)
    lead = models // 2

    def to_owner(rows):
        back = lax.all_to_all(
            rows.reshape(members, stack_part, rows.shape[1]), "cli", 0, 0, tiled=True
        ).astype(jnp.float32)
        return jnp.sum(back.reshape(models, share, stack_part, rows.shape[1]), axis=1)

    states = finish_table(d_all, head_grad, table, table_momentum, schedule, slot_token, 0, lead, ())
    stack_left, states, vector_parts = lax.optimization_barrier((stack_left, states, vector_parts))
    grad_left = to_owner(stack_left)
    states = finish_table(
        d_all, head_grad, table, table_momentum, schedule, slot_token, lead, models - lead, states
    )
    stack_right, states, grad_left = lax.optimization_barrier((stack_right, states, grad_left))
    table_grad, table_momentum_new, table_new = states
    stack_grad = jnp.concatenate([grad_left, to_owner(stack_right)], axis=2)
    vector_grad = jnp.sum(vector_parts.reshape(groups, models, share, vector_piece), axis=2)
    vector_grad = vector_grad.transpose(1, 0, 2).reshape(vectors.shape)
    stack_momentum_new, stack_new = update(stack, stack_momentum, stack_grad, stack_rate)
    vector_momentum_new, vector_new = update(vectors, vector_momentum, vector_grad, vector_rate)
    return (
        loss,
        client_losses,
        table_grad,
        table_momentum_new,
        table_new,
        stack_grad,
        stack_momentum_new,
        stack_new,
        vector_grad,
        vector_momentum_new,
        vector_new,
    )


def solution(mesh):
    rows = P(("grp", "cli"), None)
    parts = P(None, ("grp", "cli"), None)
    return jax.shard_map(
        body,
        mesh=mesh,
        in_specs=(rows, rows, rows, P(("grp", "cli")), parts, parts, parts, parts, P(), P()),
        out_specs=(P(), rows, parts, parts, parts, parts, parts, parts, P(), P(), P()),
        check_vma=False,
    )
```

```python
import functools
import math

import jax
import jax.numpy as jnp
from jax import lax
from jax.experimental import pallas as pl
from jax.experimental.pallas import tpu as pltpu
from jax.sharding import PartitionSpec as P

HEADS = 12
HEAD_DIM = 64


epsilon = 1e-05
momentum_decay = 0.9
table_rate = 4.0
stack_rate = 4.0
vector_rate = 50.0

ROUND_ROWS = 104
SLAB_STEP = 16
TILE = 400
LANES = 128
MIB = 1 << 20
POOL_BYTES = 32 * MIB
MESH = pl.DeviceIdType.MESH


def layer_norm(inputs, gain_row, shift_row):
    centred = inputs - jnp.mean(inputs, -1, keepdims=True)
    spread = jnp.mean(centred * centred, -1, keepdims=True)
    return centred * lax.rsqrt(spread + epsilon) * gain_row + shift_row


def project(inputs, matrix):
    return lax.dot_general(
        inputs, matrix, (((1,), (1,)), ((), ())), preferred_element_type=jnp.float32
    )


def product(inputs, matrix):
    return jnp.dot(inputs, matrix, preferred_element_type=jnp.float32)


def outer_rows(left, right):
    return lax.dot_general(
        left, right, (((0,), (0,)), ((), ())), preferred_element_type=jnp.float32
    )


def split_heads(rows, seq_len):
    return rows.reshape(-1, seq_len, HEADS, HEAD_DIM)


def attend(queries, key_rows, segment_rows):
    seq_len = segment_rows.shape[1]
    scores = jnp.einsum(
        "nqhd,nkhd->nhqk",
        split_heads(queries, seq_len),
        split_heads(key_rows, seq_len),
        preferred_element_type=jnp.float32,
    ) * HEAD_DIM ** (-0.5)
    positions = jnp.arange(seq_len)
    allowed = (positions[None, None, :] <= positions[None, :, None]) & (
        segment_rows[:, None, :] == segment_rows[:, :, None]
    )
    return jax.nn.softmax(jnp.where(allowed[:, None], scores, -1e30), axis=-1)


def layer_forward(weights, vector_one, inputs, segment_rows):
    row_count, model_width = inputs.shape
    seq_len = segment_rows.shape[1]
    normed = layer_norm(inputs, vector_one[0], vector_one[1]).astype(jnp.bfloat16)
    queries = (project(normed, weights[0:model_width]) + vector_one[6]).astype(jnp.bfloat16)
    key_rows = project(normed, weights[model_width : 2 * model_width]).astype(jnp.bfloat16)
    values = (project(normed, weights[2 * model_width : 3 * model_width]) + vector_one[7]).astype(
        jnp.bfloat16
    )
    attention = attend(queries, key_rows, segment_rows)
    mixture = jnp.einsum(
        "nhqk,nkhd->nqhd",
        attention.astype(jnp.bfloat16),
        split_heads(values, seq_len),
        preferred_element_type=jnp.float32,
    )
    mixture = mixture.reshape(row_count, model_width).astype(jnp.bfloat16)
    middle = inputs + (project(mixture, weights[3 * model_width : 4 * model_width]) + vector_one[8])
    normed_two = layer_norm(middle, vector_one[2], vector_one[3]).astype(jnp.bfloat16)
    hidden = project(normed_two, weights[4 * model_width : 8 * model_width]) + vector_one[
        10:14
    ].reshape(-1)
    active = jax.nn.gelu(hidden, approximate=True).astype(jnp.bfloat16)
    residual = middle + (
        product(active, weights[8 * model_width : 12 * model_width]) + vector_one[9]
    )
    normed_out = layer_norm(residual, vector_one[4], vector_one[5]).astype(jnp.bfloat16)
    return (
        normed,
        queries,
        key_rows,
        values,
        attention,
        mixture,
        middle,
        normed_two,
        hidden,
        active,
        residual,
        normed_out,
    )


def norm_grad(operand, gain_row, shift_row, cotangent):
    outcome, pullback = jax.vjp(layer_norm, operand, gain_row, shift_row)
    return pullback(cotangent)


def gelu_tanh(hidden):
    return jax.nn.gelu(hidden, approximate=True)


def layer_backward(weights, vector_one, inputs, segment_rows, saved, grad_out):
    row_count, model_width = inputs.shape
    seq_len = segment_rows.shape[1]
    scaling = HEAD_DIM ** (-0.5)
    (
        normed,
        queries,
        key_rows,
        values,
        attention,
        mixture,
        middle,
        normed_two,
        hidden,
        active,
        residual,
        normed_out,
    ) = saved
    d_residual, d_gain_out, d_shift_out = norm_grad(
        residual, vector_one[4], vector_one[5], grad_out
    )
    d_outer = d_residual.astype(jnp.bfloat16)
    d_bias_out = jnp.sum(d_outer.astype(jnp.float32), 0)
    d_active = project(d_outer, weights[8 * model_width : 12 * model_width])
    gelu_value, gelu_pull = jax.vjp(gelu_tanh, hidden)
    d_hidden = gelu_pull(d_active)[0].astype(jnp.bfloat16)
    d_bias_hidden = jnp.sum(d_hidden.astype(jnp.float32), 0)
    d_normed_two = product(d_hidden, weights[4 * model_width : 8 * model_width])
    d_middle_norm, d_gain_two, d_shift_two = norm_grad(
        middle, vector_one[2], vector_one[3], d_normed_two
    )
    d_middle = d_residual + d_middle_norm
    d_branch = d_middle.astype(jnp.bfloat16)
    d_bias_branch = jnp.sum(d_branch.astype(jnp.float32), 0)
    d_mixture = split_heads(
        product(d_branch, weights[3 * model_width : 4 * model_width]).astype(jnp.bfloat16), seq_len
    )
    d_attention = jnp.einsum(
        "nqhd,nkhd->nhqk", d_mixture, split_heads(values, seq_len), preferred_element_type=jnp.float32
    )
    d_values = jnp.einsum(
        "nhqk,nqhd->nkhd",
        attention.astype(jnp.bfloat16),
        d_mixture,
        preferred_element_type=jnp.float32,
    )
    d_values = d_values.reshape(row_count, model_width).astype(jnp.bfloat16)
    d_scores = (
        attention * (d_attention - jnp.sum(attention * d_attention, -1, keepdims=True))
    ).astype(jnp.bfloat16)
    d_queries = (
        jnp.einsum(
            "nhqk,nkhd->nqhd",
            d_scores,
            split_heads(key_rows, seq_len),
            preferred_element_type=jnp.float32,
        )
        * scaling
    )
    d_queries = d_queries.reshape(row_count, model_width).astype(jnp.bfloat16)
    d_keys = (
        jnp.einsum(
            "nhqk,nqhd->nkhd",
            d_scores,
            split_heads(queries, seq_len),
            preferred_element_type=jnp.float32,
        )
        * scaling
    )
    d_keys = d_keys.reshape(row_count, model_width).astype(jnp.bfloat16)
    d_joined = jnp.concatenate([d_queries, d_keys, d_values], axis=1)
    d_normed = product(d_joined, weights[0 : 3 * model_width])
    d_inputs_norm, d_gain_one, d_shift_one = norm_grad(
        inputs, vector_one[0], vector_one[1], d_normed
    )
    d_inputs = d_middle + d_inputs_norm
    grad_places = jnp.sum(d_inputs.reshape(-1, seq_len, model_width), axis=0)
    pairs = (
        (d_joined, normed),
        (d_branch, mixture),
        (d_hidden, normed_two),
        (active, d_outer),
    )
    bias_query = jnp.sum(d_queries.astype(jnp.float32), 0)
    bias_value = jnp.sum(d_values.astype(jnp.float32), 0)
    vector_rows = jnp.concatenate(
        [
            jnp.stack(
                [
                    d_gain_one,
                    d_shift_one,
                    d_gain_two,
                    d_shift_two,
                    d_gain_out,
                    d_shift_out,
                    bias_query,
                    bias_value,
                    d_bias_branch,
                    d_bias_out,
                ]
            ),
            d_bias_hidden.reshape(4, model_width),
        ],
        axis=0,
    )
    return (pairs, grad_places, vector_rows, d_inputs)


def share_all(rows, axes, size):
    return lax.all_to_all(
        jnp.broadcast_to(rows[None], (size,) + rows.shape), axes, 0, 0, tiled=True
    )


def update(weight, momentum, gradient, step_rate):
    renewed = momentum_decay * momentum + gradient
    return (renewed, weight - step_rate * (gradient + momentum_decay * renewed))


def flipped(value, offset, size):
    bit = 1
    while bit < size:
        digit = lax.rem(lax.div(offset, bit), 2)
        value = value + digit * bit * (1 - 2 * lax.rem(lax.div(value, bit), 2))
        bit *= 2
    return value


class Place:
    def __init__(self, groups, members):
        self.groups, self.members = groups, members
        self.ys = 2
        self.xs = groups // 4
        self.grp = lax.axis_index("grp")
        self.cli = lax.axis_index("cli")
        self.core = lax.rem(self.grp, 2)
        self.x = lax.rem(lax.div(self.grp, 2), self.xs)
        self.y = lax.div(self.grp, 2 * self.xs)

    def group(self, jx=0, jy=0, jc=0):
        x = flipped(self.x, jx, self.xs)
        y = flipped(self.y, jy, self.ys)
        core = self.core + jc * (1 - 2 * self.core)
        return (y * self.xs + x) * 2 + core

    def block(self, jx, jy, level, jc=0):
        return self.group(jx, jy, jc) * self.members + level

    def peer(self, jx=0, jy=0, jc=0):
        return (self.group(jx, jy, jc), self.cli)

    def level(self, level):
        return (self.grp, level)

    def nearest(self, i):
        z, last = self.cli, self.members - 1
        low = jnp.where(2 * z < last, 1, 0)
        sign = 2 * low - 1
        margin = low * z + (1 - low) * (last - z)
        step = lax.div(i + 1, 2)
        odd = lax.rem(i, 2)
        near = z + sign * step * (2 * odd - 1)
        far = z + sign * (i - margin)
        return jnp.where(i <= 2 * margin, near, far)


def greet(place):
    barrier = pltpu.get_barrier_semaphore()
    peers = [place.peer(jx=j) for j in range(1, place.xs)] + [place.peer(jy=j) for j in range(1, place.ys)]
    peers.append(place.peer(jc=1))
    peers += [place.level(lax.rem(place.cli + j, place.members)) for j in range(1, place.members)]
    for peer in peers:
        pl.semaphore_signal(barrier, inc=1, device_id=peer, device_id_type=MESH)
    pl.semaphore_wait(barrier, len(peers))


def spread_sems(groups, members, pieces):
    xs, ys, items = groups // 4, 2, members * pieces
    dma = pltpu.SemaphoreType.DMA
    shapes = [(items,)] * 3 + [(items, xs)] * 2 + [(items, ys)] * 2 + [(items, xs, ys)] * 6
    return [dma] + [dma(shape) for shape in shapes]


def spread_body(place, chain, pieces, src, out, sems, consume, ready=None):
    (own_sem, z_up, z_down, z_recv, x_send, x_recv, y_send, y_recv, k_send, k_recv, p_send, p_recv,
     c_send, c_recv) = sems
    xs, ys, members = place.xs, place.ys, place.members
    items = members * pieces
    size = out.shape[1] // pieces
    z = place.cli
    partner = z + 1 - 2 * lax.rem(z, 2)
    inner_x, inner_y = range(1, xs), range(1, ys)

    def move(source, target, send, recv, device):
        return pltpu.make_async_remote_copy(
            src_ref=source, dst_ref=target, send_sem=send, recv_sem=recv, device_id=device, device_id_type=MESH
        )

    class Item:
        def __init__(self, k):
            self.level = place.nearest(lax.div(k, pieces))
            self.piece = lax.rem(k, pieces)
            self.slot = self.level * pieces + self.piece
            self.even = lax.rem(self.piece, 2) == 0
            self.mine = lax.rem(self.level + z, 2) == 0 if chain else self.level >= 0
            self.rows = pl.ds(self.piece * size, size)

        def part(self, jx, jy, level=None):
            return out.at[place.block(jx, jy, self.level if level is None else level), self.rows]

        def here(self, own):
            return src.at[z if not chain else 0, self.rows] if own else self.part(0, 0)

        def up(self, own=False):
            return move(self.here(own), self.part(0, 0), z_up.at[self.slot], z_recv.at[self.slot], place.level(z + 1))

        def down(self, own=False):
            return move(self.here(own), self.part(0, 0), z_down.at[self.slot], z_recv.at[self.slot], place.level(z - 1))

        def straight(self):
            return move(
                src.at[self.level, self.rows], self.part(0, 0, z), z_up.at[self.slot],
                z_recv.at[z * pieces + self.piece], place.level(self.level),
            )

        def landed(self):
            part = self.part(0, 0)
            return move(part, part, z_up.at[self.slot], z_recv.at[self.slot], place.level(partner))

        def to_x(self, jx, own=False):
            return move(self.here(own), self.part(0, 0), x_send.at[self.slot, jx], x_recv.at[self.slot, jx], place.peer(jx=jx))

        def to_y(self, jy, own=False):
            return move(self.here(own), self.part(0, 0), y_send.at[self.slot, jy], y_recv.at[self.slot, jy], place.peer(jy=jy))

        def corner_a(self, jx, jy):
            part = self.part(jx, 0)
            return move(part, part, k_send.at[self.slot, jx, jy], k_recv.at[self.slot, jx, jy], place.peer(jy=jy))

        def corner_b(self, jx, jy):
            part = self.part(0, jy)
            return move(part, part, k_send.at[self.slot, jx, jy], k_recv.at[self.slot, jx, jy], place.peer(jx=jx))

        def corner_z(self, jx, jy):
            part = self.part(jx, jy)
            return move(part, part, p_send.at[self.slot, jx, jy], p_recv.at[self.slot, jx, jy], place.level(partner))

        def to_core(self, jx, jy, own=False):
            part = self.part(jx, jy)
            return move(self.here(True) if own else part, part, c_send.at[self.slot, jx, jy], c_recv.at[self.slot, jx, jy], place.peer(jc=1))

    own = pltpu.make_async_copy(src.at[z if not chain else 0], out.at[place.block(0, 0, z)], own_sem)
    own.start()
    if not chain:
        for piece in range(pieces):
            Item(pieces + piece).straight().start()

    def columns(k):
        item = Item(k)
        level = item.level

        @pl.when(k < pieces)
        def mine_first():
            if chain:
                @pl.when(z + 1 < members)
                def onward():
                    item.up(True).start()

                @pl.when(z > 0)
                def back():
                    item.down(True).start()

            for jx in inner_x:
                item.to_x(jx, True).start()
            for jy in inner_y:
                item.to_y(jy, True).start()
            item.to_core(0, 0, True).start()

        @pl.when(k >= pieces)
        def arrive():
            item.landed().wait_recv()
            if chain:
                @pl.when((level < z) & (z + 1 < members))
                def onward():
                    item.up().start()

                @pl.when((level > z) & (z > 0))
                def back():
                    item.down().start()
            else:
                @pl.when(k + pieces < items)
                def following():
                    Item(k + pieces).straight().start()

            for jx in inner_x:
                item.to_x(jx).start()
            for jy in inner_y:
                item.to_y(jy).start()
            item.to_core(0, 0).start()

    def edges(k):
        item = Item(k)
        for jx in inner_x:
            item.to_x(jx).wait_recv()

            @pl.when(item.mine & item.even)
            def pass_a():
                for jy in inner_y:
                    item.corner_a(jx, jy).start()

            item.to_core(jx, 0).start()
        for jy in inner_y:
            item.to_y(jy).wait_recv()

            @pl.when(item.mine & jnp.logical_not(item.even))
            def pass_b():
                for jx in inner_x:
                    item.corner_b(jx, jy).start()

            item.to_core(0, jy).start()

    def corners(k):
        item = Item(k)

        @pl.when(item.mine)
        def mine_now():
            for jx in inner_x:
                for jy in inner_y:
                    item.corner_a(jx, jy).wait_recv()
                    if chain:
                        item.corner_z(jx, jy).start()
                    item.to_core(jx, jy).start()

    def handed(k):
        item = Item(k)

        @pl.when(jnp.logical_not(item.mine))
        def from_partner():
            for jx in inner_x:
                for jy in inner_y:
                    item.corner_z(jx, jy).wait_recv()
                    item.to_core(jx, jy).start()

    spots = xs * ys
    lag_edge, lag_corner = (2, 4) if chain else (1, 3)
    lag_handed = pieces + 6 if chain else lag_corner
    lag_end = lag_handed + 1

    def tick(t, carry):
        @pl.when(t < items)
        def arrivals():
            columns(t)

        @pl.when((t >= lag_edge) & (t < items + lag_edge))
        def sides():
            edges(t - lag_edge)

        @pl.when((t >= lag_corner) & (t < items + lag_corner))
        def far():
            corners(t - lag_corner)

        if chain:
            @pl.when((t >= lag_handed) & (t < items + lag_handed))
            def others():
                handed(t - lag_handed)

        def visit(e, carry):
            jc = lax.div(e, spots)
            spot = lax.rem(e, spots)
            jx, jy = lax.rem(spot, xs), lax.div(spot, xs)
            far = jnp.minimum(jx, 1) + jnp.minimum(jy, 1)
            lag = jnp.where(far == 0, 1, jnp.where(far == 1, lag_edge + 1, lag_end))
            k = t - lag

            @pl.when((k >= 0) & (k < items))
            def valid():
                item = Item(k)

                @pl.when(jc == 1)
                def shared():
                    item.to_core(jx, jy).wait_recv()

                if consume is not None:
                    consume(place.block(jx, jy, item.level, jc), item.level, item.piece)

            return carry

        return lax.fori_loop(0, 2 * spots, visit, carry)

    if ready is not None:
        own.wait()
        ready()
    lax.fori_loop(0, items + lag_end, tick, 0)

    def close(k, carry):
        item = Item(k)
        level = item.level
        if chain:
            @pl.when((level <= z) & (z + 1 < members))
            def onward():
                item.up().wait_send()

            @pl.when((level >= z) & (z > 0))
            def back():
                item.down().wait_send()
        else:
            @pl.when(k >= pieces)
            def sent():
                item.straight().wait_send()

        for jx in inner_x:
            item.to_x(jx).wait_send()
        for jy in inner_y:
            item.to_y(jy).wait_send()
        for jx in range(xs):
            for jy in range(ys):
                item.to_core(jx, jy).wait_send()

        @pl.when(item.mine)
        def mine_done():
            for jx in inner_x:
                for jy in inner_y:
                    item.corner_a(jx, jy).wait_send()
                    if chain:
                        item.corner_z(jx, jy).wait_send()

        return carry

    lax.fori_loop(0, items, close, 0)
    if ready is None:
        own.wait()


def spread_kernel(groups, members, chain, pieces, src, out, *sems):
    place = Place(groups, members)
    greet(place)
    spread_body(place, chain, pieces, src, out, sems, None)


def spread(src, groups, members, collective_id, chain, pieces):
    count, rows, width = src.shape
    return pl.pallas_call(
        functools.partial(spread_kernel, groups, members, chain, pieces),
        out_shape=jax.ShapeDtypeStruct((groups * members, rows, width), src.dtype),
        in_specs=[pl.BlockSpec(memory_space=pl.ANY)],
        out_specs=pl.BlockSpec(memory_space=pl.ANY),
        scratch_shapes=spread_sems(groups, members, pieces),
        compiler_params=pltpu.CompilerParams(collective_id=collective_id, has_side_effects=True),
        cost_estimate=pl.CostEstimate(
            flops=0, bytes_accessed=4 * groups * members * rows * width, transcendentals=0
        ),
    )(src)


def tile_of(part_rows):
    return TILE if part_rows % TILE == 0 else part_rows


def opening_kernel(groups, members, facts_ref, table_ref, facts_out, low_ref, own_sem, send_sems, recv_sems):
    devices = groups * members
    tiles = pl.num_programs(1)
    step = pl.program_id(0) * tiles + pl.program_id(1)
    last = pl.num_programs(0) * tiles - 1
    me = lax.axis_index("grp") * members + lax.axis_index("cli")

    def other(j):
        return lax.rem(me + j, devices)

    def place(device):
        return (lax.div(device, members), lax.rem(device, members))

    def give(j):
        return pltpu.make_async_remote_copy(
            src_ref=facts_ref, dst_ref=facts_out.at[me], send_sem=send_sems.at[j], recv_sem=recv_sems.at[j],
            device_id=place(other(j)), device_id_type=MESH,
        )

    own = pltpu.make_async_copy(facts_ref, facts_out.at[me], own_sem)

    @pl.when(step == 0)
    def begin():
        barrier = pltpu.get_barrier_semaphore()

        def hello(j, carry):
            pl.semaphore_signal(barrier, inc=1, device_id=place(other(j)), device_id_type=MESH)
            return carry

        own.start()
        lax.fori_loop(1, devices, hello, 0)

    @pl.when(step == last // 2)
    def exchange():
        def start(j, carry):
            give(j).start()
            return carry

        pl.semaphore_wait(pltpu.get_barrier_semaphore(), devices - 1)
        lax.fori_loop(1, devices, start, 0)

    low_ref[...] = table_ref[...].astype(low_ref.dtype)

    @pl.when(step == last)
    def end():
        def finish(j, carry):
            give(j).wait_send()
            pltpu.make_async_remote_copy(
                src_ref=facts_ref, dst_ref=facts_out.at[lax.rem(me + devices - j, devices)],
                send_sem=send_sems.at[j], recv_sem=recv_sems.at[j], device_id=place(other(j)), device_id_type=MESH,
            ).wait_recv()
            return carry

        lax.fori_loop(1, devices, finish, 0)
        own.wait()


def opening(facts, table, groups, members, collective_id):
    devices = groups * members
    models, part_rows, width = table.shape
    tile_rows = tile_of(part_rows)
    piece = pl.BlockSpec((1, tile_rows, width), lambda m, t: (m, t, 0))
    anywhere = pl.BlockSpec(memory_space=pl.ANY)
    dma = pltpu.SemaphoreType.DMA
    return pl.pallas_call(
        functools.partial(opening_kernel, groups, members),
        out_shape=(
            jax.ShapeDtypeStruct((devices,) + facts.shape, facts.dtype),
            jax.ShapeDtypeStruct(table.shape, jnp.bfloat16),
        ),
        grid=(models, part_rows // tile_rows),
        in_specs=[anywhere, piece],
        out_specs=(anywhere, piece),
        scratch_shapes=[dma, dma((devices,)), dma((devices,))],
        compiler_params=pltpu.CompilerParams(collective_id=collective_id, has_side_effects=True),
        cost_estimate=pl.CostEstimate(flops=0, bytes_accessed=6 * table.size, transcendentals=0),
    )(facts, table)


def score_kernel(groups, members, share, pieces, src, table, target, out, stat, *rest):
    part, pool, part_sem, out_sems = rest[:4]
    sems = rest[4:]
    place = Place(groups, members)
    load_table = pltpu.make_async_copy(table, part, part_sem)
    load_table.start()
    greet(place)
    rows = pool.shape[1]
    size = rows // pieces

    def keep(block, piece):
        here = pl.ds(pl.multiple_of(piece * size, size), size)
        return pltpu.make_async_copy(pool.at[block, here], out.at[block, here], out_sems.at[block, piece])

    def consume(block, level, piece):
        keep(block, piece).start()
        here = pl.ds(pl.multiple_of(piece * size, size), size)
        model = lax.div(level, share)
        wanted = target[lax.div(block, members) * share + lax.rem(level, share), :, here]
        outs = pool[block, here]
        part_rows = part.shape[1]
        tile = tile_of(part_rows)
        marks = lax.broadcasted_iota(jnp.int32, (tile, size), 0)
        tops, totals, hits = [], [], []
        for first in range(0, part_rows, tile):
            logits = project(part[model, pl.ds(first, tile)], outs)
            hit = jnp.where(marks == wanted - first, logits, 0.0).reshape(-1, 8, size)
            hits.append(jnp.sum(hit, axis=0))
            logits = logits.reshape(-1, 8, size)
            top = jnp.max(logits, axis=0)
            tops.append(top)
            totals.append(jnp.sum(jnp.exp(logits - top[None]), axis=0))
        highest = jnp.max(functools.reduce(jnp.maximum, tops), axis=0, keepdims=True)
        total = sum(t * jnp.exp(m - highest) for t, m in zip(totals, tops))
        stat[block, 0:1, here] = highest + jnp.log(jnp.sum(total, axis=0, keepdims=True))
        stat[block, 1:2, here] = jnp.sum(sum(hits), axis=0, keepdims=True)

    spread_body(place, True, pieces, src, pool, sems, consume, load_table.wait)

    def close(block, carry):
        for piece in range(pieces):
            keep(block, piece).wait()
        return carry

    lax.fori_loop(0, groups * members, close, 0)


def spread_score(src, table_low, target_blocks, groups, members, share, collective_id, pieces=2):
    _, rows, width = src.shape
    blocks = groups * members
    return pl.pallas_call(
        functools.partial(score_kernel, groups, members, share, pieces),
        out_shape=(
            jax.ShapeDtypeStruct((blocks, rows, width), src.dtype),
            jax.ShapeDtypeStruct((blocks, 2, rows), jnp.float32),
        ),
        in_specs=[
            pl.BlockSpec(memory_space=pl.ANY),
            pl.BlockSpec(memory_space=pl.ANY),
            pl.BlockSpec(memory_space=pltpu.VMEM),
        ],
        out_specs=(pl.BlockSpec(memory_space=pl.ANY), pl.BlockSpec(memory_space=pltpu.VMEM)),
        scratch_shapes=[
            pltpu.VMEM(table_low.shape, table_low.dtype),
            pltpu.VMEM((blocks, rows, width), src.dtype),
            pltpu.SemaphoreType.DMA,
            pltpu.SemaphoreType.DMA((blocks, pieces)),
        ]
        + spread_sems(groups, members, pieces),
        compiler_params=pltpu.CompilerParams(
            collective_id=collective_id, has_side_effects=True, vmem_limit_bytes=60 * MIB
        ),
        cost_estimate=pl.CostEstimate(
            flops=2 * blocks * rows * table_low.shape[1] * width,
            bytes_accessed=2 * blocks * rows * width * 2,
            transcendentals=blocks * rows * table_low.shape[1],
        ),
    )(src, table_low, target_blocks)


def stats_kernel(outs_ref, table_ref, target_ref, stat_ref):
    logits = project(table_ref[0], outs_ref[0])
    highest = jnp.max(logits, axis=0, keepdims=True)
    total = jnp.sum(jnp.exp(logits - highest), axis=0, keepdims=True)
    rows = lax.broadcasted_iota(jnp.int32, logits.shape, 0)
    hit = jnp.sum(jnp.where(rows == target_ref[0], logits, 0.0), axis=0, keepdims=True)
    stat_ref[0, 0:1, :] = highest + jnp.log(total)
    stat_ref[0, 1:2, :] = hit


def head_stats(outs_all, table_low, target_blocks, groups, members, share):
    blocks, rows, width = outs_all.shape
    part_rows = table_low.shape[1]
    return pl.pallas_call(
        stats_kernel,
        out_shape=jax.ShapeDtypeStruct((blocks, 2, rows), jnp.float32),
        grid=(members, groups),
        in_specs=[
            pl.BlockSpec((1, rows, width), lambda z, g: (g * members + z, 0, 0)),
            pl.BlockSpec((1, part_rows, width), lambda z, g: (z // share, 0, 0)),
            pl.BlockSpec((1, 1, rows), lambda z, g: (g * share + z % share, 0, 0)),
        ],
        out_specs=pl.BlockSpec((1, 2, rows), lambda z, g: (g * members + z, 0, 0)),
        compiler_params=pltpu.CompilerParams(vmem_limit_bytes=56 * MIB),
        cost_estimate=pl.CostEstimate(
            flops=2 * blocks * rows * part_rows * width,
            bytes_accessed=2 * outs_all.size + 2 * table_low.size,
            transcendentals=blocks * rows * part_rows,
        ),
    )(outs_all, table_low, target_blocks)


def collect_kernel(groups, members, source, out, work, from_core, from_x, from_y, then_y, then_x, from_z, *sems):
    (load_sem, core_send, core_recv, x_send, x_recv, y_send, y_recv, yy_send, yy_recv, xx_send, xx_recv, z_send,
     z_recv, g_send, g_recv) = sems
    place = Place(groups, members)
    greet(place)
    xs, ys = place.xs, place.ys
    half = members // 2
    z = place.cli
    order = sorted(
        ((jx, jy) for jx in range(xs) for jy in range(ys)), key=lambda spot: -(spot[0] > 0) - (spot[1] > 0)
    )
    started = []

    def send(source_ref, target_ref, send_sem, recv_sem, device):
        copy = pltpu.make_async_remote_copy(
            src_ref=source_ref, dst_ref=target_ref, send_sem=send_sem, recv_sem=recv_sem, device_id=device,
            device_id_type=MESH,
        )
        copy.start()
        started.append(copy)

    def arrival(target_ref, send_sem, recv_sem, device):
        pltpu.make_async_remote_copy(
            src_ref=target_ref, dst_ref=target_ref, send_sem=send_sem, recv_sem=recv_sem, device_id=device,
            device_id_type=MESH,
        ).wait_recv()

    def add(ref, others):
        total = ref[...].astype(jnp.float32)
        for other in others:
            total = total + other[...].astype(jnp.float32)
        ref[...] = total.astype(ref.dtype)

    def clients(p):
        return (p, p + half)

    spots = [(jy * xs + jx, jx, jy) for jx, jy in order]
    loads = {}
    for p in range(half):
        for k, jx, jy in spots:
            for c in clients(p):
                send(
                    source.at[place.group(jx, jy, 1) * members + c], from_core.at[k, c], core_send.at[k, c],
                    core_recv.at[k, c], place.peer(jc=1),
                )
                loads[k, c] = pltpu.make_async_copy(
                    source.at[place.group(jx, jy, 0) * members + c], work.at[k, c], load_sem.at[k, c]
                )
                loads[k, c].start()
    for p in range(half):
        a, b = clients(p)
        for k, jx, jy in spots:
            for c in (a, b):
                loads[k, c].wait()
                arrival(from_core.at[k, c], core_send.at[k, c], core_recv.at[k, c], place.peer(jc=1))
                add(work.at[k, c], [from_core.at[k, c]])
            if jx:
                send(work.at[k, a], from_x.at[p, jx, jy], x_send.at[p, jx, jy], x_recv.at[p, jx, jy], place.peer(jx=jx))
            if jy:
                send(work.at[k, b], from_y.at[p, jx, jy], y_send.at[p, jx, jy], y_recv.at[p, jx, jy], place.peer(jy=jy))

    def second(p):
        a, b = clients(p)
        for jy in reversed(range(ys)):
            k = jy * xs
            for jx in range(1, xs):
                arrival(from_x.at[p, jx, jy], x_send.at[p, jx, jy], x_recv.at[p, jx, jy], place.peer(jx=jx))
            add(work.at[k, a], [from_x.at[p, jx, jy] for jx in range(1, xs)])
            if jy:
                send(work.at[k, a], then_y.at[p, jy], yy_send.at[p, jy], yy_recv.at[p, jy], place.peer(jy=jy))
        for jx in reversed(range(xs)):
            for jy in range(1, ys):
                arrival(from_y.at[p, jx, jy], y_send.at[p, jx, jy], y_recv.at[p, jx, jy], place.peer(jy=jy))
            add(work.at[jx, b], [from_y.at[p, jx, jy] for jy in range(1, ys)])
            if jx:
                send(work.at[jx, b], then_x.at[p, jx], xx_send.at[p, jx], xx_recv.at[p, jx], place.peer(jx=jx))

    def third(p):
        a, b = clients(p)
        for jy in range(1, ys):
            arrival(then_y.at[p, jy], yy_send.at[p, jy], yy_recv.at[p, jy], place.peer(jy=jy))
        add(work.at[0, a], [then_y.at[p, jy] for jy in range(1, ys)])
        for jx in range(1, xs):
            arrival(then_x.at[p, jx], xx_send.at[p, jx], xx_recv.at[p, jx], place.peer(jx=jx))
        add(work.at[0, b], [then_x.at[p, jx] for jx in range(1, xs)])
        for c in (a, b):
            @pl.when(z != c)
            def give():
                pltpu.make_async_remote_copy(
                    src_ref=work.at[0, c], dst_ref=from_z.at[z], send_sem=z_send.at[c], recv_sem=z_recv.at[z],
                    device_id=place.level(c), device_id_type=MESH,
                ).start()

    for p in range(half + 1):
        if p < half:
            second(p)
        if p:
            third(p - 1)
    total = work[0, z].astype(jnp.float32)
    for j in range(1, members):
        level = lax.rem(z + members - j, members)
        arrival(from_z.at[level], z_send.at[level], z_recv.at[level], place.level(level))
        total = total + from_z[level].astype(jnp.float32)
    out[z] = total.astype(out.dtype)
    for j in range(1, members):
        send(out.at[z], out.at[z], g_send.at[j], g_recv.at[j], place.level(lax.rem(z + j, members)))
    for j in range(1, members):
        level = lax.rem(z + members - j, members)
        arrival(out.at[level], g_send.at[j], g_recv.at[j], place.level(level))
    for copy in started:
        copy.wait_send()
    for c in range(members):
        @pl.when(z != c)
        def given():
            pltpu.make_async_remote_copy(
                src_ref=work.at[0, c], dst_ref=from_z.at[z], send_sem=z_send.at[c], recv_sem=z_recv.at[z],
                device_id=place.level(c), device_id_type=MESH,
            ).wait_send()


def collect(parts, groups, members, collective_id):
    _, seq_len, width = parts.shape
    xs, ys, half = groups // 4, 2, members // 2
    dma = pltpu.SemaphoreType.DMA

    def held(*shape):
        return pltpu.VMEM(shape + (seq_len, width), parts.dtype)

    return pl.pallas_call(
        functools.partial(collect_kernel, groups, members),
        out_shape=jax.ShapeDtypeStruct((members, seq_len, width), parts.dtype),
        in_specs=[pl.BlockSpec(memory_space=pl.ANY)],
        out_specs=pl.BlockSpec(memory_space=pltpu.VMEM),
        scratch_shapes=[
            held(xs * ys, members),
            held(xs * ys, members),
            held(half, xs, ys),
            held(half, xs, ys),
            held(half, ys),
            held(half, xs),
            held(members),
        ]
        + [dma((xs * ys, members))] * 3
        + [dma((half, xs, ys))] * 4
        + [dma((half, ys))] * 2
        + [dma((half, xs))] * 2
        + [dma((members,))] * 4,
        compiler_params=pltpu.CompilerParams(
            collective_id=collective_id, has_side_effects=True, vmem_limit_bytes=56 * MIB
        ),
        cost_estimate=pl.CostEstimate(
            flops=0, bytes_accessed=4 * groups * members * seq_len * width, transcendentals=0
        ),
    )(parts)


def unpack_kernel(start, part, at_ref, pool_ref, weights_ref, rows_ref):
    step = pl.program_id(0)
    owners, slab, width = pool_ref.shape
    weights_ref[...] = jnp.concatenate([pool_ref[j, :part] for j in range(owners)], axis=0)
    columns = lax.broadcasted_iota(jnp.int32, (at_ref.shape[0], slab - start), 1) + start
    found = jnp.zeros(rows_ref.shape, jnp.float32)
    for j in range(owners):
        at = at_ref[...] - (step * owners + j) * slab
        hits = (columns == at).astype(jnp.float32).astype(jnp.bfloat16)
        found = found + product(hits, pool_ref[j, start:])

    @pl.when(step == 0)
    def begin():
        rows_ref[...] = found

    @pl.when(step > 0)
    def more():
        rows_ref[...] += found


def unpack(pool, part, at):
    devices, slab, width = pool.shape
    owners = 8 // math.gcd(part, 8)
    start = part // 16 * 16
    tokens = at.shape[0]
    return pl.pallas_call(
        functools.partial(unpack_kernel, start, part),
        out_shape=(
            jax.ShapeDtypeStruct((devices * part, width), pool.dtype),
            jax.ShapeDtypeStruct((tokens, width), jnp.float32),
        ),
        grid=(devices // owners,),
        in_specs=[
            pl.BlockSpec((tokens, 1), lambda i: (0, 0)),
            pl.BlockSpec((owners, slab, width), lambda i: (i, 0, 0)),
        ],
        out_specs=(
            pl.BlockSpec((owners * part, width), lambda i: (i, 0)),
            pl.BlockSpec((tokens, width), lambda i: (0, 0)),
        ),
        compiler_params=pltpu.CompilerParams(vmem_limit_bytes=40 * MIB),
        cost_estimate=pl.CostEstimate(
            flops=2 * devices * tokens * (slab - start) * width,
            bytes_accessed=4 * pool.size,
            transcendentals=0,
        ),
    )(at, pool)


def back_kernel(
    model_ref, fresh_ref, first_ref, second_ref, place_ref, a_ref, b_ref, table_ref, info_ref, target_ref, d_outs_ref,
    grad_ref, held, sems,
):
    step = pl.program_id(0)
    steps = pl.num_programs(0)
    seq_len = a_ref.shape[1]
    slot = lax.rem(step, 2)

    def leave(which, where, half):
        return pltpu.make_async_copy(
            held.at[which, half], d_outs_ref.at[where], sems.at[which, half]
        )

    @pl.when(step >= 2)
    def reuse():
        leave(slot, 0, 0).wait()
        leave(slot, 0, 1).wait()
    outs = jnp.concatenate([a_ref[0], b_ref[0]], axis=0)
    @pl.when(fresh_ref[step] == 1)
    def start():
        grad_ref[...] = jnp.zeros_like(grad_ref)

    part_rows = table_ref.shape[1]
    size = tile_of(part_rows)
    d_outs = jnp.zeros((2 * seq_len, outs.shape[1]), jnp.float32)
    for first_row in range(0, part_rows, size):
        here = pl.ds(first_row, size)
        table_rows = table_ref[0, here]
        logits = project(table_rows, outs)
        rows = lax.broadcasted_iota(jnp.int32, logits.shape, 0) + first_row
        soft = jnp.exp(logits - info_ref[0, 0:1, :])
        soft = jnp.where(rows == target_ref[0], soft - 1.0, soft)
        d_logits = (info_ref[0, 1:2, :] * soft).astype(jnp.bfloat16)
        d_outs = d_outs + outer_rows(d_logits, table_rows)
        grad_ref[0, here] += product(d_logits, outs)
    held[slot, 0] = d_outs[:seq_len].astype(held.dtype)
    held[slot, 1] = d_outs[seq_len:].astype(held.dtype)
    leave(slot, place_ref[2 * step], 0).start()
    leave(slot, place_ref[2 * step + 1], 1).start()

    @pl.when(step == steps - 1)
    def drain():
        for which in range(2):
            leave(which, 0, 0).wait()
            leave(which, 0, 1).wait()


def head_back(outs_pieces, table_low, model_of, fresh, first, second, place, info, target):
    steps = model_of.shape[0]
    models, part_rows, width = table_low.shape
    seq_len = outs_pieces.shape[1]
    return pl.pallas_call(
        back_kernel,
        out_shape=(
            jax.ShapeDtypeStruct((2 * steps, seq_len, width), jnp.bfloat16),
            jax.ShapeDtypeStruct((models, part_rows, width), jnp.float32),
        ),
        grid_spec=pltpu.PrefetchScalarGridSpec(
            num_scalar_prefetch=5,
            grid=(steps,),
            in_specs=[
                pl.BlockSpec((1, seq_len, width), lambda s, m, f, a, b, p: (a[s], 0, 0)),
                pl.BlockSpec((1, seq_len, width), lambda s, m, f, a, b, p: (b[s], 0, 0)),
                pl.BlockSpec((1, part_rows, width), lambda s, m, f, a, b, p: (m[s], 0, 0)),
                pl.BlockSpec((1, 2, 2 * seq_len), lambda s, m, f, a, b, p: (s, 0, 0)),
                pl.BlockSpec((1, 1, 2 * seq_len), lambda s, m, f, a, b, p: (s, 0, 0)),
            ],
            out_specs=(
                pl.BlockSpec(memory_space=pl.ANY),
                pl.BlockSpec((1, part_rows, width), lambda s, m, f, a, b, p: (m[s], 0, 0)),
            ),
            scratch_shapes=[
                pltpu.VMEM((2, 2, seq_len, width), jnp.bfloat16),
                pltpu.SemaphoreType.DMA((2, 2)),
            ],
        ),
        compiler_params=pltpu.CompilerParams(vmem_limit_bytes=56 * MIB),
        cost_estimate=pl.CostEstimate(
            flops=12 * steps * seq_len * part_rows * width,
            bytes_accessed=4 * steps * seq_len * width * 2 + 6 * table_low.size,
            transcendentals=2 * steps * seq_len * part_rows,
        ),
    )(model_of, fresh, first, second, place, outs_pieces, outs_pieces, table_low, info, target)


def finish_kernel(
    first_model, start_ref, first_ref, second_ref, d_ref, ids_ref, head_ref, table_ref, momentum_ref, *rest
):
    grad_ref, momentum_new_ref, table_new_ref = rest[-3:]
    model = pl.program_id(0) + first_model
    tile_rows = grad_ref.shape[1]
    tokens = ids_ref.shape[2]
    rows = lax.broadcasted_iota(jnp.int32, (tile_rows, tokens), 0) + pl.program_id(1) * tile_rows
    grad_ref[0] = head_ref[0]

    def pair(step, carry):
        hits = (rows == ids_ref[step]).astype(jnp.float32).astype(jnp.bfloat16)
        outs = jnp.concatenate([d_ref[first_ref[step]], d_ref[second_ref[step]]], axis=0)
        grad_ref[0] += product(hits, outs)
        return carry

    lax.fori_loop(start_ref[model], start_ref[model + 1], pair, 0)
    renewed, fresh_table = update(table_ref[0], momentum_ref[0], grad_ref[0], table_rate)
    momentum_new_ref[0] = renewed
    table_new_ref[0] = fresh_table


def finish_table(d_inputs, head_grad, table, momentum, schedule, ids, first_model, count, earlier):
    models, part_rows, width = table.shape
    tile_rows = tile_of(part_rows)
    state = jax.ShapeDtypeStruct(table.shape, jnp.float32)
    piece = pl.BlockSpec((1, tile_rows, width), lambda m, t, *_: (m + first_model, t, 0))
    whole = pl.BlockSpec(memory_space=pltpu.VMEM)
    return pl.pallas_call(
        functools.partial(finish_kernel, first_model),
        out_shape=(state, state, state),
        grid_spec=pltpu.PrefetchScalarGridSpec(
            num_scalar_prefetch=3,
            grid=(count, part_rows // tile_rows),
            in_specs=[whole, whole, piece, piece, piece]
            + [pl.BlockSpec(memory_space=pl.ANY)] * len(earlier),
            out_specs=(piece, piece, piece),
        ),
        input_output_aliases={8 + i: i for i in range(len(earlier))},
        compiler_params=pltpu.CompilerParams(vmem_limit_bytes=56 * MIB),
        cost_estimate=pl.CostEstimate(
            flops=2 * d_inputs.size * part_rows * count // models,
            bytes_accessed=24 * count * part_rows * width,
            transcendentals=0,
        ),
    )(*schedule, d_inputs, ids, head_grad, table, momentum, *earlier)


def body(
    token_ids,
    target_ids,
    segment_ids,
    chosen,
    table,
    table_momentum,
    stack,
    stack_momentum,
    vectors,
    vector_momentum,
):
    both = ("grp", "cli")
    models, block_rows, model_width = table.shape
    stack_part = stack.shape[1]
    seq_len = token_ids.shape[1]
    groups = lax.axis_size("grp")
    members = lax.axis_size("cli")
    devices = groups * members
    share = members // models
    local = members // share
    device_index = lax.axis_index(both)
    group_index = lax.axis_index("grp")
    member_index = lax.axis_index("cli")
    model_own = member_index // share
    part_own = member_index % share
    model_range = jnp.arange(models, dtype=jnp.int32)

    def per_member(rows):
        return jnp.repeat(rows, share, axis=0) if share > 1 else rows

    slab = -(-(stack_part + ROUND_ROWS) // SLAB_STEP) * SLAB_STEP
    round_rows = slab - stack_part

    facts = jnp.concatenate([token_ids[0], target_ids[0], segment_ids[0], chosen])
    facts = jnp.pad(facts, (0, -facts.size % LANES))[None]
    facts, table_low = opening(facts, table, groups, members, 5)
    facts = facts[:, 0]
    tokens = facts[:, :seq_len]
    targets = facts[:, seq_len : 2 * seq_len]
    segments = facts[:, 2 * seq_len : 3 * seq_len]
    choices = facts[:, 3 * seq_len]
    valid = jnp.concatenate(
        [
            (segments[:, :-1] == segments[:, 1:]).astype(jnp.float32),
            jnp.zeros((devices, 1), jnp.float32),
        ],
        axis=1,
    )
    counts = jnp.sum(valid, axis=1)
    choice_table = (choices[:, None] == model_range[None, :]).astype(jnp.float32)
    totals = jnp.sum(choice_table * counts[:, None], axis=0)
    total_of = jnp.sum(choice_table * totals[None, :], axis=1)

    fine = 16 if block_rows % 64 else 64
    coarse = block_rows // fine
    flat_tokens = tokens.reshape(-1)
    high_hot = (
        (flat_tokens // fine)[:, None] == jnp.arange(devices * coarse, dtype=jnp.int32)[None, :]
    ).astype(jnp.bfloat16)
    low_hot = ((flat_tokens % fine)[:, None] == jnp.arange(fine, dtype=jnp.int32)[None, :]).astype(
        jnp.bfloat16
    )
    seen = (outer_rows(high_hot, low_hot) > 0).astype(jnp.float32)
    before = product(
        seen.astype(jnp.bfloat16),
        jnp.triu(jnp.ones((fine, fine), jnp.bfloat16), 1),
    )
    sums = jnp.sum(seen, axis=1).reshape(devices, coarse)
    uniques = jnp.sum(sums, axis=1)
    ahead = jnp.sum(
        jnp.where(
            jnp.arange(coarse)[None, None, :] < jnp.arange(coarse)[None, :, None],
            sums[:, None, :],
            0.0,
        ),
        axis=2,
    )
    places = before + ahead.reshape(-1, 1)
    rounds = jnp.max(jnp.ceil(uniques / round_rows)).astype(jnp.int32)
    own_places = lax.dynamic_slice(places, (device_index * coarse, 0), (coarse, fine)).reshape(-1)
    own_seen = lax.dynamic_slice(seen, (device_index * coarse, 0), (coarse, fine)).reshape(-1)
    own_places = jnp.where(own_seen > 0, own_places, -1.0).astype(jnp.int32)
    first_client = group_index * members + part_own * local
    my_tokens = lax.dynamic_slice(tokens, (first_client, 0), (local, seq_len)).reshape(-1)
    my_segments = lax.dynamic_slice(segments, (first_client, 0), (local, seq_len))
    my_choices = lax.dynamic_slice(choices, (first_client,), (local,))
    my_high = (
        (my_tokens // fine)[:, None] == jnp.arange(devices * coarse, dtype=jnp.int32)[None, :]
    ).astype(jnp.bfloat16)
    my_low = (my_tokens % fine)[:, None] == jnp.arange(fine, dtype=jnp.int32)[None, :]
    split_places = jnp.concatenate(
        [jnp.floor(places / 64.0), places - 64.0 * jnp.floor(places / 64.0)], axis=1
    ).astype(jnp.bfloat16)
    picked_places = product(my_high, split_places)
    picked_places = 64.0 * picked_places[:, :fine] + picked_places[:, fine:]
    my_places = jnp.sum(jnp.where(my_low, picked_places, 0.0), axis=1).astype(jnp.int32)
    my_owner = my_tokens // block_rows

    def offered(start):
        wanted = jnp.arange(round_rows, dtype=jnp.int32) + start
        pick = (own_places[None, :] == wanted[:, None]).astype(jnp.bfloat16)
        rows = jnp.einsum("ur,krd->kud", pick, table_low, preferred_element_type=jnp.float32)
        return rows.astype(jnp.bfloat16)

    def inside(start):
        offset = my_places - start
        return ((offset >= 0) & (offset < round_rows), offset)

    def another(carry):
        index, embedded = carry
        start = index * round_rows
        turned = lax.all_to_all(per_member(offered(start)), "cli", 0, 0, tiled=True)
        pool = lax.all_gather(turned, "grp", axis=0, tiled=True).reshape(-1, model_width)
        here, offset = inside(start)
        found = jnp.take(pool, jnp.where(here, my_owner * round_rows + offset, 0), axis=0)
        return (index + 1, jnp.where(here[:, None], found.astype(jnp.float32), embedded))

    slabs = jnp.concatenate([stack.astype(jnp.bfloat16), offered(0)], axis=1)
    pool = spread(per_member(slabs), groups, members, 1, False, 2)
    here, offset = inside(0)
    at = jnp.where(here, my_owner * slab + stack_part + offset, -1)
    weights, embedded = unpack(pool, stack_part, at[:, None])
    _, embedded = lax.while_loop(
        lambda carry: carry[0] < rounds, another, (jnp.int32(1), embedded)
    )
    vector_one = lax.dynamic_index_in_dim(vectors, model_own, 0, keepdims=False)
    inputs = embedded + jnp.tile(weights[12 * model_width :].astype(jnp.float32), (local, 1))
    saved = layer_forward(weights, vector_one, inputs, my_segments)
    normed_out = saved[11]

    target_local = targets - device_index * block_rows
    target_local = jnp.where((target_local >= 0) & (target_local < block_rows), target_local, -1)
    target_blocks = target_local.reshape(groups * share, 1, local * seq_len)
    if devices * normed_out.size * 2 <= POOL_BYTES:
        outs_all, stats = spread_score(
            normed_out[None], table_low, target_blocks, groups, members, share, 2
        )
    else:
        outs_all = spread(normed_out[None], groups, members, 2, True, 2)
        stats = head_stats(outs_all, table_low, target_blocks, groups, members, share)
    shares = lax.all_to_all(stats, both, 0, 0, tiled=True)
    log_total = jax.nn.logsumexp(shares[:, 0], axis=0)
    token_loss = log_total - jnp.sum(shares[:, 1], axis=0)
    everything = share_all(jnp.stack([log_total, token_loss]), both, devices)
    everything = (
        everything.reshape(groups, models, share, 2, local, seq_len)
        .transpose(3, 1, 0, 2, 4, 5)
        .reshape(2, models, devices, seq_len)
    )
    all_losses = jnp.sum(everything[1] * valid[None], axis=2)
    loss = jnp.sum(choice_table.T * all_losses / total_of[None, :])
    client_losses = lax.dynamic_slice(
        (all_losses / counts[None, :]).T, (device_index, 0), (1, models)
    )
    chosen_total = jnp.sum(choice_table.T[:, :, None] * everything[0], axis=0)

    numbers = jnp.sum(choice_table, axis=0)
    padded = 2.0 * jnp.ceil(numbers / 2.0)
    offsets = jnp.cumsum(padded) - padded
    earlier = (
        jnp.arange(devices)[None, :] < jnp.arange(devices)[:, None]
    ) & (choices[None, :] == choices[:, None])
    slot_of = jnp.sum(choice_table * offsets[None, :], axis=1) + jnp.sum(
        earlier.astype(jnp.float32), axis=1
    )
    slots = devices + models
    steps = slots // 2
    at_slot = jnp.arange(slots)[:, None] == slot_of.astype(jnp.int32)[None, :]
    filled = jnp.any(at_slot, axis=1)
    client_at = jnp.sum(jnp.where(at_slot, jnp.arange(devices)[None, :], 0), axis=1).astype(
        jnp.int32
    )
    step_start = 2.0 * jnp.arange(steps)
    model_of = (
        jnp.sum((step_start[:, None] >= offsets[None, :]).astype(jnp.int32), axis=1) - 1
    ).astype(jnp.int32)
    fresh = jnp.concatenate(
        [jnp.ones((1,), jnp.int32), (model_of[1:] != model_of[:-1]).astype(jnp.int32)]
    )
    within = client_at % members
    piece_at = (
        (client_at // members * members + jnp.repeat(model_of, 2) * share + within // local) * local
        + within % local
    ).astype(jnp.int32)
    weight_rows = valid / total_of[:, None]
    slot_log = jnp.where(filled[:, None], jnp.take(chosen_total, client_at, axis=0), 1e30)
    slot_weight = jnp.where(filled[:, None], jnp.take(weight_rows, client_at, axis=0), 0.0)
    slot_info = jnp.stack(
        [slot_log.reshape(steps, 2 * seq_len), slot_weight.reshape(steps, 2 * seq_len)], axis=1
    )
    slot_target = jnp.where(filled[:, None], jnp.take(target_local, client_at, axis=0), -1)
    spare = devices + jnp.cumsum(1 - filled.astype(jnp.int32)) - 1
    d_outs, head_grad = head_back(
        outs_all.reshape(-1, seq_len, model_width),
        table_low,
        model_of,
        fresh,
        piece_at[0::2],
        piece_at[1::2],
        jnp.where(filled, client_at, spare).astype(jnp.int32),
        slot_info,
        slot_target.reshape(steps, 1, 2 * seq_len),
    )
    d_group = collect(d_outs, groups, members, 4)
    d_mine = lax.dynamic_slice(
        d_group, (part_own * local, 0, 0), (local, seq_len, model_width)
    ).astype(jnp.float32)
    d_final = jnp.where((my_choices == model_own)[:, None, None], d_mine, 0.0).reshape(
        local * seq_len, model_width
    )
    pairs, grad_places, vector_rows, d_inputs = layer_backward(
        weights, vector_one, inputs, my_segments, saved, d_final
    )
    d_wide = d_inputs.astype(jnp.bfloat16)
    if share > 1:
        d_wide = lax.dynamic_update_slice(
            jnp.zeros((members * seq_len, model_width), jnp.bfloat16),
            d_wide,
            (part_own * local * seq_len, 0),
        )
    d_wide, pairs, vector_rows = lax.optimization_barrier((d_wide, pairs, vector_rows))
    d_turned = lax.all_to_all(
        d_wide.reshape(members, seq_len, model_width), "cli", 0, 0, tiled=True
    )
    stack_rows = jnp.concatenate(
        [outer_rows(left, right).astype(jnp.bfloat16) for left, right in pairs]
        + [grad_places.astype(jnp.bfloat16)],
        axis=0,
    )
    stack_rows, d_turned = lax.optimization_barrier((stack_rows, d_turned))
    stack_sum = lax.psum_scatter(stack_rows, "grp", scatter_dimension=0, tiled=True)
    d_client = jnp.sum(d_turned.astype(jnp.float32), axis=0, keepdims=True).astype(jnp.bfloat16)
    d_all = spread(d_client, groups, members, 3, True, 2)
    d_all, vector_rows = lax.optimization_barrier((d_all, vector_rows))
    vector_piece = vector_rows.size // groups
    vector_part = lax.all_to_all(
        vector_rows.reshape(groups, vector_piece), "grp", 0, 0, tiled=True
    )

    token_local = tokens - device_index * block_rows
    token_local = jnp.where((token_local >= 0) & (token_local < block_rows), token_local, -1)
    slot_token = jnp.where(filled[:, None], jnp.take(token_local, client_at, axis=0), -1)
    pair_start = jnp.concatenate([offsets, jnp.sum(padded)[None]]) / 2.0
    schedule = (pair_start.astype(jnp.int32), client_at[0::2], client_at[1::2])
    slot_token = slot_token.reshape(steps, 1, 2 * seq_len)
    lead = models // 2

    states = finish_table(d_all, head_grad, table, table_momentum, schedule, slot_token, 0, lead, ())
    stack_sum, states, vector_part = lax.optimization_barrier((stack_sum, states, vector_part))
    stack_back = lax.all_to_all(
        stack_sum.reshape(members, stack_part, model_width), "cli", 0, 0, tiled=True
    ).astype(jnp.float32)
    stack_grad = jnp.sum(stack_back.reshape(models, share, stack_part, model_width), axis=1)
    table_grad, table_momentum_new, table_new = finish_table(
        d_all, head_grad, table, table_momentum, schedule, slot_token, lead, models - lead, states
    )
    stack_grad, vector_part = lax.optimization_barrier((stack_grad, vector_part))
    vector_parts = share_all(jnp.sum(vector_part, axis=0), both, devices)
    vector_grad = jnp.sum(vector_parts.reshape(groups, models, share, vector_piece), axis=2)
    vector_grad = vector_grad.transpose(1, 0, 2).reshape(vectors.shape)
    stack_momentum_new, stack_new = update(stack, stack_momentum, stack_grad, stack_rate)
    vector_momentum_new, vector_new = update(vectors, vector_momentum, vector_grad, vector_rate)
    return (
        loss,
        client_losses,
        table_grad,
        table_momentum_new,
        table_new,
        stack_grad,
        stack_momentum_new,
        stack_new,
        vector_grad,
        vector_momentum_new,
        vector_new,
    )


def solution(mesh):
    rows = P(("grp", "cli"), None)
    parts = P(None, ("grp", "cli"), None)
    return jax.shard_map(
        body,
        mesh=mesh,
        in_specs=(rows, rows, rows, P(("grp", "cli")), parts, parts, parts, parts, P(), P()),
        out_specs=(P(), rows, parts, parts, parts, parts, parts, parts, P(), P(), P()),
        check_vma=False,
    )
```

```python
import functools
import math

import jax
import jax.numpy as jnp
from jax import lax
from jax.experimental import pallas as pl
from jax.experimental.pallas import tpu as pltpu
from jax.sharding import PartitionSpec as P

HEADS = 12
HEAD_DIM = 64


epsilon = 1e-05
momentum_decay = 0.9
table_rate = 4.0
stack_rate = 4.0
vector_rate = 50.0

ROUND_ROWS = 104
SLAB_STEP = 16
TILE = 400
LANES = 128
MIB = 1 << 20
POOL_BYTES = 32 * MIB
MESH = pl.DeviceIdType.MESH


def layer_norm(inputs, gain_row, shift_row):
    centred = inputs - jnp.mean(inputs, -1, keepdims=True)
    spread = jnp.mean(centred * centred, -1, keepdims=True)
    return centred * lax.rsqrt(spread + epsilon) * gain_row + shift_row


def project(inputs, matrix):
    return lax.dot_general(
        inputs, matrix, (((1,), (1,)), ((), ())), preferred_element_type=jnp.float32
    )


def product(inputs, matrix):
    return jnp.dot(inputs, matrix, preferred_element_type=jnp.float32)


def outer_rows(left, right):
    return lax.dot_general(
        left, right, (((0,), (0,)), ((), ())), preferred_element_type=jnp.float32
    )


def split_heads(rows, seq_len):
    return rows.reshape(-1, seq_len, HEADS, HEAD_DIM)


def attend(queries, key_rows, segment_rows):
    seq_len = segment_rows.shape[1]
    scores = jnp.einsum(
        "nqhd,nkhd->nhqk",
        split_heads(queries, seq_len),
        split_heads(key_rows, seq_len),
        preferred_element_type=jnp.float32,
    ) * HEAD_DIM ** (-0.5)
    positions = jnp.arange(seq_len)
    allowed = (positions[None, None, :] <= positions[None, :, None]) & (
        segment_rows[:, None, :] == segment_rows[:, :, None]
    )
    return jax.nn.softmax(jnp.where(allowed[:, None], scores, -1e30), axis=-1)


def layer_forward(weights, vector_one, inputs, segment_rows):
    row_count, model_width = inputs.shape
    seq_len = segment_rows.shape[1]
    normed = layer_norm(inputs, vector_one[0], vector_one[1]).astype(jnp.bfloat16)
    queries = (project(normed, weights[0:model_width]) + vector_one[6]).astype(jnp.bfloat16)
    key_rows = project(normed, weights[model_width : 2 * model_width]).astype(jnp.bfloat16)
    values = (project(normed, weights[2 * model_width : 3 * model_width]) + vector_one[7]).astype(
        jnp.bfloat16
    )
    attention = attend(queries, key_rows, segment_rows)
    mixture = jnp.einsum(
        "nhqk,nkhd->nqhd",
        attention.astype(jnp.bfloat16),
        split_heads(values, seq_len),
        preferred_element_type=jnp.float32,
    )
    mixture = mixture.reshape(row_count, model_width).astype(jnp.bfloat16)
    middle = inputs + (project(mixture, weights[3 * model_width : 4 * model_width]) + vector_one[8])
    normed_two = layer_norm(middle, vector_one[2], vector_one[3]).astype(jnp.bfloat16)
    hidden = project(normed_two, weights[4 * model_width : 8 * model_width]) + vector_one[
        10:14
    ].reshape(-1)
    active = jax.nn.gelu(hidden, approximate=True).astype(jnp.bfloat16)
    residual = middle + (
        product(active, weights[8 * model_width : 12 * model_width]) + vector_one[9]
    )
    normed_out = layer_norm(residual, vector_one[4], vector_one[5]).astype(jnp.bfloat16)
    return (
        normed,
        queries,
        key_rows,
        values,
        attention,
        mixture,
        middle,
        normed_two,
        hidden,
        active,
        residual,
        normed_out,
    )


def norm_grad(operand, gain_row, shift_row, cotangent):
    outcome, pullback = jax.vjp(layer_norm, operand, gain_row, shift_row)
    return pullback(cotangent)


def gelu_tanh(hidden):
    return jax.nn.gelu(hidden, approximate=True)


def layer_backward(weights, vector_one, inputs, segment_rows, saved, grad_out):
    row_count, model_width = inputs.shape
    seq_len = segment_rows.shape[1]
    scaling = HEAD_DIM ** (-0.5)
    (
        normed,
        queries,
        key_rows,
        values,
        attention,
        mixture,
        middle,
        normed_two,
        hidden,
        active,
        residual,
        normed_out,
    ) = saved
    d_residual, d_gain_out, d_shift_out = norm_grad(
        residual, vector_one[4], vector_one[5], grad_out
    )
    d_outer = d_residual.astype(jnp.bfloat16)
    d_bias_out = jnp.sum(d_outer.astype(jnp.float32), 0)
    d_active = project(d_outer, weights[8 * model_width : 12 * model_width])
    gelu_value, gelu_pull = jax.vjp(gelu_tanh, hidden)
    d_hidden = gelu_pull(d_active)[0].astype(jnp.bfloat16)
    d_bias_hidden = jnp.sum(d_hidden.astype(jnp.float32), 0)
    d_normed_two = product(d_hidden, weights[4 * model_width : 8 * model_width])
    d_middle_norm, d_gain_two, d_shift_two = norm_grad(
        middle, vector_one[2], vector_one[3], d_normed_two
    )
    d_middle = d_residual + d_middle_norm
    d_branch = d_middle.astype(jnp.bfloat16)
    d_bias_branch = jnp.sum(d_branch.astype(jnp.float32), 0)
    d_mixture = split_heads(
        product(d_branch, weights[3 * model_width : 4 * model_width]).astype(jnp.bfloat16), seq_len
    )
    d_attention = jnp.einsum(
        "nqhd,nkhd->nhqk", d_mixture, split_heads(values, seq_len), preferred_element_type=jnp.float32
    )
    d_values = jnp.einsum(
        "nhqk,nqhd->nkhd",
        attention.astype(jnp.bfloat16),
        d_mixture,
        preferred_element_type=jnp.float32,
    )
    d_values = d_values.reshape(row_count, model_width).astype(jnp.bfloat16)
    d_scores = (
        attention * (d_attention - jnp.sum(attention * d_attention, -1, keepdims=True))
    ).astype(jnp.bfloat16)
    d_queries = (
        jnp.einsum(
            "nhqk,nkhd->nqhd",
            d_scores,
            split_heads(key_rows, seq_len),
            preferred_element_type=jnp.float32,
        )
        * scaling
    )
    d_queries = d_queries.reshape(row_count, model_width).astype(jnp.bfloat16)
    d_keys = (
        jnp.einsum(
            "nhqk,nqhd->nkhd",
            d_scores,
            split_heads(queries, seq_len),
            preferred_element_type=jnp.float32,
        )
        * scaling
    )
    d_keys = d_keys.reshape(row_count, model_width).astype(jnp.bfloat16)
    d_joined = jnp.concatenate([d_queries, d_keys, d_values], axis=1)
    d_normed = product(d_joined, weights[0 : 3 * model_width])
    d_inputs_norm, d_gain_one, d_shift_one = norm_grad(
        inputs, vector_one[0], vector_one[1], d_normed
    )
    d_inputs = d_middle + d_inputs_norm
    grad_places = jnp.sum(d_inputs.reshape(-1, seq_len, model_width), axis=0)
    pairs = (
        (d_joined, normed),
        (d_branch, mixture),
        (d_hidden, normed_two),
        (active, d_outer),
    )
    bias_query = jnp.sum(d_queries.astype(jnp.float32), 0)
    bias_value = jnp.sum(d_values.astype(jnp.float32), 0)
    vector_rows = jnp.concatenate(
        [
            jnp.stack(
                [
                    d_gain_one,
                    d_shift_one,
                    d_gain_two,
                    d_shift_two,
                    d_gain_out,
                    d_shift_out,
                    bias_query,
                    bias_value,
                    d_bias_branch,
                    d_bias_out,
                ]
            ),
            d_bias_hidden.reshape(4, model_width),
        ],
        axis=0,
    )
    return (pairs, grad_places, vector_rows, d_inputs)


def share_all(rows, axes, size):
    return lax.all_to_all(
        jnp.broadcast_to(rows[None], (size,) + rows.shape), axes, 0, 0, tiled=True
    )


def update(weight, momentum, gradient, step_rate):
    renewed = momentum_decay * momentum + gradient
    return (renewed, weight - step_rate * (gradient + momentum_decay * renewed))


def flipped(value, offset, size):
    bit = 1
    while bit < size:
        digit = lax.rem(lax.div(offset, bit), 2)
        value = value + digit * bit * (1 - 2 * lax.rem(lax.div(value, bit), 2))
        bit *= 2
    return value


class Place:
    def __init__(self, groups, members):
        self.groups, self.members = groups, members
        self.ys = 2
        self.xs = groups // 4
        self.grp = lax.axis_index("grp")
        self.cli = lax.axis_index("cli")
        self.core = lax.rem(self.grp, 2)
        self.x = lax.rem(lax.div(self.grp, 2), self.xs)
        self.y = lax.div(self.grp, 2 * self.xs)

    def group(self, jx=0, jy=0, jc=0):
        x = flipped(self.x, jx, self.xs)
        y = flipped(self.y, jy, self.ys)
        core = self.core + jc * (1 - 2 * self.core)
        return (y * self.xs + x) * 2 + core

    def block(self, jx, jy, level, jc=0):
        return self.group(jx, jy, jc) * self.members + level

    def peer(self, jx=0, jy=0, jc=0):
        return (self.group(jx, jy, jc), self.cli)

    def level(self, level):
        return (self.grp, level)

    def nearest(self, i):
        z, last = self.cli, self.members - 1
        low = jnp.where(2 * z < last, 1, 0)
        sign = 2 * low - 1
        margin = low * z + (1 - low) * (last - z)
        step = lax.div(i + 1, 2)
        odd = lax.rem(i, 2)
        near = z + sign * step * (2 * odd - 1)
        far = z + sign * (i - margin)
        return jnp.where(i <= 2 * margin, near, far)


def greet(place):
    barrier = pltpu.get_barrier_semaphore()
    peers = [place.peer(jx=j) for j in range(1, place.xs)] + [place.peer(jy=j) for j in range(1, place.ys)]
    peers.append(place.peer(jc=1))
    peers += [place.level(lax.rem(place.cli + j, place.members)) for j in range(1, place.members)]
    for peer in peers:
        pl.semaphore_signal(barrier, inc=1, device_id=peer, device_id_type=MESH)
    pl.semaphore_wait(barrier, len(peers))


def greet_all(devices, members):
    barrier = pltpu.get_barrier_semaphore()
    me = lax.axis_index("grp") * members + lax.axis_index("cli")

    def hello(j, carry):
        other = lax.rem(me + j, devices)
        pl.semaphore_signal(
            barrier, inc=1, device_id=(lax.div(other, members), lax.rem(other, members)), device_id_type=MESH
        )
        return carry

    lax.fori_loop(1, devices, hello, 0)
    pl.semaphore_wait(barrier, devices - 1)


def spread_sems(groups, members, pieces):
    xs, ys, items = groups // 4, 2, members * pieces
    dma = pltpu.SemaphoreType.DMA
    shapes = [(items,)] * 3 + [(items, xs)] * 2 + [(items, ys)] * 2 + [(items, xs, ys)] * 6
    return [dma] + [dma(shape) for shape in shapes]


def spread_body(place, chain, pieces, src, out, sems, consume, ready=None):
    (own_sem, z_up, z_down, z_recv, x_send, x_recv, y_send, y_recv, k_send, k_recv, p_send, p_recv,
     c_send, c_recv) = sems
    xs, ys, members = place.xs, place.ys, place.members
    items = members * pieces
    size = out.shape[1] // pieces
    z = place.cli
    partner = z + 1 - 2 * lax.rem(z, 2)
    inner_x, inner_y = range(1, xs), range(1, ys)

    def move(source, target, send, recv, device):
        return pltpu.make_async_remote_copy(
            src_ref=source, dst_ref=target, send_sem=send, recv_sem=recv, device_id=device, device_id_type=MESH
        )

    class Item:
        def __init__(self, k):
            self.level = place.nearest(lax.div(k, pieces))
            self.piece = lax.rem(k, pieces)
            self.slot = self.level * pieces + self.piece
            self.even = lax.rem(self.piece, 2) == 0
            self.mine = lax.rem(self.level + z, 2) == 0 if chain else self.level >= 0
            self.rows = pl.ds(self.piece * size, size)

        def part(self, jx, jy, level=None):
            return out.at[place.block(jx, jy, self.level if level is None else level), self.rows]

        def here(self, own):
            return src.at[z if not chain else 0, self.rows] if own else self.part(0, 0)

        def up(self, own=False):
            return move(self.here(own), self.part(0, 0), z_up.at[self.slot], z_recv.at[self.slot], place.level(z + 1))

        def down(self, own=False):
            return move(self.here(own), self.part(0, 0), z_down.at[self.slot], z_recv.at[self.slot], place.level(z - 1))

        def straight(self):
            return move(
                src.at[self.level, self.rows], self.part(0, 0, z), z_up.at[self.slot],
                z_recv.at[z * pieces + self.piece], place.level(self.level),
            )

        def landed(self):
            part = self.part(0, 0)
            return move(part, part, z_up.at[self.slot], z_recv.at[self.slot], place.level(partner))

        def to_x(self, jx, own=False):
            return move(self.here(own), self.part(0, 0), x_send.at[self.slot, jx], x_recv.at[self.slot, jx], place.peer(jx=jx))

        def to_y(self, jy, own=False):
            return move(self.here(own), self.part(0, 0), y_send.at[self.slot, jy], y_recv.at[self.slot, jy], place.peer(jy=jy))

        def corner_a(self, jx, jy):
            part = self.part(jx, 0)
            return move(part, part, k_send.at[self.slot, jx, jy], k_recv.at[self.slot, jx, jy], place.peer(jy=jy))

        def corner_b(self, jx, jy):
            part = self.part(0, jy)
            return move(part, part, k_send.at[self.slot, jx, jy], k_recv.at[self.slot, jx, jy], place.peer(jx=jx))

        def corner_z(self, jx, jy):
            part = self.part(jx, jy)
            return move(part, part, p_send.at[self.slot, jx, jy], p_recv.at[self.slot, jx, jy], place.level(partner))

        def to_core(self, jx, jy, own=False):
            part = self.part(jx, jy)
            return move(self.here(True) if own else part, part, c_send.at[self.slot, jx, jy], c_recv.at[self.slot, jx, jy], place.peer(jc=1))

    own = pltpu.make_async_copy(src.at[z if not chain else 0], out.at[place.block(0, 0, z)], own_sem)
    own.start()
    if not chain:
        for piece in range(pieces):
            Item(pieces + piece).straight().start()

    def columns(k):
        item = Item(k)
        level = item.level

        @pl.when(k < pieces)
        def mine_first():
            if chain:
                @pl.when(z + 1 < members)
                def onward():
                    item.up(True).start()

                @pl.when(z > 0)
                def back():
                    item.down(True).start()

            for jx in inner_x:
                item.to_x(jx, True).start()
            for jy in inner_y:
                item.to_y(jy, True).start()
            item.to_core(0, 0, True).start()

        @pl.when(k >= pieces)
        def arrive():
            item.landed().wait_recv()
            if chain:
                @pl.when((level < z) & (z + 1 < members))
                def onward():
                    item.up().start()

                @pl.when((level > z) & (z > 0))
                def back():
                    item.down().start()
            else:
                @pl.when(k + pieces < items)
                def following():
                    Item(k + pieces).straight().start()

            for jx in inner_x:
                item.to_x(jx).start()
            for jy in inner_y:
                item.to_y(jy).start()
            item.to_core(0, 0).start()

    def edges(k):
        item = Item(k)
        for jx in inner_x:
            item.to_x(jx).wait_recv()

            @pl.when(item.mine & item.even)
            def pass_a():
                for jy in inner_y:
                    item.corner_a(jx, jy).start()

            item.to_core(jx, 0).start()
        for jy in inner_y:
            item.to_y(jy).wait_recv()

            @pl.when(item.mine & jnp.logical_not(item.even))
            def pass_b():
                for jx in inner_x:
                    item.corner_b(jx, jy).start()

            item.to_core(0, jy).start()

    def corners(k):
        item = Item(k)

        @pl.when(item.mine)
        def mine_now():
            for jx in inner_x:
                for jy in inner_y:
                    item.corner_a(jx, jy).wait_recv()
                    if chain:
                        item.corner_z(jx, jy).start()
                    item.to_core(jx, jy).start()

    def handed(k):
        item = Item(k)

        @pl.when(jnp.logical_not(item.mine))
        def from_partner():
            for jx in inner_x:
                for jy in inner_y:
                    item.corner_z(jx, jy).wait_recv()
                    item.to_core(jx, jy).start()

    spots = xs * ys
    lag_edge, lag_corner = (2, 4) if chain else (1, 3)
    lag_handed = pieces + 6 if chain else lag_corner
    lag_end = lag_handed + 1

    def tick(t, carry):
        @pl.when(t < items)
        def arrivals():
            columns(t)

        @pl.when((t >= lag_edge) & (t < items + lag_edge))
        def sides():
            edges(t - lag_edge)

        @pl.when((t >= lag_corner) & (t < items + lag_corner))
        def far():
            corners(t - lag_corner)

        if chain:
            @pl.when((t >= lag_handed) & (t < items + lag_handed))
            def others():
                handed(t - lag_handed)

        def visit(e, carry):
            jc = lax.div(e, spots)
            spot = lax.rem(e, spots)
            jx, jy = lax.rem(spot, xs), lax.div(spot, xs)
            far = jnp.minimum(jx, 1) + jnp.minimum(jy, 1)
            lag = jnp.where(far == 0, 1, jnp.where(far == 1, lag_edge + 1, lag_end))
            k = t - lag

            @pl.when((k >= 0) & (k < items))
            def valid():
                item = Item(k)

                @pl.when(jc == 1)
                def shared():
                    item.to_core(jx, jy).wait_recv()

                if consume is not None:
                    consume(place.block(jx, jy, item.level, jc), item.level, item.piece)

            return carry

        return lax.fori_loop(0, 2 * spots, visit, carry)

    if ready is not None:
        own.wait()
        ready()
    lax.fori_loop(0, items + lag_end, tick, 0)

    def close(k, carry):
        item = Item(k)
        level = item.level
        if chain:
            @pl.when((level <= z) & (z + 1 < members))
            def onward():
                item.up().wait_send()

            @pl.when((level >= z) & (z > 0))
            def back():
                item.down().wait_send()
        else:
            @pl.when(k >= pieces)
            def sent():
                item.straight().wait_send()

        for jx in inner_x:
            item.to_x(jx).wait_send()
        for jy in inner_y:
            item.to_y(jy).wait_send()
        for jx in range(xs):
            for jy in range(ys):
                item.to_core(jx, jy).wait_send()

        @pl.when(item.mine)
        def mine_done():
            for jx in inner_x:
                for jy in inner_y:
                    item.corner_a(jx, jy).wait_send()
                    if chain:
                        item.corner_z(jx, jy).wait_send()

        return carry

    lax.fori_loop(0, items, close, 0)
    if ready is None:
        own.wait()


def spread_kernel(groups, members, chain, pieces, src, out, *sems):
    place = Place(groups, members)
    greet(place)
    spread_body(place, chain, pieces, src, out, sems, None)


def spread(src, groups, members, collective_id, chain, pieces):
    count, rows, width = src.shape
    return pl.pallas_call(
        functools.partial(spread_kernel, groups, members, chain, pieces),
        out_shape=jax.ShapeDtypeStruct((groups * members, rows, width), src.dtype),
        in_specs=[pl.BlockSpec(memory_space=pl.ANY)],
        out_specs=pl.BlockSpec(memory_space=pl.ANY),
        scratch_shapes=spread_sems(groups, members, pieces),
        compiler_params=pltpu.CompilerParams(collective_id=collective_id, has_side_effects=True),
        cost_estimate=pl.CostEstimate(
            flops=0, bytes_accessed=4 * groups * members * rows * width, transcendentals=0
        ),
    )(src)


def tile_of(part_rows):
    return TILE if part_rows % TILE == 0 else part_rows


def opening_kernel(groups, members, facts_ref, table_ref, facts_out, low_ref, own_sem, send_sems, recv_sems):
    devices = groups * members
    tiles = pl.num_programs(1)
    step = pl.program_id(0) * tiles + pl.program_id(1)
    last = pl.num_programs(0) * tiles - 1
    me = lax.axis_index("grp") * members + lax.axis_index("cli")

    def other(j):
        return lax.rem(me + j, devices)

    def place(device):
        return (lax.div(device, members), lax.rem(device, members))

    def give(j):
        return pltpu.make_async_remote_copy(
            src_ref=facts_ref, dst_ref=facts_out.at[me], send_sem=send_sems.at[j], recv_sem=recv_sems.at[j],
            device_id=place(other(j)), device_id_type=MESH,
        )

    own = pltpu.make_async_copy(facts_ref, facts_out.at[me], own_sem)

    @pl.when(step == 0)
    def begin():
        barrier = pltpu.get_barrier_semaphore()

        def hello(j, carry):
            pl.semaphore_signal(barrier, inc=1, device_id=place(other(j)), device_id_type=MESH)
            return carry

        own.start()
        lax.fori_loop(1, devices, hello, 0)

    @pl.when(step == last // 2)
    def exchange():
        def start(j, carry):
            give(j).start()
            return carry

        pl.semaphore_wait(pltpu.get_barrier_semaphore(), devices - 1)
        lax.fori_loop(1, devices, start, 0)

    low_ref[...] = table_ref[...].astype(low_ref.dtype)

    @pl.when(step == last)
    def end():
        def finish(j, carry):
            give(j).wait_send()
            pltpu.make_async_remote_copy(
                src_ref=facts_ref, dst_ref=facts_out.at[lax.rem(me + devices - j, devices)],
                send_sem=send_sems.at[j], recv_sem=recv_sems.at[j], device_id=place(other(j)), device_id_type=MESH,
            ).wait_recv()
            return carry

        lax.fori_loop(1, devices, finish, 0)
        own.wait()


def opening(facts, table, groups, members, collective_id):
    devices = groups * members
    models, part_rows, width = table.shape
    tile_rows = tile_of(part_rows)
    piece = pl.BlockSpec((1, tile_rows, width), lambda m, t: (m, t, 0))
    anywhere = pl.BlockSpec(memory_space=pl.ANY)
    dma = pltpu.SemaphoreType.DMA
    return pl.pallas_call(
        functools.partial(opening_kernel, groups, members),
        out_shape=(
            jax.ShapeDtypeStruct((devices,) + facts.shape, facts.dtype),
            jax.ShapeDtypeStruct(table.shape, jnp.bfloat16),
        ),
        grid=(models, part_rows // tile_rows),
        in_specs=[anywhere, piece],
        out_specs=(anywhere, piece),
        scratch_shapes=[dma, dma((devices,)), dma((devices,))],
        compiler_params=pltpu.CompilerParams(collective_id=collective_id, has_side_effects=True),
        cost_estimate=pl.CostEstimate(flops=0, bytes_accessed=6 * table.size, transcendentals=0),
    )(facts, table)


def score_kernel(groups, members, share, pieces, src, table, target, out, answer, *rest):
    part, pool, stat, inbox, part_sem, out_sems, go_send, go_recv, back_send, back_recv = rest[:10]
    sems = rest[10:]
    devices = groups * members
    place = Place(groups, members)
    load_table = pltpu.make_async_copy(table, part, part_sem)
    load_table.start()
    greet_all(devices, members)
    rows = pool.shape[1]
    size = rows // pieces

    def keep(block, piece):
        here = pl.ds(pl.multiple_of(piece * size, size), size)
        return pltpu.make_async_copy(pool.at[block, here], out.at[block, here], out_sems.at[block, piece])

    def consume(block, level, piece):
        keep(block, piece).start()
        here = pl.ds(pl.multiple_of(piece * size, size), size)
        model = lax.div(level, share)
        wanted = target[lax.div(block, members) * share + lax.rem(level, share), :, here]
        outs = pool[block, here]
        part_rows = part.shape[1]
        tile = tile_of(part_rows)
        marks = lax.broadcasted_iota(jnp.int32, (tile, size), 0)
        tops, totals, hits = [], [], []
        for first in range(0, part_rows, tile):
            logits = project(part[model, pl.ds(first, tile)], outs)
            hit = jnp.where(marks == wanted - first, logits, 0.0).reshape(-1, 8, size)
            hits.append(jnp.sum(hit, axis=0))
            logits = logits.reshape(-1, 8, size)
            top = jnp.max(logits, axis=0)
            tops.append(top)
            totals.append(jnp.sum(jnp.exp(logits - top[None]), axis=0))
        highest = jnp.max(functools.reduce(jnp.maximum, tops), axis=0, keepdims=True)
        total = sum(t * jnp.exp(m - highest) for t, m in zip(totals, tops))
        stat[block, 0:1, here] = highest + jnp.log(jnp.sum(total, axis=0, keepdims=True))
        stat[block, 1:2, here] = jnp.sum(sum(hits), axis=0, keepdims=True)

    spread_body(place, True, pieces, src, pool, sems, consume, load_table.wait)

    me = place.block(0, 0, place.cli)

    def device(index):
        return (lax.div(index, members), lax.rem(index, members))

    def ahead(j):
        return lax.rem(me + j, devices)

    def behind(j):
        return lax.rem(me + devices - j, devices)

    def go(j, source, target):
        return pltpu.make_async_remote_copy(
            src_ref=stat.at[source], dst_ref=inbox.at[target], send_sem=go_send.at[j], recv_sem=go_recv.at[j],
            device_id=device(ahead(j)), device_id_type=MESH,
        )

    def back(j, source):
        return pltpu.make_async_remote_copy(
            src_ref=answer.at[source], dst_ref=answer.at[source], send_sem=back_send.at[j],
            recv_sem=back_recv.at[j], device_id=device(ahead(j)), device_id_type=MESH,
        )

    def loop(step):
        def run(j, carry):
            step(j)
            return carry

        lax.fori_loop(1, devices, run, 0)

    loop(lambda j: go(j, ahead(j), me).start())
    inbox[me] = stat[me]
    loop(lambda j: go(j, me, behind(j)).wait_recv())
    logs = inbox[:, 0, :]
    top = jnp.max(logs, axis=0, keepdims=True)
    log_total = top + jnp.log(jnp.sum(jnp.exp(logs - top), axis=0, keepdims=True))
    answer[me, 0:1, :] = log_total
    answer[me, 1:2, :] = log_total - jnp.sum(inbox[:, 1, :], axis=0, keepdims=True)
    loop(lambda j: back(j, me).start())
    loop(lambda j: back(j, behind(j)).wait_recv())
    loop(lambda j: go(j, ahead(j), me).wait_send())
    loop(lambda j: back(j, me).wait_send())

    def close(block, carry):
        for piece in range(pieces):
            keep(block, piece).wait()
        return carry

    lax.fori_loop(0, groups * members, close, 0)


def spread_score(src, table_low, target_blocks, groups, members, share, collective_id, pieces=2):
    _, rows, width = src.shape
    blocks = groups * members
    return pl.pallas_call(
        functools.partial(score_kernel, groups, members, share, pieces),
        out_shape=(
            jax.ShapeDtypeStruct((blocks, rows, width), src.dtype),
            jax.ShapeDtypeStruct((blocks, 2, rows), jnp.float32),
        ),
        in_specs=[
            pl.BlockSpec(memory_space=pl.ANY),
            pl.BlockSpec(memory_space=pl.ANY),
            pl.BlockSpec(memory_space=pltpu.VMEM),
        ],
        out_specs=(pl.BlockSpec(memory_space=pl.ANY), pl.BlockSpec(memory_space=pltpu.VMEM)),
        scratch_shapes=[
            pltpu.VMEM(table_low.shape, table_low.dtype),
            pltpu.VMEM((blocks, rows, width), src.dtype),
            pltpu.VMEM((blocks, 2, rows), jnp.float32),
            pltpu.VMEM((blocks, 2, rows), jnp.float32),
            pltpu.SemaphoreType.DMA,
            pltpu.SemaphoreType.DMA((blocks, pieces)),
        ]
        + [pltpu.SemaphoreType.DMA((blocks,))] * 4
        + spread_sems(groups, members, pieces),
        compiler_params=pltpu.CompilerParams(
            collective_id=collective_id, has_side_effects=True, vmem_limit_bytes=60 * MIB
        ),
        cost_estimate=pl.CostEstimate(
            flops=2 * blocks * rows * table_low.shape[1] * width,
            bytes_accessed=2 * blocks * rows * width * 2,
            transcendentals=blocks * rows * table_low.shape[1],
        ),
    )(src, table_low, target_blocks)


def stats_kernel(outs_ref, table_ref, target_ref, stat_ref):
    logits = project(table_ref[0], outs_ref[0])
    highest = jnp.max(logits, axis=0, keepdims=True)
    total = jnp.sum(jnp.exp(logits - highest), axis=0, keepdims=True)
    rows = lax.broadcasted_iota(jnp.int32, logits.shape, 0)
    hit = jnp.sum(jnp.where(rows == target_ref[0], logits, 0.0), axis=0, keepdims=True)
    stat_ref[0, 0:1, :] = highest + jnp.log(total)
    stat_ref[0, 1:2, :] = hit


def head_stats(outs_all, table_low, target_blocks, groups, members, share):
    blocks, rows, width = outs_all.shape
    part_rows = table_low.shape[1]
    return pl.pallas_call(
        stats_kernel,
        out_shape=jax.ShapeDtypeStruct((blocks, 2, rows), jnp.float32),
        grid=(members, groups),
        in_specs=[
            pl.BlockSpec((1, rows, width), lambda z, g: (g * members + z, 0, 0)),
            pl.BlockSpec((1, part_rows, width), lambda z, g: (z // share, 0, 0)),
            pl.BlockSpec((1, 1, rows), lambda z, g: (g * share + z % share, 0, 0)),
        ],
        out_specs=pl.BlockSpec((1, 2, rows), lambda z, g: (g * members + z, 0, 0)),
        compiler_params=pltpu.CompilerParams(vmem_limit_bytes=56 * MIB),
        cost_estimate=pl.CostEstimate(
            flops=2 * blocks * rows * part_rows * width,
            bytes_accessed=2 * outs_all.size + 2 * table_low.size,
            transcendentals=blocks * rows * part_rows,
        ),
    )(outs_all, table_low, target_blocks)


def collect_kernel(groups, members, source, out, work, from_core, from_x, from_y, then_y, then_x, from_z, *sems):
    (load_sem, core_send, core_recv, x_send, x_recv, y_send, y_recv, yy_send, yy_recv, xx_send, xx_recv, z_send,
     z_recv, g_send, g_recv) = sems
    place = Place(groups, members)
    greet(place)
    xs, ys = place.xs, place.ys
    half = members // 2
    z = place.cli
    order = sorted(
        ((jx, jy) for jx in range(xs) for jy in range(ys)), key=lambda spot: -(spot[0] > 0) - (spot[1] > 0)
    )
    started = []

    def send(source_ref, target_ref, send_sem, recv_sem, device):
        copy = pltpu.make_async_remote_copy(
            src_ref=source_ref, dst_ref=target_ref, send_sem=send_sem, recv_sem=recv_sem, device_id=device,
            device_id_type=MESH,
        )
        copy.start()
        started.append(copy)

    def arrival(target_ref, send_sem, recv_sem, device):
        pltpu.make_async_remote_copy(
            src_ref=target_ref, dst_ref=target_ref, send_sem=send_sem, recv_sem=recv_sem, device_id=device,
            device_id_type=MESH,
        ).wait_recv()

    def add(ref, others):
        total = ref[...].astype(jnp.float32)
        for other in others:
            total = total + other[...].astype(jnp.float32)
        ref[...] = total.astype(ref.dtype)

    def clients(p):
        return (p, p + half)

    spots = [(jy * xs + jx, jx, jy) for jx, jy in order]
    loads = {}
    for p in range(half):
        for k, jx, jy in spots:
            for c in clients(p):
                send(
                    source.at[place.group(jx, jy, 1) * members + c], from_core.at[k, c], core_send.at[k, c],
                    core_recv.at[k, c], place.peer(jc=1),
                )
                loads[k, c] = pltpu.make_async_copy(
                    source.at[place.group(jx, jy, 0) * members + c], work.at[k, c], load_sem.at[k, c]
                )
                loads[k, c].start()
    for p in range(half):
        a, b = clients(p)
        for k, jx, jy in spots:
            for c in (a, b):
                loads[k, c].wait()
                arrival(from_core.at[k, c], core_send.at[k, c], core_recv.at[k, c], place.peer(jc=1))
                add(work.at[k, c], [from_core.at[k, c]])
            if jx:
                send(work.at[k, a], from_x.at[p, jx, jy], x_send.at[p, jx, jy], x_recv.at[p, jx, jy], place.peer(jx=jx))
            if jy:
                send(work.at[k, b], from_y.at[p, jx, jy], y_send.at[p, jx, jy], y_recv.at[p, jx, jy], place.peer(jy=jy))

    def second(p):
        a, b = clients(p)
        for jy in reversed(range(ys)):
            k = jy * xs
            for jx in range(1, xs):
                arrival(from_x.at[p, jx, jy], x_send.at[p, jx, jy], x_recv.at[p, jx, jy], place.peer(jx=jx))
            add(work.at[k, a], [from_x.at[p, jx, jy] for jx in range(1, xs)])
            if jy:
                send(work.at[k, a], then_y.at[p, jy], yy_send.at[p, jy], yy_recv.at[p, jy], place.peer(jy=jy))
        for jx in reversed(range(xs)):
            for jy in range(1, ys):
                arrival(from_y.at[p, jx, jy], y_send.at[p, jx, jy], y_recv.at[p, jx, jy], place.peer(jy=jy))
            add(work.at[jx, b], [from_y.at[p, jx, jy] for jy in range(1, ys)])
            if jx:
                send(work.at[jx, b], then_x.at[p, jx], xx_send.at[p, jx], xx_recv.at[p, jx], place.peer(jx=jx))

    def third(p):
        a, b = clients(p)
        for jy in range(1, ys):
            arrival(then_y.at[p, jy], yy_send.at[p, jy], yy_recv.at[p, jy], place.peer(jy=jy))
        add(work.at[0, a], [then_y.at[p, jy] for jy in range(1, ys)])
        for jx in range(1, xs):
            arrival(then_x.at[p, jx], xx_send.at[p, jx], xx_recv.at[p, jx], place.peer(jx=jx))
        add(work.at[0, b], [then_x.at[p, jx] for jx in range(1, xs)])
        for c in (a, b):
            @pl.when(z != c)
            def give():
                pltpu.make_async_remote_copy(
                    src_ref=work.at[0, c], dst_ref=from_z.at[z], send_sem=z_send.at[c], recv_sem=z_recv.at[z],
                    device_id=place.level(c), device_id_type=MESH,
                ).start()

    for p in range(half + 1):
        if p < half:
            second(p)
        if p:
            third(p - 1)
    total = work[0, z].astype(jnp.float32)
    for j in range(1, members):
        level = lax.rem(z + members - j, members)
        arrival(from_z.at[level], z_send.at[level], z_recv.at[level], place.level(level))
        total = total + from_z[level].astype(jnp.float32)
    out[z] = total.astype(out.dtype)
    for j in range(1, members):
        send(out.at[z], out.at[z], g_send.at[j], g_recv.at[j], place.level(lax.rem(z + j, members)))
    for j in range(1, members):
        level = lax.rem(z + members - j, members)
        arrival(out.at[level], g_send.at[j], g_recv.at[j], place.level(level))
    for copy in started:
        copy.wait_send()
    for c in range(members):
        @pl.when(z != c)
        def given():
            pltpu.make_async_remote_copy(
                src_ref=work.at[0, c], dst_ref=from_z.at[z], send_sem=z_send.at[c], recv_sem=z_recv.at[z],
                device_id=place.level(c), device_id_type=MESH,
            ).wait_send()


def collect(parts, groups, members, collective_id):
    _, seq_len, width = parts.shape
    xs, ys, half = groups // 4, 2, members // 2
    dma = pltpu.SemaphoreType.DMA

    def held(*shape):
        return pltpu.VMEM(shape + (seq_len, width), parts.dtype)

    return pl.pallas_call(
        functools.partial(collect_kernel, groups, members),
        out_shape=jax.ShapeDtypeStruct((members, seq_len, width), parts.dtype),
        in_specs=[pl.BlockSpec(memory_space=pl.ANY)],
        out_specs=pl.BlockSpec(memory_space=pltpu.VMEM),
        scratch_shapes=[
            held(xs * ys, members),
            held(xs * ys, members),
            held(half, xs, ys),
            held(half, xs, ys),
            held(half, ys),
            held(half, xs),
            held(members),
        ]
        + [dma((xs * ys, members))] * 3
        + [dma((half, xs, ys))] * 4
        + [dma((half, ys))] * 2
        + [dma((half, xs))] * 2
        + [dma((members,))] * 4,
        compiler_params=pltpu.CompilerParams(
            collective_id=collective_id, has_side_effects=True, vmem_limit_bytes=56 * MIB
        ),
        cost_estimate=pl.CostEstimate(
            flops=0, bytes_accessed=4 * groups * members * seq_len * width, transcendentals=0
        ),
    )(parts)


def unpack_kernel(start, part, at_ref, pool_ref, weights_ref, rows_ref):
    step = pl.program_id(0)
    owners, slab, width = pool_ref.shape
    weights_ref[...] = jnp.concatenate([pool_ref[j, :part] for j in range(owners)], axis=0)
    count = slab - start
    columns = lax.broadcasted_iota(jnp.int32, (1, count), 1) + start
    columns = jnp.concatenate([columns + j * slab for j in range(owners)], axis=1)
    hits = (columns == at_ref[...] - step * owners * slab).astype(jnp.float32).astype(jnp.bfloat16)
    found = product(hits, jnp.concatenate([pool_ref[j, start:] for j in range(owners)], axis=0))

    @pl.when(step == 0)
    def begin():
        rows_ref[...] = found

    @pl.when(step > 0)
    def more():
        rows_ref[...] += found


def unpack(pool, part, at):
    devices, slab, width = pool.shape
    owners = max(4, 8 // math.gcd(part, 8))
    start = part // 16 * 16
    tokens = at.shape[0]
    return pl.pallas_call(
        functools.partial(unpack_kernel, start, part),
        out_shape=(
            jax.ShapeDtypeStruct((devices * part, width), pool.dtype),
            jax.ShapeDtypeStruct((tokens, width), jnp.float32),
        ),
        grid=(devices // owners,),
        in_specs=[
            pl.BlockSpec((tokens, 1), lambda i: (0, 0)),
            pl.BlockSpec((owners, slab, width), lambda i: (i, 0, 0)),
        ],
        out_specs=(
            pl.BlockSpec((owners * part, width), lambda i: (i, 0)),
            pl.BlockSpec((tokens, width), lambda i: (0, 0)),
        ),
        compiler_params=pltpu.CompilerParams(vmem_limit_bytes=40 * MIB),
        cost_estimate=pl.CostEstimate(
            flops=2 * devices * tokens * (slab - start) * width,
            bytes_accessed=4 * pool.size,
            transcendentals=0,
        ),
    )(at, pool)


def back_kernel(
    model_ref, fresh_ref, first_ref, second_ref, place_ref, a_ref, b_ref, table_ref, info_ref, target_ref, d_outs_ref,
    grad_ref, held, sems,
):
    step = pl.program_id(0)
    steps = pl.num_programs(0)
    seq_len = a_ref.shape[1]
    slot = lax.rem(step, 2)

    def leave(which, where, half):
        return pltpu.make_async_copy(
            held.at[which, half], d_outs_ref.at[where], sems.at[which, half]
        )

    @pl.when(step >= 2)
    def reuse():
        leave(slot, 0, 0).wait()
        leave(slot, 0, 1).wait()
    outs = jnp.concatenate([a_ref[0], b_ref[0]], axis=0)
    @pl.when(fresh_ref[step] == 1)
    def start():
        grad_ref[...] = jnp.zeros_like(grad_ref)

    part_rows = table_ref.shape[1]
    size = tile_of(part_rows)
    d_outs = jnp.zeros((2 * seq_len, outs.shape[1]), jnp.float32)
    for first_row in range(0, part_rows, size):
        here = pl.ds(first_row, size)
        table_rows = table_ref[0, here]
        logits = project(table_rows, outs)
        rows = lax.broadcasted_iota(jnp.int32, logits.shape, 0) + first_row
        soft = jnp.exp(logits - info_ref[0, 0:1, :])
        soft = jnp.where(rows == target_ref[0], soft - 1.0, soft)
        d_logits = (info_ref[0, 1:2, :] * soft).astype(jnp.bfloat16)
        d_outs = d_outs + outer_rows(d_logits, table_rows)
        grad_ref[0, here] += product(d_logits, outs)
    held[slot, 0] = d_outs[:seq_len].astype(held.dtype)
    held[slot, 1] = d_outs[seq_len:].astype(held.dtype)
    leave(slot, place_ref[2 * step], 0).start()
    leave(slot, place_ref[2 * step + 1], 1).start()

    @pl.when(step == steps - 1)
    def drain():
        for which in range(2):
            leave(which, 0, 0).wait()
            leave(which, 0, 1).wait()


def head_back(outs_pieces, table_low, model_of, fresh, first, second, place, info, target):
    steps = model_of.shape[0]
    models, part_rows, width = table_low.shape
    seq_len = outs_pieces.shape[1]
    return pl.pallas_call(
        back_kernel,
        out_shape=(
            jax.ShapeDtypeStruct((2 * steps, seq_len, width), jnp.bfloat16),
            jax.ShapeDtypeStruct((models, part_rows, width), jnp.float32),
        ),
        grid_spec=pltpu.PrefetchScalarGridSpec(
            num_scalar_prefetch=5,
            grid=(steps,),
            in_specs=[
                pl.BlockSpec((1, seq_len, width), lambda s, m, f, a, b, p: (a[s], 0, 0)),
                pl.BlockSpec((1, seq_len, width), lambda s, m, f, a, b, p: (b[s], 0, 0)),
                pl.BlockSpec((1, part_rows, width), lambda s, m, f, a, b, p: (m[s], 0, 0)),
                pl.BlockSpec((1, 2, 2 * seq_len), lambda s, m, f, a, b, p: (s, 0, 0)),
                pl.BlockSpec((1, 1, 2 * seq_len), lambda s, m, f, a, b, p: (s, 0, 0)),
            ],
            out_specs=(
                pl.BlockSpec(memory_space=pl.ANY),
                pl.BlockSpec((1, part_rows, width), lambda s, m, f, a, b, p: (m[s], 0, 0)),
            ),
            scratch_shapes=[
                pltpu.VMEM((2, 2, seq_len, width), jnp.bfloat16),
                pltpu.SemaphoreType.DMA((2, 2)),
            ],
        ),
        compiler_params=pltpu.CompilerParams(vmem_limit_bytes=56 * MIB),
        cost_estimate=pl.CostEstimate(
            flops=12 * steps * seq_len * part_rows * width,
            bytes_accessed=4 * steps * seq_len * width * 2 + 6 * table_low.size,
            transcendentals=2 * steps * seq_len * part_rows,
        ),
    )(model_of, fresh, first, second, place, outs_pieces, outs_pieces, table_low, info, target)


def finish_kernel(
    first_model, start_ref, first_ref, second_ref, d_ref, ids_ref, head_ref, table_ref, momentum_ref, *rest
):
    grad_ref, momentum_new_ref, table_new_ref = rest[-3:]
    model = pl.program_id(0) + first_model
    tile_rows = grad_ref.shape[1]
    tokens = ids_ref.shape[2]
    rows = lax.broadcasted_iota(jnp.int32, (tile_rows, tokens), 0) + pl.program_id(1) * tile_rows
    grad_ref[0] = head_ref[0]

    def pair(step, carry):
        hits = (rows == ids_ref[step]).astype(jnp.float32).astype(jnp.bfloat16)
        outs = jnp.concatenate([d_ref[first_ref[step]], d_ref[second_ref[step]]], axis=0)
        grad_ref[0] += product(hits, outs)
        return carry

    lax.fori_loop(start_ref[model], start_ref[model + 1], pair, 0)
    renewed, fresh_table = update(table_ref[0], momentum_ref[0], grad_ref[0], table_rate)
    momentum_new_ref[0] = renewed
    table_new_ref[0] = fresh_table


def finish_table(d_inputs, head_grad, table, momentum, schedule, ids, first_model, count, earlier):
    models, part_rows, width = table.shape
    tile_rows = tile_of(part_rows)
    state = jax.ShapeDtypeStruct(table.shape, jnp.float32)
    piece = pl.BlockSpec((1, tile_rows, width), lambda m, t, *_: (m + first_model, t, 0))
    whole = pl.BlockSpec(memory_space=pltpu.VMEM)
    return pl.pallas_call(
        functools.partial(finish_kernel, first_model),
        out_shape=(state, state, state),
        grid_spec=pltpu.PrefetchScalarGridSpec(
            num_scalar_prefetch=3,
            grid=(count, part_rows // tile_rows),
            in_specs=[whole, whole, piece, piece, piece]
            + [pl.BlockSpec(memory_space=pl.ANY)] * len(earlier),
            out_specs=(piece, piece, piece),
        ),
        input_output_aliases={8 + i: i for i in range(len(earlier))},
        compiler_params=pltpu.CompilerParams(vmem_limit_bytes=56 * MIB),
        cost_estimate=pl.CostEstimate(
            flops=2 * d_inputs.size * part_rows * count // models,
            bytes_accessed=24 * count * part_rows * width,
            transcendentals=0,
        ),
    )(*schedule, d_inputs, ids, head_grad, table, momentum, *earlier)


def body(
    token_ids,
    target_ids,
    segment_ids,
    chosen,
    table,
    table_momentum,
    stack,
    stack_momentum,
    vectors,
    vector_momentum,
):
    both = ("grp", "cli")
    models, block_rows, model_width = table.shape
    stack_part = stack.shape[1]
    seq_len = token_ids.shape[1]
    groups = lax.axis_size("grp")
    members = lax.axis_size("cli")
    devices = groups * members
    share = members // models
    local = members // share
    device_index = lax.axis_index(both)
    group_index = lax.axis_index("grp")
    member_index = lax.axis_index("cli")
    model_own = member_index // share
    part_own = member_index % share
    model_range = jnp.arange(models, dtype=jnp.int32)

    def per_member(rows):
        return jnp.repeat(rows, share, axis=0) if share > 1 else rows

    slab = -(-(stack_part + ROUND_ROWS) // SLAB_STEP) * SLAB_STEP
    round_rows = slab - stack_part

    facts = jnp.concatenate([token_ids[0], target_ids[0], segment_ids[0], chosen])
    facts = jnp.pad(facts, (0, -facts.size % LANES))[None]
    facts, table_low = opening(facts, table, groups, members, 5)
    facts = facts[:, 0]
    tokens = facts[:, :seq_len]
    targets = facts[:, seq_len : 2 * seq_len]
    segments = facts[:, 2 * seq_len : 3 * seq_len]
    choices = facts[:, 3 * seq_len]
    valid = jnp.concatenate(
        [
            (segments[:, :-1] == segments[:, 1:]).astype(jnp.float32),
            jnp.zeros((devices, 1), jnp.float32),
        ],
        axis=1,
    )
    counts = jnp.sum(valid, axis=1)
    choice_table = (choices[:, None] == model_range[None, :]).astype(jnp.float32)
    totals = jnp.sum(choice_table * counts[:, None], axis=0)
    total_of = jnp.sum(choice_table * totals[None, :], axis=1)

    fine = 16 if block_rows % 64 else 64
    coarse = block_rows // fine
    flat_tokens = tokens.reshape(-1)
    high_hot = (
        (flat_tokens // fine)[:, None] == jnp.arange(devices * coarse, dtype=jnp.int32)[None, :]
    ).astype(jnp.bfloat16)
    low_hot = ((flat_tokens % fine)[:, None] == jnp.arange(fine, dtype=jnp.int32)[None, :]).astype(
        jnp.bfloat16
    )
    seen = (outer_rows(high_hot, low_hot) > 0).astype(jnp.float32)
    before = product(
        seen.astype(jnp.bfloat16),
        jnp.triu(jnp.ones((fine, fine), jnp.bfloat16), 1),
    )
    sums = jnp.sum(seen, axis=1).reshape(devices, coarse)
    uniques = jnp.sum(sums, axis=1)
    ahead = jnp.sum(
        jnp.where(
            jnp.arange(coarse)[None, None, :] < jnp.arange(coarse)[None, :, None],
            sums[:, None, :],
            0.0,
        ),
        axis=2,
    )
    places = before + ahead.reshape(-1, 1)
    rounds = jnp.max(jnp.ceil(uniques / round_rows)).astype(jnp.int32)
    own_places = lax.dynamic_slice(places, (device_index * coarse, 0), (coarse, fine)).reshape(-1)
    own_seen = lax.dynamic_slice(seen, (device_index * coarse, 0), (coarse, fine)).reshape(-1)
    own_places = jnp.where(own_seen > 0, own_places, -1.0).astype(jnp.int32)
    first_client = group_index * members + part_own * local
    my_tokens = lax.dynamic_slice(tokens, (first_client, 0), (local, seq_len)).reshape(-1)
    my_segments = lax.dynamic_slice(segments, (first_client, 0), (local, seq_len))
    my_choices = lax.dynamic_slice(choices, (first_client,), (local,))
    my_high = (
        (my_tokens // fine)[:, None] == jnp.arange(devices * coarse, dtype=jnp.int32)[None, :]
    ).astype(jnp.bfloat16)
    my_low = (my_tokens % fine)[:, None] == jnp.arange(fine, dtype=jnp.int32)[None, :]
    split_places = jnp.concatenate(
        [jnp.floor(places / 64.0), places - 64.0 * jnp.floor(places / 64.0)], axis=1
    ).astype(jnp.bfloat16)
    picked_places = product(my_high, split_places)
    picked_places = 64.0 * picked_places[:, :fine] + picked_places[:, fine:]
    my_places = jnp.sum(jnp.where(my_low, picked_places, 0.0), axis=1).astype(jnp.int32)
    my_owner = my_tokens // block_rows

    def offered(start):
        wanted = jnp.arange(round_rows, dtype=jnp.int32) + start
        pick = (own_places[None, :] == wanted[:, None]).astype(jnp.bfloat16)
        rows = jnp.einsum("ur,krd->kud", pick, table_low, preferred_element_type=jnp.float32)
        return rows.astype(jnp.bfloat16)

    def inside(start):
        offset = my_places - start
        return ((offset >= 0) & (offset < round_rows), offset)

    def another(carry):
        index, embedded = carry
        start = index * round_rows
        turned = lax.all_to_all(per_member(offered(start)), "cli", 0, 0, tiled=True)
        pool = lax.all_gather(turned, "grp", axis=0, tiled=True).reshape(-1, model_width)
        here, offset = inside(start)
        found = jnp.take(pool, jnp.where(here, my_owner * round_rows + offset, 0), axis=0)
        return (index + 1, jnp.where(here[:, None], found.astype(jnp.float32), embedded))

    slabs = jnp.concatenate([stack.astype(jnp.bfloat16), offered(0)], axis=1)
    pool = spread(per_member(slabs), groups, members, 1, False, 2)
    here, offset = inside(0)
    at = jnp.where(here, my_owner * slab + stack_part + offset, -1)
    weights, embedded = unpack(pool, stack_part, at[:, None])
    _, embedded = lax.while_loop(
        lambda carry: carry[0] < rounds, another, (jnp.int32(1), embedded)
    )
    vector_one = lax.dynamic_index_in_dim(vectors, model_own, 0, keepdims=False)
    inputs = embedded + jnp.tile(weights[12 * model_width :].astype(jnp.float32), (local, 1))
    saved = layer_forward(weights, vector_one, inputs, my_segments)
    normed_out = saved[11]

    target_local = targets - device_index * block_rows
    target_local = jnp.where((target_local >= 0) & (target_local < block_rows), target_local, -1)
    target_blocks = target_local.reshape(groups * share, 1, local * seq_len)
    if devices * normed_out.size * 2 <= POOL_BYTES:
        outs_all, everything = spread_score(
            normed_out[None], table_low, target_blocks, groups, members, share, 2
        )
    else:
        outs_all = spread(normed_out[None], groups, members, 2, True, 2)
        stats = head_stats(outs_all, table_low, target_blocks, groups, members, share)
        shares = lax.all_to_all(stats, both, 0, 0, tiled=True)
        log_total = jax.nn.logsumexp(shares[:, 0], axis=0)
        token_loss = log_total - jnp.sum(shares[:, 1], axis=0)
        everything = share_all(jnp.stack([log_total, token_loss]), both, devices)
    everything = (
        everything.reshape(groups, models, share, 2, local, seq_len)
        .transpose(3, 1, 0, 2, 4, 5)
        .reshape(2, models, devices, seq_len)
    )
    all_losses = jnp.sum(everything[1] * valid[None], axis=2)
    loss = jnp.sum(choice_table.T * all_losses / total_of[None, :])
    client_losses = lax.dynamic_slice(
        (all_losses / counts[None, :]).T, (device_index, 0), (1, models)
    )
    chosen_total = jnp.sum(choice_table.T[:, :, None] * everything[0], axis=0)

    numbers = jnp.sum(choice_table, axis=0)
    padded = 2.0 * jnp.ceil(numbers / 2.0)
    offsets = jnp.cumsum(padded) - padded
    earlier = (
        jnp.arange(devices)[None, :] < jnp.arange(devices)[:, None]
    ) & (choices[None, :] == choices[:, None])
    slot_of = jnp.sum(choice_table * offsets[None, :], axis=1) + jnp.sum(
        earlier.astype(jnp.float32), axis=1
    )
    slots = devices + models
    steps = slots // 2
    at_slot = jnp.arange(slots)[:, None] == slot_of.astype(jnp.int32)[None, :]
    filled = jnp.any(at_slot, axis=1)
    client_at = jnp.sum(jnp.where(at_slot, jnp.arange(devices)[None, :], 0), axis=1).astype(
        jnp.int32
    )
    step_start = 2.0 * jnp.arange(steps)
    model_of = (
        jnp.sum((step_start[:, None] >= offsets[None, :]).astype(jnp.int32), axis=1) - 1
    ).astype(jnp.int32)
    fresh = jnp.concatenate(
        [jnp.ones((1,), jnp.int32), (model_of[1:] != model_of[:-1]).astype(jnp.int32)]
    )
    within = client_at % members
    piece_at = (
        (client_at // members * members + jnp.repeat(model_of, 2) * share + within // local) * local
        + within % local
    ).astype(jnp.int32)
    weight_rows = valid / total_of[:, None]
    slot_log = jnp.where(filled[:, None], jnp.take(chosen_total, client_at, axis=0), 1e30)
    slot_weight = jnp.where(filled[:, None], jnp.take(weight_rows, client_at, axis=0), 0.0)
    slot_info = jnp.stack(
        [slot_log.reshape(steps, 2 * seq_len), slot_weight.reshape(steps, 2 * seq_len)], axis=1
    )
    slot_target = jnp.where(filled[:, None], jnp.take(target_local, client_at, axis=0), -1)
    spare = devices + jnp.cumsum(1 - filled.astype(jnp.int32)) - 1
    d_outs, head_grad = head_back(
        outs_all.reshape(-1, seq_len, model_width),
        table_low,
        model_of,
        fresh,
        piece_at[0::2],
        piece_at[1::2],
        jnp.where(filled, client_at, spare).astype(jnp.int32),
        slot_info,
        slot_target.reshape(steps, 1, 2 * seq_len),
    )
    d_group = collect(d_outs, groups, members, 4)
    d_mine = lax.dynamic_slice(
        d_group, (part_own * local, 0, 0), (local, seq_len, model_width)
    ).astype(jnp.float32)
    d_final = jnp.where((my_choices == model_own)[:, None, None], d_mine, 0.0).reshape(
        local * seq_len, model_width
    )
    pairs, grad_places, vector_rows, d_inputs = layer_backward(
        weights, vector_one, inputs, my_segments, saved, d_final
    )
    d_wide = d_inputs.astype(jnp.bfloat16)
    if share > 1:
        d_wide = lax.dynamic_update_slice(
            jnp.zeros((members * seq_len, model_width), jnp.bfloat16),
            d_wide,
            (part_own * local * seq_len, 0),
        )
    d_wide, pairs, vector_rows = lax.optimization_barrier((d_wide, pairs, vector_rows))
    d_turned = lax.all_to_all(
        d_wide.reshape(members, seq_len, model_width), "cli", 0, 0, tiled=True
    )
    stack_rows = jnp.concatenate(
        [outer_rows(left, right).astype(jnp.bfloat16) for left, right in pairs]
        + [grad_places.astype(jnp.bfloat16)],
        axis=0,
    )
    stack_rows, d_turned = lax.optimization_barrier((stack_rows, d_turned))
    stack_sum = lax.psum_scatter(stack_rows, "grp", scatter_dimension=0, tiled=True)
    d_client = jnp.sum(d_turned.astype(jnp.float32), axis=0, keepdims=True).astype(jnp.bfloat16)
    d_all = spread(d_client, groups, members, 3, True, 2)
    d_all, vector_rows = lax.optimization_barrier((d_all, vector_rows))
    vector_piece = vector_rows.size // groups
    vector_part = lax.all_to_all(
        vector_rows.reshape(groups, vector_piece), "grp", 0, 0, tiled=True
    )

    token_local = tokens - device_index * block_rows
    token_local = jnp.where((token_local >= 0) & (token_local < block_rows), token_local, -1)
    slot_token = jnp.where(filled[:, None], jnp.take(token_local, client_at, axis=0), -1)
    pair_start = jnp.concatenate([offsets, jnp.sum(padded)[None]]) / 2.0
    schedule = (pair_start.astype(jnp.int32), client_at[0::2], client_at[1::2])
    slot_token = slot_token.reshape(steps, 1, 2 * seq_len)
    lead = models // 2

    states = finish_table(d_all, head_grad, table, table_momentum, schedule, slot_token, 0, lead, ())
    stack_sum, states, vector_part = lax.optimization_barrier((stack_sum, states, vector_part))
    stack_back = lax.all_to_all(
        stack_sum.reshape(members, stack_part, model_width), "cli", 0, 0, tiled=True
    ).astype(jnp.float32)
    stack_grad = jnp.sum(stack_back.reshape(models, share, stack_part, model_width), axis=1)
    table_grad, table_momentum_new, table_new = finish_table(
        d_all, head_grad, table, table_momentum, schedule, slot_token, lead, models - lead, states
    )
    stack_grad, vector_part = lax.optimization_barrier((stack_grad, vector_part))
    vector_parts = share_all(jnp.sum(vector_part, axis=0), both, devices)
    vector_grad = jnp.sum(vector_parts.reshape(groups, models, share, vector_piece), axis=2)
    vector_grad = vector_grad.transpose(1, 0, 2).reshape(vectors.shape)
    stack_momentum_new, stack_new = update(stack, stack_momentum, stack_grad, stack_rate)
    vector_momentum_new, vector_new = update(vectors, vector_momentum, vector_grad, vector_rate)
    return (
        loss,
        client_losses,
        table_grad,
        table_momentum_new,
        table_new,
        stack_grad,
        stack_momentum_new,
        stack_new,
        vector_grad,
        vector_momentum_new,
        vector_new,
    )


def solution(mesh):
    rows = P(("grp", "cli"), None)
    parts = P(None, ("grp", "cli"), None)
    return jax.shard_map(
        body,
        mesh=mesh,
        in_specs=(rows, rows, rows, P(("grp", "cli")), parts, parts, parts, parts, P(), P()),
        out_specs=(P(), rows, parts, parts, parts, parts, parts, parts, P(), P(), P()),
        check_vma=False,
    )
```

```python
import functools
import math

import jax
import jax.numpy as jnp
from jax import lax
from jax.experimental import pallas as pl
from jax.experimental.pallas import tpu as pltpu
from jax.sharding import PartitionSpec as P

HEADS = 12
HEAD_DIM = 64


epsilon = 1e-05
momentum_decay = 0.9
table_rate = 4.0
stack_rate = 4.0
vector_rate = 50.0

ROUND_ROWS = 104
SLAB_STEP = 16
TILE = 400
LANES = 128
QUAD = 4
MIB = 1 << 20
POOL_BYTES = 32 * MIB
MESH = pl.DeviceIdType.MESH


def layer_norm(inputs, gain_row, shift_row):
    centred = inputs - jnp.mean(inputs, -1, keepdims=True)
    spread = jnp.mean(centred * centred, -1, keepdims=True)
    return centred * lax.rsqrt(spread + epsilon) * gain_row + shift_row


def project(inputs, matrix):
    return lax.dot_general(
        inputs, matrix, (((1,), (1,)), ((), ())), preferred_element_type=jnp.float32
    )


def product(inputs, matrix):
    return jnp.dot(inputs, matrix, preferred_element_type=jnp.float32)


def outer_rows(left, right):
    return lax.dot_general(
        left, right, (((0,), (0,)), ((), ())), preferred_element_type=jnp.float32
    )


def split_heads(rows, seq_len):
    return rows.reshape(-1, seq_len, HEADS, HEAD_DIM)


def attend(queries, key_rows, segment_rows):
    seq_len = segment_rows.shape[1]
    scores = jnp.einsum(
        "nqhd,nkhd->nhqk",
        split_heads(queries, seq_len),
        split_heads(key_rows, seq_len),
        preferred_element_type=jnp.float32,
    ) * HEAD_DIM ** (-0.5)
    positions = jnp.arange(seq_len)
    allowed = (positions[None, None, :] <= positions[None, :, None]) & (
        segment_rows[:, None, :] == segment_rows[:, :, None]
    )
    return jax.nn.softmax(jnp.where(allowed[:, None], scores, -1e30), axis=-1)


def layer_forward(weights, vector_one, inputs, segment_rows):
    row_count, model_width = inputs.shape
    seq_len = segment_rows.shape[1]
    normed = layer_norm(inputs, vector_one[0], vector_one[1]).astype(jnp.bfloat16)
    queries = (project(normed, weights[0:model_width]) + vector_one[6]).astype(jnp.bfloat16)
    key_rows = project(normed, weights[model_width : 2 * model_width]).astype(jnp.bfloat16)
    values = (project(normed, weights[2 * model_width : 3 * model_width]) + vector_one[7]).astype(
        jnp.bfloat16
    )
    attention = attend(queries, key_rows, segment_rows)
    mixture = jnp.einsum(
        "nhqk,nkhd->nqhd",
        attention.astype(jnp.bfloat16),
        split_heads(values, seq_len),
        preferred_element_type=jnp.float32,
    )
    mixture = mixture.reshape(row_count, model_width).astype(jnp.bfloat16)
    middle = inputs + (project(mixture, weights[3 * model_width : 4 * model_width]) + vector_one[8])
    normed_two = layer_norm(middle, vector_one[2], vector_one[3]).astype(jnp.bfloat16)
    hidden = project(normed_two, weights[4 * model_width : 8 * model_width]) + vector_one[
        10:14
    ].reshape(-1)
    active = jax.nn.gelu(hidden, approximate=True).astype(jnp.bfloat16)
    residual = middle + (
        product(active, weights[8 * model_width : 12 * model_width]) + vector_one[9]
    )
    normed_out = layer_norm(residual, vector_one[4], vector_one[5]).astype(jnp.bfloat16)
    return (
        normed,
        queries,
        key_rows,
        values,
        attention,
        mixture,
        middle,
        normed_two,
        hidden,
        active,
        residual,
        normed_out,
    )


def norm_grad(operand, gain_row, shift_row, cotangent):
    outcome, pullback = jax.vjp(layer_norm, operand, gain_row, shift_row)
    return pullback(cotangent)


def gelu_tanh(hidden):
    return jax.nn.gelu(hidden, approximate=True)


def layer_backward(weights, vector_one, inputs, segment_rows, saved, grad_out):
    row_count, model_width = inputs.shape
    seq_len = segment_rows.shape[1]
    scaling = HEAD_DIM ** (-0.5)
    (
        normed,
        queries,
        key_rows,
        values,
        attention,
        mixture,
        middle,
        normed_two,
        hidden,
        active,
        residual,
        normed_out,
    ) = saved
    d_residual, d_gain_out, d_shift_out = norm_grad(
        residual, vector_one[4], vector_one[5], grad_out
    )
    d_outer = d_residual.astype(jnp.bfloat16)
    d_bias_out = jnp.sum(d_outer.astype(jnp.float32), 0)
    d_active = project(d_outer, weights[8 * model_width : 12 * model_width])
    gelu_value, gelu_pull = jax.vjp(gelu_tanh, hidden)
    d_hidden = gelu_pull(d_active)[0].astype(jnp.bfloat16)
    d_bias_hidden = jnp.sum(d_hidden.astype(jnp.float32), 0)
    d_normed_two = product(d_hidden, weights[4 * model_width : 8 * model_width])
    d_middle_norm, d_gain_two, d_shift_two = norm_grad(
        middle, vector_one[2], vector_one[3], d_normed_two
    )
    d_middle = d_residual + d_middle_norm
    d_branch = d_middle.astype(jnp.bfloat16)
    d_bias_branch = jnp.sum(d_branch.astype(jnp.float32), 0)
    d_mixture = split_heads(
        product(d_branch, weights[3 * model_width : 4 * model_width]).astype(jnp.bfloat16), seq_len
    )
    d_attention = jnp.einsum(
        "nqhd,nkhd->nhqk", d_mixture, split_heads(values, seq_len), preferred_element_type=jnp.float32
    )
    d_values = jnp.einsum(
        "nhqk,nqhd->nkhd",
        attention.astype(jnp.bfloat16),
        d_mixture,
        preferred_element_type=jnp.float32,
    )
    d_values = d_values.reshape(row_count, model_width).astype(jnp.bfloat16)
    d_scores = (
        attention * (d_attention - jnp.sum(attention * d_attention, -1, keepdims=True))
    ).astype(jnp.bfloat16)
    d_queries = (
        jnp.einsum(
            "nhqk,nkhd->nqhd",
            d_scores,
            split_heads(key_rows, seq_len),
            preferred_element_type=jnp.float32,
        )
        * scaling
    )
    d_queries = d_queries.reshape(row_count, model_width).astype(jnp.bfloat16)
    d_keys = (
        jnp.einsum(
            "nhqk,nqhd->nkhd",
            d_scores,
            split_heads(queries, seq_len),
            preferred_element_type=jnp.float32,
        )
        * scaling
    )
    d_keys = d_keys.reshape(row_count, model_width).astype(jnp.bfloat16)
    d_joined = jnp.concatenate([d_queries, d_keys, d_values], axis=1)
    d_normed = product(d_joined, weights[0 : 3 * model_width])
    d_inputs_norm, d_gain_one, d_shift_one = norm_grad(
        inputs, vector_one[0], vector_one[1], d_normed
    )
    d_inputs = d_middle + d_inputs_norm
    grad_places = jnp.sum(d_inputs.reshape(-1, seq_len, model_width), axis=0)
    pairs = (
        (d_joined, normed),
        (d_branch, mixture),
        (d_hidden, normed_two),
        (active, d_outer),
    )
    bias_query = jnp.sum(d_queries.astype(jnp.float32), 0)
    bias_value = jnp.sum(d_values.astype(jnp.float32), 0)
    vector_rows = jnp.concatenate(
        [
            jnp.stack(
                [
                    d_gain_one,
                    d_shift_one,
                    d_gain_two,
                    d_shift_two,
                    d_gain_out,
                    d_shift_out,
                    bias_query,
                    bias_value,
                    d_bias_branch,
                    d_bias_out,
                ]
            ),
            d_bias_hidden.reshape(4, model_width),
        ],
        axis=0,
    )
    return (pairs, grad_places, vector_rows, d_inputs)


def share_all(rows, axes, size):
    return lax.all_to_all(
        jnp.broadcast_to(rows[None], (size,) + rows.shape), axes, 0, 0, tiled=True
    )


def update(weight, momentum, gradient, step_rate):
    renewed = momentum_decay * momentum + gradient
    return (renewed, weight - step_rate * (gradient + momentum_decay * renewed))


def flipped(value, offset, size):
    bit = 1
    while bit < size:
        digit = lax.rem(lax.div(offset, bit), 2)
        value = value + digit * bit * (1 - 2 * lax.rem(lax.div(value, bit), 2))
        bit *= 2
    return value


class Place:
    def __init__(self, groups, members):
        self.groups, self.members = groups, members
        self.ys = 2
        self.xs = groups // 4
        self.grp = lax.axis_index("grp")
        self.cli = lax.axis_index("cli")
        self.core = lax.rem(self.grp, 2)
        self.x = lax.rem(lax.div(self.grp, 2), self.xs)
        self.y = lax.div(self.grp, 2 * self.xs)

    def group(self, jx=0, jy=0, jc=0):
        x = flipped(self.x, jx, self.xs)
        y = flipped(self.y, jy, self.ys)
        core = self.core + jc * (1 - 2 * self.core)
        return (y * self.xs + x) * 2 + core

    def block(self, jx, jy, level, jc=0):
        return self.group(jx, jy, jc) * self.members + level

    def peer(self, jx=0, jy=0, jc=0):
        return (self.group(jx, jy, jc), self.cli)

    def level(self, level):
        return (self.grp, level)

    def nearest(self, i):
        z, last = self.cli, self.members - 1
        low = jnp.where(2 * z < last, 1, 0)
        sign = 2 * low - 1
        margin = low * z + (1 - low) * (last - z)
        step = lax.div(i + 1, 2)
        odd = lax.rem(i, 2)
        near = z + sign * step * (2 * odd - 1)
        far = z + sign * (i - margin)
        return jnp.where(i <= 2 * margin, near, far)


def greet(place):
    barrier = pltpu.get_barrier_semaphore()
    peers = [place.peer(jx=j) for j in range(1, place.xs)] + [place.peer(jy=j) for j in range(1, place.ys)]
    peers.append(place.peer(jc=1))
    peers += [place.level(lax.rem(place.cli + j, place.members)) for j in range(1, place.members)]
    for peer in peers:
        pl.semaphore_signal(barrier, inc=1, device_id=peer, device_id_type=MESH)
    pl.semaphore_wait(barrier, len(peers))


def greet_all(devices, members):
    barrier = pltpu.get_barrier_semaphore()
    me = lax.axis_index("grp") * members + lax.axis_index("cli")

    def hello(j, carry):
        other = lax.rem(me + j, devices)
        pl.semaphore_signal(
            barrier, inc=1, device_id=(lax.div(other, members), lax.rem(other, members)), device_id_type=MESH
        )
        return carry

    lax.fori_loop(1, devices, hello, 0)
    pl.semaphore_wait(barrier, devices - 1)


def spread_sems(groups, members, pieces):
    xs, ys, items = groups // 4, 2, members * pieces
    dma = pltpu.SemaphoreType.DMA
    shapes = [(items,)] * 3 + [(items, xs)] * 2 + [(items, ys)] * 2 + [(items, xs, ys)] * 6
    return [dma] + [dma(shape) for shape in shapes]


def spread_body(place, chain, pieces, src, out, sems, consume, ready=None):
    (own_sem, z_up, z_down, z_recv, x_send, x_recv, y_send, y_recv, k_send, k_recv, p_send, p_recv,
     c_send, c_recv) = sems
    xs, ys, members = place.xs, place.ys, place.members
    items = members * pieces
    size = out.shape[1] // pieces
    z = place.cli
    partner = z + 1 - 2 * lax.rem(z, 2)
    inner_x, inner_y = range(1, xs), range(1, ys)

    def move(source, target, send, recv, device):
        return pltpu.make_async_remote_copy(
            src_ref=source, dst_ref=target, send_sem=send, recv_sem=recv, device_id=device, device_id_type=MESH
        )

    class Item:
        def __init__(self, k):
            self.level = place.nearest(lax.div(k, pieces))
            self.piece = lax.rem(k, pieces)
            self.slot = self.level * pieces + self.piece
            self.even = lax.rem(self.piece, 2) == 0
            self.mine = lax.rem(self.level + z, 2) == 0 if chain else self.level >= 0
            self.rows = pl.ds(self.piece * size, size)

        def part(self, jx, jy, level=None):
            return out.at[place.block(jx, jy, self.level if level is None else level), self.rows]

        def here(self, own):
            return src.at[z if not chain else 0, self.rows] if own else self.part(0, 0)

        def up(self, own=False):
            return move(self.here(own), self.part(0, 0), z_up.at[self.slot], z_recv.at[self.slot], place.level(z + 1))

        def down(self, own=False):
            return move(self.here(own), self.part(0, 0), z_down.at[self.slot], z_recv.at[self.slot], place.level(z - 1))

        def straight(self):
            return move(
                src.at[self.level, self.rows], self.part(0, 0, z), z_up.at[self.slot],
                z_recv.at[z * pieces + self.piece], place.level(self.level),
            )

        def landed(self):
            part = self.part(0, 0)
            return move(part, part, z_up.at[self.slot], z_recv.at[self.slot], place.level(partner))

        def to_x(self, jx, own=False):
            return move(self.here(own), self.part(0, 0), x_send.at[self.slot, jx], x_recv.at[self.slot, jx], place.peer(jx=jx))

        def to_y(self, jy, own=False):
            return move(self.here(own), self.part(0, 0), y_send.at[self.slot, jy], y_recv.at[self.slot, jy], place.peer(jy=jy))

        def corner_a(self, jx, jy):
            part = self.part(jx, 0)
            return move(part, part, k_send.at[self.slot, jx, jy], k_recv.at[self.slot, jx, jy], place.peer(jy=jy))

        def corner_b(self, jx, jy):
            part = self.part(0, jy)
            return move(part, part, k_send.at[self.slot, jx, jy], k_recv.at[self.slot, jx, jy], place.peer(jx=jx))

        def corner_z(self, jx, jy):
            part = self.part(jx, jy)
            return move(part, part, p_send.at[self.slot, jx, jy], p_recv.at[self.slot, jx, jy], place.level(partner))

        def to_core(self, jx, jy, own=False):
            part = self.part(jx, jy)
            return move(self.here(True) if own else part, part, c_send.at[self.slot, jx, jy], c_recv.at[self.slot, jx, jy], place.peer(jc=1))

    own = pltpu.make_async_copy(src.at[z if not chain else 0], out.at[place.block(0, 0, z)], own_sem)
    own.start()
    if not chain:
        for piece in range(pieces):
            Item(pieces + piece).straight().start()

    def columns(k):
        item = Item(k)
        level = item.level

        @pl.when(k < pieces)
        def mine_first():
            if chain:
                @pl.when(z + 1 < members)
                def onward():
                    item.up(True).start()

                @pl.when(z > 0)
                def back():
                    item.down(True).start()

            for jx in inner_x:
                item.to_x(jx, True).start()
            for jy in inner_y:
                item.to_y(jy, True).start()
            item.to_core(0, 0, True).start()

        @pl.when(k >= pieces)
        def arrive():
            item.landed().wait_recv()
            if chain:
                @pl.when((level < z) & (z + 1 < members))
                def onward():
                    item.up().start()

                @pl.when((level > z) & (z > 0))
                def back():
                    item.down().start()
            else:
                @pl.when(k + pieces < items)
                def following():
                    Item(k + pieces).straight().start()

            for jx in inner_x:
                item.to_x(jx).start()
            for jy in inner_y:
                item.to_y(jy).start()
            item.to_core(0, 0).start()

    def edges(k):
        item = Item(k)
        for jx in inner_x:
            item.to_x(jx).wait_recv()

            @pl.when(item.mine & item.even)
            def pass_a():
                for jy in inner_y:
                    item.corner_a(jx, jy).start()

            item.to_core(jx, 0).start()
        for jy in inner_y:
            item.to_y(jy).wait_recv()

            @pl.when(item.mine & jnp.logical_not(item.even))
            def pass_b():
                for jx in inner_x:
                    item.corner_b(jx, jy).start()

            item.to_core(0, jy).start()

    def corners(k):
        item = Item(k)

        @pl.when(item.mine)
        def mine_now():
            for jx in inner_x:
                for jy in inner_y:
                    item.corner_a(jx, jy).wait_recv()
                    if chain:
                        item.corner_z(jx, jy).start()
                    item.to_core(jx, jy).start()

    def handed(k):
        item = Item(k)

        @pl.when(jnp.logical_not(item.mine))
        def from_partner():
            for jx in inner_x:
                for jy in inner_y:
                    item.corner_z(jx, jy).wait_recv()
                    item.to_core(jx, jy).start()

    spots = xs * ys
    lag_edge, lag_corner = (2, 4) if chain else (1, 3)
    lag_handed = pieces + 6 if chain else lag_corner
    lag_end = lag_handed + 1

    def tick(t, carry):
        @pl.when(t < items)
        def arrivals():
            columns(t)

        @pl.when((t >= lag_edge) & (t < items + lag_edge))
        def sides():
            edges(t - lag_edge)

        @pl.when((t >= lag_corner) & (t < items + lag_corner))
        def far():
            corners(t - lag_corner)

        if chain:
            @pl.when((t >= lag_handed) & (t < items + lag_handed))
            def others():
                handed(t - lag_handed)

        def visit(e, carry):
            jc = lax.div(e, spots)
            spot = lax.rem(e, spots)
            jx, jy = lax.rem(spot, xs), lax.div(spot, xs)
            far = jnp.minimum(jx, 1) + jnp.minimum(jy, 1)
            lag = jnp.where(far == 0, 1, jnp.where(far == 1, lag_edge + 1, lag_end))
            k = t - lag

            @pl.when((k >= 0) & (k < items))
            def valid():
                item = Item(k)

                @pl.when(jc == 1)
                def shared():
                    item.to_core(jx, jy).wait_recv()

                if consume is not None:
                    consume(place.block(jx, jy, item.level, jc), item.level, item.piece)

            return carry

        return lax.fori_loop(0, 2 * spots, visit, carry)

    if ready is not None:
        own.wait()
        ready()
    lax.fori_loop(0, items + lag_end, tick, 0)

    def close(k, carry):
        item = Item(k)
        level = item.level
        if chain:
            @pl.when((level <= z) & (z + 1 < members))
            def onward():
                item.up().wait_send()

            @pl.when((level >= z) & (z > 0))
            def back():
                item.down().wait_send()
        else:
            @pl.when(k >= pieces)
            def sent():
                item.straight().wait_send()

        for jx in inner_x:
            item.to_x(jx).wait_send()
        for jy in inner_y:
            item.to_y(jy).wait_send()
        for jx in range(xs):
            for jy in range(ys):
                item.to_core(jx, jy).wait_send()

        @pl.when(item.mine)
        def mine_done():
            for jx in inner_x:
                for jy in inner_y:
                    item.corner_a(jx, jy).wait_send()
                    if chain:
                        item.corner_z(jx, jy).wait_send()

        return carry

    lax.fori_loop(0, items, close, 0)
    if ready is None:
        own.wait()


def spread_kernel(groups, members, chain, pieces, src, out, *sems):
    place = Place(groups, members)
    greet(place)
    spread_body(place, chain, pieces, src, out, sems, None)


def spread(src, groups, members, collective_id, chain, pieces):
    count, rows, width = src.shape
    return pl.pallas_call(
        functools.partial(spread_kernel, groups, members, chain, pieces),
        out_shape=jax.ShapeDtypeStruct((groups * members, rows, width), src.dtype),
        in_specs=[pl.BlockSpec(memory_space=pl.ANY)],
        out_specs=pl.BlockSpec(memory_space=pl.ANY),
        scratch_shapes=spread_sems(groups, members, pieces),
        compiler_params=pltpu.CompilerParams(collective_id=collective_id, has_side_effects=True),
        cost_estimate=pl.CostEstimate(
            flops=0, bytes_accessed=4 * groups * members * rows * width, transcendentals=0
        ),
    )(src)


def tile_of(part_rows):
    return TILE if part_rows % TILE == 0 else part_rows


def opening_kernel(groups, members, facts_ref, table_ref, facts_out, low_ref, own_sem, send_sems, recv_sems):
    devices = groups * members
    tiles = pl.num_programs(1)
    step = pl.program_id(0) * tiles + pl.program_id(1)
    last = pl.num_programs(0) * tiles - 1
    me = lax.axis_index("grp") * members + lax.axis_index("cli")

    def other(j):
        return lax.rem(me + j, devices)

    def place(device):
        return (lax.div(device, members), lax.rem(device, members))

    def give(j):
        return pltpu.make_async_remote_copy(
            src_ref=facts_ref, dst_ref=facts_out.at[me], send_sem=send_sems.at[j], recv_sem=recv_sems.at[j],
            device_id=place(other(j)), device_id_type=MESH,
        )

    own = pltpu.make_async_copy(facts_ref, facts_out.at[me], own_sem)

    @pl.when(step == 0)
    def begin():
        barrier = pltpu.get_barrier_semaphore()

        def hello(j, carry):
            pl.semaphore_signal(barrier, inc=1, device_id=place(other(j)), device_id_type=MESH)
            return carry

        own.start()
        lax.fori_loop(1, devices, hello, 0)

    @pl.when(step == last // 2)
    def exchange():
        def start(j, carry):
            give(j).start()
            return carry

        pl.semaphore_wait(pltpu.get_barrier_semaphore(), devices - 1)
        lax.fori_loop(1, devices, start, 0)

    low_ref[...] = table_ref[...].astype(low_ref.dtype)

    @pl.when(step == last)
    def end():
        def finish(j, carry):
            give(j).wait_send()
            pltpu.make_async_remote_copy(
                src_ref=facts_ref, dst_ref=facts_out.at[lax.rem(me + devices - j, devices)],
                send_sem=send_sems.at[j], recv_sem=recv_sems.at[j], device_id=place(other(j)), device_id_type=MESH,
            ).wait_recv()
            return carry

        lax.fori_loop(1, devices, finish, 0)
        own.wait()


def opening(facts, table, groups, members, collective_id):
    devices = groups * members
    models, part_rows, width = table.shape
    tile_rows = tile_of(part_rows)
    piece = pl.BlockSpec((1, tile_rows, width), lambda m, t: (m, t, 0))
    anywhere = pl.BlockSpec(memory_space=pl.ANY)
    dma = pltpu.SemaphoreType.DMA
    return pl.pallas_call(
        functools.partial(opening_kernel, groups, members),
        out_shape=(
            jax.ShapeDtypeStruct((devices,) + facts.shape, facts.dtype),
            jax.ShapeDtypeStruct(table.shape, jnp.bfloat16),
        ),
        grid=(models, part_rows // tile_rows),
        in_specs=[anywhere, piece],
        out_specs=(anywhere, piece),
        scratch_shapes=[dma, dma((devices,)), dma((devices,))],
        compiler_params=pltpu.CompilerParams(collective_id=collective_id, has_side_effects=True),
        cost_estimate=pl.CostEstimate(flops=0, bytes_accessed=6 * table.size, transcendentals=0),
    )(facts, table)


def score_kernel(groups, members, share, pieces, src, table, target, out, answer, *rest):
    part, pool, stat, inbox, part_sem, out_sems, go_send, go_recv, back_send, back_recv = rest[:10]
    sems = rest[10:]
    devices = groups * members
    place = Place(groups, members)
    load_table = pltpu.make_async_copy(table, part, part_sem)
    load_table.start()
    greet_all(devices, members)
    rows = pool.shape[1]
    size = rows // pieces

    def keep(block, piece):
        here = pl.ds(pl.multiple_of(piece * size, size), size)
        return pltpu.make_async_copy(pool.at[block, here], out.at[block, here], out_sems.at[block, piece])

    def consume(block, level, piece):
        keep(block, piece).start()
        here = pl.ds(pl.multiple_of(piece * size, size), size)
        model = lax.div(level, share)
        wanted = target[lax.div(block, members) * share + lax.rem(level, share), :, here]
        outs = pool[block, here]
        part_rows = part.shape[1]
        tile = tile_of(part_rows)
        marks = lax.broadcasted_iota(jnp.int32, (tile, size), 0)
        tops, totals, hits = [], [], []
        for first in range(0, part_rows, tile):
            logits = project(part[model, pl.ds(first, tile)], outs)
            hit = jnp.where(marks == wanted - first, logits, 0.0).reshape(-1, 8, size)
            hits.append(jnp.sum(hit, axis=0))
            logits = logits.reshape(-1, 8, size)
            top = jnp.max(logits, axis=0)
            tops.append(top)
            totals.append(jnp.sum(jnp.exp(logits - top[None]), axis=0))
        highest = jnp.max(functools.reduce(jnp.maximum, tops), axis=0, keepdims=True)
        total = sum(t * jnp.exp(m - highest) for t, m in zip(totals, tops))
        stat[block, 0:1, here] = highest + jnp.log(jnp.sum(total, axis=0, keepdims=True))
        stat[block, 1:2, here] = jnp.sum(sum(hits), axis=0, keepdims=True)

    spread_body(place, True, pieces, src, pool, sems, consume, load_table.wait)

    me = place.block(0, 0, place.cli)

    def device(index):
        return (lax.div(index, members), lax.rem(index, members))

    def ahead(j):
        return lax.rem(me + j, devices)

    def behind(j):
        return lax.rem(me + devices - j, devices)

    def go(j, source, target):
        return pltpu.make_async_remote_copy(
            src_ref=stat.at[source], dst_ref=inbox.at[target], send_sem=go_send.at[j], recv_sem=go_recv.at[j],
            device_id=device(ahead(j)), device_id_type=MESH,
        )

    def back(j, source):
        return pltpu.make_async_remote_copy(
            src_ref=answer.at[source], dst_ref=answer.at[source], send_sem=back_send.at[j],
            recv_sem=back_recv.at[j], device_id=device(ahead(j)), device_id_type=MESH,
        )

    def loop(step):
        def run(j, carry):
            step(j)
            return carry

        lax.fori_loop(1, devices, run, 0)

    loop(lambda j: go(j, ahead(j), me).start())
    inbox[me] = stat[me]
    loop(lambda j: go(j, me, behind(j)).wait_recv())
    logs = inbox[:, 0, :]
    top = jnp.max(logs, axis=0, keepdims=True)
    log_total = top + jnp.log(jnp.sum(jnp.exp(logs - top), axis=0, keepdims=True))
    answer[me, 0:1, :] = log_total
    answer[me, 1:2, :] = log_total - jnp.sum(inbox[:, 1, :], axis=0, keepdims=True)
    loop(lambda j: back(j, me).start())
    loop(lambda j: back(j, behind(j)).wait_recv())
    loop(lambda j: go(j, ahead(j), me).wait_send())
    loop(lambda j: back(j, me).wait_send())

    def close(block, carry):
        for piece in range(pieces):
            keep(block, piece).wait()
        return carry

    lax.fori_loop(0, groups * members, close, 0)


def spread_score(src, table_low, target_blocks, groups, members, share, collective_id, pieces=2):
    _, rows, width = src.shape
    blocks = groups * members
    return pl.pallas_call(
        functools.partial(score_kernel, groups, members, share, pieces),
        out_shape=(
            jax.ShapeDtypeStruct((blocks, rows, width), src.dtype),
            jax.ShapeDtypeStruct((blocks, 2, rows), jnp.float32),
        ),
        in_specs=[
            pl.BlockSpec(memory_space=pl.ANY),
            pl.BlockSpec(memory_space=pl.ANY),
            pl.BlockSpec(memory_space=pltpu.VMEM),
        ],
        out_specs=(pl.BlockSpec(memory_space=pl.ANY), pl.BlockSpec(memory_space=pltpu.VMEM)),
        scratch_shapes=[
            pltpu.VMEM(table_low.shape, table_low.dtype),
            pltpu.VMEM((blocks, rows, width), src.dtype),
            pltpu.VMEM((blocks, 2, rows), jnp.float32),
            pltpu.VMEM((blocks, 2, rows), jnp.float32),
            pltpu.SemaphoreType.DMA,
            pltpu.SemaphoreType.DMA((blocks, pieces)),
        ]
        + [pltpu.SemaphoreType.DMA((blocks,))] * 4
        + spread_sems(groups, members, pieces),
        compiler_params=pltpu.CompilerParams(
            collective_id=collective_id, has_side_effects=True, vmem_limit_bytes=60 * MIB
        ),
        cost_estimate=pl.CostEstimate(
            flops=2 * blocks * rows * table_low.shape[1] * width,
            bytes_accessed=2 * blocks * rows * width * 2,
            transcendentals=blocks * rows * table_low.shape[1],
        ),
    )(src, table_low, target_blocks)


def stats_kernel(outs_ref, table_ref, target_ref, stat_ref):
    logits = project(table_ref[0], outs_ref[0])
    highest = jnp.max(logits, axis=0, keepdims=True)
    total = jnp.sum(jnp.exp(logits - highest), axis=0, keepdims=True)
    rows = lax.broadcasted_iota(jnp.int32, logits.shape, 0)
    hit = jnp.sum(jnp.where(rows == target_ref[0], logits, 0.0), axis=0, keepdims=True)
    stat_ref[0, 0:1, :] = highest + jnp.log(total)
    stat_ref[0, 1:2, :] = hit


def head_stats(outs_all, table_low, target_blocks, groups, members, share):
    blocks, rows, width = outs_all.shape
    part_rows = table_low.shape[1]
    return pl.pallas_call(
        stats_kernel,
        out_shape=jax.ShapeDtypeStruct((blocks, 2, rows), jnp.float32),
        grid=(members, groups),
        in_specs=[
            pl.BlockSpec((1, rows, width), lambda z, g: (g * members + z, 0, 0)),
            pl.BlockSpec((1, part_rows, width), lambda z, g: (z // share, 0, 0)),
            pl.BlockSpec((1, 1, rows), lambda z, g: (g * share + z % share, 0, 0)),
        ],
        out_specs=pl.BlockSpec((1, 2, rows), lambda z, g: (g * members + z, 0, 0)),
        compiler_params=pltpu.CompilerParams(vmem_limit_bytes=56 * MIB),
        cost_estimate=pl.CostEstimate(
            flops=2 * blocks * rows * part_rows * width,
            bytes_accessed=2 * outs_all.size + 2 * table_low.size,
            transcendentals=blocks * rows * part_rows,
        ),
    )(outs_all, table_low, target_blocks)


def collect_kernel(groups, members, source, out, work, from_core, from_x, from_y, then_y, then_x, from_z, *sems):
    (load_sem, core_send, core_recv, x_send, x_recv, y_send, y_recv, yy_send, yy_recv, xx_send, xx_recv, z_send,
     z_recv, g_send, g_recv) = sems
    place = Place(groups, members)
    greet(place)
    xs, ys = place.xs, place.ys
    half = members // 2
    z = place.cli
    order = sorted(
        ((jx, jy) for jx in range(xs) for jy in range(ys)), key=lambda spot: -(spot[0] > 0) - (spot[1] > 0)
    )
    started = []

    def send(source_ref, target_ref, send_sem, recv_sem, device):
        copy = pltpu.make_async_remote_copy(
            src_ref=source_ref, dst_ref=target_ref, send_sem=send_sem, recv_sem=recv_sem, device_id=device,
            device_id_type=MESH,
        )
        copy.start()
        started.append(copy)

    def arrival(target_ref, send_sem, recv_sem, device):
        pltpu.make_async_remote_copy(
            src_ref=target_ref, dst_ref=target_ref, send_sem=send_sem, recv_sem=recv_sem, device_id=device,
            device_id_type=MESH,
        ).wait_recv()

    def add(ref, others):
        total = ref[...].astype(jnp.float32)
        for other in others:
            total = total + other[...].astype(jnp.float32)
        ref[...] = total.astype(ref.dtype)

    def clients(p):
        return (p, p + half)

    spots = [(jy * xs + jx, jx, jy) for jx, jy in order]
    loads = {}
    for p in range(half):
        for k, jx, jy in spots:
            for c in clients(p):
                send(
                    source.at[place.group(jx, jy, 1) * members + c], from_core.at[k, c], core_send.at[k, c],
                    core_recv.at[k, c], place.peer(jc=1),
                )
                loads[k, c] = pltpu.make_async_copy(
                    source.at[place.group(jx, jy, 0) * members + c], work.at[k, c], load_sem.at[k, c]
                )
                loads[k, c].start()
    for p in range(half):
        a, b = clients(p)
        for k, jx, jy in spots:
            for c in (a, b):
                loads[k, c].wait()
                arrival(from_core.at[k, c], core_send.at[k, c], core_recv.at[k, c], place.peer(jc=1))
                add(work.at[k, c], [from_core.at[k, c]])
            if jx:
                send(work.at[k, a], from_x.at[p, jx, jy], x_send.at[p, jx, jy], x_recv.at[p, jx, jy], place.peer(jx=jx))
            if jy:
                send(work.at[k, b], from_y.at[p, jx, jy], y_send.at[p, jx, jy], y_recv.at[p, jx, jy], place.peer(jy=jy))

    def second(p):
        a, b = clients(p)
        for jy in reversed(range(ys)):
            k = jy * xs
            for jx in range(1, xs):
                arrival(from_x.at[p, jx, jy], x_send.at[p, jx, jy], x_recv.at[p, jx, jy], place.peer(jx=jx))
            add(work.at[k, a], [from_x.at[p, jx, jy] for jx in range(1, xs)])
            if jy:
                send(work.at[k, a], then_y.at[p, jy], yy_send.at[p, jy], yy_recv.at[p, jy], place.peer(jy=jy))
        for jx in reversed(range(xs)):
            for jy in range(1, ys):
                arrival(from_y.at[p, jx, jy], y_send.at[p, jx, jy], y_recv.at[p, jx, jy], place.peer(jy=jy))
            add(work.at[jx, b], [from_y.at[p, jx, jy] for jy in range(1, ys)])
            if jx:
                send(work.at[jx, b], then_x.at[p, jx], xx_send.at[p, jx], xx_recv.at[p, jx], place.peer(jx=jx))

    def third(p):
        a, b = clients(p)
        for jy in range(1, ys):
            arrival(then_y.at[p, jy], yy_send.at[p, jy], yy_recv.at[p, jy], place.peer(jy=jy))
        add(work.at[0, a], [then_y.at[p, jy] for jy in range(1, ys)])
        for jx in range(1, xs):
            arrival(then_x.at[p, jx], xx_send.at[p, jx], xx_recv.at[p, jx], place.peer(jx=jx))
        add(work.at[0, b], [then_x.at[p, jx] for jx in range(1, xs)])
        for c in (a, b):
            @pl.when(z != c)
            def give():
                pltpu.make_async_remote_copy(
                    src_ref=work.at[0, c], dst_ref=from_z.at[z], send_sem=z_send.at[c], recv_sem=z_recv.at[z],
                    device_id=place.level(c), device_id_type=MESH,
                ).start()

    for p in range(half + 1):
        if p < half:
            second(p)
        if p:
            third(p - 1)
    total = work[0, z].astype(jnp.float32)
    for j in range(1, members):
        level = lax.rem(z + members - j, members)
        arrival(from_z.at[level], z_send.at[level], z_recv.at[level], place.level(level))
        total = total + from_z[level].astype(jnp.float32)
    out[z] = total.astype(out.dtype)
    for j in range(1, members):
        send(out.at[z], out.at[z], g_send.at[j], g_recv.at[j], place.level(lax.rem(z + j, members)))
    for j in range(1, members):
        level = lax.rem(z + members - j, members)
        arrival(out.at[level], g_send.at[j], g_recv.at[j], place.level(level))
    for copy in started:
        copy.wait_send()
    for c in range(members):
        @pl.when(z != c)
        def given():
            pltpu.make_async_remote_copy(
                src_ref=work.at[0, c], dst_ref=from_z.at[z], send_sem=z_send.at[c], recv_sem=z_recv.at[z],
                device_id=place.level(c), device_id_type=MESH,
            ).wait_send()


def collect(parts, groups, members, collective_id):
    _, seq_len, width = parts.shape
    xs, ys, half = groups // 4, 2, members // 2
    dma = pltpu.SemaphoreType.DMA

    def held(*shape):
        return pltpu.VMEM(shape + (seq_len, width), parts.dtype)

    return pl.pallas_call(
        functools.partial(collect_kernel, groups, members),
        out_shape=jax.ShapeDtypeStruct((members, seq_len, width), parts.dtype),
        in_specs=[pl.BlockSpec(memory_space=pl.ANY)],
        out_specs=pl.BlockSpec(memory_space=pltpu.VMEM),
        scratch_shapes=[
            held(xs * ys, members),
            held(xs * ys, members),
            held(half, xs, ys),
            held(half, xs, ys),
            held(half, ys),
            held(half, xs),
            held(members),
        ]
        + [dma((xs * ys, members))] * 3
        + [dma((half, xs, ys))] * 4
        + [dma((half, ys))] * 2
        + [dma((half, xs))] * 2
        + [dma((members,))] * 4,
        compiler_params=pltpu.CompilerParams(
            collective_id=collective_id, has_side_effects=True, vmem_limit_bytes=56 * MIB
        ),
        cost_estimate=pl.CostEstimate(
            flops=0, bytes_accessed=4 * groups * members * seq_len * width, transcendentals=0
        ),
    )(parts)


def unpack_kernel(start, part, at_ref, pool_ref, weights_ref, rows_ref):
    step = pl.program_id(0)
    owners, slab, width = pool_ref.shape
    weights_ref[...] = jnp.concatenate([pool_ref[j, :part] for j in range(owners)], axis=0)
    count = slab - start
    columns = lax.broadcasted_iota(jnp.int32, (1, count), 1) + start
    columns = jnp.concatenate([columns + j * slab for j in range(owners)], axis=1)
    hits = (columns == at_ref[...] - step * owners * slab).astype(jnp.float32).astype(jnp.bfloat16)
    found = product(hits, jnp.concatenate([pool_ref[j, start:] for j in range(owners)], axis=0))

    @pl.when(step == 0)
    def begin():
        rows_ref[...] = found

    @pl.when(step > 0)
    def more():
        rows_ref[...] += found


def unpack(pool, part, at):
    devices, slab, width = pool.shape
    owners = max(4, 8 // math.gcd(part, 8))
    start = part // 16 * 16
    tokens = at.shape[0]
    return pl.pallas_call(
        functools.partial(unpack_kernel, start, part),
        out_shape=(
            jax.ShapeDtypeStruct((devices * part, width), pool.dtype),
            jax.ShapeDtypeStruct((tokens, width), jnp.float32),
        ),
        grid=(devices // owners,),
        in_specs=[
            pl.BlockSpec((tokens, 1), lambda i: (0, 0)),
            pl.BlockSpec((owners, slab, width), lambda i: (i, 0, 0)),
        ],
        out_specs=(
            pl.BlockSpec((owners * part, width), lambda i: (i, 0)),
            pl.BlockSpec((tokens, width), lambda i: (0, 0)),
        ),
        compiler_params=pltpu.CompilerParams(vmem_limit_bytes=40 * MIB),
        cost_estimate=pl.CostEstimate(
            flops=2 * devices * tokens * (slab - start) * width,
            bytes_accessed=4 * pool.size,
            transcendentals=0,
        ),
    )(at, pool)


def back_kernel(
    model_ref, fresh_ref, used_ref, piece_ref, place_ref, *rest
):
    pieces = rest[:QUAD]
    table_ref, info_ref, target_ref, d_outs_ref, grad_ref, held, sems = rest[QUAD:]
    step = pl.program_id(0)
    seq_len = pieces[0].shape[1]
    slot = lax.rem(step, 2)

    def leave(which, where, i):
        return pltpu.make_async_copy(held.at[which, i], d_outs_ref.at[where], sems.at[which, i])

    def settle(which):
        for i in range(QUAD):
            leave(which, 0, i).wait()

    @pl.when(step < used_ref[0])
    def work():
        @pl.when(step >= 2)
        def reuse():
            settle(slot)

        @pl.when(fresh_ref[step] == 1)
        def start():
            grad_ref[...] = jnp.zeros_like(grad_ref)

        outs = jnp.concatenate([piece[0] for piece in pieces], axis=0)
        part_rows = table_ref.shape[1]
        size = tile_of(part_rows)
        d_outs = jnp.zeros(outs.shape, jnp.float32)
        for first_row in range(0, part_rows, size):
            here = pl.ds(first_row, size)
            table_rows = table_ref[0, here]
            logits = project(table_rows, outs)
            rows = lax.broadcasted_iota(jnp.int32, logits.shape, 0) + first_row
            soft = jnp.exp(logits - info_ref[0, 0:1, :])
            soft = jnp.where(rows == target_ref[0], soft - 1.0, soft)
            d_logits = (info_ref[0, 1:2, :] * soft).astype(jnp.bfloat16)
            d_outs = d_outs + outer_rows(d_logits, table_rows)
            grad_ref[0, here] += product(d_logits, outs)
        for i in range(QUAD):
            held[slot, i] = d_outs[i * seq_len : (i + 1) * seq_len].astype(held.dtype)
            leave(slot, place_ref[QUAD * step + i], i).start()

        @pl.when(step == used_ref[0] - 1)
        def drain():
            settle(slot)

            @pl.when(step >= 1)
            def earlier():
                settle(1 - slot)


def head_back(outs_pieces, table_low, model_of, fresh, used, piece_at, place, info, target):
    steps = model_of.shape[0]
    models, part_rows, width = table_low.shape
    seq_len = outs_pieces.shape[1]
    tokens = QUAD * seq_len

    def piece(i):
        return pl.BlockSpec((1, seq_len, width), lambda s, m, f, u, q, p: (q[QUAD * s + i], 0, 0))

    return pl.pallas_call(
        back_kernel,
        out_shape=(
            jax.ShapeDtypeStruct((QUAD * steps, seq_len, width), jnp.bfloat16),
            jax.ShapeDtypeStruct((models, part_rows, width), jnp.float32),
        ),
        grid_spec=pltpu.PrefetchScalarGridSpec(
            num_scalar_prefetch=5,
            grid=(steps,),
            in_specs=[piece(i) for i in range(QUAD)]
            + [
                pl.BlockSpec((1, part_rows, width), lambda s, m, *_: (m[s], 0, 0)),
                pl.BlockSpec((1, 2, tokens), lambda s, *_: (s, 0, 0)),
                pl.BlockSpec((1, 1, tokens), lambda s, *_: (s, 0, 0)),
            ],
            out_specs=(
                pl.BlockSpec(memory_space=pl.ANY),
                pl.BlockSpec((1, part_rows, width), lambda s, m, *_: (m[s], 0, 0)),
            ),
            scratch_shapes=[
                pltpu.VMEM((2, QUAD, seq_len, width), jnp.bfloat16),
                pltpu.SemaphoreType.DMA((2, QUAD)),
            ],
        ),
        compiler_params=pltpu.CompilerParams(vmem_limit_bytes=56 * MIB),
        cost_estimate=pl.CostEstimate(
            flops=6 * steps * tokens * part_rows * width,
            bytes_accessed=4 * steps * tokens * width + 6 * table_low.size,
            transcendentals=steps * tokens * part_rows,
        ),
    )(model_of, fresh, used, piece_at, place, *([outs_pieces] * QUAD), table_low, info, target)


def finish_kernel(
    first_model, start_ref, end_ref, first_ref, second_ref, d_ref, ids_ref, head_ref, table_ref, momentum_ref, *rest
):
    grad_ref, momentum_new_ref, table_new_ref = rest[-3:]
    model = pl.program_id(0) + first_model
    tile_rows = grad_ref.shape[1]
    tokens = ids_ref.shape[2]
    rows = lax.broadcasted_iota(jnp.int32, (tile_rows, tokens), 0) + pl.program_id(1) * tile_rows
    grad_ref[0] = head_ref[0]

    def pair(step, carry):
        hits = (rows == ids_ref[step]).astype(jnp.float32).astype(jnp.bfloat16)
        outs = jnp.concatenate([d_ref[first_ref[step]], d_ref[second_ref[step]]], axis=0)
        grad_ref[0] += product(hits, outs)
        return carry

    lax.fori_loop(start_ref[model], end_ref[model], pair, 0)
    renewed, fresh_table = update(table_ref[0], momentum_ref[0], grad_ref[0], table_rate)
    momentum_new_ref[0] = renewed
    table_new_ref[0] = fresh_table


def finish_table(d_inputs, head_grad, table, momentum, schedule, ids, first_model, count, earlier):
    models, part_rows, width = table.shape
    tile_rows = tile_of(part_rows)
    state = jax.ShapeDtypeStruct(table.shape, jnp.float32)
    piece = pl.BlockSpec((1, tile_rows, width), lambda m, t, *_: (m + first_model, t, 0))
    whole = pl.BlockSpec(memory_space=pltpu.VMEM)
    return pl.pallas_call(
        functools.partial(finish_kernel, first_model),
        out_shape=(state, state, state),
        grid_spec=pltpu.PrefetchScalarGridSpec(
            num_scalar_prefetch=4,
            grid=(count, part_rows // tile_rows),
            in_specs=[whole, whole, piece, piece, piece]
            + [pl.BlockSpec(memory_space=pl.ANY)] * len(earlier),
            out_specs=(piece, piece, piece),
        ),
        input_output_aliases={9 + i: i for i in range(len(earlier))},
        compiler_params=pltpu.CompilerParams(vmem_limit_bytes=56 * MIB),
        cost_estimate=pl.CostEstimate(
            flops=2 * d_inputs.size * part_rows * count // models,
            bytes_accessed=24 * count * part_rows * width,
            transcendentals=0,
        ),
    )(*schedule, d_inputs, ids, head_grad, table, momentum, *earlier)


def body(
    token_ids,
    target_ids,
    segment_ids,
    chosen,
    table,
    table_momentum,
    stack,
    stack_momentum,
    vectors,
    vector_momentum,
):
    both = ("grp", "cli")
    models, block_rows, model_width = table.shape
    stack_part = stack.shape[1]
    seq_len = token_ids.shape[1]
    groups = lax.axis_size("grp")
    members = lax.axis_size("cli")
    devices = groups * members
    share = members // models
    local = members // share
    device_index = lax.axis_index(both)
    group_index = lax.axis_index("grp")
    member_index = lax.axis_index("cli")
    model_own = member_index // share
    part_own = member_index % share
    model_range = jnp.arange(models, dtype=jnp.int32)

    def per_member(rows):
        return jnp.repeat(rows, share, axis=0) if share > 1 else rows

    slab = -(-(stack_part + ROUND_ROWS) // SLAB_STEP) * SLAB_STEP
    round_rows = slab - stack_part

    facts = jnp.concatenate([token_ids[0], target_ids[0], segment_ids[0], chosen])
    facts = jnp.pad(facts, (0, -facts.size % LANES))[None]
    facts, table_low = opening(facts, table, groups, members, 5)
    facts = facts[:, 0]
    tokens = facts[:, :seq_len]
    targets = facts[:, seq_len : 2 * seq_len]
    segments = facts[:, 2 * seq_len : 3 * seq_len]
    choices = facts[:, 3 * seq_len]
    valid = jnp.concatenate(
        [
            (segments[:, :-1] == segments[:, 1:]).astype(jnp.float32),
            jnp.zeros((devices, 1), jnp.float32),
        ],
        axis=1,
    )
    counts = jnp.sum(valid, axis=1)
    choice_table = (choices[:, None] == model_range[None, :]).astype(jnp.float32)
    totals = jnp.sum(choice_table * counts[:, None], axis=0)
    total_of = jnp.sum(choice_table * totals[None, :], axis=1)

    fine = 16 if block_rows % 64 else 64
    coarse = block_rows // fine
    flat_tokens = tokens.reshape(-1)
    high_hot = (
        (flat_tokens // fine)[:, None] == jnp.arange(devices * coarse, dtype=jnp.int32)[None, :]
    ).astype(jnp.bfloat16)
    low_hot = ((flat_tokens % fine)[:, None] == jnp.arange(fine, dtype=jnp.int32)[None, :]).astype(
        jnp.bfloat16
    )
    seen = (outer_rows(high_hot, low_hot) > 0).astype(jnp.float32)
    before = product(
        seen.astype(jnp.bfloat16),
        jnp.triu(jnp.ones((fine, fine), jnp.bfloat16), 1),
    )
    sums = jnp.sum(seen, axis=1).reshape(devices, coarse)
    uniques = jnp.sum(sums, axis=1)
    ahead = jnp.sum(
        jnp.where(
            jnp.arange(coarse)[None, None, :] < jnp.arange(coarse)[None, :, None],
            sums[:, None, :],
            0.0,
        ),
        axis=2,
    )
    places = before + ahead.reshape(-1, 1)
    rounds = jnp.max(jnp.ceil(uniques / round_rows)).astype(jnp.int32)
    own_places = lax.dynamic_slice(places, (device_index * coarse, 0), (coarse, fine)).reshape(-1)
    own_seen = lax.dynamic_slice(seen, (device_index * coarse, 0), (coarse, fine)).reshape(-1)
    own_places = jnp.where(own_seen > 0, own_places, -1.0).astype(jnp.int32)
    first_client = group_index * members + part_own * local
    my_tokens = lax.dynamic_slice(tokens, (first_client, 0), (local, seq_len)).reshape(-1)
    my_segments = lax.dynamic_slice(segments, (first_client, 0), (local, seq_len))
    my_choices = lax.dynamic_slice(choices, (first_client,), (local,))
    my_high = (
        (my_tokens // fine)[:, None] == jnp.arange(devices * coarse, dtype=jnp.int32)[None, :]
    ).astype(jnp.bfloat16)
    my_low = (my_tokens % fine)[:, None] == jnp.arange(fine, dtype=jnp.int32)[None, :]
    split_places = jnp.concatenate(
        [jnp.floor(places / 64.0), places - 64.0 * jnp.floor(places / 64.0)], axis=1
    ).astype(jnp.bfloat16)
    picked_places = product(my_high, split_places)
    picked_places = 64.0 * picked_places[:, :fine] + picked_places[:, fine:]
    my_places = jnp.sum(jnp.where(my_low, picked_places, 0.0), axis=1).astype(jnp.int32)
    my_owner = my_tokens // block_rows

    def offered(start):
        wanted = jnp.arange(round_rows, dtype=jnp.int32) + start
        pick = (own_places[None, :] == wanted[:, None]).astype(jnp.bfloat16)
        rows = jnp.einsum("ur,krd->kud", pick, table_low, preferred_element_type=jnp.float32)
        return rows.astype(jnp.bfloat16)

    def inside(start):
        offset = my_places - start
        return ((offset >= 0) & (offset < round_rows), offset)

    def another(carry):
        index, embedded = carry
        start = index * round_rows
        turned = lax.all_to_all(per_member(offered(start)), "cli", 0, 0, tiled=True)
        pool = lax.all_gather(turned, "grp", axis=0, tiled=True).reshape(-1, model_width)
        here, offset = inside(start)
        found = jnp.take(pool, jnp.where(here, my_owner * round_rows + offset, 0), axis=0)
        return (index + 1, jnp.where(here[:, None], found.astype(jnp.float32), embedded))

    slabs = jnp.concatenate([stack.astype(jnp.bfloat16), offered(0)], axis=1)
    pool = spread(per_member(slabs), groups, members, 1, False, 2)
    here, offset = inside(0)
    at = jnp.where(here, my_owner * slab + stack_part + offset, -1)
    weights, embedded = unpack(pool, stack_part, at[:, None])
    _, embedded = lax.while_loop(
        lambda carry: carry[0] < rounds, another, (jnp.int32(1), embedded)
    )
    vector_one = lax.dynamic_index_in_dim(vectors, model_own, 0, keepdims=False)
    inputs = embedded + jnp.tile(weights[12 * model_width :].astype(jnp.float32), (local, 1))
    saved = layer_forward(weights, vector_one, inputs, my_segments)
    normed_out = saved[11]

    target_local = targets - device_index * block_rows
    target_local = jnp.where((target_local >= 0) & (target_local < block_rows), target_local, -1)
    target_blocks = target_local.reshape(groups * share, 1, local * seq_len)
    if devices * normed_out.size * 2 <= POOL_BYTES:
        outs_all, everything = spread_score(
            normed_out[None], table_low, target_blocks, groups, members, share, 2
        )
    else:
        outs_all = spread(normed_out[None], groups, members, 2, True, 2)
        stats = head_stats(outs_all, table_low, target_blocks, groups, members, share)
        shares = lax.all_to_all(stats, both, 0, 0, tiled=True)
        log_total = jax.nn.logsumexp(shares[:, 0], axis=0)
        token_loss = log_total - jnp.sum(shares[:, 1], axis=0)
        everything = share_all(jnp.stack([log_total, token_loss]), both, devices)
    everything = (
        everything.reshape(groups, models, share, 2, local, seq_len)
        .transpose(3, 1, 0, 2, 4, 5)
        .reshape(2, models, devices, seq_len)
    )
    all_losses = jnp.sum(everything[1] * valid[None], axis=2)
    loss = jnp.sum(choice_table.T * all_losses / total_of[None, :])
    client_losses = lax.dynamic_slice(
        (all_losses / counts[None, :]).T, (device_index, 0), (1, models)
    )
    chosen_total = jnp.sum(choice_table.T[:, :, None] * everything[0], axis=0)

    numbers = jnp.sum(choice_table, axis=0)
    padded = QUAD * jnp.ceil(numbers / QUAD)
    offsets = jnp.cumsum(padded) - padded
    earlier = (
        jnp.arange(devices)[None, :] < jnp.arange(devices)[:, None]
    ) & (choices[None, :] == choices[:, None])
    slot_of = jnp.sum(choice_table * offsets[None, :], axis=1) + jnp.sum(
        earlier.astype(jnp.float32), axis=1
    )
    steps = (devices + (QUAD - 1) * models) // QUAD
    slots = QUAD * steps
    tokens_step = QUAD * seq_len
    at_slot = jnp.arange(slots)[:, None] == slot_of.astype(jnp.int32)[None, :]
    filled = jnp.any(at_slot, axis=1)
    client_at = jnp.sum(jnp.where(at_slot, jnp.arange(devices)[None, :], 0), axis=1).astype(
        jnp.int32
    )
    step_start = float(QUAD) * jnp.arange(steps)
    used = (jnp.sum(padded) / QUAD).astype(jnp.int32)[None]
    model_of = (
        jnp.sum((step_start[:, None] >= offsets[None, :]).astype(jnp.int32), axis=1) - 1
    ).astype(jnp.int32)
    fresh = jnp.concatenate(
        [jnp.ones((1,), jnp.int32), (model_of[1:] != model_of[:-1]).astype(jnp.int32)]
    )
    within = client_at % members
    piece_at = (
        (client_at // members * members + jnp.repeat(model_of, QUAD) * share + within // local) * local
        + within % local
    ).astype(jnp.int32)
    weight_rows = valid / total_of[:, None]
    slot_log = jnp.where(filled[:, None], jnp.take(chosen_total, client_at, axis=0), 1e30)
    slot_weight = jnp.where(filled[:, None], jnp.take(weight_rows, client_at, axis=0), 0.0)
    slot_info = jnp.stack(
        [slot_log.reshape(steps, tokens_step), slot_weight.reshape(steps, tokens_step)], axis=1
    )
    slot_target = jnp.where(filled[:, None], jnp.take(target_local, client_at, axis=0), -1)
    spare = devices + jnp.cumsum(1 - filled.astype(jnp.int32)) - 1
    d_outs, head_grad = head_back(
        outs_all.reshape(-1, seq_len, model_width),
        table_low,
        model_of,
        fresh,
        used,
        piece_at,
        jnp.where(filled, client_at, spare).astype(jnp.int32),
        slot_info,
        slot_target.reshape(steps, 1, tokens_step),
    )
    d_group = collect(d_outs, groups, members, 4)
    d_mine = lax.dynamic_slice(
        d_group, (part_own * local, 0, 0), (local, seq_len, model_width)
    ).astype(jnp.float32)
    d_final = jnp.where((my_choices == model_own)[:, None, None], d_mine, 0.0).reshape(
        local * seq_len, model_width
    )
    pairs, grad_places, vector_rows, d_inputs = layer_backward(
        weights, vector_one, inputs, my_segments, saved, d_final
    )
    d_wide = d_inputs.astype(jnp.bfloat16)
    if share > 1:
        d_wide = lax.dynamic_update_slice(
            jnp.zeros((members * seq_len, model_width), jnp.bfloat16),
            d_wide,
            (part_own * local * seq_len, 0),
        )
    d_wide, pairs, vector_rows = lax.optimization_barrier((d_wide, pairs, vector_rows))
    d_turned = lax.all_to_all(
        d_wide.reshape(members, seq_len, model_width), "cli", 0, 0, tiled=True
    )
    stack_rows = jnp.concatenate(
        [outer_rows(left, right).astype(jnp.bfloat16) for left, right in pairs]
        + [grad_places.astype(jnp.bfloat16)],
        axis=0,
    )
    stack_rows, d_turned = lax.optimization_barrier((stack_rows, d_turned))
    stack_sum = lax.psum_scatter(stack_rows, "grp", scatter_dimension=0, tiled=True)
    d_client = jnp.sum(d_turned.astype(jnp.float32), axis=0, keepdims=True).astype(jnp.bfloat16)
    d_all = spread(d_client, groups, members, 3, True, 2)
    d_all, vector_rows = lax.optimization_barrier((d_all, vector_rows))
    vector_piece = vector_rows.size // groups
    vector_part = lax.all_to_all(
        vector_rows.reshape(groups, vector_piece), "grp", 0, 0, tiled=True
    )

    token_local = tokens - device_index * block_rows
    token_local = jnp.where((token_local >= 0) & (token_local < block_rows), token_local, -1)
    slot_token = jnp.where(filled[:, None], jnp.take(token_local, client_at, axis=0), -1)
    pair_start = (offsets / 2.0).astype(jnp.int32)
    pair_end = pair_start + jnp.ceil(numbers / 2.0).astype(jnp.int32)
    schedule = (pair_start, pair_end, client_at[0::2], client_at[1::2])
    slot_token = slot_token.reshape(slots // 2, 1, 2 * seq_len)
    lead = models // 2

    states = finish_table(d_all, head_grad, table, table_momentum, schedule, slot_token, 0, lead, ())
    stack_sum, states, vector_part = lax.optimization_barrier((stack_sum, states, vector_part))
    stack_back = lax.all_to_all(
        stack_sum.reshape(members, stack_part, model_width), "cli", 0, 0, tiled=True
    ).astype(jnp.float32)
    stack_grad = jnp.sum(stack_back.reshape(models, share, stack_part, model_width), axis=1)
    table_grad, table_momentum_new, table_new = finish_table(
        d_all, head_grad, table, table_momentum, schedule, slot_token, lead, models - lead, states
    )
    stack_grad, vector_part = lax.optimization_barrier((stack_grad, vector_part))
    vector_parts = share_all(jnp.sum(vector_part, axis=0), both, devices)
    vector_grad = jnp.sum(vector_parts.reshape(groups, models, share, vector_piece), axis=2)
    vector_grad = vector_grad.transpose(1, 0, 2).reshape(vectors.shape)
    stack_momentum_new, stack_new = update(stack, stack_momentum, stack_grad, stack_rate)
    vector_momentum_new, vector_new = update(vectors, vector_momentum, vector_grad, vector_rate)
    return (
        loss,
        client_losses,
        table_grad,
        table_momentum_new,
        table_new,
        stack_grad,
        stack_momentum_new,
        stack_new,
        vector_grad,
        vector_momentum_new,
        vector_new,
    )


def solution(mesh):
    rows = P(("grp", "cli"), None)
    parts = P(None, ("grp", "cli"), None)
    return jax.shard_map(
        body,
        mesh=mesh,
        in_specs=(rows, rows, rows, P(("grp", "cli")), parts, parts, parts, parts, P(), P()),
        out_specs=(P(), rows, parts, parts, parts, parts, parts, parts, P(), P(), P()),
        check_vma=False,
    )
```

```python
import functools
import math

import jax
import jax.numpy as jnp
from jax import lax
from jax.experimental import pallas as pl
from jax.experimental.pallas import tpu as pltpu
from jax.sharding import PartitionSpec as P

HEADS = 12
HEAD_DIM = 64


epsilon = 1e-05
momentum_decay = 0.9
table_rate = 4.0
stack_rate = 4.0
vector_rate = 50.0

ROUND_ROWS = 104
SLAB_STEP = 16
TILE = 400
LANES = 128
QUAD = 4
MIB = 1 << 20
POOL_BYTES = 32 * MIB
MESH = pl.DeviceIdType.MESH


def layer_norm(inputs, gain_row, shift_row):
    centred = inputs - jnp.mean(inputs, -1, keepdims=True)
    spread = jnp.mean(centred * centred, -1, keepdims=True)
    return centred * lax.rsqrt(spread + epsilon) * gain_row + shift_row


def project(inputs, matrix):
    return lax.dot_general(
        inputs, matrix, (((1,), (1,)), ((), ())), preferred_element_type=jnp.float32
    )


def product(inputs, matrix):
    return jnp.dot(inputs, matrix, preferred_element_type=jnp.float32)


def outer_rows(left, right):
    return lax.dot_general(
        left, right, (((0,), (0,)), ((), ())), preferred_element_type=jnp.float32
    )


def split_heads(rows, seq_len):
    return rows.reshape(-1, seq_len, HEADS, HEAD_DIM)


def attend(queries, key_rows, segment_rows):
    seq_len = segment_rows.shape[1]
    scores = jnp.einsum(
        "nqhd,nkhd->nhqk",
        split_heads(queries, seq_len),
        split_heads(key_rows, seq_len),
        preferred_element_type=jnp.float32,
    ) * HEAD_DIM ** (-0.5)
    positions = jnp.arange(seq_len)
    allowed = (positions[None, None, :] <= positions[None, :, None]) & (
        segment_rows[:, None, :] == segment_rows[:, :, None]
    )
    return jax.nn.softmax(jnp.where(allowed[:, None], scores, -1e30), axis=-1)


def layer_forward(weights, vector_one, inputs, segment_rows):
    row_count, model_width = inputs.shape
    seq_len = segment_rows.shape[1]
    normed = layer_norm(inputs, vector_one[0], vector_one[1]).astype(jnp.bfloat16)
    queries = (project(normed, weights[0:model_width]) + vector_one[6]).astype(jnp.bfloat16)
    key_rows = project(normed, weights[model_width : 2 * model_width]).astype(jnp.bfloat16)
    values = (project(normed, weights[2 * model_width : 3 * model_width]) + vector_one[7]).astype(
        jnp.bfloat16
    )
    attention = attend(queries, key_rows, segment_rows)
    mixture = jnp.einsum(
        "nhqk,nkhd->nqhd",
        attention.astype(jnp.bfloat16),
        split_heads(values, seq_len),
        preferred_element_type=jnp.float32,
    )
    mixture = mixture.reshape(row_count, model_width).astype(jnp.bfloat16)
    middle = inputs + (project(mixture, weights[3 * model_width : 4 * model_width]) + vector_one[8])
    normed_two = layer_norm(middle, vector_one[2], vector_one[3]).astype(jnp.bfloat16)
    hidden = project(normed_two, weights[4 * model_width : 8 * model_width]) + vector_one[
        10:14
    ].reshape(-1)
    active = jax.nn.gelu(hidden, approximate=True).astype(jnp.bfloat16)
    residual = middle + (
        product(active, weights[8 * model_width : 12 * model_width]) + vector_one[9]
    )
    normed_out = layer_norm(residual, vector_one[4], vector_one[5]).astype(jnp.bfloat16)
    return (
        normed,
        queries,
        key_rows,
        values,
        attention,
        mixture,
        middle,
        normed_two,
        hidden,
        active,
        residual,
        normed_out,
    )


def norm_grad(operand, gain_row, shift_row, cotangent):
    outcome, pullback = jax.vjp(layer_norm, operand, gain_row, shift_row)
    return pullback(cotangent)


def gelu_tanh(hidden):
    return jax.nn.gelu(hidden, approximate=True)


def layer_backward(weights, vector_one, inputs, segment_rows, saved, grad_out):
    row_count, model_width = inputs.shape
    seq_len = segment_rows.shape[1]
    scaling = HEAD_DIM ** (-0.5)
    (
        normed,
        queries,
        key_rows,
        values,
        attention,
        mixture,
        middle,
        normed_two,
        hidden,
        active,
        residual,
        normed_out,
    ) = saved
    d_residual, d_gain_out, d_shift_out = norm_grad(
        residual, vector_one[4], vector_one[5], grad_out
    )
    d_outer = d_residual.astype(jnp.bfloat16)
    d_bias_out = jnp.sum(d_outer.astype(jnp.float32), 0)
    d_active = project(d_outer, weights[8 * model_width : 12 * model_width])
    gelu_value, gelu_pull = jax.vjp(gelu_tanh, hidden)
    d_hidden = gelu_pull(d_active)[0].astype(jnp.bfloat16)
    d_bias_hidden = jnp.sum(d_hidden.astype(jnp.float32), 0)
    d_normed_two = product(d_hidden, weights[4 * model_width : 8 * model_width])
    d_middle_norm, d_gain_two, d_shift_two = norm_grad(
        middle, vector_one[2], vector_one[3], d_normed_two
    )
    d_middle = d_residual + d_middle_norm
    d_branch = d_middle.astype(jnp.bfloat16)
    d_bias_branch = jnp.sum(d_branch.astype(jnp.float32), 0)
    d_mixture = split_heads(
        product(d_branch, weights[3 * model_width : 4 * model_width]).astype(jnp.bfloat16), seq_len
    )
    d_attention = jnp.einsum(
        "nqhd,nkhd->nhqk", d_mixture, split_heads(values, seq_len), preferred_element_type=jnp.float32
    )
    d_values = jnp.einsum(
        "nhqk,nqhd->nkhd",
        attention.astype(jnp.bfloat16),
        d_mixture,
        preferred_element_type=jnp.float32,
    )
    d_values = d_values.reshape(row_count, model_width).astype(jnp.bfloat16)
    d_scores = (
        attention * (d_attention - jnp.sum(attention * d_attention, -1, keepdims=True))
    ).astype(jnp.bfloat16)
    d_queries = (
        jnp.einsum(
            "nhqk,nkhd->nqhd",
            d_scores,
            split_heads(key_rows, seq_len),
            preferred_element_type=jnp.float32,
        )
        * scaling
    )
    d_queries = d_queries.reshape(row_count, model_width).astype(jnp.bfloat16)
    d_keys = (
        jnp.einsum(
            "nhqk,nqhd->nkhd",
            d_scores,
            split_heads(queries, seq_len),
            preferred_element_type=jnp.float32,
        )
        * scaling
    )
    d_keys = d_keys.reshape(row_count, model_width).astype(jnp.bfloat16)
    d_joined = jnp.concatenate([d_queries, d_keys, d_values], axis=1)
    d_normed = product(d_joined, weights[0 : 3 * model_width])
    d_inputs_norm, d_gain_one, d_shift_one = norm_grad(
        inputs, vector_one[0], vector_one[1], d_normed
    )
    d_inputs = d_middle + d_inputs_norm
    grad_places = jnp.sum(d_inputs.reshape(-1, seq_len, model_width), axis=0)
    pairs = (
        (d_joined, normed),
        (d_branch, mixture),
        (d_hidden, normed_two),
        (active, d_outer),
    )
    bias_query = jnp.sum(d_queries.astype(jnp.float32), 0)
    bias_value = jnp.sum(d_values.astype(jnp.float32), 0)
    vector_rows = jnp.concatenate(
        [
            jnp.stack(
                [
                    d_gain_one,
                    d_shift_one,
                    d_gain_two,
                    d_shift_two,
                    d_gain_out,
                    d_shift_out,
                    bias_query,
                    bias_value,
                    d_bias_branch,
                    d_bias_out,
                ]
            ),
            d_bias_hidden.reshape(4, model_width),
        ],
        axis=0,
    )
    return (pairs, grad_places, vector_rows, d_inputs)


def share_all(rows, axes, size):
    return lax.all_to_all(
        jnp.broadcast_to(rows[None], (size,) + rows.shape), axes, 0, 0, tiled=True
    )


def update(weight, momentum, gradient, step_rate):
    renewed = momentum_decay * momentum + gradient
    return (renewed, weight - step_rate * (gradient + momentum_decay * renewed))


def flipped(value, offset, size):
    bit = 1
    while bit < size:
        digit = lax.rem(lax.div(offset, bit), 2)
        value = value + digit * bit * (1 - 2 * lax.rem(lax.div(value, bit), 2))
        bit *= 2
    return value


class Place:
    def __init__(self, groups, members):
        self.groups, self.members = groups, members
        self.ys = 2
        self.xs = groups // 4
        self.grp = lax.axis_index("grp")
        self.cli = lax.axis_index("cli")
        self.core = lax.rem(self.grp, 2)
        self.x = lax.rem(lax.div(self.grp, 2), self.xs)
        self.y = lax.div(self.grp, 2 * self.xs)

    def group(self, jx=0, jy=0, jc=0):
        x = flipped(self.x, jx, self.xs)
        y = flipped(self.y, jy, self.ys)
        core = self.core + jc * (1 - 2 * self.core)
        return (y * self.xs + x) * 2 + core

    def block(self, jx, jy, level, jc=0):
        return self.group(jx, jy, jc) * self.members + level

    def peer(self, jx=0, jy=0, jc=0):
        return (self.group(jx, jy, jc), self.cli)

    def level(self, level):
        return (self.grp, level)

    def nearest(self, i):
        z, last = self.cli, self.members - 1
        low = jnp.where(2 * z < last, 1, 0)
        sign = 2 * low - 1
        margin = low * z + (1 - low) * (last - z)
        step = lax.div(i + 1, 2)
        odd = lax.rem(i, 2)
        near = z + sign * step * (2 * odd - 1)
        far = z + sign * (i - margin)
        return jnp.where(i <= 2 * margin, near, far)


def greet(place):
    barrier = pltpu.get_barrier_semaphore()
    peers = [place.peer(jx=j) for j in range(1, place.xs)] + [place.peer(jy=j) for j in range(1, place.ys)]
    peers.append(place.peer(jc=1))
    peers += [place.level(lax.rem(place.cli + j, place.members)) for j in range(1, place.members)]
    for peer in peers:
        pl.semaphore_signal(barrier, inc=1, device_id=peer, device_id_type=MESH)
    pl.semaphore_wait(barrier, len(peers))


def greet_all(devices, members):
    barrier = pltpu.get_barrier_semaphore()
    me = lax.axis_index("grp") * members + lax.axis_index("cli")

    def hello(j, carry):
        other = lax.rem(me + j, devices)
        pl.semaphore_signal(
            barrier, inc=1, device_id=(lax.div(other, members), lax.rem(other, members)), device_id_type=MESH
        )
        return carry

    lax.fori_loop(1, devices, hello, 0)
    pl.semaphore_wait(barrier, devices - 1)


def spread_sems(groups, members, pieces):
    xs, ys, items = groups // 4, 2, members * pieces
    dma = pltpu.SemaphoreType.DMA
    shapes = [(items,)] * 3 + [(items, xs)] * 2 + [(items, ys)] * 2 + [(items, xs, ys)] * 6
    return [dma] + [dma(shape) for shape in shapes]


def spread_body(place, chain, pieces, src, out, sems, consume, ready=None):
    (own_sem, z_up, z_down, z_recv, x_send, x_recv, y_send, y_recv, k_send, k_recv, p_send, p_recv,
     c_send, c_recv) = sems
    xs, ys, members = place.xs, place.ys, place.members
    items = members * pieces
    size = out.shape[1] // pieces
    z = place.cli
    partner = z + 1 - 2 * lax.rem(z, 2)
    inner_x, inner_y = range(1, xs), range(1, ys)

    def move(source, target, send, recv, device):
        return pltpu.make_async_remote_copy(
            src_ref=source, dst_ref=target, send_sem=send, recv_sem=recv, device_id=device, device_id_type=MESH
        )

    class Item:
        def __init__(self, k):
            self.level = place.nearest(lax.div(k, pieces))
            self.piece = lax.rem(k, pieces)
            self.slot = self.level * pieces + self.piece
            self.even = lax.rem(self.piece, 2) == 0
            self.mine = lax.rem(self.level + z, 2) == 0 if chain else self.level >= 0
            self.rows = pl.ds(self.piece * size, size)

        def part(self, jx, jy, level=None):
            return out.at[place.block(jx, jy, self.level if level is None else level), self.rows]

        def here(self, own):
            return src.at[z if not chain else 0, self.rows] if own else self.part(0, 0)

        def up(self, own=False):
            return move(self.here(own), self.part(0, 0), z_up.at[self.slot], z_recv.at[self.slot], place.level(z + 1))

        def down(self, own=False):
            return move(self.here(own), self.part(0, 0), z_down.at[self.slot], z_recv.at[self.slot], place.level(z - 1))

        def straight(self):
            return move(
                src.at[self.level, self.rows], self.part(0, 0, z), z_up.at[self.slot],
                z_recv.at[z * pieces + self.piece], place.level(self.level),
            )

        def landed(self):
            part = self.part(0, 0)
            return move(part, part, z_up.at[self.slot], z_recv.at[self.slot], place.level(partner))

        def to_x(self, jx, own=False):
            return move(self.here(own), self.part(0, 0), x_send.at[self.slot, jx], x_recv.at[self.slot, jx], place.peer(jx=jx))

        def to_y(self, jy, own=False):
            return move(self.here(own), self.part(0, 0), y_send.at[self.slot, jy], y_recv.at[self.slot, jy], place.peer(jy=jy))

        def corner_a(self, jx, jy):
            part = self.part(jx, 0)
            return move(part, part, k_send.at[self.slot, jx, jy], k_recv.at[self.slot, jx, jy], place.peer(jy=jy))

        def corner_b(self, jx, jy):
            part = self.part(0, jy)
            return move(part, part, k_send.at[self.slot, jx, jy], k_recv.at[self.slot, jx, jy], place.peer(jx=jx))

        def corner_z(self, jx, jy):
            part = self.part(jx, jy)
            return move(part, part, p_send.at[self.slot, jx, jy], p_recv.at[self.slot, jx, jy], place.level(partner))

        def to_core(self, jx, jy, own=False):
            part = self.part(jx, jy)
            return move(self.here(True) if own else part, part, c_send.at[self.slot, jx, jy], c_recv.at[self.slot, jx, jy], place.peer(jc=1))

    own = pltpu.make_async_copy(src.at[z if not chain else 0], out.at[place.block(0, 0, z)], own_sem)
    own.start()
    if not chain:
        for piece in range(pieces):
            Item(pieces + piece).straight().start()

    def columns(k):
        item = Item(k)
        level = item.level

        @pl.when(k < pieces)
        def mine_first():
            if chain:
                @pl.when(z + 1 < members)
                def onward():
                    item.up(True).start()

                @pl.when(z > 0)
                def back():
                    item.down(True).start()

            for jx in inner_x:
                item.to_x(jx, True).start()
            for jy in inner_y:
                item.to_y(jy, True).start()
            item.to_core(0, 0, True).start()

        @pl.when(k >= pieces)
        def arrive():
            item.landed().wait_recv()
            if chain:
                @pl.when((level < z) & (z + 1 < members))
                def onward():
                    item.up().start()

                @pl.when((level > z) & (z > 0))
                def back():
                    item.down().start()
            else:
                @pl.when(k + pieces < items)
                def following():
                    Item(k + pieces).straight().start()

            for jx in inner_x:
                item.to_x(jx).start()
            for jy in inner_y:
                item.to_y(jy).start()
            item.to_core(0, 0).start()

    def edges(k):
        item = Item(k)
        for jx in inner_x:
            item.to_x(jx).wait_recv()

            @pl.when(item.mine & item.even)
            def pass_a():
                for jy in inner_y:
                    item.corner_a(jx, jy).start()

            item.to_core(jx, 0).start()
        for jy in inner_y:
            item.to_y(jy).wait_recv()

            @pl.when(item.mine & jnp.logical_not(item.even))
            def pass_b():
                for jx in inner_x:
                    item.corner_b(jx, jy).start()

            item.to_core(0, jy).start()

    def corners(k):
        item = Item(k)

        @pl.when(item.mine)
        def mine_now():
            for jx in inner_x:
                for jy in inner_y:
                    item.corner_a(jx, jy).wait_recv()
                    if chain:
                        item.corner_z(jx, jy).start()
                    item.to_core(jx, jy).start()

    def handed(k):
        item = Item(k)

        @pl.when(jnp.logical_not(item.mine))
        def from_partner():
            for jx in inner_x:
                for jy in inner_y:
                    item.corner_z(jx, jy).wait_recv()
                    item.to_core(jx, jy).start()

    spots = xs * ys
    lag_edge, lag_corner = (2, 4) if chain else (1, 3)
    lag_handed = pieces + 6 if chain else lag_corner
    lag_end = lag_handed + 1

    def tick(t, carry):
        @pl.when(t < items)
        def arrivals():
            columns(t)

        @pl.when((t >= lag_edge) & (t < items + lag_edge))
        def sides():
            edges(t - lag_edge)

        @pl.when((t >= lag_corner) & (t < items + lag_corner))
        def far():
            corners(t - lag_corner)

        if chain:
            @pl.when((t >= lag_handed) & (t < items + lag_handed))
            def others():
                handed(t - lag_handed)

        def visit(e, carry):
            jc = lax.div(e, spots)
            spot = lax.rem(e, spots)
            jx, jy = lax.rem(spot, xs), lax.div(spot, xs)
            far = jnp.minimum(jx, 1) + jnp.minimum(jy, 1)
            lag = jnp.where(far == 0, 1, jnp.where(far == 1, lag_edge + 1, lag_end))
            k = t - lag

            @pl.when((k >= 0) & (k < items))
            def valid():
                item = Item(k)

                @pl.when(jc == 1)
                def shared():
                    item.to_core(jx, jy).wait_recv()

                if consume is not None:
                    consume(place.block(jx, jy, item.level, jc), item.level, item.piece)

            return carry

        return lax.fori_loop(0, 2 * spots, visit, carry)

    if ready is not None:
        own.wait()
        ready()
    lax.fori_loop(0, items + lag_end, tick, 0)

    def close(k, carry):
        item = Item(k)
        level = item.level
        if chain:
            @pl.when((level <= z) & (z + 1 < members))
            def onward():
                item.up().wait_send()

            @pl.when((level >= z) & (z > 0))
            def back():
                item.down().wait_send()
        else:
            @pl.when(k >= pieces)
            def sent():
                item.straight().wait_send()

        for jx in inner_x:
            item.to_x(jx).wait_send()
        for jy in inner_y:
            item.to_y(jy).wait_send()
        for jx in range(xs):
            for jy in range(ys):
                item.to_core(jx, jy).wait_send()

        @pl.when(item.mine)
        def mine_done():
            for jx in inner_x:
                for jy in inner_y:
                    item.corner_a(jx, jy).wait_send()
                    if chain:
                        item.corner_z(jx, jy).wait_send()

        return carry

    lax.fori_loop(0, items, close, 0)
    if ready is None:
        own.wait()


def spread_kernel(groups, members, chain, pieces, src, out, *sems):
    place = Place(groups, members)
    greet(place)
    spread_body(place, chain, pieces, src, out, sems, None)


def spread(src, groups, members, collective_id, chain, pieces):
    count, rows, width = src.shape
    return pl.pallas_call(
        functools.partial(spread_kernel, groups, members, chain, pieces),
        out_shape=jax.ShapeDtypeStruct((groups * members, rows, width), src.dtype),
        in_specs=[pl.BlockSpec(memory_space=pl.ANY)],
        out_specs=pl.BlockSpec(memory_space=pl.ANY),
        scratch_shapes=spread_sems(groups, members, pieces),
        compiler_params=pltpu.CompilerParams(collective_id=collective_id, has_side_effects=True),
        cost_estimate=pl.CostEstimate(
            flops=0, bytes_accessed=4 * groups * members * rows * width, transcendentals=0
        ),
    )(src)


def tile_of(part_rows):
    return TILE if part_rows % TILE == 0 else part_rows


def opening_kernel(groups, members, facts_ref, table_ref, facts_out, low_ref, own_sem, send_sems, recv_sems):
    devices = groups * members
    tiles = pl.num_programs(1)
    step = pl.program_id(0) * tiles + pl.program_id(1)
    last = pl.num_programs(0) * tiles - 1
    me = lax.axis_index("grp") * members + lax.axis_index("cli")

    def other(j):
        return lax.rem(me + j, devices)

    def place(device):
        return (lax.div(device, members), lax.rem(device, members))

    def give(j):
        return pltpu.make_async_remote_copy(
            src_ref=facts_ref, dst_ref=facts_out.at[me], send_sem=send_sems.at[j], recv_sem=recv_sems.at[j],
            device_id=place(other(j)), device_id_type=MESH,
        )

    own = pltpu.make_async_copy(facts_ref, facts_out.at[me], own_sem)

    @pl.when(step == 0)
    def begin():
        barrier = pltpu.get_barrier_semaphore()

        def hello(j, carry):
            pl.semaphore_signal(barrier, inc=1, device_id=place(other(j)), device_id_type=MESH)
            return carry

        own.start()
        lax.fori_loop(1, devices, hello, 0)

    @pl.when(step == last // 2)
    def exchange():
        def start(j, carry):
            give(j).start()
            return carry

        pl.semaphore_wait(pltpu.get_barrier_semaphore(), devices - 1)
        lax.fori_loop(1, devices, start, 0)

    low_ref[...] = table_ref[...].astype(low_ref.dtype)

    @pl.when(step == last)
    def end():
        def finish(j, carry):
            give(j).wait_send()
            pltpu.make_async_remote_copy(
                src_ref=facts_ref, dst_ref=facts_out.at[lax.rem(me + devices - j, devices)],
                send_sem=send_sems.at[j], recv_sem=recv_sems.at[j], device_id=place(other(j)), device_id_type=MESH,
            ).wait_recv()
            return carry

        lax.fori_loop(1, devices, finish, 0)
        own.wait()


def opening(facts, table, groups, members, collective_id):
    devices = groups * members
    models, part_rows, width = table.shape
    tile_rows = tile_of(part_rows)
    piece = pl.BlockSpec((1, tile_rows, width), lambda m, t: (m, t, 0))
    anywhere = pl.BlockSpec(memory_space=pl.ANY)
    dma = pltpu.SemaphoreType.DMA
    return pl.pallas_call(
        functools.partial(opening_kernel, groups, members),
        out_shape=(
            jax.ShapeDtypeStruct((devices,) + facts.shape, facts.dtype),
            jax.ShapeDtypeStruct(table.shape, jnp.bfloat16),
        ),
        grid=(models, part_rows // tile_rows),
        in_specs=[anywhere, piece],
        out_specs=(anywhere, piece),
        scratch_shapes=[dma, dma((devices,)), dma((devices,))],
        compiler_params=pltpu.CompilerParams(collective_id=collective_id, has_side_effects=True),
        cost_estimate=pl.CostEstimate(flops=0, bytes_accessed=6 * table.size, transcendentals=0),
    )(facts, table)


def score_kernel(groups, members, share, pieces, src, table, target, out, answer, *rest):
    part, pool, stat, inbox, part_sem, out_sems, go_send, go_recv, back_send, back_recv = rest[:10]
    sems = rest[10:]
    devices = groups * members
    place = Place(groups, members)
    load_table = pltpu.make_async_copy(table, part, part_sem)
    load_table.start()
    greet_all(devices, members)
    rows = pool.shape[1]
    size = rows // pieces

    def keep(block, piece):
        here = pl.ds(pl.multiple_of(piece * size, size), size)
        return pltpu.make_async_copy(pool.at[block, here], out.at[block, here], out_sems.at[block, piece])

    def consume(block, level, piece):
        keep(block, piece).start()
        here = pl.ds(pl.multiple_of(piece * size, size), size)
        model = lax.div(level, share)
        wanted = target[lax.div(block, members) * share + lax.rem(level, share), :, here]
        outs = pool[block, here]
        part_rows = part.shape[1]
        tile = tile_of(part_rows)
        marks = lax.broadcasted_iota(jnp.int32, (tile, size), 0)
        tops, totals, hits = [], [], []
        for first in range(0, part_rows, tile):
            logits = project(part[model, pl.ds(first, tile)], outs)
            hit = jnp.where(marks == wanted - first, logits, 0.0).reshape(-1, 8, size)
            hits.append(jnp.sum(hit, axis=0))
            logits = logits.reshape(-1, 8, size)
            top = jnp.max(logits, axis=0)
            tops.append(top)
            totals.append(jnp.sum(jnp.exp(logits - top[None]), axis=0))
        highest = jnp.max(functools.reduce(jnp.maximum, tops), axis=0, keepdims=True)
        total = sum(t * jnp.exp(m - highest) for t, m in zip(totals, tops))
        stat[block, 0:1, here] = highest + jnp.log(jnp.sum(total, axis=0, keepdims=True))
        stat[block, 1:2, here] = jnp.sum(sum(hits), axis=0, keepdims=True)

    spread_body(place, True, pieces, src, pool, sems, consume, load_table.wait)

    me = place.block(0, 0, place.cli)

    def device(index):
        return (lax.div(index, members), lax.rem(index, members))

    def ahead(j):
        return lax.rem(me + j, devices)

    def behind(j):
        return lax.rem(me + devices - j, devices)

    def go(j, source, target):
        return pltpu.make_async_remote_copy(
            src_ref=stat.at[source], dst_ref=inbox.at[target], send_sem=go_send.at[j], recv_sem=go_recv.at[j],
            device_id=device(ahead(j)), device_id_type=MESH,
        )

    def back(j, source):
        return pltpu.make_async_remote_copy(
            src_ref=answer.at[source], dst_ref=answer.at[source], send_sem=back_send.at[j],
            recv_sem=back_recv.at[j], device_id=device(ahead(j)), device_id_type=MESH,
        )

    def loop(step):
        def run(j, carry):
            step(j)
            return carry

        lax.fori_loop(1, devices, run, 0)

    loop(lambda j: go(j, ahead(j), me).start())
    inbox[me] = stat[me]
    loop(lambda j: go(j, me, behind(j)).wait_recv())
    logs = inbox[:, 0, :]
    top = jnp.max(logs, axis=0, keepdims=True)
    log_total = top + jnp.log(jnp.sum(jnp.exp(logs - top), axis=0, keepdims=True))
    answer[me, 0:1, :] = log_total
    answer[me, 1:2, :] = log_total - jnp.sum(inbox[:, 1, :], axis=0, keepdims=True)
    loop(lambda j: back(j, me).start())
    loop(lambda j: back(j, behind(j)).wait_recv())
    loop(lambda j: go(j, ahead(j), me).wait_send())
    loop(lambda j: back(j, me).wait_send())

    def close(block, carry):
        for piece in range(pieces):
            keep(block, piece).wait()
        return carry

    lax.fori_loop(0, groups * members, close, 0)


def spread_score(src, table_low, target_blocks, groups, members, share, collective_id, pieces=2):
    _, rows, width = src.shape
    blocks = groups * members
    return pl.pallas_call(
        functools.partial(score_kernel, groups, members, share, pieces),
        out_shape=(
            jax.ShapeDtypeStruct((blocks, rows, width), src.dtype),
            jax.ShapeDtypeStruct((blocks, 2, rows), jnp.float32),
        ),
        in_specs=[
            pl.BlockSpec(memory_space=pl.ANY),
            pl.BlockSpec(memory_space=pl.ANY),
            pl.BlockSpec(memory_space=pltpu.VMEM),
        ],
        out_specs=(pl.BlockSpec(memory_space=pl.ANY), pl.BlockSpec(memory_space=pltpu.VMEM)),
        scratch_shapes=[
            pltpu.VMEM(table_low.shape, table_low.dtype),
            pltpu.VMEM((blocks, rows, width), src.dtype),
            pltpu.VMEM((blocks, 2, rows), jnp.float32),
            pltpu.VMEM((blocks, 2, rows), jnp.float32),
            pltpu.SemaphoreType.DMA,
            pltpu.SemaphoreType.DMA((blocks, pieces)),
        ]
        + [pltpu.SemaphoreType.DMA((blocks,))] * 4
        + spread_sems(groups, members, pieces),
        compiler_params=pltpu.CompilerParams(
            collective_id=collective_id, has_side_effects=True, vmem_limit_bytes=60 * MIB
        ),
        cost_estimate=pl.CostEstimate(
            flops=2 * blocks * rows * table_low.shape[1] * width,
            bytes_accessed=2 * blocks * rows * width * 2,
            transcendentals=blocks * rows * table_low.shape[1],
        ),
    )(src, table_low, target_blocks)


def stats_kernel(outs_ref, table_ref, target_ref, stat_ref):
    logits = project(table_ref[0], outs_ref[0])
    highest = jnp.max(logits, axis=0, keepdims=True)
    total = jnp.sum(jnp.exp(logits - highest), axis=0, keepdims=True)
    rows = lax.broadcasted_iota(jnp.int32, logits.shape, 0)
    hit = jnp.sum(jnp.where(rows == target_ref[0], logits, 0.0), axis=0, keepdims=True)
    stat_ref[0, 0:1, :] = highest + jnp.log(total)
    stat_ref[0, 1:2, :] = hit


def head_stats(outs_all, table_low, target_blocks, groups, members, share):
    blocks, rows, width = outs_all.shape
    part_rows = table_low.shape[1]
    return pl.pallas_call(
        stats_kernel,
        out_shape=jax.ShapeDtypeStruct((blocks, 2, rows), jnp.float32),
        grid=(members, groups),
        in_specs=[
            pl.BlockSpec((1, rows, width), lambda z, g: (g * members + z, 0, 0)),
            pl.BlockSpec((1, part_rows, width), lambda z, g: (z // share, 0, 0)),
            pl.BlockSpec((1, 1, rows), lambda z, g: (g * share + z % share, 0, 0)),
        ],
        out_specs=pl.BlockSpec((1, 2, rows), lambda z, g: (g * members + z, 0, 0)),
        compiler_params=pltpu.CompilerParams(vmem_limit_bytes=56 * MIB),
        cost_estimate=pl.CostEstimate(
            flops=2 * blocks * rows * part_rows * width,
            bytes_accessed=2 * outs_all.size + 2 * table_low.size,
            transcendentals=blocks * rows * part_rows,
        ),
    )(outs_all, table_low, target_blocks)


def collect_kernel(groups, members, source, out, work, from_core, from_x, from_y, then_y, then_x, from_z, *sems):
    (load_sem, core_send, core_recv, x_send, x_recv, y_send, y_recv, yy_send, yy_recv, xx_send, xx_recv, z_send,
     z_recv, g_send, g_recv) = sems
    place = Place(groups, members)
    greet(place)
    xs, ys = place.xs, place.ys
    half = members // 2
    z = place.cli
    order = sorted(
        ((jx, jy) for jx in range(xs) for jy in range(ys)), key=lambda spot: -(spot[0] > 0) - (spot[1] > 0)
    )
    started = []

    def send(source_ref, target_ref, send_sem, recv_sem, device):
        copy = pltpu.make_async_remote_copy(
            src_ref=source_ref, dst_ref=target_ref, send_sem=send_sem, recv_sem=recv_sem, device_id=device,
            device_id_type=MESH,
        )
        copy.start()
        started.append(copy)

    def arrival(target_ref, send_sem, recv_sem, device):
        pltpu.make_async_remote_copy(
            src_ref=target_ref, dst_ref=target_ref, send_sem=send_sem, recv_sem=recv_sem, device_id=device,
            device_id_type=MESH,
        ).wait_recv()

    def add(ref, others):
        total = ref[...].astype(jnp.float32)
        for other in others:
            total = total + other[...].astype(jnp.float32)
        ref[...] = total.astype(ref.dtype)

    def clients(p):
        return (p, p + half)

    spots = [(jy * xs + jx, jx, jy) for jx, jy in order]
    loads = {}
    for p in range(half):
        for k, jx, jy in spots:
            for c in clients(p):
                send(
                    source.at[place.group(jx, jy, 1) * members + c], from_core.at[k, c], core_send.at[k, c],
                    core_recv.at[k, c], place.peer(jc=1),
                )
                loads[k, c] = pltpu.make_async_copy(
                    source.at[place.group(jx, jy, 0) * members + c], work.at[k, c], load_sem.at[k, c]
                )
                loads[k, c].start()
    for p in range(half):
        a, b = clients(p)
        for k, jx, jy in spots:
            for c in (a, b):
                loads[k, c].wait()
                arrival(from_core.at[k, c], core_send.at[k, c], core_recv.at[k, c], place.peer(jc=1))
                add(work.at[k, c], [from_core.at[k, c]])
            if jx:
                send(work.at[k, a], from_x.at[p, jx, jy], x_send.at[p, jx, jy], x_recv.at[p, jx, jy], place.peer(jx=jx))
            if jy:
                send(work.at[k, b], from_y.at[p, jx, jy], y_send.at[p, jx, jy], y_recv.at[p, jx, jy], place.peer(jy=jy))

    def second(p):
        a, b = clients(p)
        for jy in reversed(range(ys)):
            k = jy * xs
            for jx in range(1, xs):
                arrival(from_x.at[p, jx, jy], x_send.at[p, jx, jy], x_recv.at[p, jx, jy], place.peer(jx=jx))
            add(work.at[k, a], [from_x.at[p, jx, jy] for jx in range(1, xs)])
            if jy:
                send(work.at[k, a], then_y.at[p, jy], yy_send.at[p, jy], yy_recv.at[p, jy], place.peer(jy=jy))
        for jx in reversed(range(xs)):
            for jy in range(1, ys):
                arrival(from_y.at[p, jx, jy], y_send.at[p, jx, jy], y_recv.at[p, jx, jy], place.peer(jy=jy))
            add(work.at[jx, b], [from_y.at[p, jx, jy] for jy in range(1, ys)])
            if jx:
                send(work.at[jx, b], then_x.at[p, jx], xx_send.at[p, jx], xx_recv.at[p, jx], place.peer(jx=jx))

    def third(p):
        a, b = clients(p)
        for jy in range(1, ys):
            arrival(then_y.at[p, jy], yy_send.at[p, jy], yy_recv.at[p, jy], place.peer(jy=jy))
        add(work.at[0, a], [then_y.at[p, jy] for jy in range(1, ys)])
        for jx in range(1, xs):
            arrival(then_x.at[p, jx], xx_send.at[p, jx], xx_recv.at[p, jx], place.peer(jx=jx))
        add(work.at[0, b], [then_x.at[p, jx] for jx in range(1, xs)])
        for c in (a, b):
            @pl.when(z != c)
            def give():
                pltpu.make_async_remote_copy(
                    src_ref=work.at[0, c], dst_ref=from_z.at[z], send_sem=z_send.at[c], recv_sem=z_recv.at[z],
                    device_id=place.level(c), device_id_type=MESH,
                ).start()

    for p in range(half + 1):
        if p < half:
            second(p)
        if p:
            third(p - 1)
    total = work[0, z].astype(jnp.float32)
    for j in range(1, members):
        level = lax.rem(z + members - j, members)
        arrival(from_z.at[level], z_send.at[level], z_recv.at[level], place.level(level))
        total = total + from_z[level].astype(jnp.float32)
    out[z] = total.astype(out.dtype)
    for j in range(1, members):
        send(out.at[z], out.at[z], g_send.at[j], g_recv.at[j], place.level(lax.rem(z + j, members)))
    for j in range(1, members):
        level = lax.rem(z + members - j, members)
        arrival(out.at[level], g_send.at[j], g_recv.at[j], place.level(level))
    for copy in started:
        copy.wait_send()
    for c in range(members):
        @pl.when(z != c)
        def given():
            pltpu.make_async_remote_copy(
                src_ref=work.at[0, c], dst_ref=from_z.at[z], send_sem=z_send.at[c], recv_sem=z_recv.at[z],
                device_id=place.level(c), device_id_type=MESH,
            ).wait_send()


def collect(parts, groups, members, collective_id):
    _, seq_len, width = parts.shape
    xs, ys, half = groups // 4, 2, members // 2
    dma = pltpu.SemaphoreType.DMA

    def held(*shape):
        return pltpu.VMEM(shape + (seq_len, width), parts.dtype)

    return pl.pallas_call(
        functools.partial(collect_kernel, groups, members),
        out_shape=jax.ShapeDtypeStruct((members, seq_len, width), parts.dtype),
        in_specs=[pl.BlockSpec(memory_space=pl.ANY)],
        out_specs=pl.BlockSpec(memory_space=pltpu.VMEM),
        scratch_shapes=[
            held(xs * ys, members),
            held(xs * ys, members),
            held(half, xs, ys),
            held(half, xs, ys),
            held(half, ys),
            held(half, xs),
            held(members),
        ]
        + [dma((xs * ys, members))] * 3
        + [dma((half, xs, ys))] * 4
        + [dma((half, ys))] * 2
        + [dma((half, xs))] * 2
        + [dma((members,))] * 4,
        compiler_params=pltpu.CompilerParams(
            collective_id=collective_id, has_side_effects=True, vmem_limit_bytes=56 * MIB
        ),
        cost_estimate=pl.CostEstimate(
            flops=0, bytes_accessed=4 * groups * members * seq_len * width, transcendentals=0
        ),
    )(parts)


def unpack_kernel(start, part, at_ref, pool_ref, weights_ref, rows_ref):
    step = pl.program_id(0)
    owners, slab, width = pool_ref.shape
    weights_ref[...] = jnp.concatenate([pool_ref[j, :part] for j in range(owners)], axis=0)
    count = slab - start
    columns = lax.broadcasted_iota(jnp.int32, (1, count), 1) + start
    columns = jnp.concatenate([columns + j * slab for j in range(owners)], axis=1)
    hits = (columns == at_ref[...] - step * owners * slab).astype(jnp.float32).astype(jnp.bfloat16)
    found = product(hits, jnp.concatenate([pool_ref[j, start:] for j in range(owners)], axis=0))

    @pl.when(step == 0)
    def begin():
        rows_ref[...] = found

    @pl.when(step > 0)
    def more():
        rows_ref[...] += found


def unpack(pool, part, at):
    devices, slab, width = pool.shape
    owners = max(4, 8 // math.gcd(part, 8))
    start = part // 16 * 16
    tokens = at.shape[0]
    return pl.pallas_call(
        functools.partial(unpack_kernel, start, part),
        out_shape=(
            jax.ShapeDtypeStruct((devices * part, width), pool.dtype),
            jax.ShapeDtypeStruct((tokens, width), jnp.float32),
        ),
        grid=(devices // owners,),
        in_specs=[
            pl.BlockSpec((tokens, 1), lambda i: (0, 0)),
            pl.BlockSpec((owners, slab, width), lambda i: (i, 0, 0)),
        ],
        out_specs=(
            pl.BlockSpec((owners * part, width), lambda i: (i, 0)),
            pl.BlockSpec((tokens, width), lambda i: (0, 0)),
        ),
        compiler_params=pltpu.CompilerParams(vmem_limit_bytes=40 * MIB),
        cost_estimate=pl.CostEstimate(
            flops=2 * devices * tokens * (slab - start) * width,
            bytes_accessed=4 * pool.size,
            transcendentals=0,
        ),
    )(at, pool)


def back_kernel(
    model_ref, fresh_ref, used_ref, piece_ref, place_ref, *rest
):
    pieces = rest[:QUAD]
    table_ref, info_ref, target_ref, d_outs_ref, grad_ref, held, sems = rest[QUAD:]
    step = pl.program_id(0)
    seq_len = pieces[0].shape[1]
    slot = lax.rem(step, 2)

    def leave(which, where, i):
        return pltpu.make_async_copy(held.at[which, i], d_outs_ref.at[where], sems.at[which, i])

    def settle(which):
        for i in range(QUAD):
            leave(which, 0, i).wait()

    @pl.when(step < used_ref[0])
    def work():
        @pl.when(step >= 2)
        def reuse():
            settle(slot)

        @pl.when(fresh_ref[step] == 1)
        def start():
            grad_ref[...] = jnp.zeros_like(grad_ref)

        outs = jnp.concatenate([piece[0] for piece in pieces], axis=0)
        part_rows = table_ref.shape[1]
        size = tile_of(part_rows)
        d_outs = jnp.zeros(outs.shape, jnp.float32)
        for first_row in range(0, part_rows, size):
            here = pl.ds(first_row, size)
            table_rows = table_ref[0, here]
            logits = project(table_rows, outs)
            rows = lax.broadcasted_iota(jnp.int32, logits.shape, 0) + first_row
            soft = jnp.exp(logits - info_ref[0, 0:1, :])
            soft = jnp.where(rows == target_ref[0], soft - 1.0, soft)
            d_logits = (info_ref[0, 1:2, :] * soft).astype(jnp.bfloat16)
            d_outs = d_outs + outer_rows(d_logits, table_rows)
            grad_ref[0, here] += product(d_logits, outs)
        for i in range(QUAD):
            held[slot, i] = d_outs[i * seq_len : (i + 1) * seq_len].astype(held.dtype)
            leave(slot, place_ref[QUAD * step + i], i).start()

        @pl.when(step == used_ref[0] - 1)
        def drain():
            settle(slot)

            @pl.when(step >= 1)
            def earlier():
                settle(1 - slot)


def head_back(outs_pieces, table_low, model_of, fresh, used, piece_at, place, info, target):
    steps = model_of.shape[0]
    models, part_rows, width = table_low.shape
    seq_len = outs_pieces.shape[1]
    tokens = QUAD * seq_len

    def piece(i):
        return pl.BlockSpec((1, seq_len, width), lambda s, m, f, u, q, p: (q[QUAD * s + i], 0, 0))

    return pl.pallas_call(
        back_kernel,
        out_shape=(
            jax.ShapeDtypeStruct((QUAD * steps, seq_len, width), jnp.bfloat16),
            jax.ShapeDtypeStruct((models, part_rows, width), jnp.float32),
        ),
        grid_spec=pltpu.PrefetchScalarGridSpec(
            num_scalar_prefetch=5,
            grid=(steps,),
            in_specs=[piece(i) for i in range(QUAD)]
            + [
                pl.BlockSpec((1, part_rows, width), lambda s, m, *_: (m[s], 0, 0)),
                pl.BlockSpec((1, 2, tokens), lambda s, *_: (s, 0, 0)),
                pl.BlockSpec((1, 1, tokens), lambda s, *_: (s, 0, 0)),
            ],
            out_specs=(
                pl.BlockSpec(memory_space=pl.ANY),
                pl.BlockSpec((1, part_rows, width), lambda s, m, *_: (m[s], 0, 0)),
            ),
            scratch_shapes=[
                pltpu.VMEM((2, QUAD, seq_len, width), jnp.bfloat16),
                pltpu.SemaphoreType.DMA((2, QUAD)),
            ],
        ),
        compiler_params=pltpu.CompilerParams(vmem_limit_bytes=56 * MIB),
        cost_estimate=pl.CostEstimate(
            flops=6 * steps * tokens * part_rows * width,
            bytes_accessed=4 * steps * tokens * width + 6 * table_low.size,
            transcendentals=steps * tokens * part_rows,
        ),
    )(model_of, fresh, used, piece_at, place, *([outs_pieces] * QUAD), table_low, info, target)


def finish_kernel(
    first_model, start_ref, end_ref, first_ref, second_ref, d_ref, ids_ref, head_ref, table_ref, momentum_ref, *rest
):
    grad_ref, momentum_new_ref, table_new_ref = rest[-3:]
    model = pl.program_id(0) + first_model
    tile_rows = grad_ref.shape[1]
    tokens = ids_ref.shape[2]
    rows = lax.broadcasted_iota(jnp.int32, (tile_rows, tokens), 0) + pl.program_id(1) * tile_rows
    grad_ref[0] = head_ref[0]

    def pair(step, carry):
        hits = (rows == ids_ref[step]).astype(jnp.float32).astype(jnp.bfloat16)
        outs = jnp.concatenate([d_ref[first_ref[step]], d_ref[second_ref[step]]], axis=0)
        grad_ref[0] += product(hits, outs)
        return carry

    lax.fori_loop(start_ref[model], end_ref[model], pair, 0)
    renewed, fresh_table = update(table_ref[0], momentum_ref[0], grad_ref[0], table_rate)
    momentum_new_ref[0] = renewed
    table_new_ref[0] = fresh_table


def finish_table(d_inputs, head_grad, table, momentum, schedule, ids, first_model, count, earlier):
    models, part_rows, width = table.shape
    tile_rows = tile_of(part_rows)
    state = jax.ShapeDtypeStruct(table.shape, jnp.float32)
    piece = pl.BlockSpec((1, tile_rows, width), lambda m, t, *_: (m + first_model, t, 0))
    whole = pl.BlockSpec(memory_space=pltpu.VMEM)
    return pl.pallas_call(
        functools.partial(finish_kernel, first_model),
        out_shape=(state, state, state),
        grid_spec=pltpu.PrefetchScalarGridSpec(
            num_scalar_prefetch=4,
            grid=(count, part_rows // tile_rows),
            in_specs=[whole, whole, piece, piece, piece]
            + [pl.BlockSpec(memory_space=pl.ANY)] * len(earlier),
            out_specs=(piece, piece, piece),
        ),
        input_output_aliases={9 + i: i for i in range(len(earlier))},
        compiler_params=pltpu.CompilerParams(vmem_limit_bytes=56 * MIB),
        cost_estimate=pl.CostEstimate(
            flops=2 * d_inputs.size * part_rows * count // models,
            bytes_accessed=24 * count * part_rows * width,
            transcendentals=0,
        ),
    )(*schedule, d_inputs, ids, head_grad, table, momentum, *earlier)


def stack_kernel(gradient_ref, weight_ref, momentum_ref, grad_ref, renewed_ref, fresh_ref):
    for model in range(gradient_ref.shape[0]):
        gradient = gradient_ref[model].astype(jnp.float32)
        renewed, fresh = update(weight_ref[:, model, :], momentum_ref[:, model, :], gradient, stack_rate)
        grad_ref[:, model, :] = gradient
        renewed_ref[:, model, :] = renewed
        fresh_ref[:, model, :] = fresh


def update_stack(gradient, weight, momentum):
    turn = functools.partial(jnp.transpose, axes=(1, 0, 2))
    turned = jax.ShapeDtypeStruct(turn(weight).shape, jnp.float32)
    whole = pl.BlockSpec(memory_space=pltpu.VMEM)
    results = pl.pallas_call(
        stack_kernel,
        out_shape=(turned, turned, turned),
        in_specs=[whole] * 3,
        out_specs=(whole,) * 3,
        compiler_params=pltpu.CompilerParams(vmem_limit_bytes=56 * MIB),
        cost_estimate=pl.CostEstimate(
            flops=6 * weight.size, bytes_accessed=22 * weight.size, transcendentals=0
        ),
    )(gradient, turn(weight), turn(momentum))
    return tuple(turn(result) for result in results)


def body(
    token_ids,
    target_ids,
    segment_ids,
    chosen,
    table,
    table_momentum,
    stack,
    stack_momentum,
    vectors,
    vector_momentum,
):
    both = ("grp", "cli")
    models, block_rows, model_width = table.shape
    stack_part = stack.shape[1]
    seq_len = token_ids.shape[1]
    groups = lax.axis_size("grp")
    members = lax.axis_size("cli")
    devices = groups * members
    share = members // models
    local = members // share
    device_index = lax.axis_index(both)
    group_index = lax.axis_index("grp")
    member_index = lax.axis_index("cli")
    model_own = member_index // share
    part_own = member_index % share
    model_range = jnp.arange(models, dtype=jnp.int32)

    def per_member(rows):
        return jnp.repeat(rows, share, axis=0) if share > 1 else rows

    slab = -(-(stack_part + ROUND_ROWS) // SLAB_STEP) * SLAB_STEP
    round_rows = slab - stack_part

    facts = jnp.concatenate([token_ids[0], target_ids[0], segment_ids[0], chosen])
    facts = jnp.pad(facts, (0, -facts.size % LANES))[None]
    facts, table_low = opening(facts, table, groups, members, 5)
    facts = facts[:, 0]
    tokens = facts[:, :seq_len]
    targets = facts[:, seq_len : 2 * seq_len]
    segments = facts[:, 2 * seq_len : 3 * seq_len]
    choices = facts[:, 3 * seq_len]
    valid = jnp.concatenate(
        [
            (segments[:, :-1] == segments[:, 1:]).astype(jnp.float32),
            jnp.zeros((devices, 1), jnp.float32),
        ],
        axis=1,
    )
    counts = jnp.sum(valid, axis=1)
    choice_table = (choices[:, None] == model_range[None, :]).astype(jnp.float32)
    totals = jnp.sum(choice_table * counts[:, None], axis=0)
    total_of = jnp.sum(choice_table * totals[None, :], axis=1)

    fine = 16 if block_rows % 64 else 64
    coarse = block_rows // fine
    flat_tokens = tokens.reshape(-1)
    high_hot = (
        (flat_tokens // fine)[:, None] == jnp.arange(devices * coarse, dtype=jnp.int32)[None, :]
    ).astype(jnp.bfloat16)
    low_hot = ((flat_tokens % fine)[:, None] == jnp.arange(fine, dtype=jnp.int32)[None, :]).astype(
        jnp.bfloat16
    )
    seen = (outer_rows(high_hot, low_hot) > 0).astype(jnp.float32)
    before = product(
        seen.astype(jnp.bfloat16),
        jnp.triu(jnp.ones((fine, fine), jnp.bfloat16), 1),
    )
    sums = jnp.sum(seen, axis=1).reshape(devices, coarse)
    uniques = jnp.sum(sums, axis=1)
    ahead = jnp.sum(
        jnp.where(
            jnp.arange(coarse)[None, None, :] < jnp.arange(coarse)[None, :, None],
            sums[:, None, :],
            0.0,
        ),
        axis=2,
    )
    places = before + ahead.reshape(-1, 1)
    rounds = jnp.max(jnp.ceil(uniques / round_rows)).astype(jnp.int32)
    own_places = lax.dynamic_slice(places, (device_index * coarse, 0), (coarse, fine)).reshape(-1)
    own_seen = lax.dynamic_slice(seen, (device_index * coarse, 0), (coarse, fine)).reshape(-1)
    own_places = jnp.where(own_seen > 0, own_places, -1.0).astype(jnp.int32)
    first_client = group_index * members + part_own * local
    my_tokens = lax.dynamic_slice(tokens, (first_client, 0), (local, seq_len)).reshape(-1)
    my_segments = lax.dynamic_slice(segments, (first_client, 0), (local, seq_len))
    my_choices = lax.dynamic_slice(choices, (first_client,), (local,))
    my_high = (
        (my_tokens // fine)[:, None] == jnp.arange(devices * coarse, dtype=jnp.int32)[None, :]
    ).astype(jnp.bfloat16)
    my_low = (my_tokens % fine)[:, None] == jnp.arange(fine, dtype=jnp.int32)[None, :]
    split_places = jnp.concatenate(
        [jnp.floor(places / 64.0), places - 64.0 * jnp.floor(places / 64.0)], axis=1
    ).astype(jnp.bfloat16)
    picked_places = product(my_high, split_places)
    picked_places = 64.0 * picked_places[:, :fine] + picked_places[:, fine:]
    my_places = jnp.sum(jnp.where(my_low, picked_places, 0.0), axis=1).astype(jnp.int32)
    my_owner = my_tokens // block_rows

    def offered(start):
        wanted = jnp.arange(round_rows, dtype=jnp.int32) + start
        pick = (own_places[None, :] == wanted[:, None]).astype(jnp.bfloat16)
        rows = jnp.einsum("ur,krd->kud", pick, table_low, preferred_element_type=jnp.float32)
        return rows.astype(jnp.bfloat16)

    def inside(start):
        offset = my_places - start
        return ((offset >= 0) & (offset < round_rows), offset)

    def another(carry):
        index, embedded = carry
        start = index * round_rows
        turned = lax.all_to_all(per_member(offered(start)), "cli", 0, 0, tiled=True)
        pool = lax.all_gather(turned, "grp", axis=0, tiled=True).reshape(-1, model_width)
        here, offset = inside(start)
        found = jnp.take(pool, jnp.where(here, my_owner * round_rows + offset, 0), axis=0)
        return (index + 1, jnp.where(here[:, None], found.astype(jnp.float32), embedded))

    slabs = jnp.concatenate([stack.astype(jnp.bfloat16), offered(0)], axis=1)
    pool = spread(per_member(slabs), groups, members, 1, False, 2)
    here, offset = inside(0)
    at = jnp.where(here, my_owner * slab + stack_part + offset, -1)
    weights, embedded = unpack(pool, stack_part, at[:, None])
    _, embedded = lax.while_loop(
        lambda carry: carry[0] < rounds, another, (jnp.int32(1), embedded)
    )
    vector_one = lax.dynamic_index_in_dim(vectors, model_own, 0, keepdims=False)
    inputs = embedded + jnp.tile(weights[12 * model_width :].astype(jnp.float32), (local, 1))
    saved = layer_forward(weights, vector_one, inputs, my_segments)
    normed_out = saved[11]

    target_local = targets - device_index * block_rows
    target_local = jnp.where((target_local >= 0) & (target_local < block_rows), target_local, -1)
    target_blocks = target_local.reshape(groups * share, 1, local * seq_len)
    if devices * normed_out.size * 2 <= POOL_BYTES:
        outs_all, everything = spread_score(
            normed_out[None], table_low, target_blocks, groups, members, share, 2
        )
    else:
        outs_all = spread(normed_out[None], groups, members, 2, True, 2)
        stats = head_stats(outs_all, table_low, target_blocks, groups, members, share)
        shares = lax.all_to_all(stats, both, 0, 0, tiled=True)
        log_total = jax.nn.logsumexp(shares[:, 0], axis=0)
        token_loss = log_total - jnp.sum(shares[:, 1], axis=0)
        everything = share_all(jnp.stack([log_total, token_loss]), both, devices)
    everything = (
        everything.reshape(groups, models, share, 2, local, seq_len)
        .transpose(3, 1, 0, 2, 4, 5)
        .reshape(2, models, devices, seq_len)
    )
    all_losses = jnp.sum(everything[1] * valid[None], axis=2)
    loss = jnp.sum(choice_table.T * all_losses / total_of[None, :])
    client_losses = lax.dynamic_slice(
        (all_losses / counts[None, :]).T, (device_index, 0), (1, models)
    )
    chosen_total = jnp.sum(choice_table.T[:, :, None] * everything[0], axis=0)

    numbers = jnp.sum(choice_table, axis=0)
    padded = QUAD * jnp.ceil(numbers / QUAD)
    offsets = jnp.cumsum(padded) - padded
    earlier = (
        jnp.arange(devices)[None, :] < jnp.arange(devices)[:, None]
    ) & (choices[None, :] == choices[:, None])
    slot_of = jnp.sum(choice_table * offsets[None, :], axis=1) + jnp.sum(
        earlier.astype(jnp.float32), axis=1
    )
    steps = (devices + (QUAD - 1) * models) // QUAD
    slots = QUAD * steps
    tokens_step = QUAD * seq_len
    at_slot = jnp.arange(slots)[:, None] == slot_of.astype(jnp.int32)[None, :]
    filled = jnp.any(at_slot, axis=1)
    client_at = jnp.sum(jnp.where(at_slot, jnp.arange(devices)[None, :], 0), axis=1).astype(
        jnp.int32
    )
    step_start = float(QUAD) * jnp.arange(steps)
    used = (jnp.sum(padded) / QUAD).astype(jnp.int32)[None]
    model_of = (
        jnp.sum((step_start[:, None] >= offsets[None, :]).astype(jnp.int32), axis=1) - 1
    ).astype(jnp.int32)
    fresh = jnp.concatenate(
        [jnp.ones((1,), jnp.int32), (model_of[1:] != model_of[:-1]).astype(jnp.int32)]
    )
    within = client_at % members
    piece_at = (
        (client_at // members * members + jnp.repeat(model_of, QUAD) * share + within // local) * local
        + within % local
    ).astype(jnp.int32)
    weight_rows = valid / total_of[:, None]
    slot_log = jnp.where(filled[:, None], jnp.take(chosen_total, client_at, axis=0), 1e30)
    slot_weight = jnp.where(filled[:, None], jnp.take(weight_rows, client_at, axis=0), 0.0)
    slot_info = jnp.stack(
        [slot_log.reshape(steps, tokens_step), slot_weight.reshape(steps, tokens_step)], axis=1
    )
    slot_target = jnp.where(filled[:, None], jnp.take(target_local, client_at, axis=0), -1)
    spare = devices + jnp.cumsum(1 - filled.astype(jnp.int32)) - 1
    d_outs, head_grad = head_back(
        outs_all.reshape(-1, seq_len, model_width),
        table_low,
        model_of,
        fresh,
        used,
        piece_at,
        jnp.where(filled, client_at, spare).astype(jnp.int32),
        slot_info,
        slot_target.reshape(steps, 1, tokens_step),
    )
    d_group = collect(d_outs, groups, members, 4)
    d_mine = lax.dynamic_slice(
        d_group, (part_own * local, 0, 0), (local, seq_len, model_width)
    ).astype(jnp.float32)
    d_final = jnp.where((my_choices == model_own)[:, None, None], d_mine, 0.0).reshape(
        local * seq_len, model_width
    )
    pairs, grad_places, vector_rows, d_inputs = layer_backward(
        weights, vector_one, inputs, my_segments, saved, d_final
    )
    d_wide = d_inputs.astype(jnp.bfloat16)
    if share > 1:
        d_wide = lax.dynamic_update_slice(
            jnp.zeros((members * seq_len, model_width), jnp.bfloat16),
            d_wide,
            (part_own * local * seq_len, 0),
        )
    d_wide, pairs, vector_rows = lax.optimization_barrier((d_wide, pairs, vector_rows))
    d_turned = lax.all_to_all(
        d_wide.reshape(members, seq_len, model_width), "cli", 0, 0, tiled=True
    )
    stack_rows = jnp.concatenate(
        [outer_rows(left, right).astype(jnp.bfloat16) for left, right in pairs]
        + [grad_places.astype(jnp.bfloat16)],
        axis=0,
    )
    stack_rows, d_turned = lax.optimization_barrier((stack_rows, d_turned))
    stack_sum = lax.psum_scatter(stack_rows, "grp", scatter_dimension=0, tiled=True)
    d_client = jnp.sum(d_turned.astype(jnp.float32), axis=0, keepdims=True).astype(jnp.bfloat16)
    d_all = spread(d_client, groups, members, 3, True, 2)
    d_all, vector_rows = lax.optimization_barrier((d_all, vector_rows))
    vector_piece = vector_rows.size // groups
    vector_part = lax.all_to_all(
        vector_rows.reshape(groups, vector_piece), "grp", 0, 0, tiled=True
    )

    token_local = tokens - device_index * block_rows
    token_local = jnp.where((token_local >= 0) & (token_local < block_rows), token_local, -1)
    slot_token = jnp.where(filled[:, None], jnp.take(token_local, client_at, axis=0), -1)
    pair_start = (offsets / 2.0).astype(jnp.int32)
    pair_end = pair_start + jnp.ceil(numbers / 2.0).astype(jnp.int32)
    schedule = (pair_start, pair_end, client_at[0::2], client_at[1::2])
    slot_token = slot_token.reshape(slots // 2, 1, 2 * seq_len)
    lead = models - 1

    states = finish_table(d_all, head_grad, table, table_momentum, schedule, slot_token, 0, lead, ())
    stack_sum, states, vector_part = lax.optimization_barrier((stack_sum, states, vector_part))
    stack_back = lax.all_to_all(
        stack_sum.reshape(members, stack_part, model_width), "cli", 0, 0, tiled=True
    )
    if share > 1:
        stack_back = jnp.sum(
            stack_back.astype(jnp.float32).reshape(models, share, stack_part, model_width), axis=1
        )
    states = finish_table(
        d_all, head_grad, table, table_momentum, schedule, slot_token, lead, models - lead, states
    )
    stack_back, vector_part, states = lax.optimization_barrier((stack_back, vector_part, states))
    table_grad, table_momentum_new, table_new = states
    vector_parts = share_all(jnp.sum(vector_part, axis=0), both, devices)
    vector_grad = jnp.sum(vector_parts.reshape(groups, models, share, vector_piece), axis=2)
    vector_grad = vector_grad.transpose(1, 0, 2).reshape(vectors.shape)
    stack_grad, stack_momentum_new, stack_new = update_stack(stack_back, stack, stack_momentum)
    vector_momentum_new, vector_new = update(vectors, vector_momentum, vector_grad, vector_rate)
    return (
        loss,
        client_losses,
        table_grad,
        table_momentum_new,
        table_new,
        stack_grad,
        stack_momentum_new,
        stack_new,
        vector_grad,
        vector_momentum_new,
        vector_new,
    )


def solution(mesh):
    rows = P(("grp", "cli"), None)
    parts = P(None, ("grp", "cli"), None)
    return jax.shard_map(
        body,
        mesh=mesh,
        in_specs=(rows, rows, rows, P(("grp", "cli")), parts, parts, parts, parts, P(), P()),
        out_specs=(P(), rows, parts, parts, parts, parts, parts, parts, P(), P(), P()),
        check_vma=False,
    )
```

```python
import functools
import math

import jax
import jax.numpy as jnp
from jax import lax
from jax.experimental import pallas as pl
from jax.experimental.pallas import tpu as pltpu
from jax.sharding import PartitionSpec as P

HEADS = 12
HEAD_DIM = 64


epsilon = 1e-05
momentum_decay = 0.9
table_rate = 4.0
stack_rate = 4.0
vector_rate = 50.0

ROUND_ROWS = 104
SLAB_STEP = 16
TILE = 400
LANES = 128
QUAD = 4
MIB = 1 << 20
POOL_BYTES = 32 * MIB
MESH = pl.DeviceIdType.MESH


def layer_norm(inputs, gain_row, shift_row):
    centred = inputs - jnp.mean(inputs, -1, keepdims=True)
    spread = jnp.mean(centred * centred, -1, keepdims=True)
    return centred * lax.rsqrt(spread + epsilon) * gain_row + shift_row


def project(inputs, matrix):
    return lax.dot_general(
        inputs, matrix, (((1,), (1,)), ((), ())), preferred_element_type=jnp.float32
    )


def product(inputs, matrix):
    return jnp.dot(inputs, matrix, preferred_element_type=jnp.float32)


def outer_rows(left, right):
    return lax.dot_general(
        left, right, (((0,), (0,)), ((), ())), preferred_element_type=jnp.float32
    )


def split_heads(rows, seq_len):
    return rows.reshape(-1, seq_len, HEADS, HEAD_DIM)


def attend(queries, key_rows, segment_rows):
    seq_len = segment_rows.shape[1]
    scores = jnp.einsum(
        "nqhd,nkhd->nhqk",
        split_heads(queries, seq_len),
        split_heads(key_rows, seq_len),
        preferred_element_type=jnp.float32,
    ) * HEAD_DIM ** (-0.5)
    positions = jnp.arange(seq_len)
    allowed = (positions[None, None, :] <= positions[None, :, None]) & (
        segment_rows[:, None, :] == segment_rows[:, :, None]
    )
    return jax.nn.softmax(jnp.where(allowed[:, None], scores, -1e30), axis=-1)


def layer_forward(weights, vector_one, inputs, segment_rows):
    row_count, model_width = inputs.shape
    seq_len = segment_rows.shape[1]
    normed = layer_norm(inputs, vector_one[0], vector_one[1]).astype(jnp.bfloat16)
    queries = (project(normed, weights[0:model_width]) + vector_one[6]).astype(jnp.bfloat16)
    key_rows = project(normed, weights[model_width : 2 * model_width]).astype(jnp.bfloat16)
    values = (project(normed, weights[2 * model_width : 3 * model_width]) + vector_one[7]).astype(
        jnp.bfloat16
    )
    attention = attend(queries, key_rows, segment_rows)
    mixture = jnp.einsum(
        "nhqk,nkhd->nqhd",
        attention.astype(jnp.bfloat16),
        split_heads(values, seq_len),
        preferred_element_type=jnp.float32,
    )
    mixture = mixture.reshape(row_count, model_width).astype(jnp.bfloat16)
    middle = inputs + (project(mixture, weights[3 * model_width : 4 * model_width]) + vector_one[8])
    normed_two = layer_norm(middle, vector_one[2], vector_one[3]).astype(jnp.bfloat16)
    hidden = project(normed_two, weights[4 * model_width : 8 * model_width]) + vector_one[
        10:14
    ].reshape(-1)
    active = jax.nn.gelu(hidden, approximate=True).astype(jnp.bfloat16)
    residual = middle + (
        product(active, weights[8 * model_width : 12 * model_width]) + vector_one[9]
    )
    normed_out = layer_norm(residual, vector_one[4], vector_one[5]).astype(jnp.bfloat16)
    return (
        normed,
        queries,
        key_rows,
        values,
        attention,
        mixture,
        middle,
        normed_two,
        hidden,
        active,
        residual,
        normed_out,
    )


def norm_grad(operand, gain_row, shift_row, cotangent):
    outcome, pullback = jax.vjp(layer_norm, operand, gain_row, shift_row)
    return pullback(cotangent)


def gelu_tanh(hidden):
    return jax.nn.gelu(hidden, approximate=True)


def layer_backward(weights, vector_one, inputs, segment_rows, saved, grad_out):
    row_count, model_width = inputs.shape
    seq_len = segment_rows.shape[1]
    scaling = HEAD_DIM ** (-0.5)
    (
        normed,
        queries,
        key_rows,
        values,
        attention,
        mixture,
        middle,
        normed_two,
        hidden,
        active,
        residual,
        normed_out,
    ) = saved
    d_residual, d_gain_out, d_shift_out = norm_grad(
        residual, vector_one[4], vector_one[5], grad_out
    )
    d_outer = d_residual.astype(jnp.bfloat16)
    d_bias_out = jnp.sum(d_outer.astype(jnp.float32), 0)
    d_active = project(d_outer, weights[8 * model_width : 12 * model_width])
    gelu_value, gelu_pull = jax.vjp(gelu_tanh, hidden)
    d_hidden = gelu_pull(d_active)[0].astype(jnp.bfloat16)
    d_bias_hidden = jnp.sum(d_hidden.astype(jnp.float32), 0)
    d_normed_two = product(d_hidden, weights[4 * model_width : 8 * model_width])
    d_middle_norm, d_gain_two, d_shift_two = norm_grad(
        middle, vector_one[2], vector_one[3], d_normed_two
    )
    d_middle = d_residual + d_middle_norm
    d_branch = d_middle.astype(jnp.bfloat16)
    d_bias_branch = jnp.sum(d_branch.astype(jnp.float32), 0)
    d_mixture = split_heads(
        product(d_branch, weights[3 * model_width : 4 * model_width]).astype(jnp.bfloat16), seq_len
    )
    d_attention = jnp.einsum(
        "nqhd,nkhd->nhqk", d_mixture, split_heads(values, seq_len), preferred_element_type=jnp.float32
    )
    d_values = jnp.einsum(
        "nhqk,nqhd->nkhd",
        attention.astype(jnp.bfloat16),
        d_mixture,
        preferred_element_type=jnp.float32,
    )
    d_values = d_values.reshape(row_count, model_width).astype(jnp.bfloat16)
    d_scores = (
        attention * (d_attention - jnp.sum(attention * d_attention, -1, keepdims=True))
    ).astype(jnp.bfloat16)
    d_queries = (
        jnp.einsum(
            "nhqk,nkhd->nqhd",
            d_scores,
            split_heads(key_rows, seq_len),
            preferred_element_type=jnp.float32,
        )
        * scaling
    )
    d_queries = d_queries.reshape(row_count, model_width).astype(jnp.bfloat16)
    d_keys = (
        jnp.einsum(
            "nhqk,nqhd->nkhd",
            d_scores,
            split_heads(queries, seq_len),
            preferred_element_type=jnp.float32,
        )
        * scaling
    )
    d_keys = d_keys.reshape(row_count, model_width).astype(jnp.bfloat16)
    d_joined = jnp.concatenate([d_queries, d_keys, d_values], axis=1)
    d_normed = product(d_joined, weights[0 : 3 * model_width])
    d_inputs_norm, d_gain_one, d_shift_one = norm_grad(
        inputs, vector_one[0], vector_one[1], d_normed
    )
    d_inputs = d_middle + d_inputs_norm
    grad_places = jnp.sum(d_inputs.reshape(-1, seq_len, model_width), axis=0)
    pairs = (
        (d_joined, normed),
        (d_branch, mixture),
        (d_hidden, normed_two),
        (active, d_outer),
    )
    bias_query = jnp.sum(d_queries.astype(jnp.float32), 0)
    bias_value = jnp.sum(d_values.astype(jnp.float32), 0)
    vector_rows = jnp.concatenate(
        [
            jnp.stack(
                [
                    d_gain_one,
                    d_shift_one,
                    d_gain_two,
                    d_shift_two,
                    d_gain_out,
                    d_shift_out,
                    bias_query,
                    bias_value,
                    d_bias_branch,
                    d_bias_out,
                ]
            ),
            d_bias_hidden.reshape(4, model_width),
        ],
        axis=0,
    )
    return (pairs, grad_places, vector_rows, d_inputs)


def share_all(rows, axes, size):
    return lax.all_to_all(
        jnp.broadcast_to(rows[None], (size,) + rows.shape), axes, 0, 0, tiled=True
    )


def update(weight, momentum, gradient, step_rate):
    renewed = momentum_decay * momentum + gradient
    return (renewed, weight - step_rate * (gradient + momentum_decay * renewed))


def flipped(value, offset, size):
    bit = 1
    while bit < size:
        digit = lax.rem(lax.div(offset, bit), 2)
        value = value + digit * bit * (1 - 2 * lax.rem(lax.div(value, bit), 2))
        bit *= 2
    return value


class Place:
    def __init__(self, groups, members):
        self.groups, self.members = groups, members
        self.ys = 2
        self.xs = groups // 4
        self.grp = lax.axis_index("grp")
        self.cli = lax.axis_index("cli")
        self.core = lax.rem(self.grp, 2)
        self.x = lax.rem(lax.div(self.grp, 2), self.xs)
        self.y = lax.div(self.grp, 2 * self.xs)

    def group(self, jx=0, jy=0, jc=0):
        x = flipped(self.x, jx, self.xs)
        y = flipped(self.y, jy, self.ys)
        core = self.core + jc * (1 - 2 * self.core)
        return (y * self.xs + x) * 2 + core

    def block(self, jx, jy, level, jc=0):
        return self.group(jx, jy, jc) * self.members + level

    def peer(self, jx=0, jy=0, jc=0):
        return (self.group(jx, jy, jc), self.cli)

    def level(self, level):
        return (self.grp, level)

    def nearest(self, i):
        z, last = self.cli, self.members - 1
        low = jnp.where(2 * z < last, 1, 0)
        sign = 2 * low - 1
        margin = low * z + (1 - low) * (last - z)
        step = lax.div(i + 1, 2)
        odd = lax.rem(i, 2)
        near = z + sign * step * (2 * odd - 1)
        far = z + sign * (i - margin)
        return jnp.where(i <= 2 * margin, near, far)


def greet(place):
    barrier = pltpu.get_barrier_semaphore()
    peers = [place.peer(jx=j) for j in range(1, place.xs)] + [place.peer(jy=j) for j in range(1, place.ys)]
    peers.append(place.peer(jc=1))
    peers += [place.level(lax.rem(place.cli + j, place.members)) for j in range(1, place.members)]
    for peer in peers:
        pl.semaphore_signal(barrier, inc=1, device_id=peer, device_id_type=MESH)
    pl.semaphore_wait(barrier, len(peers))


def greet_all(devices, members):
    barrier = pltpu.get_barrier_semaphore()
    me = lax.axis_index("grp") * members + lax.axis_index("cli")

    def hello(j, carry):
        other = lax.rem(me + j, devices)
        pl.semaphore_signal(
            barrier, inc=1, device_id=(lax.div(other, members), lax.rem(other, members)), device_id_type=MESH
        )
        return carry

    lax.fori_loop(1, devices, hello, 0)
    pl.semaphore_wait(barrier, devices - 1)


def spread_sems(groups, members, pieces):
    xs, ys, items = groups // 4, 2, members * pieces
    dma = pltpu.SemaphoreType.DMA
    shapes = [(items,)] * 3 + [(items, xs)] * 2 + [(items, ys)] * 2 + [(items, xs, ys)] * 6
    return [dma] + [dma(shape) for shape in shapes]


def spread_body(place, chain, pieces, src, out, sems, consume, ready=None):
    (own_sem, z_up, z_down, z_recv, x_send, x_recv, y_send, y_recv, k_send, k_recv, p_send, p_recv,
     c_send, c_recv) = sems
    xs, ys, members = place.xs, place.ys, place.members
    items = members * pieces
    size = out.shape[1] // pieces
    z = place.cli
    partner = z + 1 - 2 * lax.rem(z, 2)
    inner_x, inner_y = range(1, xs), range(1, ys)

    def move(source, target, send, recv, device):
        return pltpu.make_async_remote_copy(
            src_ref=source, dst_ref=target, send_sem=send, recv_sem=recv, device_id=device, device_id_type=MESH
        )

    class Item:
        def __init__(self, k):
            self.level = place.nearest(lax.div(k, pieces))
            self.piece = lax.rem(k, pieces)
            self.slot = self.level * pieces + self.piece
            self.even = lax.rem(self.piece, 2) == 0
            self.mine = lax.rem(self.level + z, 2) == 0 if chain else self.level >= 0
            self.rows = pl.ds(self.piece * size, size)

        def part(self, jx, jy, level=None):
            return out.at[place.block(jx, jy, self.level if level is None else level), self.rows]

        def here(self, own):
            return src.at[z if not chain else 0, self.rows] if own else self.part(0, 0)

        def up(self, own=False):
            return move(self.here(own), self.part(0, 0), z_up.at[self.slot], z_recv.at[self.slot], place.level(z + 1))

        def down(self, own=False):
            return move(self.here(own), self.part(0, 0), z_down.at[self.slot], z_recv.at[self.slot], place.level(z - 1))

        def straight(self):
            return move(
                src.at[self.level, self.rows], self.part(0, 0, z), z_up.at[self.slot],
                z_recv.at[z * pieces + self.piece], place.level(self.level),
            )

        def landed(self):
            part = self.part(0, 0)
            return move(part, part, z_up.at[self.slot], z_recv.at[self.slot], place.level(partner))

        def to_x(self, jx, own=False):
            return move(self.here(own), self.part(0, 0), x_send.at[self.slot, jx], x_recv.at[self.slot, jx], place.peer(jx=jx))

        def to_y(self, jy, own=False):
            return move(self.here(own), self.part(0, 0), y_send.at[self.slot, jy], y_recv.at[self.slot, jy], place.peer(jy=jy))

        def corner_a(self, jx, jy):
            part = self.part(jx, 0)
            return move(part, part, k_send.at[self.slot, jx, jy], k_recv.at[self.slot, jx, jy], place.peer(jy=jy))

        def corner_b(self, jx, jy):
            part = self.part(0, jy)
            return move(part, part, k_send.at[self.slot, jx, jy], k_recv.at[self.slot, jx, jy], place.peer(jx=jx))

        def corner_z(self, jx, jy):
            part = self.part(jx, jy)
            return move(part, part, p_send.at[self.slot, jx, jy], p_recv.at[self.slot, jx, jy], place.level(partner))

        def to_core(self, jx, jy, own=False):
            part = self.part(jx, jy)
            return move(self.here(True) if own else part, part, c_send.at[self.slot, jx, jy], c_recv.at[self.slot, jx, jy], place.peer(jc=1))

    own = pltpu.make_async_copy(src.at[z if not chain else 0], out.at[place.block(0, 0, z)], own_sem)
    own.start()
    if not chain:
        for piece in range(pieces):
            Item(pieces + piece).straight().start()

    def columns(k):
        item = Item(k)
        level = item.level

        @pl.when(k < pieces)
        def mine_first():
            if chain:
                @pl.when(z + 1 < members)
                def onward():
                    item.up(True).start()

                @pl.when(z > 0)
                def back():
                    item.down(True).start()

            for jx in inner_x:
                item.to_x(jx, True).start()
            for jy in inner_y:
                item.to_y(jy, True).start()
            item.to_core(0, 0, True).start()

        @pl.when(k >= pieces)
        def arrive():
            item.landed().wait_recv()
            if chain:
                @pl.when((level < z) & (z + 1 < members))
                def onward():
                    item.up().start()

                @pl.when((level > z) & (z > 0))
                def back():
                    item.down().start()
            else:
                @pl.when(k + pieces < items)
                def following():
                    Item(k + pieces).straight().start()

            for jx in inner_x:
                item.to_x(jx).start()
            for jy in inner_y:
                item.to_y(jy).start()
            item.to_core(0, 0).start()

    def edges(k):
        item = Item(k)
        for jx in inner_x:
            item.to_x(jx).wait_recv()

            @pl.when(item.mine & item.even)
            def pass_a():
                for jy in inner_y:
                    item.corner_a(jx, jy).start()

            item.to_core(jx, 0).start()
        for jy in inner_y:
            item.to_y(jy).wait_recv()

            @pl.when(item.mine & jnp.logical_not(item.even))
            def pass_b():
                for jx in inner_x:
                    item.corner_b(jx, jy).start()

            item.to_core(0, jy).start()

    def corners(k):
        item = Item(k)

        @pl.when(item.mine)
        def mine_now():
            for jx in inner_x:
                for jy in inner_y:
                    item.corner_a(jx, jy).wait_recv()
                    if chain:
                        item.corner_z(jx, jy).start()
                    item.to_core(jx, jy).start()

    def handed(k):
        item = Item(k)

        @pl.when(jnp.logical_not(item.mine))
        def from_partner():
            for jx in inner_x:
                for jy in inner_y:
                    item.corner_z(jx, jy).wait_recv()
                    item.to_core(jx, jy).start()

    spots = xs * ys
    lag_edge, lag_corner = (2, 4) if chain else (1, 3)
    lag_handed = pieces + 6 if chain else lag_corner
    lag_end = lag_handed + 1

    def tick(t, carry):
        @pl.when(t < items)
        def arrivals():
            columns(t)

        @pl.when((t >= lag_edge) & (t < items + lag_edge))
        def sides():
            edges(t - lag_edge)

        @pl.when((t >= lag_corner) & (t < items + lag_corner))
        def far():
            corners(t - lag_corner)

        if chain:
            @pl.when((t >= lag_handed) & (t < items + lag_handed))
            def others():
                handed(t - lag_handed)

        def visit(e, carry):
            jc = lax.div(e, spots)
            spot = lax.rem(e, spots)
            jx, jy = lax.rem(spot, xs), lax.div(spot, xs)
            far = jnp.minimum(jx, 1) + jnp.minimum(jy, 1)
            lag = jnp.where(far == 0, 1, jnp.where(far == 1, lag_edge + 1, lag_end))
            k = t - lag

            @pl.when((k >= 0) & (k < items))
            def valid():
                item = Item(k)

                @pl.when(jc == 1)
                def shared():
                    item.to_core(jx, jy).wait_recv()

                if consume is not None:
                    consume(place.block(jx, jy, item.level, jc), item.level, item.piece)

            return carry

        return lax.fori_loop(0, 2 * spots, visit, carry)

    if ready is not None:
        own.wait()
        ready()
    lax.fori_loop(0, items + lag_end, tick, 0)

    def close(k, carry):
        item = Item(k)
        level = item.level
        if chain:
            @pl.when((level <= z) & (z + 1 < members))
            def onward():
                item.up().wait_send()

            @pl.when((level >= z) & (z > 0))
            def back():
                item.down().wait_send()
        else:
            @pl.when(k >= pieces)
            def sent():
                item.straight().wait_send()

        for jx in inner_x:
            item.to_x(jx).wait_send()
        for jy in inner_y:
            item.to_y(jy).wait_send()
        for jx in range(xs):
            for jy in range(ys):
                item.to_core(jx, jy).wait_send()

        @pl.when(item.mine)
        def mine_done():
            for jx in inner_x:
                for jy in inner_y:
                    item.corner_a(jx, jy).wait_send()
                    if chain:
                        item.corner_z(jx, jy).wait_send()

        return carry

    lax.fori_loop(0, items, close, 0)
    if ready is None:
        own.wait()


def spread_kernel(groups, members, chain, pieces, src, out, *sems):
    place = Place(groups, members)
    greet(place)
    spread_body(place, chain, pieces, src, out, sems, None)


def spread(src, groups, members, collective_id, chain, pieces):
    count, rows, width = src.shape
    return pl.pallas_call(
        functools.partial(spread_kernel, groups, members, chain, pieces),
        out_shape=jax.ShapeDtypeStruct((groups * members, rows, width), src.dtype),
        in_specs=[pl.BlockSpec(memory_space=pl.ANY)],
        out_specs=pl.BlockSpec(memory_space=pl.ANY),
        scratch_shapes=spread_sems(groups, members, pieces),
        compiler_params=pltpu.CompilerParams(collective_id=collective_id, has_side_effects=True),
        cost_estimate=pl.CostEstimate(
            flops=0, bytes_accessed=4 * groups * members * rows * width, transcendentals=0
        ),
    )(src)


def tile_of(part_rows):
    return TILE if part_rows % TILE == 0 else part_rows


def opening_kernel(groups, members, facts_ref, table_ref, facts_out, low_ref, own_sem, send_sems, recv_sems):
    devices = groups * members
    tiles = pl.num_programs(1)
    step = pl.program_id(0) * tiles + pl.program_id(1)
    last = pl.num_programs(0) * tiles - 1
    me = lax.axis_index("grp") * members + lax.axis_index("cli")

    def other(j):
        return lax.rem(me + j, devices)

    def place(device):
        return (lax.div(device, members), lax.rem(device, members))

    def give(j):
        return pltpu.make_async_remote_copy(
            src_ref=facts_ref, dst_ref=facts_out.at[me], send_sem=send_sems.at[j], recv_sem=recv_sems.at[j],
            device_id=place(other(j)), device_id_type=MESH,
        )

    own = pltpu.make_async_copy(facts_ref, facts_out.at[me], own_sem)

    @pl.when(step == 0)
    def begin():
        barrier = pltpu.get_barrier_semaphore()

        def hello(j, carry):
            pl.semaphore_signal(barrier, inc=1, device_id=place(other(j)), device_id_type=MESH)
            return carry

        own.start()
        lax.fori_loop(1, devices, hello, 0)

    @pl.when(step == last // 2)
    def exchange():
        def start(j, carry):
            give(j).start()
            return carry

        pl.semaphore_wait(pltpu.get_barrier_semaphore(), devices - 1)
        lax.fori_loop(1, devices, start, 0)

    low_ref[...] = table_ref[...].astype(low_ref.dtype)

    @pl.when(step == last)
    def end():
        def finish(j, carry):
            give(j).wait_send()
            pltpu.make_async_remote_copy(
                src_ref=facts_ref, dst_ref=facts_out.at[lax.rem(me + devices - j, devices)],
                send_sem=send_sems.at[j], recv_sem=recv_sems.at[j], device_id=place(other(j)), device_id_type=MESH,
            ).wait_recv()
            return carry

        lax.fori_loop(1, devices, finish, 0)
        own.wait()


def opening(facts, table, groups, members, collective_id):
    devices = groups * members
    models, part_rows, width = table.shape
    tile_rows = tile_of(part_rows)
    piece = pl.BlockSpec((1, tile_rows, width), lambda m, t: (m, t, 0))
    anywhere = pl.BlockSpec(memory_space=pl.ANY)
    dma = pltpu.SemaphoreType.DMA
    return pl.pallas_call(
        functools.partial(opening_kernel, groups, members),
        out_shape=(
            jax.ShapeDtypeStruct((devices,) + facts.shape, facts.dtype),
            jax.ShapeDtypeStruct(table.shape, jnp.bfloat16),
        ),
        grid=(models, part_rows // tile_rows),
        in_specs=[anywhere, piece],
        out_specs=(anywhere, piece),
        scratch_shapes=[dma, dma((devices,)), dma((devices,))],
        compiler_params=pltpu.CompilerParams(collective_id=collective_id, has_side_effects=True),
        cost_estimate=pl.CostEstimate(flops=0, bytes_accessed=6 * table.size, transcendentals=0),
    )(facts, table)


def score_kernel(groups, members, share, pieces, src, table, target, out, answer, *rest):
    part, pool, stat, inbox, part_sem, out_sems, go_send, go_recv, back_send, back_recv = rest[:10]
    sems = rest[10:]
    devices = groups * members
    place = Place(groups, members)
    load_table = pltpu.make_async_copy(table, part, part_sem)
    load_table.start()
    greet_all(devices, members)
    rows = pool.shape[1]
    size = rows // pieces

    def keep(block, piece):
        here = pl.ds(pl.multiple_of(piece * size, size), size)
        return pltpu.make_async_copy(pool.at[block, here], out.at[block, here], out_sems.at[block, piece])

    def consume(block, level, piece):
        keep(block, piece).start()
        here = pl.ds(pl.multiple_of(piece * size, size), size)
        model = lax.div(level, share)
        wanted = target[lax.div(block, members) * share + lax.rem(level, share), :, here]
        outs = pool[block, here]
        part_rows = part.shape[1]
        tile = tile_of(part_rows)
        marks = lax.broadcasted_iota(jnp.int32, (tile, size), 0)
        tops, totals, hits = [], [], []
        for first in range(0, part_rows, tile):
            logits = project(part[model, pl.ds(first, tile)], outs)
            hit = jnp.where(marks == wanted - first, logits, 0.0).reshape(-1, 8, size)
            hits.append(jnp.sum(hit, axis=0))
            logits = logits.reshape(-1, 8, size)
            top = jnp.max(logits, axis=0)
            tops.append(top)
            totals.append(jnp.sum(jnp.exp(logits - top[None]), axis=0))
        highest = jnp.max(functools.reduce(jnp.maximum, tops), axis=0, keepdims=True)
        total = sum(t * jnp.exp(m - highest) for t, m in zip(totals, tops))
        stat[block, 0:1, here] = highest + jnp.log(jnp.sum(total, axis=0, keepdims=True))
        stat[block, 1:2, here] = jnp.sum(sum(hits), axis=0, keepdims=True)

    spread_body(place, True, pieces, src, pool, sems, consume, load_table.wait)

    me = place.block(0, 0, place.cli)

    def device(index):
        return (lax.div(index, members), lax.rem(index, members))

    def ahead(j):
        return lax.rem(me + j, devices)

    def behind(j):
        return lax.rem(me + devices - j, devices)

    def go(j, source, target):
        return pltpu.make_async_remote_copy(
            src_ref=stat.at[source], dst_ref=inbox.at[target], send_sem=go_send.at[j], recv_sem=go_recv.at[j],
            device_id=device(ahead(j)), device_id_type=MESH,
        )

    def back(j, source):
        return pltpu.make_async_remote_copy(
            src_ref=answer.at[source], dst_ref=answer.at[source], send_sem=back_send.at[j],
            recv_sem=back_recv.at[j], device_id=device(ahead(j)), device_id_type=MESH,
        )

    def loop(step):
        def run(j, carry):
            step(j)
            return carry

        lax.fori_loop(1, devices, run, 0)

    loop(lambda j: go(j, ahead(j), me).start())
    inbox[me] = stat[me]
    loop(lambda j: go(j, me, behind(j)).wait_recv())
    logs = inbox[:, 0, :]
    top = jnp.max(logs, axis=0, keepdims=True)
    log_total = top + jnp.log(jnp.sum(jnp.exp(logs - top), axis=0, keepdims=True))
    answer[me, 0:1, :] = log_total
    answer[me, 1:2, :] = log_total - jnp.sum(inbox[:, 1, :], axis=0, keepdims=True)
    loop(lambda j: back(j, me).start())
    loop(lambda j: back(j, behind(j)).wait_recv())
    loop(lambda j: go(j, ahead(j), me).wait_send())
    loop(lambda j: back(j, me).wait_send())

    def close(block, carry):
        for piece in range(pieces):
            keep(block, piece).wait()
        return carry

    lax.fori_loop(0, groups * members, close, 0)


def spread_score(src, table_low, target_blocks, groups, members, share, collective_id, pieces=2):
    _, rows, width = src.shape
    blocks = groups * members
    return pl.pallas_call(
        functools.partial(score_kernel, groups, members, share, pieces),
        out_shape=(
            jax.ShapeDtypeStruct((blocks, rows, width), src.dtype),
            jax.ShapeDtypeStruct((blocks, 2, rows), jnp.float32),
        ),
        in_specs=[
            pl.BlockSpec(memory_space=pl.ANY),
            pl.BlockSpec(memory_space=pl.ANY),
            pl.BlockSpec(memory_space=pltpu.VMEM),
        ],
        out_specs=(pl.BlockSpec(memory_space=pl.ANY), pl.BlockSpec(memory_space=pltpu.VMEM)),
        scratch_shapes=[
            pltpu.VMEM(table_low.shape, table_low.dtype),
            pltpu.VMEM((blocks, rows, width), src.dtype),
            pltpu.VMEM((blocks, 2, rows), jnp.float32),
            pltpu.VMEM((blocks, 2, rows), jnp.float32),
            pltpu.SemaphoreType.DMA,
            pltpu.SemaphoreType.DMA((blocks, pieces)),
        ]
        + [pltpu.SemaphoreType.DMA((blocks,))] * 4
        + spread_sems(groups, members, pieces),
        compiler_params=pltpu.CompilerParams(
            collective_id=collective_id, has_side_effects=True, vmem_limit_bytes=60 * MIB
        ),
        cost_estimate=pl.CostEstimate(
            flops=2 * blocks * rows * table_low.shape[1] * width,
            bytes_accessed=2 * blocks * rows * width * 2,
            transcendentals=blocks * rows * table_low.shape[1],
        ),
    )(src, table_low, target_blocks)


def stats_kernel(outs_ref, table_ref, target_ref, stat_ref):
    logits = project(table_ref[0], outs_ref[0])
    highest = jnp.max(logits, axis=0, keepdims=True)
    total = jnp.sum(jnp.exp(logits - highest), axis=0, keepdims=True)
    rows = lax.broadcasted_iota(jnp.int32, logits.shape, 0)
    hit = jnp.sum(jnp.where(rows == target_ref[0], logits, 0.0), axis=0, keepdims=True)
    stat_ref[0, 0:1, :] = highest + jnp.log(total)
    stat_ref[0, 1:2, :] = hit


def head_stats(outs_all, table_low, target_blocks, groups, members, share):
    blocks, rows, width = outs_all.shape
    part_rows = table_low.shape[1]
    return pl.pallas_call(
        stats_kernel,
        out_shape=jax.ShapeDtypeStruct((blocks, 2, rows), jnp.float32),
        grid=(members, groups),
        in_specs=[
            pl.BlockSpec((1, rows, width), lambda z, g: (g * members + z, 0, 0)),
            pl.BlockSpec((1, part_rows, width), lambda z, g: (z // share, 0, 0)),
            pl.BlockSpec((1, 1, rows), lambda z, g: (g * share + z % share, 0, 0)),
        ],
        out_specs=pl.BlockSpec((1, 2, rows), lambda z, g: (g * members + z, 0, 0)),
        compiler_params=pltpu.CompilerParams(vmem_limit_bytes=56 * MIB),
        cost_estimate=pl.CostEstimate(
            flops=2 * blocks * rows * part_rows * width,
            bytes_accessed=2 * outs_all.size + 2 * table_low.size,
            transcendentals=blocks * rows * part_rows,
        ),
    )(outs_all, table_low, target_blocks)


def collect_kernel(groups, members, source, out, work, from_core, from_x, from_y, then_y, then_x, from_z, *sems):
    (load_sem, core_send, core_recv, x_send, x_recv, y_send, y_recv, yy_send, yy_recv, xx_send, xx_recv, z_send,
     z_recv, g_send, g_recv) = sems
    place = Place(groups, members)
    greet(place)
    xs, ys = place.xs, place.ys
    half = members // 2
    z = place.cli
    order = sorted(
        ((jx, jy) for jx in range(xs) for jy in range(ys)), key=lambda spot: -(spot[0] > 0) - (spot[1] > 0)
    )
    started = []

    def send(source_ref, target_ref, send_sem, recv_sem, device):
        copy = pltpu.make_async_remote_copy(
            src_ref=source_ref, dst_ref=target_ref, send_sem=send_sem, recv_sem=recv_sem, device_id=device,
            device_id_type=MESH,
        )
        copy.start()
        started.append(copy)

    def arrival(target_ref, send_sem, recv_sem, device):
        pltpu.make_async_remote_copy(
            src_ref=target_ref, dst_ref=target_ref, send_sem=send_sem, recv_sem=recv_sem, device_id=device,
            device_id_type=MESH,
        ).wait_recv()

    def add(ref, others):
        total = ref[...].astype(jnp.float32)
        for other in others:
            total = total + other[...].astype(jnp.float32)
        ref[...] = total.astype(ref.dtype)

    def clients(p):
        return (p, p + half)

    spots = [(jy * xs + jx, jx, jy) for jx, jy in order]
    loads = {}
    for p in range(half):
        for k, jx, jy in spots:
            for c in clients(p):
                send(
                    source.at[place.group(jx, jy, 1) * members + c], from_core.at[k, c], core_send.at[k, c],
                    core_recv.at[k, c], place.peer(jc=1),
                )
                loads[k, c] = pltpu.make_async_copy(
                    source.at[place.group(jx, jy, 0) * members + c], work.at[k, c], load_sem.at[k, c]
                )
                loads[k, c].start()
    for p in range(half):
        a, b = clients(p)
        for k, jx, jy in spots:
            for c in (a, b):
                loads[k, c].wait()
                arrival(from_core.at[k, c], core_send.at[k, c], core_recv.at[k, c], place.peer(jc=1))
                add(work.at[k, c], [from_core.at[k, c]])
            if jx:
                send(work.at[k, a], from_x.at[p, jx, jy], x_send.at[p, jx, jy], x_recv.at[p, jx, jy], place.peer(jx=jx))
            if jy:
                send(work.at[k, b], from_y.at[p, jx, jy], y_send.at[p, jx, jy], y_recv.at[p, jx, jy], place.peer(jy=jy))

    def second(p):
        a, b = clients(p)
        for jy in reversed(range(ys)):
            k = jy * xs
            for jx in range(1, xs):
                arrival(from_x.at[p, jx, jy], x_send.at[p, jx, jy], x_recv.at[p, jx, jy], place.peer(jx=jx))
            add(work.at[k, a], [from_x.at[p, jx, jy] for jx in range(1, xs)])
            if jy:
                send(work.at[k, a], then_y.at[p, jy], yy_send.at[p, jy], yy_recv.at[p, jy], place.peer(jy=jy))
        for jx in reversed(range(xs)):
            for jy in range(1, ys):
                arrival(from_y.at[p, jx, jy], y_send.at[p, jx, jy], y_recv.at[p, jx, jy], place.peer(jy=jy))
            add(work.at[jx, b], [from_y.at[p, jx, jy] for jy in range(1, ys)])
            if jx:
                send(work.at[jx, b], then_x.at[p, jx], xx_send.at[p, jx], xx_recv.at[p, jx], place.peer(jx=jx))

    def third(p):
        a, b = clients(p)
        for jy in range(1, ys):
            arrival(then_y.at[p, jy], yy_send.at[p, jy], yy_recv.at[p, jy], place.peer(jy=jy))
        add(work.at[0, a], [then_y.at[p, jy] for jy in range(1, ys)])
        for jx in range(1, xs):
            arrival(then_x.at[p, jx], xx_send.at[p, jx], xx_recv.at[p, jx], place.peer(jx=jx))
        add(work.at[0, b], [then_x.at[p, jx] for jx in range(1, xs)])
        for c in (a, b):
            @pl.when(z != c)
            def give():
                pltpu.make_async_remote_copy(
                    src_ref=work.at[0, c], dst_ref=from_z.at[z], send_sem=z_send.at[c], recv_sem=z_recv.at[z],
                    device_id=place.level(c), device_id_type=MESH,
                ).start()

    for p in range(half + 1):
        if p < half:
            second(p)
        if p:
            third(p - 1)
    total = work[0, z].astype(jnp.float32)
    for j in range(1, members):
        level = lax.rem(z + members - j, members)
        arrival(from_z.at[level], z_send.at[level], z_recv.at[level], place.level(level))
        total = total + from_z[level].astype(jnp.float32)
    out[z] = total.astype(out.dtype)
    for j in range(1, members):
        send(out.at[z], out.at[z], g_send.at[j], g_recv.at[j], place.level(lax.rem(z + j, members)))
    for j in range(1, members):
        level = lax.rem(z + members - j, members)
        arrival(out.at[level], g_send.at[j], g_recv.at[j], place.level(level))
    for copy in started:
        copy.wait_send()
    for c in range(members):
        @pl.when(z != c)
        def given():
            pltpu.make_async_remote_copy(
                src_ref=work.at[0, c], dst_ref=from_z.at[z], send_sem=z_send.at[c], recv_sem=z_recv.at[z],
                device_id=place.level(c), device_id_type=MESH,
            ).wait_send()


def collect(parts, groups, members, collective_id):
    _, seq_len, width = parts.shape
    xs, ys, half = groups // 4, 2, members // 2
    dma = pltpu.SemaphoreType.DMA

    def held(*shape):
        return pltpu.VMEM(shape + (seq_len, width), parts.dtype)

    return pl.pallas_call(
        functools.partial(collect_kernel, groups, members),
        out_shape=jax.ShapeDtypeStruct((members, seq_len, width), parts.dtype),
        in_specs=[pl.BlockSpec(memory_space=pl.ANY)],
        out_specs=pl.BlockSpec(memory_space=pltpu.VMEM),
        scratch_shapes=[
            held(xs * ys, members),
            held(xs * ys, members),
            held(half, xs, ys),
            held(half, xs, ys),
            held(half, ys),
            held(half, xs),
            held(members),
        ]
        + [dma((xs * ys, members))] * 3
        + [dma((half, xs, ys))] * 4
        + [dma((half, ys))] * 2
        + [dma((half, xs))] * 2
        + [dma((members,))] * 4,
        compiler_params=pltpu.CompilerParams(
            collective_id=collective_id, has_side_effects=True, vmem_limit_bytes=56 * MIB
        ),
        cost_estimate=pl.CostEstimate(
            flops=0, bytes_accessed=4 * groups * members * seq_len * width, transcendentals=0
        ),
    )(parts)


def unpack_kernel(start, part, at_ref, pool_ref, weights_ref, rows_ref):
    step = pl.program_id(0)
    owners, slab, width = pool_ref.shape
    weights_ref[...] = jnp.concatenate([pool_ref[j, :part] for j in range(owners)], axis=0)
    count = slab - start
    columns = lax.broadcasted_iota(jnp.int32, (1, count), 1) + start
    columns = jnp.concatenate([columns + j * slab for j in range(owners)], axis=1)
    hits = (columns == at_ref[...] - step * owners * slab).astype(jnp.float32).astype(jnp.bfloat16)
    found = product(hits, jnp.concatenate([pool_ref[j, start:] for j in range(owners)], axis=0))

    @pl.when(step == 0)
    def begin():
        rows_ref[...] = found

    @pl.when(step > 0)
    def more():
        rows_ref[...] += found


def unpack(pool, part, at):
    devices, slab, width = pool.shape
    owners = max(4, 8 // math.gcd(part, 8))
    start = part // 16 * 16
    tokens = at.shape[0]
    return pl.pallas_call(
        functools.partial(unpack_kernel, start, part),
        out_shape=(
            jax.ShapeDtypeStruct((devices * part, width), pool.dtype),
            jax.ShapeDtypeStruct((tokens, width), jnp.float32),
        ),
        grid=(devices // owners,),
        in_specs=[
            pl.BlockSpec((tokens, 1), lambda i: (0, 0)),
            pl.BlockSpec((owners, slab, width), lambda i: (i, 0, 0)),
        ],
        out_specs=(
            pl.BlockSpec((owners * part, width), lambda i: (i, 0)),
            pl.BlockSpec((tokens, width), lambda i: (0, 0)),
        ),
        compiler_params=pltpu.CompilerParams(vmem_limit_bytes=40 * MIB),
        cost_estimate=pl.CostEstimate(
            flops=2 * devices * tokens * (slab - start) * width,
            bytes_accessed=4 * pool.size,
            transcendentals=0,
        ),
    )(at, pool)


def back_kernel(
    model_ref, fresh_ref, used_ref, piece_ref, place_ref, *rest
):
    pieces = rest[:QUAD]
    table_ref, info_ref, target_ref, d_outs_ref, grad_ref, held, sems = rest[QUAD:]
    step = pl.program_id(0)
    seq_len = pieces[0].shape[1]
    slot = lax.rem(step, 2)

    def leave(which, where, i):
        return pltpu.make_async_copy(held.at[which, i], d_outs_ref.at[where], sems.at[which, i])

    def settle(which):
        for i in range(QUAD):
            leave(which, 0, i).wait()

    @pl.when(step < used_ref[0])
    def work():
        @pl.when(step >= 2)
        def reuse():
            settle(slot)

        @pl.when(fresh_ref[step] == 1)
        def start():
            grad_ref[...] = jnp.zeros_like(grad_ref)

        outs = jnp.concatenate([piece[0] for piece in pieces], axis=0)
        part_rows = table_ref.shape[1]
        size = tile_of(part_rows)
        d_outs = jnp.zeros(outs.shape, jnp.float32)
        for first_row in range(0, part_rows, size):
            here = pl.ds(first_row, size)
            table_rows = table_ref[0, here]
            logits = project(table_rows, outs)
            rows = lax.broadcasted_iota(jnp.int32, logits.shape, 0) + first_row
            soft = jnp.exp(logits - info_ref[0, 0:1, :])
            soft = jnp.where(rows == target_ref[0], soft - 1.0, soft)
            d_logits = (info_ref[0, 1:2, :] * soft).astype(jnp.bfloat16)
            d_outs = d_outs + outer_rows(d_logits, table_rows)
            grad_ref[0, here] += product(d_logits, outs)
        for i in range(QUAD):
            held[slot, i] = d_outs[i * seq_len : (i + 1) * seq_len].astype(held.dtype)
            leave(slot, place_ref[QUAD * step + i], i).start()

        @pl.when(step == used_ref[0] - 1)
        def drain():
            settle(slot)

            @pl.when(step >= 1)
            def earlier():
                settle(1 - slot)


def head_back(outs_pieces, table_low, model_of, fresh, used, piece_at, place, info, target):
    steps = model_of.shape[0]
    models, part_rows, width = table_low.shape
    seq_len = outs_pieces.shape[1]
    tokens = QUAD * seq_len

    def piece(i):
        return pl.BlockSpec((1, seq_len, width), lambda s, m, f, u, q, p: (q[QUAD * s + i], 0, 0))

    return pl.pallas_call(
        back_kernel,
        out_shape=(
            jax.ShapeDtypeStruct((QUAD * steps, seq_len, width), jnp.bfloat16),
            jax.ShapeDtypeStruct((models, part_rows, width), jnp.float32),
        ),
        grid_spec=pltpu.PrefetchScalarGridSpec(
            num_scalar_prefetch=5,
            grid=(steps,),
            in_specs=[piece(i) for i in range(QUAD)]
            + [
                pl.BlockSpec((1, part_rows, width), lambda s, m, *_: (m[s], 0, 0)),
                pl.BlockSpec((1, 2, tokens), lambda s, *_: (s, 0, 0)),
                pl.BlockSpec((1, 1, tokens), lambda s, *_: (s, 0, 0)),
            ],
            out_specs=(
                pl.BlockSpec(memory_space=pl.ANY),
                pl.BlockSpec((1, part_rows, width), lambda s, m, *_: (m[s], 0, 0)),
            ),
            scratch_shapes=[
                pltpu.VMEM((2, QUAD, seq_len, width), jnp.bfloat16),
                pltpu.SemaphoreType.DMA((2, QUAD)),
            ],
        ),
        compiler_params=pltpu.CompilerParams(vmem_limit_bytes=56 * MIB),
        cost_estimate=pl.CostEstimate(
            flops=6 * steps * tokens * part_rows * width,
            bytes_accessed=4 * steps * tokens * width + 6 * table_low.size,
            transcendentals=steps * tokens * part_rows,
        ),
    )(model_of, fresh, used, piece_at, place, *([outs_pieces] * QUAD), table_low, info, target)


def finish_kernel(
    first_model, start_ref, end_ref, first_ref, second_ref, d_ref, ids_ref, head_ref, table_ref, momentum_ref, *rest
):
    grad_ref, momentum_new_ref, table_new_ref = rest[-3:]
    model = pl.program_id(0) + first_model
    tile_rows = grad_ref.shape[1]
    tokens = ids_ref.shape[2]
    rows = lax.broadcasted_iota(jnp.int32, (tile_rows, tokens), 0) + pl.program_id(1) * tile_rows
    grad_ref[0] = head_ref[0]

    def pair(step, carry):
        hits = (rows == ids_ref[step]).astype(jnp.float32).astype(jnp.bfloat16)
        outs = jnp.concatenate([d_ref[first_ref[step]], d_ref[second_ref[step]]], axis=0)
        grad_ref[0] += product(hits, outs)
        return carry

    lax.fori_loop(start_ref[model], end_ref[model], pair, 0)
    renewed, fresh_table = update(table_ref[0], momentum_ref[0], grad_ref[0], table_rate)
    momentum_new_ref[0] = renewed
    table_new_ref[0] = fresh_table


def finish_table(d_inputs, head_grad, table, momentum, schedule, ids, first_model, count, earlier):
    models, part_rows, width = table.shape
    tile_rows = tile_of(part_rows)
    state = jax.ShapeDtypeStruct(table.shape, jnp.float32)
    piece = pl.BlockSpec((1, tile_rows, width), lambda m, t, *_: (m + first_model, t, 0))
    whole = pl.BlockSpec(memory_space=pltpu.VMEM)
    return pl.pallas_call(
        functools.partial(finish_kernel, first_model),
        out_shape=(state, state, state),
        grid_spec=pltpu.PrefetchScalarGridSpec(
            num_scalar_prefetch=4,
            grid=(count, part_rows // tile_rows),
            in_specs=[whole, whole, piece, piece, piece]
            + [pl.BlockSpec(memory_space=pl.ANY)] * len(earlier),
            out_specs=(piece, piece, piece),
        ),
        input_output_aliases={9 + i: i for i in range(len(earlier))},
        compiler_params=pltpu.CompilerParams(vmem_limit_bytes=56 * MIB),
        cost_estimate=pl.CostEstimate(
            flops=2 * d_inputs.size * part_rows * count // models,
            bytes_accessed=24 * count * part_rows * width,
            transcendentals=0,
        ),
    )(*schedule, d_inputs, ids, head_grad, table, momentum, *earlier)


def stack_kernel(gradient_ref, weight_ref, momentum_ref, grad_ref, renewed_ref, fresh_ref):
    for model in range(gradient_ref.shape[0]):
        gradient = gradient_ref[model].astype(jnp.float32)
        renewed, fresh = update(weight_ref[:, model, :], momentum_ref[:, model, :], gradient, stack_rate)
        grad_ref[:, model, :] = gradient
        renewed_ref[:, model, :] = renewed
        fresh_ref[:, model, :] = fresh


def update_stack(gradient, weight, momentum):
    turn = functools.partial(jnp.transpose, axes=(1, 0, 2))
    turned = jax.ShapeDtypeStruct(turn(weight).shape, jnp.float32)
    whole = pl.BlockSpec(memory_space=pltpu.VMEM)
    results = pl.pallas_call(
        stack_kernel,
        out_shape=(turned, turned, turned),
        in_specs=[whole] * 3,
        out_specs=(whole,) * 3,
        compiler_params=pltpu.CompilerParams(vmem_limit_bytes=56 * MIB),
        cost_estimate=pl.CostEstimate(
            flops=6 * weight.size, bytes_accessed=22 * weight.size, transcendentals=0
        ),
    )(gradient, turn(weight), turn(momentum))
    return tuple(turn(result) for result in results)


def body(
    token_ids,
    target_ids,
    segment_ids,
    chosen,
    table,
    table_momentum,
    stack,
    stack_momentum,
    vectors,
    vector_momentum,
):
    both = ("grp", "cli")
    models, block_rows, model_width = table.shape
    stack_part = stack.shape[1]
    seq_len = token_ids.shape[1]
    groups = lax.axis_size("grp")
    members = lax.axis_size("cli")
    devices = groups * members
    share = members // models
    local = members // share
    device_index = lax.axis_index(both)
    group_index = lax.axis_index("grp")
    member_index = lax.axis_index("cli")
    model_own = member_index // share
    part_own = member_index % share
    model_range = jnp.arange(models, dtype=jnp.int32)

    def per_member(rows):
        return jnp.repeat(rows, share, axis=0) if share > 1 else rows

    slab = -(-(stack_part + ROUND_ROWS) // SLAB_STEP) * SLAB_STEP
    round_rows = slab - stack_part

    facts = jnp.concatenate([token_ids[0], target_ids[0], segment_ids[0], chosen])
    facts = jnp.pad(facts, (0, -facts.size % LANES))[None]
    facts, table_low = opening(facts, table, groups, members, 5)
    facts = facts[:, 0]
    tokens = facts[:, :seq_len]
    targets = facts[:, seq_len : 2 * seq_len]
    segments = facts[:, 2 * seq_len : 3 * seq_len]
    choices = facts[:, 3 * seq_len]
    valid = jnp.concatenate(
        [
            (segments[:, :-1] == segments[:, 1:]).astype(jnp.float32),
            jnp.zeros((devices, 1), jnp.float32),
        ],
        axis=1,
    )
    counts = jnp.sum(valid, axis=1)
    choice_table = (choices[:, None] == model_range[None, :]).astype(jnp.float32)
    totals = jnp.sum(choice_table * counts[:, None], axis=0)
    total_of = jnp.sum(choice_table * totals[None, :], axis=1)

    fine = 16 if block_rows % 64 else 64
    coarse = block_rows // fine
    flat_tokens = tokens.reshape(-1)
    high_hot = (
        (flat_tokens // fine)[:, None] == jnp.arange(devices * coarse, dtype=jnp.int32)[None, :]
    ).astype(jnp.bfloat16)
    low_hot = ((flat_tokens % fine)[:, None] == jnp.arange(fine, dtype=jnp.int32)[None, :]).astype(
        jnp.bfloat16
    )
    seen = (outer_rows(high_hot, low_hot) > 0).astype(jnp.float32)
    before = product(
        seen.astype(jnp.bfloat16),
        jnp.triu(jnp.ones((fine, fine), jnp.bfloat16), 1),
    )
    sums = jnp.sum(seen, axis=1).reshape(devices, coarse)
    uniques = jnp.sum(sums, axis=1)
    ahead = jnp.sum(
        jnp.where(
            jnp.arange(coarse)[None, None, :] < jnp.arange(coarse)[None, :, None],
            sums[:, None, :],
            0.0,
        ),
        axis=2,
    )
    places = before + ahead.reshape(-1, 1)
    rounds = jnp.max(jnp.ceil(uniques / round_rows)).astype(jnp.int32)
    own_places = lax.dynamic_slice(places, (device_index * coarse, 0), (coarse, fine)).reshape(-1)
    own_seen = lax.dynamic_slice(seen, (device_index * coarse, 0), (coarse, fine)).reshape(-1)
    own_places = jnp.where(own_seen > 0, own_places, -1.0).astype(jnp.int32)
    first_client = group_index * members + part_own * local
    my_tokens = lax.dynamic_slice(tokens, (first_client, 0), (local, seq_len)).reshape(-1)
    my_segments = lax.dynamic_slice(segments, (first_client, 0), (local, seq_len))
    my_choices = lax.dynamic_slice(choices, (first_client,), (local,))
    my_high = (
        (my_tokens // fine)[:, None] == jnp.arange(devices * coarse, dtype=jnp.int32)[None, :]
    ).astype(jnp.bfloat16)
    my_low = (my_tokens % fine)[:, None] == jnp.arange(fine, dtype=jnp.int32)[None, :]
    split_places = jnp.concatenate(
        [jnp.floor(places / 64.0), places - 64.0 * jnp.floor(places / 64.0)], axis=1
    ).astype(jnp.bfloat16)
    picked_places = product(my_high, split_places)
    picked_places = 64.0 * picked_places[:, :fine] + picked_places[:, fine:]
    my_places = jnp.sum(jnp.where(my_low, picked_places, 0.0), axis=1).astype(jnp.int32)
    my_owner = my_tokens // block_rows

    def offered(start):
        wanted = jnp.arange(round_rows, dtype=jnp.int32) + start
        pick = (own_places[None, :] == wanted[:, None]).astype(jnp.bfloat16)
        rows = jnp.einsum("ur,krd->kud", pick, table_low, preferred_element_type=jnp.float32)
        return rows.astype(jnp.bfloat16)

    def inside(start):
        offset = my_places - start
        return ((offset >= 0) & (offset < round_rows), offset)

    def another(carry):
        index, embedded = carry
        start = index * round_rows
        turned = lax.all_to_all(per_member(offered(start)), "cli", 0, 0, tiled=True)
        pool = lax.all_gather(turned, "grp", axis=0, tiled=True).reshape(-1, model_width)
        here, offset = inside(start)
        found = jnp.take(pool, jnp.where(here, my_owner * round_rows + offset, 0), axis=0)
        return (index + 1, jnp.where(here[:, None], found.astype(jnp.float32), embedded))

    slabs = jnp.concatenate([stack.astype(jnp.bfloat16), offered(0)], axis=1)
    pool = spread(per_member(slabs), groups, members, 1, False, 2)
    here, offset = inside(0)
    at = jnp.where(here, my_owner * slab + stack_part + offset, -1)
    weights, embedded = unpack(pool, stack_part, at[:, None])
    _, embedded = lax.while_loop(
        lambda carry: carry[0] < rounds, another, (jnp.int32(1), embedded)
    )
    vector_one = lax.dynamic_index_in_dim(vectors, model_own, 0, keepdims=False)
    inputs = embedded + jnp.tile(weights[12 * model_width :].astype(jnp.float32), (local, 1))
    saved = layer_forward(weights, vector_one, inputs, my_segments)
    normed_out = saved[11]

    target_local = targets - device_index * block_rows
    target_local = jnp.where((target_local >= 0) & (target_local < block_rows), target_local, -1)
    target_blocks = target_local.reshape(groups * share, 1, local * seq_len)
    if devices * normed_out.size * 2 <= POOL_BYTES:
        outs_all, everything = spread_score(
            normed_out[None], table_low, target_blocks, groups, members, share, 2
        )
    else:
        outs_all = spread(normed_out[None], groups, members, 2, True, 2)
        stats = head_stats(outs_all, table_low, target_blocks, groups, members, share)
        shares = lax.all_to_all(stats, both, 0, 0, tiled=True)
        log_total = jax.nn.logsumexp(shares[:, 0], axis=0)
        token_loss = log_total - jnp.sum(shares[:, 1], axis=0)
        everything = share_all(jnp.stack([log_total, token_loss]), both, devices)
    everything = (
        everything.reshape(groups, models, share, 2, local, seq_len)
        .transpose(3, 1, 0, 2, 4, 5)
        .reshape(2, models, devices, seq_len)
    )
    all_losses = jnp.sum(everything[1] * valid[None], axis=2)
    loss = jnp.sum(choice_table.T * all_losses / total_of[None, :])
    client_losses = lax.dynamic_slice(
        (all_losses / counts[None, :]).T, (device_index, 0), (1, models)
    )
    chosen_total = jnp.sum(choice_table.T[:, :, None] * everything[0], axis=0)

    numbers = jnp.sum(choice_table, axis=0)
    padded = QUAD * jnp.ceil(numbers / QUAD)
    offsets = jnp.cumsum(padded) - padded
    earlier = (
        jnp.arange(devices)[None, :] < jnp.arange(devices)[:, None]
    ) & (choices[None, :] == choices[:, None])
    slot_of = jnp.sum(choice_table * offsets[None, :], axis=1) + jnp.sum(
        earlier.astype(jnp.float32), axis=1
    )
    steps = (devices + (QUAD - 1) * models) // QUAD
    slots = QUAD * steps
    tokens_step = QUAD * seq_len
    at_slot = jnp.arange(slots)[:, None] == slot_of.astype(jnp.int32)[None, :]
    filled = jnp.any(at_slot, axis=1)
    client_at = jnp.sum(jnp.where(at_slot, jnp.arange(devices)[None, :], 0), axis=1).astype(
        jnp.int32
    )
    step_start = float(QUAD) * jnp.arange(steps)
    used = (jnp.sum(padded) / QUAD).astype(jnp.int32)[None]
    model_of = (
        jnp.sum((step_start[:, None] >= offsets[None, :]).astype(jnp.int32), axis=1) - 1
    ).astype(jnp.int32)
    fresh = jnp.concatenate(
        [jnp.ones((1,), jnp.int32), (model_of[1:] != model_of[:-1]).astype(jnp.int32)]
    )
    within = client_at % members
    piece_at = (
        (client_at // members * members + jnp.repeat(model_of, QUAD) * share + within // local) * local
        + within % local
    ).astype(jnp.int32)
    weight_rows = valid / total_of[:, None]
    slot_log = jnp.where(filled[:, None], jnp.take(chosen_total, client_at, axis=0), 1e30)
    slot_weight = jnp.where(filled[:, None], jnp.take(weight_rows, client_at, axis=0), 0.0)
    slot_info = jnp.stack(
        [slot_log.reshape(steps, tokens_step), slot_weight.reshape(steps, tokens_step)], axis=1
    )
    slot_target = jnp.where(filled[:, None], jnp.take(target_local, client_at, axis=0), -1)
    spare = devices + jnp.cumsum(1 - filled.astype(jnp.int32)) - 1
    d_outs, head_grad = head_back(
        outs_all.reshape(-1, seq_len, model_width),
        table_low,
        model_of,
        fresh,
        used,
        piece_at,
        jnp.where(filled, client_at, spare).astype(jnp.int32),
        slot_info,
        slot_target.reshape(steps, 1, tokens_step),
    )
    d_group = collect(d_outs, groups, members, 4)
    d_mine = lax.dynamic_slice(
        d_group, (part_own * local, 0, 0), (local, seq_len, model_width)
    ).astype(jnp.float32)
    d_final = jnp.where((my_choices == model_own)[:, None, None], d_mine, 0.0).reshape(
        local * seq_len, model_width
    )
    pairs, grad_places, vector_rows, d_inputs = layer_backward(
        weights, vector_one, inputs, my_segments, saved, d_final
    )
    d_wide = d_inputs.astype(jnp.bfloat16)
    if share > 1:
        d_wide = lax.dynamic_update_slice(
            jnp.zeros((members * seq_len, model_width), jnp.bfloat16),
            d_wide,
            (part_own * local * seq_len, 0),
        )
    d_wide, pairs = lax.optimization_barrier((d_wide, pairs))
    d_turned = lax.all_to_all(
        d_wide.reshape(members, seq_len, model_width), "cli", 0, 0, tiled=True
    )
    stack_rows = jnp.concatenate(
        [outer_rows(left, right).astype(jnp.bfloat16) for left, right in pairs]
        + [grad_places.astype(jnp.bfloat16)],
        axis=0,
    )
    stack_rows, d_turned = lax.optimization_barrier((stack_rows, d_turned))
    stack_sum = lax.psum_scatter(stack_rows, "grp", scatter_dimension=0, tiled=True)
    d_client = jnp.sum(d_turned.astype(jnp.float32), axis=0, keepdims=True).astype(jnp.bfloat16)
    d_all = spread(d_client, groups, members, 3, True, 2)
    token_local = tokens - device_index * block_rows
    token_local = jnp.where((token_local >= 0) & (token_local < block_rows), token_local, -1)
    slot_token = jnp.where(filled[:, None], jnp.take(token_local, client_at, axis=0), -1)
    pair_start = (offsets / 2.0).astype(jnp.int32)
    pair_end = pair_start + jnp.ceil(numbers / 2.0).astype(jnp.int32)
    schedule = (pair_start, pair_end, client_at[0::2], client_at[1::2])
    slot_token = slot_token.reshape(slots // 2, 1, 2 * seq_len)
    lead = models - 1

    states = finish_table(d_all, head_grad, table, table_momentum, schedule, slot_token, 0, lead, ())
    states, vector_rows = lax.optimization_barrier((states, vector_rows))
    vector_piece = vector_rows.size // groups
    vector_part = lax.all_to_all(
        vector_rows.reshape(groups, vector_piece), "grp", 0, 0, tiled=True
    )
    stack_sum, states, vector_part = lax.optimization_barrier((stack_sum, states, vector_part))
    stack_back = lax.all_to_all(
        stack_sum.reshape(members, stack_part, model_width), "cli", 0, 0, tiled=True
    )
    if share > 1:
        stack_back = jnp.sum(
            stack_back.astype(jnp.float32).reshape(models, share, stack_part, model_width), axis=1
        )
    states = finish_table(
        d_all, head_grad, table, table_momentum, schedule, slot_token, lead, models - lead, states
    )
    stack_back, vector_part, states = lax.optimization_barrier((stack_back, vector_part, states))
    table_grad, table_momentum_new, table_new = states
    vector_parts = share_all(jnp.sum(vector_part, axis=0), both, devices)
    vector_grad = jnp.sum(vector_parts.reshape(groups, models, share, vector_piece), axis=2)
    vector_grad = vector_grad.transpose(1, 0, 2).reshape(vectors.shape)
    stack_grad, stack_momentum_new, stack_new = update_stack(stack_back, stack, stack_momentum)
    vector_momentum_new, vector_new = update(vectors, vector_momentum, vector_grad, vector_rate)
    return (
        loss,
        client_losses,
        table_grad,
        table_momentum_new,
        table_new,
        stack_grad,
        stack_momentum_new,
        stack_new,
        vector_grad,
        vector_momentum_new,
        vector_new,
    )


def solution(mesh):
    rows = P(("grp", "cli"), None)
    parts = P(None, ("grp", "cli"), None)
    return jax.shard_map(
        body,
        mesh=mesh,
        in_specs=(rows, rows, rows, P(("grp", "cli")), parts, parts, parts, parts, P(), P()),
        out_specs=(P(), rows, parts, parts, parts, parts, parts, parts, P(), P(), P()),
        check_vma=False,
    )
```

```python
import functools
import math

import jax
import jax.numpy as jnp
from jax import lax
from jax.experimental import pallas as pl
from jax.experimental.pallas import tpu as pltpu
from jax.sharding import PartitionSpec as P

HEADS = 12
HEAD_DIM = 64


epsilon = 1e-05
momentum_decay = 0.9
table_rate = 4.0
stack_rate = 4.0
vector_rate = 50.0

ROUND_ROWS = 104
SLAB_STEP = 16
TILE = 400
LANES = 128
QUAD = 4
MIB = 1 << 20
POOL_BYTES = 32 * MIB
MESH = pl.DeviceIdType.MESH


def layer_norm(inputs, gain_row, shift_row):
    centred = inputs - jnp.mean(inputs, -1, keepdims=True)
    spread = jnp.mean(centred * centred, -1, keepdims=True)
    return centred * lax.rsqrt(spread + epsilon) * gain_row + shift_row


def project(inputs, matrix):
    return lax.dot_general(
        inputs, matrix, (((1,), (1,)), ((), ())), preferred_element_type=jnp.float32
    )


def product(inputs, matrix):
    return jnp.dot(inputs, matrix, preferred_element_type=jnp.float32)


def outer_rows(left, right):
    return lax.dot_general(
        left, right, (((0,), (0,)), ((), ())), preferred_element_type=jnp.float32
    )


def split_heads(rows, seq_len):
    return rows.reshape(-1, seq_len, HEADS, HEAD_DIM)


def attend(queries, key_rows, segment_rows):
    seq_len = segment_rows.shape[1]
    scores = jnp.einsum(
        "nqhd,nkhd->nhqk",
        split_heads(queries, seq_len),
        split_heads(key_rows, seq_len),
        preferred_element_type=jnp.float32,
    ) * HEAD_DIM ** (-0.5)
    positions = jnp.arange(seq_len)
    allowed = (positions[None, None, :] <= positions[None, :, None]) & (
        segment_rows[:, None, :] == segment_rows[:, :, None]
    )
    return jax.nn.softmax(jnp.where(allowed[:, None], scores, -1e30), axis=-1)


def layer_forward(weights, vector_one, inputs, segment_rows):
    row_count, model_width = inputs.shape
    seq_len = segment_rows.shape[1]
    normed = layer_norm(inputs, vector_one[0], vector_one[1]).astype(jnp.bfloat16)
    queries = (project(normed, weights[0:model_width]) + vector_one[6]).astype(jnp.bfloat16)
    key_rows = project(normed, weights[model_width : 2 * model_width]).astype(jnp.bfloat16)
    values = (project(normed, weights[2 * model_width : 3 * model_width]) + vector_one[7]).astype(
        jnp.bfloat16
    )
    attention = attend(queries, key_rows, segment_rows)
    mixture = jnp.einsum(
        "nhqk,nkhd->nqhd",
        attention.astype(jnp.bfloat16),
        split_heads(values, seq_len),
        preferred_element_type=jnp.float32,
    )
    mixture = mixture.reshape(row_count, model_width).astype(jnp.bfloat16)
    middle = inputs + (project(mixture, weights[3 * model_width : 4 * model_width]) + vector_one[8])
    normed_two = layer_norm(middle, vector_one[2], vector_one[3]).astype(jnp.bfloat16)
    hidden = project(normed_two, weights[4 * model_width : 8 * model_width]) + vector_one[
        10:14
    ].reshape(-1)
    active = jax.nn.gelu(hidden, approximate=True).astype(jnp.bfloat16)
    residual = middle + (
        product(active, weights[8 * model_width : 12 * model_width]) + vector_one[9]
    )
    normed_out = layer_norm(residual, vector_one[4], vector_one[5]).astype(jnp.bfloat16)
    return (
        normed,
        queries,
        key_rows,
        values,
        attention,
        mixture,
        middle,
        normed_two,
        hidden,
        active,
        residual,
        normed_out,
    )


def norm_grad(operand, gain_row, shift_row, cotangent):
    outcome, pullback = jax.vjp(layer_norm, operand, gain_row, shift_row)
    return pullback(cotangent)


def gelu_tanh(hidden):
    return jax.nn.gelu(hidden, approximate=True)


def layer_backward(weights, vector_one, inputs, segment_rows, saved, grad_out):
    row_count, model_width = inputs.shape
    seq_len = segment_rows.shape[1]
    scaling = HEAD_DIM ** (-0.5)
    (
        normed,
        queries,
        key_rows,
        values,
        attention,
        mixture,
        middle,
        normed_two,
        hidden,
        active,
        residual,
        normed_out,
    ) = saved
    d_residual, d_gain_out, d_shift_out = norm_grad(
        residual, vector_one[4], vector_one[5], grad_out
    )
    d_outer = d_residual.astype(jnp.bfloat16)
    d_bias_out = jnp.sum(d_outer.astype(jnp.float32), 0)
    d_active = project(d_outer, weights[8 * model_width : 12 * model_width])
    gelu_value, gelu_pull = jax.vjp(gelu_tanh, hidden)
    d_hidden = gelu_pull(d_active)[0].astype(jnp.bfloat16)
    d_bias_hidden = jnp.sum(d_hidden.astype(jnp.float32), 0)
    d_normed_two = product(d_hidden, weights[4 * model_width : 8 * model_width])
    d_middle_norm, d_gain_two, d_shift_two = norm_grad(
        middle, vector_one[2], vector_one[3], d_normed_two
    )
    d_middle = d_residual + d_middle_norm
    d_branch = d_middle.astype(jnp.bfloat16)
    d_bias_branch = jnp.sum(d_branch.astype(jnp.float32), 0)
    d_mixture = split_heads(
        product(d_branch, weights[3 * model_width : 4 * model_width]).astype(jnp.bfloat16), seq_len
    )
    d_attention = jnp.einsum(
        "nqhd,nkhd->nhqk", d_mixture, split_heads(values, seq_len), preferred_element_type=jnp.float32
    )
    d_values = jnp.einsum(
        "nhqk,nqhd->nkhd",
        attention.astype(jnp.bfloat16),
        d_mixture,
        preferred_element_type=jnp.float32,
    )
    d_values = d_values.reshape(row_count, model_width).astype(jnp.bfloat16)
    d_scores = (
        attention * (d_attention - jnp.sum(attention * d_attention, -1, keepdims=True))
    ).astype(jnp.bfloat16)
    d_queries = (
        jnp.einsum(
            "nhqk,nkhd->nqhd",
            d_scores,
            split_heads(key_rows, seq_len),
            preferred_element_type=jnp.float32,
        )
        * scaling
    )
    d_queries = d_queries.reshape(row_count, model_width).astype(jnp.bfloat16)
    d_keys = (
        jnp.einsum(
            "nhqk,nqhd->nkhd",
            d_scores,
            split_heads(queries, seq_len),
            preferred_element_type=jnp.float32,
        )
        * scaling
    )
    d_keys = d_keys.reshape(row_count, model_width).astype(jnp.bfloat16)
    d_joined = jnp.concatenate([d_queries, d_keys, d_values], axis=1)
    d_normed = product(d_joined, weights[0 : 3 * model_width])
    d_inputs_norm, d_gain_one, d_shift_one = norm_grad(
        inputs, vector_one[0], vector_one[1], d_normed
    )
    d_inputs = d_middle + d_inputs_norm
    grad_places = jnp.sum(d_inputs.reshape(-1, seq_len, model_width), axis=0)
    pairs = (
        (d_joined, normed),
        (d_branch, mixture),
        (d_hidden, normed_two),
        (active, d_outer),
    )
    bias_query = jnp.sum(d_queries.astype(jnp.float32), 0)
    bias_value = jnp.sum(d_values.astype(jnp.float32), 0)
    vector_rows = jnp.concatenate(
        [
            jnp.stack(
                [
                    d_gain_one,
                    d_shift_one,
                    d_gain_two,
                    d_shift_two,
                    d_gain_out,
                    d_shift_out,
                    bias_query,
                    bias_value,
                    d_bias_branch,
                    d_bias_out,
                ]
            ),
            d_bias_hidden.reshape(4, model_width),
        ],
        axis=0,
    )
    return (pairs, grad_places, vector_rows, d_inputs)


def share_all(rows, axes, size):
    return lax.all_to_all(
        jnp.broadcast_to(rows[None], (size,) + rows.shape), axes, 0, 0, tiled=True
    )


def update(weight, momentum, gradient, step_rate):
    renewed = momentum_decay * momentum + gradient
    return (renewed, weight - step_rate * (gradient + momentum_decay * renewed))


def flipped(value, offset, size):
    bit = 1
    while bit < size:
        digit = lax.rem(lax.div(offset, bit), 2)
        value = value + digit * bit * (1 - 2 * lax.rem(lax.div(value, bit), 2))
        bit *= 2
    return value


class Place:
    def __init__(self, groups, members):
        self.groups, self.members = groups, members
        self.ys = 2
        self.xs = groups // 4
        self.grp = lax.axis_index("grp")
        self.cli = lax.axis_index("cli")
        self.core = lax.rem(self.grp, 2)
        self.x = lax.rem(lax.div(self.grp, 2), self.xs)
        self.y = lax.div(self.grp, 2 * self.xs)

    def group(self, jx=0, jy=0, jc=0):
        x = flipped(self.x, jx, self.xs)
        y = flipped(self.y, jy, self.ys)
        core = self.core + jc * (1 - 2 * self.core)
        return (y * self.xs + x) * 2 + core

    def block(self, jx, jy, level, jc=0):
        return self.group(jx, jy, jc) * self.members + level

    def peer(self, jx=0, jy=0, jc=0):
        return (self.group(jx, jy, jc), self.cli)

    def level(self, level):
        return (self.grp, level)

    def nearest(self, i):
        z, last = self.cli, self.members - 1
        low = jnp.where(2 * z < last, 1, 0)
        sign = 2 * low - 1
        margin = low * z + (1 - low) * (last - z)
        step = lax.div(i + 1, 2)
        odd = lax.rem(i, 2)
        near = z + sign * step * (2 * odd - 1)
        far = z + sign * (i - margin)
        return jnp.where(i <= 2 * margin, near, far)


def greet(place):
    barrier = pltpu.get_barrier_semaphore()
    peers = [place.peer(jx=j) for j in range(1, place.xs)] + [place.peer(jy=j) for j in range(1, place.ys)]
    peers.append(place.peer(jc=1))
    peers += [place.level(lax.rem(place.cli + j, place.members)) for j in range(1, place.members)]
    for peer in peers:
        pl.semaphore_signal(barrier, inc=1, device_id=peer, device_id_type=MESH)
    pl.semaphore_wait(barrier, len(peers))


def greet_all(devices, members):
    barrier = pltpu.get_barrier_semaphore()
    me = lax.axis_index("grp") * members + lax.axis_index("cli")

    def hello(j, carry):
        other = lax.rem(me + j, devices)
        pl.semaphore_signal(
            barrier, inc=1, device_id=(lax.div(other, members), lax.rem(other, members)), device_id_type=MESH
        )
        return carry

    lax.fori_loop(1, devices, hello, 0)
    pl.semaphore_wait(barrier, devices - 1)


def spread_sems(groups, members, pieces):
    xs, ys, items = groups // 4, 2, members * pieces
    dma = pltpu.SemaphoreType.DMA
    shapes = [(items,)] * 3 + [(items, xs)] * 2 + [(items, ys)] * 2 + [(items, xs, ys)] * 6
    return [dma] + [dma(shape) for shape in shapes]


def spread_body(place, chain, pieces, src, out, sems, consume, ready=None):
    (own_sem, z_up, z_down, z_recv, x_send, x_recv, y_send, y_recv, k_send, k_recv, p_send, p_recv,
     c_send, c_recv) = sems
    xs, ys, members = place.xs, place.ys, place.members
    items = members * pieces
    size = out.shape[1] // pieces
    z = place.cli
    partner = z + 1 - 2 * lax.rem(z, 2)
    inner_x, inner_y = range(1, xs), range(1, ys)

    def move(source, target, send, recv, device):
        return pltpu.make_async_remote_copy(
            src_ref=source, dst_ref=target, send_sem=send, recv_sem=recv, device_id=device, device_id_type=MESH
        )

    class Item:
        def __init__(self, k):
            self.level = place.nearest(lax.div(k, pieces))
            self.piece = lax.rem(k, pieces)
            self.slot = self.level * pieces + self.piece
            self.even = lax.rem(self.piece, 2) == 0
            self.mine = lax.rem(self.level + z, 2) == 0 if chain else self.level >= 0
            self.rows = pl.ds(self.piece * size, size)

        def part(self, jx, jy, level=None):
            return out.at[place.block(jx, jy, self.level if level is None else level), self.rows]

        def here(self, own):
            return src.at[z if not chain else 0, self.rows] if own else self.part(0, 0)

        def up(self, own=False):
            return move(self.here(own), self.part(0, 0), z_up.at[self.slot], z_recv.at[self.slot], place.level(z + 1))

        def down(self, own=False):
            return move(self.here(own), self.part(0, 0), z_down.at[self.slot], z_recv.at[self.slot], place.level(z - 1))

        def straight(self):
            return move(
                src.at[self.level, self.rows], self.part(0, 0, z), z_up.at[self.slot],
                z_recv.at[z * pieces + self.piece], place.level(self.level),
            )

        def landed(self):
            part = self.part(0, 0)
            return move(part, part, z_up.at[self.slot], z_recv.at[self.slot], place.level(partner))

        def to_x(self, jx, own=False):
            return move(self.here(own), self.part(0, 0), x_send.at[self.slot, jx], x_recv.at[self.slot, jx], place.peer(jx=jx))

        def to_y(self, jy, own=False):
            return move(self.here(own), self.part(0, 0), y_send.at[self.slot, jy], y_recv.at[self.slot, jy], place.peer(jy=jy))

        def corner_a(self, jx, jy):
            part = self.part(jx, 0)
            return move(part, part, k_send.at[self.slot, jx, jy], k_recv.at[self.slot, jx, jy], place.peer(jy=jy))

        def corner_b(self, jx, jy):
            part = self.part(0, jy)
            return move(part, part, k_send.at[self.slot, jx, jy], k_recv.at[self.slot, jx, jy], place.peer(jx=jx))

        def corner_z(self, jx, jy):
            part = self.part(jx, jy)
            return move(part, part, p_send.at[self.slot, jx, jy], p_recv.at[self.slot, jx, jy], place.level(partner))

        def to_core(self, jx, jy, own=False):
            part = self.part(jx, jy)
            return move(self.here(True) if own else part, part, c_send.at[self.slot, jx, jy], c_recv.at[self.slot, jx, jy], place.peer(jc=1))

    own = pltpu.make_async_copy(src.at[z if not chain else 0], out.at[place.block(0, 0, z)], own_sem)
    own.start()
    if not chain:
        for piece in range(pieces):
            Item(pieces + piece).straight().start()

    def columns(k):
        item = Item(k)
        level = item.level

        @pl.when(k < pieces)
        def mine_first():
            if chain:
                @pl.when(z + 1 < members)
                def onward():
                    item.up(True).start()

                @pl.when(z > 0)
                def back():
                    item.down(True).start()

            for jx in inner_x:
                item.to_x(jx, True).start()
            for jy in inner_y:
                item.to_y(jy, True).start()
            item.to_core(0, 0, True).start()

        @pl.when(k >= pieces)
        def arrive():
            item.landed().wait_recv()
            if chain:
                @pl.when((level < z) & (z + 1 < members))
                def onward():
                    item.up().start()

                @pl.when((level > z) & (z > 0))
                def back():
                    item.down().start()
            else:
                @pl.when(k + pieces < items)
                def following():
                    Item(k + pieces).straight().start()

            for jx in inner_x:
                item.to_x(jx).start()
            for jy in inner_y:
                item.to_y(jy).start()
            item.to_core(0, 0).start()

    def edges(k):
        item = Item(k)
        for jx in inner_x:
            item.to_x(jx).wait_recv()

            @pl.when(item.mine & item.even)
            def pass_a():
                for jy in inner_y:
                    item.corner_a(jx, jy).start()

            item.to_core(jx, 0).start()
        for jy in inner_y:
            item.to_y(jy).wait_recv()

            @pl.when(item.mine & jnp.logical_not(item.even))
            def pass_b():
                for jx in inner_x:
                    item.corner_b(jx, jy).start()

            item.to_core(0, jy).start()

    def corners(k):
        item = Item(k)

        @pl.when(item.mine)
        def mine_now():
            for jx in inner_x:
                for jy in inner_y:
                    item.corner_a(jx, jy).wait_recv()
                    if chain:
                        item.corner_z(jx, jy).start()
                    item.to_core(jx, jy).start()

    def handed(k):
        item = Item(k)

        @pl.when(jnp.logical_not(item.mine))
        def from_partner():
            for jx in inner_x:
                for jy in inner_y:
                    item.corner_z(jx, jy).wait_recv()
                    item.to_core(jx, jy).start()

    spots = xs * ys
    lag_edge, lag_corner = (2, 4) if chain else (1, 3)
    lag_handed = pieces + 6 if chain else lag_corner
    lag_end = lag_handed + 1

    def tick(t, carry):
        @pl.when(t < items)
        def arrivals():
            columns(t)

        @pl.when((t >= lag_edge) & (t < items + lag_edge))
        def sides():
            edges(t - lag_edge)

        @pl.when((t >= lag_corner) & (t < items + lag_corner))
        def far():
            corners(t - lag_corner)

        if chain:
            @pl.when((t >= lag_handed) & (t < items + lag_handed))
            def others():
                handed(t - lag_handed)

        def visit(e, carry):
            jc = lax.div(e, spots)
            spot = lax.rem(e, spots)
            jx, jy = lax.rem(spot, xs), lax.div(spot, xs)
            far = jnp.minimum(jx, 1) + jnp.minimum(jy, 1)
            lag = jnp.where(far == 0, 1, jnp.where(far == 1, lag_edge + 1, lag_end))
            k = t - lag

            @pl.when((k >= 0) & (k < items))
            def valid():
                item = Item(k)

                @pl.when(jc == 1)
                def shared():
                    item.to_core(jx, jy).wait_recv()

                if consume is not None:
                    consume(place.block(jx, jy, item.level, jc), item.level, item.piece)

            return carry

        return lax.fori_loop(0, 2 * spots, visit, carry)

    if ready is not None:
        own.wait()
        ready()
    lax.fori_loop(0, items + lag_end, tick, 0)

    def close(k, carry):
        item = Item(k)
        level = item.level
        if chain:
            @pl.when((level <= z) & (z + 1 < members))
            def onward():
                item.up().wait_send()

            @pl.when((level >= z) & (z > 0))
            def back():
                item.down().wait_send()
        else:
            @pl.when(k >= pieces)
            def sent():
                item.straight().wait_send()

        for jx in inner_x:
            item.to_x(jx).wait_send()
        for jy in inner_y:
            item.to_y(jy).wait_send()
        for jx in range(xs):
            for jy in range(ys):
                item.to_core(jx, jy).wait_send()

        @pl.when(item.mine)
        def mine_done():
            for jx in inner_x:
                for jy in inner_y:
                    item.corner_a(jx, jy).wait_send()
                    if chain:
                        item.corner_z(jx, jy).wait_send()

        return carry

    lax.fori_loop(0, items, close, 0)
    if ready is None:
        own.wait()


def spread_kernel(groups, members, chain, pieces, src, out, *sems):
    place = Place(groups, members)
    greet(place)
    spread_body(place, chain, pieces, src, out, sems, None)


def spread(src, groups, members, collective_id, chain, pieces):
    count, rows, width = src.shape
    return pl.pallas_call(
        functools.partial(spread_kernel, groups, members, chain, pieces),
        out_shape=jax.ShapeDtypeStruct((groups * members, rows, width), src.dtype),
        in_specs=[pl.BlockSpec(memory_space=pl.ANY)],
        out_specs=pl.BlockSpec(memory_space=pl.ANY),
        scratch_shapes=spread_sems(groups, members, pieces),
        compiler_params=pltpu.CompilerParams(collective_id=collective_id, has_side_effects=True),
        cost_estimate=pl.CostEstimate(
            flops=0, bytes_accessed=4 * groups * members * rows * width, transcendentals=0
        ),
    )(src)


def tile_of(part_rows, size=TILE):
    return size if part_rows % size == 0 else part_rows


def opening_kernel(groups, members, facts_ref, table_ref, facts_out, low_ref, own_sem, send_sems, recv_sems):
    devices = groups * members
    tiles = pl.num_programs(1)
    step = pl.program_id(0) * tiles + pl.program_id(1)
    last = pl.num_programs(0) * tiles - 1
    me = lax.axis_index("grp") * members + lax.axis_index("cli")

    def other(j):
        return lax.rem(me + j, devices)

    def place(device):
        return (lax.div(device, members), lax.rem(device, members))

    def give(j):
        return pltpu.make_async_remote_copy(
            src_ref=facts_ref, dst_ref=facts_out.at[me], send_sem=send_sems.at[j], recv_sem=recv_sems.at[j],
            device_id=place(other(j)), device_id_type=MESH,
        )

    own = pltpu.make_async_copy(facts_ref, facts_out.at[me], own_sem)

    @pl.when(step == 0)
    def begin():
        barrier = pltpu.get_barrier_semaphore()

        def hello(j, carry):
            pl.semaphore_signal(barrier, inc=1, device_id=place(other(j)), device_id_type=MESH)
            return carry

        own.start()
        lax.fori_loop(1, devices, hello, 0)

    @pl.when(step == last // 4)
    def exchange():
        def start(j, carry):
            give(j).start()
            return carry

        pl.semaphore_wait(pltpu.get_barrier_semaphore(), devices - 1)
        lax.fori_loop(1, devices, start, 0)

    low_ref[...] = table_ref[...].astype(low_ref.dtype)

    @pl.when(step == last)
    def end():
        def finish(j, carry):
            give(j).wait_send()
            pltpu.make_async_remote_copy(
                src_ref=facts_ref, dst_ref=facts_out.at[lax.rem(me + devices - j, devices)],
                send_sem=send_sems.at[j], recv_sem=recv_sems.at[j], device_id=place(other(j)), device_id_type=MESH,
            ).wait_recv()
            return carry

        lax.fori_loop(1, devices, finish, 0)
        own.wait()


def opening(facts, table, groups, members, collective_id):
    devices = groups * members
    models, part_rows, width = table.shape
    tile_rows = tile_of(part_rows)
    piece = pl.BlockSpec((1, tile_rows, width), lambda m, t: (m, t, 0))
    anywhere = pl.BlockSpec(memory_space=pl.ANY)
    dma = pltpu.SemaphoreType.DMA
    return pl.pallas_call(
        functools.partial(opening_kernel, groups, members),
        out_shape=(
            jax.ShapeDtypeStruct((devices,) + facts.shape, facts.dtype),
            jax.ShapeDtypeStruct(table.shape, jnp.bfloat16),
        ),
        grid=(models, part_rows // tile_rows),
        in_specs=[anywhere, piece],
        out_specs=(anywhere, piece),
        scratch_shapes=[dma, dma((devices,)), dma((devices,))],
        compiler_params=pltpu.CompilerParams(collective_id=collective_id, has_side_effects=True),
        cost_estimate=pl.CostEstimate(flops=0, bytes_accessed=6 * table.size, transcendentals=0),
    )(facts, table)


def score_kernel(groups, members, share, pieces, src, table, target, out, answer, *rest):
    part, pool, stat, inbox, part_sem, out_sems, go_send, go_recv, back_send, back_recv = rest[:10]
    sems = rest[10:]
    devices = groups * members
    place = Place(groups, members)
    load_table = pltpu.make_async_copy(table, part, part_sem)
    load_table.start()
    greet_all(devices, members)
    rows = pool.shape[1]
    size = rows // pieces

    def keep(block, piece):
        here = pl.ds(pl.multiple_of(piece * size, size), size)
        return pltpu.make_async_copy(pool.at[block, here], out.at[block, here], out_sems.at[block, piece])

    def consume(block, level, piece):
        keep(block, piece).start()
        here = pl.ds(pl.multiple_of(piece * size, size), size)
        model = lax.div(level, share)
        wanted = target[lax.div(block, members) * share + lax.rem(level, share), :, here]
        outs = pool[block, here]
        part_rows = part.shape[1]
        tile = tile_of(part_rows)
        marks = lax.broadcasted_iota(jnp.int32, (tile, size), 0)
        tops, totals, hits = [], [], []
        for first in range(0, part_rows, tile):
            logits = project(part[model, pl.ds(first, tile)], outs)
            hit = jnp.where(marks == wanted - first, logits, 0.0).reshape(-1, 8, size)
            hits.append(jnp.sum(hit, axis=0))
            logits = logits.reshape(-1, 8, size)
            top = jnp.max(logits, axis=0)
            tops.append(top)
            totals.append(jnp.sum(jnp.exp(logits - top[None]), axis=0))
        highest = jnp.max(functools.reduce(jnp.maximum, tops), axis=0, keepdims=True)
        total = sum(t * jnp.exp(m - highest) for t, m in zip(totals, tops))
        stat[block, 0:1, here] = highest + jnp.log(jnp.sum(total, axis=0, keepdims=True))
        stat[block, 1:2, here] = jnp.sum(sum(hits), axis=0, keepdims=True)

    spread_body(place, True, pieces, src, pool, sems, consume, load_table.wait)

    me = place.block(0, 0, place.cli)

    def device(index):
        return (lax.div(index, members), lax.rem(index, members))

    def ahead(j):
        return lax.rem(me + j, devices)

    def behind(j):
        return lax.rem(me + devices - j, devices)

    def go(j, source, target):
        return pltpu.make_async_remote_copy(
            src_ref=stat.at[source], dst_ref=inbox.at[target], send_sem=go_send.at[j], recv_sem=go_recv.at[j],
            device_id=device(ahead(j)), device_id_type=MESH,
        )

    def back(j, source):
        return pltpu.make_async_remote_copy(
            src_ref=answer.at[source], dst_ref=answer.at[source], send_sem=back_send.at[j],
            recv_sem=back_recv.at[j], device_id=device(ahead(j)), device_id_type=MESH,
        )

    def loop(step):
        def run(j, carry):
            step(j)
            return carry

        lax.fori_loop(1, devices, run, 0)

    loop(lambda j: go(j, ahead(j), me).start())
    inbox[me] = stat[me]
    loop(lambda j: go(j, me, behind(j)).wait_recv())
    logs = inbox[:, 0, :]
    top = jnp.max(logs, axis=0, keepdims=True)
    log_total = top + jnp.log(jnp.sum(jnp.exp(logs - top), axis=0, keepdims=True))
    answer[me, 0:1, :] = log_total
    answer[me, 1:2, :] = log_total - jnp.sum(inbox[:, 1, :], axis=0, keepdims=True)
    loop(lambda j: back(j, me).start())
    loop(lambda j: back(j, behind(j)).wait_recv())
    loop(lambda j: go(j, ahead(j), me).wait_send())
    loop(lambda j: back(j, me).wait_send())

    def close(block, carry):
        for piece in range(pieces):
            keep(block, piece).wait()
        return carry

    lax.fori_loop(0, groups * members, close, 0)


def spread_score(src, table_low, target_blocks, groups, members, share, collective_id, pieces=2):
    _, rows, width = src.shape
    blocks = groups * members
    return pl.pallas_call(
        functools.partial(score_kernel, groups, members, share, pieces),
        out_shape=(
            jax.ShapeDtypeStruct((blocks, rows, width), src.dtype),
            jax.ShapeDtypeStruct((blocks, 2, rows), jnp.float32),
        ),
        in_specs=[
            pl.BlockSpec(memory_space=pl.ANY),
            pl.BlockSpec(memory_space=pl.ANY),
            pl.BlockSpec(memory_space=pltpu.VMEM),
        ],
        out_specs=(pl.BlockSpec(memory_space=pl.ANY), pl.BlockSpec(memory_space=pltpu.VMEM)),
        scratch_shapes=[
            pltpu.VMEM(table_low.shape, table_low.dtype),
            pltpu.VMEM((blocks, rows, width), src.dtype),
            pltpu.VMEM((blocks, 2, rows), jnp.float32),
            pltpu.VMEM((blocks, 2, rows), jnp.float32),
            pltpu.SemaphoreType.DMA,
            pltpu.SemaphoreType.DMA((blocks, pieces)),
        ]
        + [pltpu.SemaphoreType.DMA((blocks,))] * 4
        + spread_sems(groups, members, pieces),
        compiler_params=pltpu.CompilerParams(
            collective_id=collective_id, has_side_effects=True, vmem_limit_bytes=60 * MIB
        ),
        cost_estimate=pl.CostEstimate(
            flops=2 * blocks * rows * table_low.shape[1] * width,
            bytes_accessed=2 * blocks * rows * width * 2,
            transcendentals=blocks * rows * table_low.shape[1],
        ),
    )(src, table_low, target_blocks)


def stats_kernel(outs_ref, table_ref, target_ref, stat_ref):
    logits = project(table_ref[0], outs_ref[0])
    highest = jnp.max(logits, axis=0, keepdims=True)
    total = jnp.sum(jnp.exp(logits - highest), axis=0, keepdims=True)
    rows = lax.broadcasted_iota(jnp.int32, logits.shape, 0)
    hit = jnp.sum(jnp.where(rows == target_ref[0], logits, 0.0), axis=0, keepdims=True)
    stat_ref[0, 0:1, :] = highest + jnp.log(total)
    stat_ref[0, 1:2, :] = hit


def head_stats(outs_all, table_low, target_blocks, groups, members, share):
    blocks, rows, width = outs_all.shape
    part_rows = table_low.shape[1]
    return pl.pallas_call(
        stats_kernel,
        out_shape=jax.ShapeDtypeStruct((blocks, 2, rows), jnp.float32),
        grid=(members, groups),
        in_specs=[
            pl.BlockSpec((1, rows, width), lambda z, g: (g * members + z, 0, 0)),
            pl.BlockSpec((1, part_rows, width), lambda z, g: (z // share, 0, 0)),
            pl.BlockSpec((1, 1, rows), lambda z, g: (g * share + z % share, 0, 0)),
        ],
        out_specs=pl.BlockSpec((1, 2, rows), lambda z, g: (g * members + z, 0, 0)),
        compiler_params=pltpu.CompilerParams(vmem_limit_bytes=56 * MIB),
        cost_estimate=pl.CostEstimate(
            flops=2 * blocks * rows * part_rows * width,
            bytes_accessed=2 * outs_all.size + 2 * table_low.size,
            transcendentals=blocks * rows * part_rows,
        ),
    )(outs_all, table_low, target_blocks)


def collect_kernel(groups, members, source, out, work, from_core, from_x, from_y, then_y, then_x, from_z, *sems):
    (load_sem, core_send, core_recv, x_send, x_recv, y_send, y_recv, yy_send, yy_recv, xx_send, xx_recv, z_send,
     z_recv, g_send, g_recv) = sems
    place = Place(groups, members)
    greet(place)
    xs, ys = place.xs, place.ys
    half = members // 2
    z = place.cli
    order = sorted(
        ((jx, jy) for jx in range(xs) for jy in range(ys)), key=lambda spot: -(spot[0] > 0) - (spot[1] > 0)
    )
    started = []

    def send(source_ref, target_ref, send_sem, recv_sem, device):
        copy = pltpu.make_async_remote_copy(
            src_ref=source_ref, dst_ref=target_ref, send_sem=send_sem, recv_sem=recv_sem, device_id=device,
            device_id_type=MESH,
        )
        copy.start()
        started.append(copy)

    def arrival(target_ref, send_sem, recv_sem, device):
        pltpu.make_async_remote_copy(
            src_ref=target_ref, dst_ref=target_ref, send_sem=send_sem, recv_sem=recv_sem, device_id=device,
            device_id_type=MESH,
        ).wait_recv()

    def add(ref, others):
        total = ref[...].astype(jnp.float32)
        for other in others:
            total = total + other[...].astype(jnp.float32)
        ref[...] = total.astype(ref.dtype)

    def clients(p):
        return (p, p + half)

    spots = [(jy * xs + jx, jx, jy) for jx, jy in order]
    loads = {}
    for p in range(half):
        for k, jx, jy in spots:
            for c in clients(p):
                send(
                    source.at[place.group(jx, jy, 1) * members + c], from_core.at[k, c], core_send.at[k, c],
                    core_recv.at[k, c], place.peer(jc=1),
                )
                loads[k, c] = pltpu.make_async_copy(
                    source.at[place.group(jx, jy, 0) * members + c], work.at[k, c], load_sem.at[k, c]
                )
                loads[k, c].start()
    for p in range(half):
        a, b = clients(p)
        for k, jx, jy in spots:
            for c in (a, b):
                loads[k, c].wait()
                arrival(from_core.at[k, c], core_send.at[k, c], core_recv.at[k, c], place.peer(jc=1))
                add(work.at[k, c], [from_core.at[k, c]])
            if jx:
                send(work.at[k, a], from_x.at[p, jx, jy], x_send.at[p, jx, jy], x_recv.at[p, jx, jy], place.peer(jx=jx))
            if jy:
                send(work.at[k, b], from_y.at[p, jx, jy], y_send.at[p, jx, jy], y_recv.at[p, jx, jy], place.peer(jy=jy))

    def second(p):
        a, b = clients(p)
        for jy in reversed(range(ys)):
            k = jy * xs
            for jx in range(1, xs):
                arrival(from_x.at[p, jx, jy], x_send.at[p, jx, jy], x_recv.at[p, jx, jy], place.peer(jx=jx))
            add(work.at[k, a], [from_x.at[p, jx, jy] for jx in range(1, xs)])
            if jy:
                send(work.at[k, a], then_y.at[p, jy], yy_send.at[p, jy], yy_recv.at[p, jy], place.peer(jy=jy))
        for jx in reversed(range(xs)):
            for jy in range(1, ys):
                arrival(from_y.at[p, jx, jy], y_send.at[p, jx, jy], y_recv.at[p, jx, jy], place.peer(jy=jy))
            add(work.at[jx, b], [from_y.at[p, jx, jy] for jy in range(1, ys)])
            if jx:
                send(work.at[jx, b], then_x.at[p, jx], xx_send.at[p, jx], xx_recv.at[p, jx], place.peer(jx=jx))

    def third(p):
        a, b = clients(p)
        for jy in range(1, ys):
            arrival(then_y.at[p, jy], yy_send.at[p, jy], yy_recv.at[p, jy], place.peer(jy=jy))
        add(work.at[0, a], [then_y.at[p, jy] for jy in range(1, ys)])
        for jx in range(1, xs):
            arrival(then_x.at[p, jx], xx_send.at[p, jx], xx_recv.at[p, jx], place.peer(jx=jx))
        add(work.at[0, b], [then_x.at[p, jx] for jx in range(1, xs)])
        for c in (a, b):
            @pl.when(z != c)
            def give():
                pltpu.make_async_remote_copy(
                    src_ref=work.at[0, c], dst_ref=from_z.at[z], send_sem=z_send.at[c], recv_sem=z_recv.at[z],
                    device_id=place.level(c), device_id_type=MESH,
                ).start()

    for p in range(half + 1):
        if p < half:
            second(p)
        if p:
            third(p - 1)
    total = work[0, z].astype(jnp.float32)
    for j in range(1, members):
        level = lax.rem(z + members - j, members)
        arrival(from_z.at[level], z_send.at[level], z_recv.at[level], place.level(level))
        total = total + from_z[level].astype(jnp.float32)
    out[z] = total.astype(out.dtype)
    for j in range(1, members):
        send(out.at[z], out.at[z], g_send.at[j], g_recv.at[j], place.level(lax.rem(z + j, members)))
    for j in range(1, members):
        level = lax.rem(z + members - j, members)
        arrival(out.at[level], g_send.at[j], g_recv.at[j], place.level(level))
    for copy in started:
        copy.wait_send()
    for c in range(members):
        @pl.when(z != c)
        def given():
            pltpu.make_async_remote_copy(
                src_ref=work.at[0, c], dst_ref=from_z.at[z], send_sem=z_send.at[c], recv_sem=z_recv.at[z],
                device_id=place.level(c), device_id_type=MESH,
            ).wait_send()


def collect(parts, groups, members, collective_id):
    _, seq_len, width = parts.shape
    xs, ys, half = groups // 4, 2, members // 2
    dma = pltpu.SemaphoreType.DMA

    def held(*shape):
        return pltpu.VMEM(shape + (seq_len, width), parts.dtype)

    return pl.pallas_call(
        functools.partial(collect_kernel, groups, members),
        out_shape=jax.ShapeDtypeStruct((members, seq_len, width), parts.dtype),
        in_specs=[pl.BlockSpec(memory_space=pl.ANY)],
        out_specs=pl.BlockSpec(memory_space=pltpu.VMEM),
        scratch_shapes=[
            held(xs * ys, members),
            held(xs * ys, members),
            held(half, xs, ys),
            held(half, xs, ys),
            held(half, ys),
            held(half, xs),
            held(members),
        ]
        + [dma((xs * ys, members))] * 3
        + [dma((half, xs, ys))] * 4
        + [dma((half, ys))] * 2
        + [dma((half, xs))] * 2
        + [dma((members,))] * 4,
        compiler_params=pltpu.CompilerParams(
            collective_id=collective_id, has_side_effects=True, vmem_limit_bytes=56 * MIB
        ),
        cost_estimate=pl.CostEstimate(
            flops=0, bytes_accessed=4 * groups * members * seq_len * width, transcendentals=0
        ),
    )(parts)


def unpack_kernel(start, part, at_ref, pool_ref, weights_ref, rows_ref):
    step = pl.program_id(0)
    owners, slab, width = pool_ref.shape
    weights_ref[...] = jnp.concatenate([pool_ref[j, :part] for j in range(owners)], axis=0)
    count = slab - start
    columns = lax.broadcasted_iota(jnp.int32, (1, count), 1) + start
    columns = jnp.concatenate([columns + j * slab for j in range(owners)], axis=1)
    hits = (columns == at_ref[...] - step * owners * slab).astype(jnp.float32).astype(jnp.bfloat16)
    found = product(hits, jnp.concatenate([pool_ref[j, start:] for j in range(owners)], axis=0))

    @pl.when(step == 0)
    def begin():
        rows_ref[...] = found

    @pl.when(step > 0)
    def more():
        rows_ref[...] += found


def unpack(pool, part, at):
    devices, slab, width = pool.shape
    owners = max(4, 8 // math.gcd(part, 8))
    start = part // 16 * 16
    tokens = at.shape[0]
    return pl.pallas_call(
        functools.partial(unpack_kernel, start, part),
        out_shape=(
            jax.ShapeDtypeStruct((devices * part, width), pool.dtype),
            jax.ShapeDtypeStruct((tokens, width), jnp.float32),
        ),
        grid=(devices // owners,),
        in_specs=[
            pl.BlockSpec((tokens, 1), lambda i: (0, 0)),
            pl.BlockSpec((owners, slab, width), lambda i: (i, 0, 0)),
        ],
        out_specs=(
            pl.BlockSpec((owners * part, width), lambda i: (i, 0)),
            pl.BlockSpec((tokens, width), lambda i: (0, 0)),
        ),
        compiler_params=pltpu.CompilerParams(vmem_limit_bytes=40 * MIB),
        cost_estimate=pl.CostEstimate(
            flops=2 * devices * tokens * (slab - start) * width,
            bytes_accessed=4 * pool.size,
            transcendentals=0,
        ),
    )(at, pool)


def back_kernel(
    model_ref, fresh_ref, used_ref, piece_ref, place_ref, *rest
):
    pieces = rest[:QUAD]
    table_ref, info_ref, target_ref, d_outs_ref, grad_ref, held, sems = rest[QUAD:]
    step = pl.program_id(0)
    seq_len = pieces[0].shape[1]
    slot = lax.rem(step, 2)

    def leave(which, where, i):
        return pltpu.make_async_copy(held.at[which, i], d_outs_ref.at[where], sems.at[which, i])

    def settle(which):
        for i in range(QUAD):
            leave(which, 0, i).wait()

    @pl.when(step < used_ref[0])
    def work():
        @pl.when(step >= 2)
        def reuse():
            settle(slot)

        @pl.when(fresh_ref[step] == 1)
        def start():
            grad_ref[...] = jnp.zeros_like(grad_ref)

        outs = jnp.concatenate([piece[0] for piece in pieces], axis=0)
        part_rows = table_ref.shape[1]
        size = tile_of(part_rows, 2 * TILE)
        d_outs = jnp.zeros(outs.shape, jnp.float32)
        for first_row in range(0, part_rows, size):
            here = pl.ds(first_row, size)
            table_rows = table_ref[0, here]
            logits = project(table_rows, outs)
            rows = lax.broadcasted_iota(jnp.int32, logits.shape, 0) + first_row
            soft = jnp.exp(logits - info_ref[0, 0:1, :])
            soft = jnp.where(rows == target_ref[0], soft - 1.0, soft)
            d_logits = (info_ref[0, 1:2, :] * soft).astype(jnp.bfloat16)
            d_outs = d_outs + outer_rows(d_logits, table_rows)
            grad_ref[0, here] += product(d_logits, outs)
        for i in range(QUAD):
            held[slot, i] = d_outs[i * seq_len : (i + 1) * seq_len].astype(held.dtype)
            leave(slot, place_ref[QUAD * step + i], i).start()

        @pl.when(step == used_ref[0] - 1)
        def drain():
            settle(slot)

            @pl.when(step >= 1)
            def earlier():
                settle(1 - slot)


def head_back(outs_pieces, table_low, model_of, fresh, used, piece_at, place, info, target):
    steps = model_of.shape[0]
    models, part_rows, width = table_low.shape
    seq_len = outs_pieces.shape[1]
    tokens = QUAD * seq_len

    def piece(i):
        return pl.BlockSpec((1, seq_len, width), lambda s, m, f, u, q, p: (q[QUAD * s + i], 0, 0))

    return pl.pallas_call(
        back_kernel,
        out_shape=(
            jax.ShapeDtypeStruct((QUAD * steps, seq_len, width), jnp.bfloat16),
            jax.ShapeDtypeStruct((models, part_rows, width), jnp.float32),
        ),
        grid_spec=pltpu.PrefetchScalarGridSpec(
            num_scalar_prefetch=5,
            grid=(steps,),
            in_specs=[piece(i) for i in range(QUAD)]
            + [
                pl.BlockSpec((1, part_rows, width), lambda s, m, *_: (m[s], 0, 0)),
                pl.BlockSpec((1, 2, tokens), lambda s, *_: (s, 0, 0)),
                pl.BlockSpec((1, 1, tokens), lambda s, *_: (s, 0, 0)),
            ],
            out_specs=(
                pl.BlockSpec(memory_space=pl.ANY),
                pl.BlockSpec((1, part_rows, width), lambda s, m, *_: (m[s], 0, 0)),
            ),
            scratch_shapes=[
                pltpu.VMEM((2, QUAD, seq_len, width), jnp.bfloat16),
                pltpu.SemaphoreType.DMA((2, QUAD)),
            ],
        ),
        compiler_params=pltpu.CompilerParams(vmem_limit_bytes=56 * MIB),
        cost_estimate=pl.CostEstimate(
            flops=6 * steps * tokens * part_rows * width,
            bytes_accessed=4 * steps * tokens * width + 6 * table_low.size,
            transcendentals=steps * tokens * part_rows,
        ),
    )(model_of, fresh, used, piece_at, place, *([outs_pieces] * QUAD), table_low, info, target)


def finish_kernel(
    first_model, start_ref, end_ref, first_ref, second_ref, d_ref, ids_ref, head_ref, table_ref, momentum_ref, *rest
):
    grad_ref, momentum_new_ref, table_new_ref = rest[-3:]
    model = pl.program_id(0) + first_model
    tile_rows = grad_ref.shape[1]
    tokens = ids_ref.shape[2]
    rows = lax.broadcasted_iota(jnp.int32, (tile_rows, tokens), 0) + pl.program_id(1) * tile_rows
    grad_ref[0] = head_ref[0]

    def pair(step, carry):
        hits = (rows == ids_ref[step]).astype(jnp.float32).astype(jnp.bfloat16)
        outs = jnp.concatenate([d_ref[first_ref[step]], d_ref[second_ref[step]]], axis=0)
        grad_ref[0] += product(hits, outs)
        return carry

    lax.fori_loop(start_ref[model], end_ref[model], pair, 0)
    renewed, fresh_table = update(table_ref[0], momentum_ref[0], grad_ref[0], table_rate)
    momentum_new_ref[0] = renewed
    table_new_ref[0] = fresh_table


def finish_table(d_inputs, head_grad, table, momentum, schedule, ids, first_model, count, earlier):
    models, part_rows, width = table.shape
    tile_rows = tile_of(part_rows)
    state = jax.ShapeDtypeStruct(table.shape, jnp.float32)
    piece = pl.BlockSpec((1, tile_rows, width), lambda m, t, *_: (m + first_model, t, 0))
    whole = pl.BlockSpec(memory_space=pltpu.VMEM)
    return pl.pallas_call(
        functools.partial(finish_kernel, first_model),
        out_shape=(state, state, state),
        grid_spec=pltpu.PrefetchScalarGridSpec(
            num_scalar_prefetch=4,
            grid=(count, part_rows // tile_rows),
            in_specs=[whole, whole, piece, piece, piece]
            + [pl.BlockSpec(memory_space=pl.ANY)] * len(earlier),
            out_specs=(piece, piece, piece),
        ),
        input_output_aliases={9 + i: i for i in range(len(earlier))},
        compiler_params=pltpu.CompilerParams(vmem_limit_bytes=56 * MIB),
        cost_estimate=pl.CostEstimate(
            flops=2 * d_inputs.size * part_rows * count // models,
            bytes_accessed=24 * count * part_rows * width,
            transcendentals=0,
        ),
    )(*schedule, d_inputs, ids, head_grad, table, momentum, *earlier)


def stack_kernel(gradient_ref, weight_ref, momentum_ref, grad_ref, renewed_ref, fresh_ref):
    for model in range(gradient_ref.shape[0]):
        gradient = gradient_ref[model].astype(jnp.float32)
        renewed, fresh = update(weight_ref[:, model, :], momentum_ref[:, model, :], gradient, stack_rate)
        grad_ref[:, model, :] = gradient
        renewed_ref[:, model, :] = renewed
        fresh_ref[:, model, :] = fresh


def update_stack(gradient, weight, momentum):
    turn = functools.partial(jnp.transpose, axes=(1, 0, 2))
    turned = jax.ShapeDtypeStruct(turn(weight).shape, jnp.float32)
    whole = pl.BlockSpec(memory_space=pltpu.VMEM)
    results = pl.pallas_call(
        stack_kernel,
        out_shape=(turned, turned, turned),
        in_specs=[whole] * 3,
        out_specs=(whole,) * 3,
        compiler_params=pltpu.CompilerParams(vmem_limit_bytes=56 * MIB),
        cost_estimate=pl.CostEstimate(
            flops=6 * weight.size, bytes_accessed=22 * weight.size, transcendentals=0
        ),
    )(gradient, turn(weight), turn(momentum))
    return tuple(turn(result) for result in results)


def body(
    token_ids,
    target_ids,
    segment_ids,
    chosen,
    table,
    table_momentum,
    stack,
    stack_momentum,
    vectors,
    vector_momentum,
):
    both = ("grp", "cli")
    models, block_rows, model_width = table.shape
    stack_part = stack.shape[1]
    seq_len = token_ids.shape[1]
    groups = lax.axis_size("grp")
    members = lax.axis_size("cli")
    devices = groups * members
    share = members // models
    local = members // share
    device_index = lax.axis_index(both)
    group_index = lax.axis_index("grp")
    member_index = lax.axis_index("cli")
    model_own = member_index // share
    part_own = member_index % share
    model_range = jnp.arange(models, dtype=jnp.int32)

    def per_member(rows):
        return jnp.repeat(rows, share, axis=0) if share > 1 else rows

    slab = -(-(stack_part + ROUND_ROWS) // SLAB_STEP) * SLAB_STEP
    round_rows = slab - stack_part

    facts = jnp.concatenate([token_ids[0], target_ids[0], segment_ids[0], chosen])
    facts = jnp.pad(facts, (0, -facts.size % LANES))[None]
    facts, table_low = opening(facts, table, groups, members, 5)
    facts = facts[:, 0]
    tokens = facts[:, :seq_len]
    targets = facts[:, seq_len : 2 * seq_len]
    segments = facts[:, 2 * seq_len : 3 * seq_len]
    choices = facts[:, 3 * seq_len]
    valid = jnp.concatenate(
        [
            (segments[:, :-1] == segments[:, 1:]).astype(jnp.float32),
            jnp.zeros((devices, 1), jnp.float32),
        ],
        axis=1,
    )
    counts = jnp.sum(valid, axis=1)
    choice_table = (choices[:, None] == model_range[None, :]).astype(jnp.float32)
    totals = jnp.sum(choice_table * counts[:, None], axis=0)
    total_of = jnp.sum(choice_table * totals[None, :], axis=1)

    fine = 16 if block_rows % 64 else 64
    coarse = block_rows // fine
    flat_tokens = tokens.reshape(-1)
    high_hot = (
        (flat_tokens // fine)[:, None] == jnp.arange(devices * coarse, dtype=jnp.int32)[None, :]
    ).astype(jnp.bfloat16)
    low_hot = ((flat_tokens % fine)[:, None] == jnp.arange(fine, dtype=jnp.int32)[None, :]).astype(
        jnp.bfloat16
    )
    seen = (outer_rows(high_hot, low_hot) > 0).astype(jnp.float32)
    before = product(
        seen.astype(jnp.bfloat16),
        jnp.triu(jnp.ones((fine, fine), jnp.bfloat16), 1),
    )
    sums = jnp.sum(seen, axis=1).reshape(devices, coarse)
    uniques = jnp.sum(sums, axis=1)
    ahead = jnp.sum(
        jnp.where(
            jnp.arange(coarse)[None, None, :] < jnp.arange(coarse)[None, :, None],
            sums[:, None, :],
            0.0,
        ),
        axis=2,
    )
    places = before + ahead.reshape(-1, 1)
    rounds = jnp.max(jnp.ceil(uniques / round_rows)).astype(jnp.int32)
    own_places = lax.dynamic_slice(places, (device_index * coarse, 0), (coarse, fine)).reshape(-1)
    own_seen = lax.dynamic_slice(seen, (device_index * coarse, 0), (coarse, fine)).reshape(-1)
    own_places = jnp.where(own_seen > 0, own_places, -1.0).astype(jnp.int32)
    first_client = group_index * members + part_own * local
    my_tokens = lax.dynamic_slice(tokens, (first_client, 0), (local, seq_len)).reshape(-1)
    my_segments = lax.dynamic_slice(segments, (first_client, 0), (local, seq_len))
    my_choices = lax.dynamic_slice(choices, (first_client,), (local,))
    my_high = (
        (my_tokens // fine)[:, None] == jnp.arange(devices * coarse, dtype=jnp.int32)[None, :]
    ).astype(jnp.bfloat16)
    my_low = (my_tokens % fine)[:, None] == jnp.arange(fine, dtype=jnp.int32)[None, :]
    split_places = jnp.concatenate(
        [jnp.floor(places / 64.0), places - 64.0 * jnp.floor(places / 64.0)], axis=1
    ).astype(jnp.bfloat16)
    picked_places = product(my_high, split_places)
    picked_places = 64.0 * picked_places[:, :fine] + picked_places[:, fine:]
    my_places = jnp.sum(jnp.where(my_low, picked_places, 0.0), axis=1).astype(jnp.int32)
    my_owner = my_tokens // block_rows

    def offered(start):
        wanted = jnp.arange(round_rows, dtype=jnp.int32) + start
        pick = (own_places[None, :] == wanted[:, None]).astype(jnp.bfloat16)
        rows = jnp.einsum("ur,krd->kud", pick, table_low, preferred_element_type=jnp.float32)
        return rows.astype(jnp.bfloat16)

    def inside(start):
        offset = my_places - start
        return ((offset >= 0) & (offset < round_rows), offset)

    def another(carry):
        index, embedded = carry
        start = index * round_rows
        turned = lax.all_to_all(per_member(offered(start)), "cli", 0, 0, tiled=True)
        pool = lax.all_gather(turned, "grp", axis=0, tiled=True).reshape(-1, model_width)
        here, offset = inside(start)
        found = jnp.take(pool, jnp.where(here, my_owner * round_rows + offset, 0), axis=0)
        return (index + 1, jnp.where(here[:, None], found.astype(jnp.float32), embedded))

    slabs = jnp.concatenate([stack.astype(jnp.bfloat16), offered(0)], axis=1)
    pool = spread(per_member(slabs), groups, members, 1, False, 2)
    here, offset = inside(0)
    at = jnp.where(here, my_owner * slab + stack_part + offset, -1)
    weights, embedded = unpack(pool, stack_part, at[:, None])
    _, embedded = lax.while_loop(
        lambda carry: carry[0] < rounds, another, (jnp.int32(1), embedded)
    )
    vector_one = lax.dynamic_index_in_dim(vectors, model_own, 0, keepdims=False)
    inputs = embedded + jnp.tile(weights[12 * model_width :].astype(jnp.float32), (local, 1))
    saved = layer_forward(weights, vector_one, inputs, my_segments)
    normed_out = saved[11]

    target_local = targets - device_index * block_rows
    target_local = jnp.where((target_local >= 0) & (target_local < block_rows), target_local, -1)
    target_blocks = target_local.reshape(groups * share, 1, local * seq_len)
    if devices * normed_out.size * 2 <= POOL_BYTES:
        outs_all, everything = spread_score(
            normed_out[None], table_low, target_blocks, groups, members, share, 2
        )
    else:
        outs_all = spread(normed_out[None], groups, members, 2, True, 2)
        stats = head_stats(outs_all, table_low, target_blocks, groups, members, share)
        shares = lax.all_to_all(stats, both, 0, 0, tiled=True)
        log_total = jax.nn.logsumexp(shares[:, 0], axis=0)
        token_loss = log_total - jnp.sum(shares[:, 1], axis=0)
        everything = share_all(jnp.stack([log_total, token_loss]), both, devices)
    everything = (
        everything.reshape(groups, models, share, 2, local, seq_len)
        .transpose(3, 1, 0, 2, 4, 5)
        .reshape(2, models, devices, seq_len)
    )
    all_losses = jnp.sum(everything[1] * valid[None], axis=2)
    loss = jnp.sum(choice_table.T * all_losses / total_of[None, :])
    client_losses = lax.dynamic_slice(
        (all_losses / counts[None, :]).T, (device_index, 0), (1, models)
    )
    chosen_total = jnp.sum(choice_table.T[:, :, None] * everything[0], axis=0)

    numbers = jnp.sum(choice_table, axis=0)
    padded = QUAD * jnp.ceil(numbers / QUAD)
    offsets = jnp.cumsum(padded) - padded
    earlier = (
        jnp.arange(devices)[None, :] < jnp.arange(devices)[:, None]
    ) & (choices[None, :] == choices[:, None])
    slot_of = jnp.sum(choice_table * offsets[None, :], axis=1) + jnp.sum(
        earlier.astype(jnp.float32), axis=1
    )
    steps = (devices + (QUAD - 1) * models) // QUAD
    slots = QUAD * steps
    tokens_step = QUAD * seq_len
    at_slot = jnp.arange(slots)[:, None] == slot_of.astype(jnp.int32)[None, :]
    filled = jnp.any(at_slot, axis=1)
    client_at = jnp.sum(jnp.where(at_slot, jnp.arange(devices)[None, :], 0), axis=1).astype(
        jnp.int32
    )
    step_start = float(QUAD) * jnp.arange(steps)
    used = (jnp.sum(padded) / QUAD).astype(jnp.int32)[None]
    model_of = (
        jnp.sum((step_start[:, None] >= offsets[None, :]).astype(jnp.int32), axis=1) - 1
    ).astype(jnp.int32)
    fresh = jnp.concatenate(
        [jnp.ones((1,), jnp.int32), (model_of[1:] != model_of[:-1]).astype(jnp.int32)]
    )
    within = client_at % members
    piece_at = (
        (client_at // members * members + jnp.repeat(model_of, QUAD) * share + within // local) * local
        + within % local
    ).astype(jnp.int32)
    weight_rows = valid / total_of[:, None]
    slot_log = jnp.where(filled[:, None], jnp.take(chosen_total, client_at, axis=0), 1e30)
    slot_weight = jnp.where(filled[:, None], jnp.take(weight_rows, client_at, axis=0), 0.0)
    slot_info = jnp.stack(
        [slot_log.reshape(steps, tokens_step), slot_weight.reshape(steps, tokens_step)], axis=1
    )
    slot_target = jnp.where(filled[:, None], jnp.take(target_local, client_at, axis=0), -1)
    spare = devices + jnp.cumsum(1 - filled.astype(jnp.int32)) - 1
    d_outs, head_grad = head_back(
        outs_all.reshape(-1, seq_len, model_width),
        table_low,
        model_of,
        fresh,
        used,
        piece_at,
        jnp.where(filled, client_at, spare).astype(jnp.int32),
        slot_info,
        slot_target.reshape(steps, 1, tokens_step),
    )
    d_group = collect(d_outs, groups, members, 4)
    d_mine = lax.dynamic_slice(
        d_group, (part_own * local, 0, 0), (local, seq_len, model_width)
    ).astype(jnp.float32)
    d_final = jnp.where((my_choices == model_own)[:, None, None], d_mine, 0.0).reshape(
        local * seq_len, model_width
    )
    pairs, grad_places, vector_rows, d_inputs = layer_backward(
        weights, vector_one, inputs, my_segments, saved, d_final
    )
    d_wide = d_inputs.astype(jnp.bfloat16)
    if share > 1:
        d_wide = lax.dynamic_update_slice(
            jnp.zeros((members * seq_len, model_width), jnp.bfloat16),
            d_wide,
            (part_own * local * seq_len, 0),
        )
    d_wide, pairs = lax.optimization_barrier((d_wide, pairs))
    d_turned = lax.all_to_all(
        d_wide.reshape(members, seq_len, model_width), "cli", 0, 0, tiled=True
    )
    stack_rows = jnp.concatenate(
        [outer_rows(left, right).astype(jnp.bfloat16) for left, right in pairs]
        + [grad_places.astype(jnp.bfloat16)],
        axis=0,
    )
    stack_rows, d_turned = lax.optimization_barrier((stack_rows, d_turned))
    stack_sum = lax.psum_scatter(stack_rows, "grp", scatter_dimension=0, tiled=True)
    d_client = jnp.sum(d_turned.astype(jnp.float32), axis=0, keepdims=True).astype(jnp.bfloat16)
    d_all = spread(d_client, groups, members, 3, True, 2)
    token_local = tokens - device_index * block_rows
    token_local = jnp.where((token_local >= 0) & (token_local < block_rows), token_local, -1)
    slot_token = jnp.where(filled[:, None], jnp.take(token_local, client_at, axis=0), -1)
    pair_start = (offsets / 2.0).astype(jnp.int32)
    pair_end = pair_start + jnp.ceil(numbers / 2.0).astype(jnp.int32)
    schedule = (pair_start, pair_end, client_at[0::2], client_at[1::2])
    slot_token = slot_token.reshape(slots // 2, 1, 2 * seq_len)
    lead = models - 1

    states = finish_table(d_all, head_grad, table, table_momentum, schedule, slot_token, 0, lead, ())
    states, vector_rows = lax.optimization_barrier((states, vector_rows))
    vector_piece = vector_rows.size // groups
    vector_part = lax.all_to_all(
        vector_rows.reshape(groups, vector_piece), "grp", 0, 0, tiled=True
    )
    stack_sum, states, vector_part = lax.optimization_barrier((stack_sum, states, vector_part))
    stack_back = lax.all_to_all(
        stack_sum.reshape(members, stack_part, model_width), "cli", 0, 0, tiled=True
    )
    if share > 1:
        stack_back = jnp.sum(
            stack_back.astype(jnp.float32).reshape(models, share, stack_part, model_width), axis=1
        )
    states = finish_table(
        d_all, head_grad, table, table_momentum, schedule, slot_token, lead, models - lead, states
    )
    stack_back, vector_part, states = lax.optimization_barrier((stack_back, vector_part, states))
    table_grad, table_momentum_new, table_new = states
    vector_parts = share_all(jnp.sum(vector_part, axis=0), both, devices)
    vector_grad = jnp.sum(vector_parts.reshape(groups, models, share, vector_piece), axis=2)
    vector_grad = vector_grad.transpose(1, 0, 2).reshape(vectors.shape)
    stack_grad, stack_momentum_new, stack_new = update_stack(stack_back, stack, stack_momentum)
    vector_momentum_new, vector_new = update(vectors, vector_momentum, vector_grad, vector_rate)
    return (
        loss,
        client_losses,
        table_grad,
        table_momentum_new,
        table_new,
        stack_grad,
        stack_momentum_new,
        stack_new,
        vector_grad,
        vector_momentum_new,
        vector_new,
    )


def solution(mesh):
    rows = P(("grp", "cli"), None)
    parts = P(None, ("grp", "cli"), None)
    return jax.shard_map(
        body,
        mesh=mesh,
        in_specs=(rows, rows, rows, P(("grp", "cli")), parts, parts, parts, parts, P(), P()),
        out_specs=(P(), rows, parts, parts, parts, parts, parts, parts, P(), P(), P()),
        check_vma=False,
    )
```
